32 devices in a mesh: dp: 8 (over z, y), fsdp: 4 (over x, core).
Axes of the slice: x: 2, y: 2, z: 4, core: 2. Of those that a mesh axis runs over, the one named last changes fastest.
Arguments:
- pixels: bfloat16 [8, 512, 192], P('dp', 'fsdp'), may hold values from -6 to 6
- targets: bfloat16 [8, 512, 192], P('dp', 'fsdp'), may hold values from 2 to 6
- valid_mask: int32 [8, 512, 192], P('dp', 'fsdp'), may hold values 0 or 1
- lat_weight: float32 [8, 512], P('dp', 'fsdp'), may hold values from 0.1 to 1
- segment_ids: int32 [8, 512], P('dp'), may hold values from 0 to 3, never falling along the last dimension, each value on 1 to 256 neighbouring positions
- present_vars: int32 [8, 48], P('dp'), may hold values from 0 to 1, as said below
- lead_index: int32 [8], P('dp'), may hold values from 0 to 7
- step_count: int32 [1], replicated, may hold values from 1 to 20
- w_agg: float32 [1024, 3072], P(('dp', 'fsdp')), may hold values from -0.1875 to 0.1875
- w_attn: float32 [1024, 4096], P(('dp', 'fsdp')), may hold values from -0.1875 to 0.1875
- w_mlp: float32 [1024, 8192], P(('dp', 'fsdp')), may hold values from -0.1875 to 0.1875
- w_io: float32 [1024, 944], P(('dp', 'fsdp')), may hold values from -3 to 3
- w_small: float32 [1024, 9], P(('dp', 'fsdp')), may hold values from 0.5 to 1.5
- m_agg: float32 [1024, 3072], P(('dp', 'fsdp')), may hold values from -0.00390625 to 0.00390625
- m_attn: float32 [1024, 4096], P(('dp', 'fsdp')), may hold values from -0.00390625 to 0.00390625
- m_mlp: float32 [1024, 8192], P(('dp', 'fsdp')), may hold values from -0.00390625 to 0.00390625
- m_io: float32 [1024, 944], P(('dp', 'fsdp')), may hold values from -0.00390625 to 0.00390625
- m_small: float32 [1024, 9], P(('dp', 'fsdp')), may hold values from -0.015625 to 0.015625
- v_agg: float32 [1024, 3072], P(('dp', 'fsdp')), may hold values from 2.9932032e-08 to 4.789125e-07
- v_attn: float32 [1024, 4096], P(('dp', 'fsdp')), may hold values from 2.9932032e-08 to 4.789125e-07
- v_mlp: float32 [1024, 8192], P(('dp', 'fsdp')), may hold values from 2.9932032e-08 to 4.789125e-07
- v_io: float32 [1024, 944], P(('dp', 'fsdp')), may hold values from 2.9932032e-08 to 4.789125e-07
- v_small: float32 [1024, 9], P(('dp', 'fsdp')), may hold values from 4.789125e-07 to 7.6626e-06
Outputs:
- loss: float32 [], replicated
- grad_norm: float32 [], replicated
- new_agg: float32 [1024, 3072], P(('dp', 'fsdp'))
- new_attn: float32 [1024, 4096], P(('dp', 'fsdp'))
- new_mlp: float32 [1024, 8192], P(('dp', 'fsdp'))
- new_io: float32 [1024, 944], P(('dp', 'fsdp'))
- new_small: float32 [1024, 9], P(('dp', 'fsdp'))
- copy_agg: bfloat16 [1024, 3072], P(('dp', 'fsdp'))
- copy_attn: bfloat16 [1024, 4096], P(('dp', 'fsdp'))
- copy_mlp: bfloat16 [1024, 8192], P(('dp', 'fsdp'))
- copy_io: bfloat16 [1024, 944], P(('dp', 'fsdp'))
- copy_small: bfloat16 [1024, 9], P(('dp', 'fsdp'))
- moment_agg: float32 [1024, 3072], P(('dp', 'fsdp'))
- moment_attn: float32 [1024, 4096], P(('dp', 'fsdp'))
- moment_mlp: float32 [1024, 8192], P(('dp', 'fsdp'))
- moment_io: float32 [1024, 944], P(('dp', 'fsdp'))
- moment_small: float32 [1024, 9], P(('dp', 'fsdp'))
- square_agg: float32 [1024, 3072], P(('dp', 'fsdp'))
- square_attn: float32 [1024, 4096], P(('dp', 'fsdp'))
- square_mlp: float32 [1024, 8192], P(('dp', 'fsdp'))
- square_io: float32 [1024, 944], P(('dp', 'fsdp'))
- square_small: float32 [1024, 9], P(('dp', 'fsdp'))
The draws below stay inside these ranges and needn't reach their ends.
Inputs may be any that keep to these rules, and one draw needn't show every extreme that they name: `present_vars`: every row has at least one present variable.
All inputs are finite; a program needn't handle non-finite values. No bound on the sum of `valid_mask` on one device may be relied on, other than what follows from the above.
Results may differ from the reference program's by a relative error of at most 0.0019.
The reference program's roundings to bfloat16 on the way count: a program that leaves them out, or rounds other values in their place, can miss the bound.
Values may be sent and summed in bfloat16 or wider, within the bound.
A program may use at most 384 MiB of HBM per device.

```python
import math
import jax
import jax.numpy as jnp
import numpy as np
from jax import lax

D = 1024
HEADS = 16
HEAD_DIM = 64
FF = 4096
VARS = 48
PIX = 4
LEAD_STEPS = 8
ROW_LEN = 512
ROWS = 8
IOW = 944
NPARAM = 16704512


def draw_present_vars(key, part):
    first_key = jax.random.fold_in(key, 11)
    second_key = jax.random.fold_in(key, 12)
    base = (jax.random.randint(first_key, (ROWS, VARS), 0, 4) > 0).astype(jnp.int32)
    forced = jax.random.randint(second_key, (ROWS, 1), 0, VARS)
    columns = jnp.arange(VARS, dtype=jnp.int32)[None, :]
    return jnp.maximum(base, (columns == forced).astype(jnp.int32))


def plant(result, key, low, largest):
    place = [jax.random.randint(jax.random.fold_in(key, axis), (), 0, length) for axis, length in enumerate(result.shape)]
    longest = result.shape.index(max(result.shape))
    beside = place[:longest] + [(place[longest] + 1) % result.shape[longest]] + place[longest + 1:]
    return result.at[tuple(place)].set(low).at[tuple(beside)].set(largest)


def shard_levels(own_key, shape, split, smallest, largest):
    level, own = 1.0, jax.random.fold_in(own_key, 6)
    for axis_at, parts in split:
        draws = jnp.exp(jax.random.uniform(jax.random.fold_in(own, axis_at), (parts,), jnp.float32, smallest / len(split), largest / len(split)))
        level = level * jnp.repeat(draws, shape[axis_at] // parts).reshape([-1 if axis == axis_at else 1 for axis in range(len(shape))])
    return level


def split_up(amount, total, most, skew):
    portions = [(1 << 20) // math.isqrt(rank ** skew) + 1 for rank in range(2, amount + 1)]
    spare, holding = total - most - (amount - 1), [1] * (amount - 1)
    while spare > 0:
        candidates = [i for i in range(amount - 1) if holding[i] < most]
        whole, budget = sum([portions[i] for i in candidates]), spare
        for i in candidates:
            more = min(most - holding[i], max(1, budget * portions[i] // whole), spare)
            holding[i] = holding[i] + more
            spare = spare - more
    return np.array([most] + holding)


def ragged(stream_key, number_of, total, most, lean):
    if number_of == 2:
        one = jax.random.randint(stream_key, (), max(1, total - most), min(most, total - 1) + 1)
        return jnp.stack([one, total - one])
    sizes = jnp.asarray(split_up(number_of, total, most, lean), jnp.int32)
    couples = (number_of - 1) // 2
    source_of, sink = sizes[1:1 + 2 * couples:2], sizes[2:2 + 2 * couples:2]
    room = jnp.minimum(source_of - 1, most - sink)
    passed = jax.random.randint(jax.random.fold_in(stream_key, 1), (couples,), 0, 1 << 20) % (room + 1)
    sizes = sizes.at[1:1 + 2 * couples:2].set(source_of - passed).at[2:2 + 2 * couples:2].set(sink + passed)
    return sizes[jax.random.permutation(jax.random.fold_in(stream_key, 2), number_of)]


def normal_values(stream_key, extent, scale, most, shards=(), kind=jnp.bfloat16):
    result = jax.random.normal(stream_key, extent, jnp.float32) * scale
    if len(shards) > 0:
        result = shard_levels(stream_key, extent, shards, -0.22, 0.18) * result
    return jnp.clip(result, min=-most, max=most).astype(kind)


def setup_inputs(seed: int = 0) -> dict:
    arg_keys = jax.random.split(jax.random.key(seed), 24)
    pixels = normal_values(arg_keys[0], (ROWS, ROW_LEN, VARS * PIX), 1.0, 6.0, ((0, 8), (1, 4)))
    targets = jnp.clip(2.0 + 4.0 * jax.random.uniform(arg_keys[1], (ROWS, ROW_LEN, VARS * PIX), jnp.float32) ** shard_levels(arg_keys[1], (ROWS, ROW_LEN, VARS * PIX), ((0, 8), (1, 4)), -0.2, 0.2), 2.0, 6.0).astype(jnp.bfloat16)
    valid_mask = plant((jax.random.randint(arg_keys[2], (ROWS, ROW_LEN, VARS * PIX), 0, 4) < 3).astype(jnp.int32), jax.random.fold_in(arg_keys[2], 1), 0, 1)
    lat_weight = jnp.clip(0.1 + 0.9 * jax.random.uniform(arg_keys[3], (ROWS, ROW_LEN), jnp.float32) ** shard_levels(arg_keys[3], (ROWS, ROW_LEN), ((0, 8), (1, 4)), -0.2, 0.2), 0.1, 1.0)
    segment_ids = jax.vmap(lambda own: jnp.searchsorted(jnp.cumsum(ragged(own, 4, ROW_LEN, ROW_LEN // 2, 1)), jnp.arange(ROW_LEN), side="right"))(jax.random.split(arg_keys[4], ROWS)).reshape((ROWS, ROW_LEN)).astype(jnp.int32)
    present_vars = draw_present_vars(jax.random.fold_in(arg_keys[23], 71), 0)
    lead_index = plant(jax.random.randint(arg_keys[6], (ROWS,), 0, LEAD_STEPS), jax.random.fold_in(arg_keys[6], 1), 0, LEAD_STEPS - 1).astype(jnp.int32)
    step_count = jax.random.randint(arg_keys[7], (1,), 1, 21).astype(jnp.int32)
    w_agg = normal_values(arg_keys[8], (D, 3 * D), D ** -0.5, 0.1875, ((0, 32),), jnp.float32)
    w_attn = normal_values(arg_keys[9], (D, 4 * D), D ** -0.5, 0.1875, ((0, 32),), jnp.float32)
    w_mlp = normal_values(arg_keys[10], (D, 2 * FF), D ** -0.5, 0.1875, ((0, 32),), jnp.float32)
    w_io = normal_values(arg_keys[11], (D, IOW), 4 ** -0.5, 3.0, ((0, 32),), jnp.float32)
    w_small = jnp.clip(0.5 + 1.0 * jax.random.uniform(arg_keys[12], (D, 9), jnp.float32) ** shard_levels(arg_keys[12], (D, 9), ((0, 32),), -0.2, 0.2), 0.5, 1.5)
    m_agg = normal_values(arg_keys[13], (D, 3 * D), (NPARAM ** -0.5), 0.00390625, ((0, 32),), jnp.float32)
    m_attn = normal_values(arg_keys[14], (D, 4 * D), (NPARAM ** -0.5), 0.00390625, ((0, 32),), jnp.float32)
    m_mlp = normal_values(arg_keys[15], (D, 2 * FF), (NPARAM ** -0.5), 0.00390625, ((0, 32),), jnp.float32)
    m_io = normal_values(arg_keys[16], (D, IOW), (NPARAM ** -0.5), 0.00390625, ((0, 32),), jnp.float32)
    m_small = normal_values(arg_keys[17], (D, 9), (4 * NPARAM ** -0.5), 0.015625, ((0, 32),), jnp.float32)
    v_agg = jnp.clip(jnp.exp(math.log(4.789125114257331e-07) - 2.7725887 * jax.random.uniform(arg_keys[18], (D, 3 * D), jnp.float32) ** shard_levels(arg_keys[18], (D, 3 * D), ((0, 32),), -0.2, 0.2)), 2.993203196410832e-08, 4.789125114257331e-07)
    v_attn = jnp.clip(jnp.exp(math.log(4.789125114257331e-07) - 2.7725887 * jax.random.uniform(arg_keys[19], (D, 4 * D), jnp.float32) ** shard_levels(arg_keys[19], (D, 4 * D), ((0, 32),), -0.2, 0.2)), 2.993203196410832e-08, 4.789125114257331e-07)
    v_mlp = jnp.clip(jnp.exp(math.log(4.789125114257331e-07) - 2.7725887 * jax.random.uniform(arg_keys[20], (D, 2 * FF), jnp.float32) ** shard_levels(arg_keys[20], (D, 2 * FF), ((0, 32),), -0.2, 0.2)), 2.993203196410832e-08, 4.789125114257331e-07)
    v_io = jnp.clip(jnp.exp(math.log(4.789125114257331e-07) - 2.7725887 * jax.random.uniform(arg_keys[21], (D, IOW), jnp.float32) ** shard_levels(arg_keys[21], (D, IOW), ((0, 32),), -0.2, 0.2)), 2.993203196410832e-08, 4.789125114257331e-07)
    v_small = jnp.clip(jnp.exp(math.log(7.66260018281173e-06) - 2.7725887 * jax.random.uniform(arg_keys[22], (D, 9), jnp.float32) ** shard_levels(arg_keys[22], (D, 9), ((0, 32),), -0.2, 0.2)), 4.789125114257331e-07, 7.66260018281173e-06)
    return dict(pixels=pixels, targets=targets, valid_mask=valid_mask, lat_weight=lat_weight, segment_ids=segment_ids, present_vars=present_vars, lead_index=lead_index, step_count=step_count, w_agg=w_agg, w_attn=w_attn, w_mlp=w_mlp, w_io=w_io, w_small=w_small, m_agg=m_agg, m_attn=m_attn, m_mlp=m_mlp, m_io=m_io, m_small=m_small, v_agg=v_agg, v_attn=v_attn, v_mlp=v_mlp, v_io=v_io, v_small=v_small)


@jax.custom_vjp
def low(v):
    return lax.optimization_barrier(v.astype(jnp.bfloat16)).astype(jnp.float32)

@jax.custom_vjp
def low_back(v):
    return v

def low_keep(v):
    return (low(v), None)

def low_pass(kept, grad):
    return (grad,)

def back_keep(v):
    return (v, None)

def back_low(kept, grad):
    return (low(grad),)
low.defvjp(low_keep, low_pass)
low_back.defvjp(back_keep, back_low)
highest = lax.Precision.HIGHEST
norm_eps = 1e-05
clip_limit = 1.0
decay_rate = 0.05
adam_eps = 1e-08
learn_rates = (0.03, 0.03, 0.03, 0.2, 0.3)

def matmul(left, right):
    return low_back(jnp.dot(low(left), right, precision=highest))

def layer_norm(values, gain, offset):
    average = lax.optimization_barrier(jnp.mean(values, axis=-1, keepdims=True))
    centred = values - average
    spread = lax.optimization_barrier(jnp.mean(centred * centred, axis=-1, keepdims=True))
    return centred * lax.rsqrt(spread + norm_eps) * gain + offset

def softmax_rows(scores):
    top = lax.optimization_barrier(jnp.max(scores, axis=-1, keepdims=True))
    powers = jnp.exp(scores - top)
    return powers / lax.optimization_barrier(jnp.sum(powers, axis=-1, keepdims=True))

def positions(segment_row):
    places = jnp.arange(segment_row.shape[0], dtype=jnp.int32)
    starts = jnp.concatenate([jnp.ones((1,), dtype=jnp.bool_), segment_row[1:] != segment_row[:-1]])
    first = lax.cummax(jnp.where(starts, places, 0), axis=0)
    return places - first

def front_part(weights, pixel_rows, present_row, lead_value, pos_index):
    w_agg, w_attn, w_mlp, w_io, w_small = weights
    rows_here = pixel_rows.shape[0]
    width = VARS * PIX
    patch_w = w_io[:, :width].reshape(D, VARS, PIX)
    embedded = jnp.einsum('lvp,dvp->lvd', pixel_rows.reshape(rows_here, VARS, PIX), patch_w, precision=highest)
    embedded = low_back(embedded + w_io[:, 2 * width:2 * width + VARS].T[None])
    pairs = low(matmul(embedded.reshape(rows_here * VARS, D), w_agg[:, :2 * D]))
    pairs = pairs.reshape(rows_here, VARS, 2, HEADS, HEAD_DIM)
    queries = w_small[:, 0].reshape(HEADS, HEAD_DIM)
    scores = low_back(jnp.einsum('he,lvhe->lhv', queries, pairs[:, :, 0], precision=highest)) * HEAD_DIM ** (-0.5)
    scores = jnp.where(present_row[None, None, :] > 0, scores, -1000000000.0)
    attend = low(softmax_rows(scores))
    mixed = low_back(jnp.einsum('lhv,lvhe->lhe', attend, pairs[:, :, 1], precision=highest)).reshape(rows_here, D)
    pooled = matmul(mixed, w_agg[:, 2 * D:])
    lead_embed = lead_value * w_small[:, 7] + w_small[:, 8]
    state = pooled + jnp.take(w_io[:, 2 * width + VARS:].T, pos_index, axis=0) + lead_embed[None]
    normed = layer_norm(state, w_small[:, 1], w_small[:, 2])
    projected = low(matmul(normed, w_attn[:, :3 * D]))
    return (projected[:, :D], projected[:, D:], state)

def rear_part(weights, queries, pairs_full, state, seg_query, seg_keys, target, pixel_weight):
    w_agg, w_attn, w_mlp, w_io, w_small = weights
    rows_here = queries.shape[0]
    keys_here = pairs_full.shape[0]
    width = VARS * PIX
    q_heads = queries.reshape(rows_here, HEADS, HEAD_DIM)
    key_heads = pairs_full[:, :D].reshape(keys_here, HEADS, HEAD_DIM)
    value_heads = pairs_full[:, D:].reshape(keys_here, HEADS, HEAD_DIM)
    scores = low_back(jnp.einsum('qhe,khe->hqk', q_heads, key_heads, precision=highest)) * HEAD_DIM ** (-0.5)
    same_crop = seg_query[:, None] == seg_keys[None, :]
    scores = jnp.where(same_crop[None], scores, -1000000000.0)
    attend = low(softmax_rows(scores))
    mixed = low_back(jnp.einsum('hqk,khe->qhe', attend, value_heads, precision=highest)).reshape(rows_here, D)
    hidden = state + matmul(mixed, w_attn[:, 3 * D:])
    normed = layer_norm(hidden, w_small[:, 3], w_small[:, 4])
    lifted = jax.nn.gelu(matmul(normed, w_mlp[:, :FF]), approximate=False)
    hidden = hidden + matmul(lifted, w_mlp[:, FF:].T)
    normed = layer_norm(hidden, w_small[:, 5], w_small[:, 6])
    predicted = matmul(normed, w_io[:, width:2 * width]) * D ** (-0.5)
    error = predicted - target
    return jnp.sum(pixel_weight * error * error)

def adamw(weight, grad, moment, second, step_value, learn_rate):
    moment = 0.5 * moment + 0.5 * grad
    second = 0.5 * second + 0.5 * grad * grad
    correct = 1.0 - jnp.power(jnp.float32(0.5), step_value)
    update = moment / correct / (jnp.sqrt(second / correct) + adam_eps) + decay_rate * weight
    fresh = weight - learn_rate * update
    return (fresh, fresh.astype(jnp.bfloat16), moment, second)

def reference(pixels, targets, valid_mask, lat_weight, segment_ids, present_vars, lead_index, step_count, w_agg, w_attn, w_mlp, w_io, w_small, m_agg, m_attn, m_mlp, m_io, m_small, v_agg, v_attn, v_mlp, v_io, v_small):
    masters = (w_agg, w_attn, w_mlp, w_io, w_small)
    firsts = (m_agg, m_attn, m_mlp, m_io, m_small)
    seconds = (v_agg, v_attn, v_mlp, v_io, v_small)
    present_cols = jnp.repeat(present_vars.astype(jnp.float32), PIX, axis=1)
    pixel_weight = lat_weight[:, :, None] * valid_mask.astype(jnp.float32) * present_cols[:, None, :]
    total_weight = jnp.sum(pixel_weight)

    def numerator(weights):
        weights = tuple((low(piece) for piece in weights))

        @jax.checkpoint
        def one_row(carry, items):
            pixel_row, target_row, weight_row, segment_row, present_row, lead_row = items
            lead_value = (lead_row.astype(jnp.float32) + 1.0) / LEAD_STEPS
            queries, pairs, state = front_part(weights, pixel_row.astype(jnp.float32), present_row, lead_value, positions(segment_row))
            part_sum = rear_part(weights, queries, pairs, state, segment_row, segment_row, target_row.astype(jnp.float32), weight_row)
            return (carry + part_sum, None)
        total, unused = lax.scan(one_row, jnp.zeros((), jnp.float32), (pixels, targets, pixel_weight, segment_ids, present_vars, lead_index))
        return total
    loss_sum, pull = jax.vjp(numerator, masters)
    gradient, = pull((1.0 / total_weight).astype(jnp.float32))
    loss = loss_sum / total_weight
    squares = sum((jnp.sum(piece * piece) for piece in gradient))
    grad_norm = jnp.sqrt(squares)
    factor = jnp.minimum(1.0, clip_limit / grad_norm)
    step_value = step_count[0].astype(jnp.float32)
    results = [adamw(masters[index], gradient[index] * factor, firsts[index], seconds[index], step_value, learn_rates[index]) for index in range(5)]
    news = tuple((entry[0] for entry in results))
    copies = tuple((entry[1] for entry in results))
    moments = tuple((entry[2] for entry in results))
    squared = tuple((entry[3] for entry in results))
    return (loss, grad_norm, news[0], news[1], news[2], news[3], news[4], copies[0], copies[1], copies[2], copies[3], copies[4], moments[0], moments[1], moments[2], moments[3], moments[4], squared[0], squared[1], squared[2], squared[3], squared[4])
```

```python
import jax
import jax.numpy as jnp
from jax import lax
from jax.sharding import PartitionSpec as P

D = 1024
HEADS = 16
HEAD_DIM = 64
FF = 4096
VARS = 48
PIX = 4
LEAD_STEPS = 8
WIDTH = VARS * PIX
SPAN = 256
MIX = WIDTH + VARS
USED = 2 * WIDTH + VARS + SPAN

norm_eps = 1e-05
clip_limit = 1.0
decay_rate = 0.05
adam_eps = 1e-08
learn_rates = (0.03, 0.03, 0.03, 0.2, 0.3)
f32 = jnp.float32
bf16 = jnp.bfloat16
highest = lax.Precision.HIGHEST


def dot(left, right, dims):
    return lax.dot_general(left, right, (dims, ((), ())), preferred_element_type=f32)


def mm(left, right):
    return dot(left, right, ((1,), (0,)))


def mm_t(left, right):
    return dot(left, right, ((1,), (1,)))


def t_mm(left, right):
    return dot(left, right, ((0,), (0,)))


def exact(eq, left, right):
    return jnp.einsum(eq, left, right, precision=highest, preferred_element_type=f32)


def norm_forward(values, gain, offset):
    average = jnp.mean(values, axis=-1, keepdims=True)
    centred = values - average
    scale = lax.rsqrt(jnp.mean(centred * centred, axis=-1, keepdims=True) + norm_eps)
    unit = centred * scale
    return (unit * gain[None] + offset[None]).astype(bf16), unit, scale


def norm_backward(grad, unit, scale, gain):
    inner = grad * gain[None]
    mean_inner = jnp.mean(inner, axis=-1, keepdims=True)
    mean_product = jnp.mean(inner * unit, axis=-1, keepdims=True)
    back = scale * (inner - mean_inner - unit * mean_product)
    return back, jnp.sum(grad * unit, axis=0), jnp.sum(grad, axis=0)


def adamw(weight, grad, moment, second, step_value, learn_rate):
    moment = 0.5 * moment + 0.5 * grad
    second = 0.5 * second + 0.5 * grad * grad
    correct = 1.0 - jnp.power(f32(0.5), step_value)
    update = moment / correct / (jnp.sqrt(second / correct) + adam_eps) + decay_rate * weight
    fresh = weight - learn_rate * update
    return (fresh, fresh.astype(bf16), moment, second)


def ag(part):
    return lax.all_gather(part, "fsdp", axis=0, tiled=True)


def make_local(n_dp, n_f):
    def local(
        pixels, targets, valid_mask, lat_weight, segment_ids, present_vars, lead_index, step_count,
        w_agg, w_attn, w_mlp, w_io, w_small,
        m_agg, m_attn, m_mlp, m_io, m_small,
        v_agg, v_attn, v_mlp, v_io, v_small,
    ):
        masters = (w_agg, w_attn, w_mlp, w_io, w_small)
        firsts = (m_agg, m_attn, m_mlp, m_io, m_small)
        seconds = (v_agg, v_attn, v_mlp, v_io, v_small)
        rows = pixels.shape[1]
        row_len = segment_ids.shape[1]
        strip = w_agg.shape[0]
        own = lax.axis_index("fsdp")
        heads_here = HEADS // n_f
        wide = heads_here * HEAD_DIM

        seg = segment_ids[0]
        seg_own = lax.dynamic_slice_in_dim(seg, own * rows, rows)
        below = jnp.sum((seg[None, :] < seg_own[:, None]).astype(jnp.int32), axis=1)
        pos = own * rows + jnp.arange(rows, dtype=jnp.int32) - below
        onehot = (pos[:, None] == jnp.arange(SPAN, dtype=jnp.int32)[None, :]).astype(bf16)
        lead = (lead_index[0].astype(f32) + 1.0) / LEAD_STEPS
        pixel_rows = pixels[0]
        target = targets[0].astype(f32)
        present = present_vars[0]
        spread = (jnp.arange(MIX) // PIX)[None, :] == jnp.arange(VARS)[:, None]
        embed_col = (jnp.arange(MIX) - WIDTH)[None, :] == jnp.arange(VARS)[:, None]
        in_pixels = (jnp.arange(MIX) < WIDTH)[None, :]
        expand = jnp.where(in_pixels, spread, embed_col).astype(bf16)
        present_cols = jnp.repeat(present.astype(f32), PIX)
        pixel_weight = lat_weight[0][:, None] * valid_mask[0].astype(f32) * present_cols[None, :]
        total = lax.psum(jnp.sum(pixel_weight), ("dp", "fsdp"))

        pack = jnp.concatenate(
            [
                w_io[:, :USED].astype(bf16),
                w_small.astype(bf16),
                jnp.zeros((strip, 768 - USED - 9), bf16),
                w_agg.astype(bf16),
            ],
            axis=1,
        )
        head = lax.all_gather(pack, ("dp", "fsdp"), axis=0, tiled=True)
        attn = lax.all_gather(w_attn.astype(bf16), ("dp", "fsdp"), axis=0, tiled=True)
        mlp = lax.all_gather(w_mlp.astype(bf16), ("dp", "fsdp"), axis=0, tiled=True)
        w240 = jnp.concatenate([head[:, :WIDTH], head[:, 2 * WIDTH : 2 * WIDTH + VARS]], axis=1)
        w_pred = head[:, WIDTH : 2 * WIDTH]
        w_pos = head[:, 2 * WIDTH + VARS : USED]
        small = head[:, USED : USED + 9].astype(f32).T
        agg_kv = head[:, 768 : 768 + 2 * D]
        agg_out = head[:, 768 + 2 * D :]
        w_qkv = attn[:, : 3 * D]
        w_out = attn[:, 3 * D :]
        w_up = mlp[:, :FF]
        w_down = mlp[:, FF:]

        pix_t = jnp.concatenate([pixel_rows.T, jnp.ones((VARS, rows), bf16)], axis=0)
        table = t_mm(w240, agg_kv)
        table_k = table[:, :D].reshape(MIX, HEADS, HEAD_DIM)
        table_v = table[:, D:].reshape(MIX, HEADS, HEAD_DIM)
        query = small[0].reshape(HEADS, HEAD_DIM)
        folded = jnp.sum(table_k * query[None], axis=2)
        block = folded.T[:, None, :] * expand.astype(f32)[None]
        score = exact("xc,cl->xl", block.reshape(HEADS * VARS, MIX), pix_t.astype(f32))
        score = score.reshape(HEADS, VARS, rows) * HEAD_DIM ** (-0.5)
        score = jnp.where(present[None, :, None] > 0, score, -1000000000.0)
        top = jnp.max(score, axis=1, keepdims=True)
        power = jnp.exp(score - top)
        soft = power / jnp.sum(power, axis=1, keepdims=True)
        share = soft.astype(bf16)
        pix_f = pix_t.astype(f32)
        lifted_share = jnp.einsum("vc,hvl->hcl", expand, share, preferred_element_type=f32) * pix_f[None]
        mixed_a = exact("che,hcl->hel", table_v, lifted_share).reshape(D, rows).T.astype(bf16)
        lead_embed = lead * small[7] + small[8]
        h0 = mm(mixed_a, agg_out) + mm_t(onehot, w_pos) + lead_embed[None]
        norm0, unit0, scale0 = norm_forward(h0, small[1], small[2])
        qkv = mm(norm0, w_qkv).astype(bf16)
        part = qkv.reshape(rows, 3, n_f, wide)
        part = lax.all_to_all(part, "fsdp", split_axis=2, concat_axis=0, tiled=True)
        part = part.reshape(row_len, 3, heads_here, HEAD_DIM)
        q, k, v = (part[:, i].transpose(1, 0, 2) for i in range(3))
        att_score = jnp.einsum("hqe,hke->hqk", q, k, preferred_element_type=f32) * HEAD_DIM ** (-0.5)
        same = seg[:, None] == seg[None, :]
        att_score = jnp.where(same[None], att_score, -1000000000.0)
        att_top = jnp.max(att_score, axis=-1, keepdims=True)
        att_power = jnp.exp(att_score - att_top)
        att_soft = att_power / jnp.sum(att_power, axis=-1, keepdims=True)
        att = att_soft.astype(bf16)
        mixed_h = jnp.einsum("hqk,hke->qhe", att, v, preferred_element_type=f32)
        mixed_h = mixed_h.reshape(row_len, wide).astype(bf16)
        mixed_all = lax.all_gather(mixed_h, "fsdp", axis=1, tiled=True)
        mixed = lax.dynamic_slice_in_dim(mixed_all, own * rows, rows, axis=0)
        h1 = h0 + mm(mixed, w_out)
        norm1, unit1, scale1 = norm_forward(h1, small[3], small[4])
        up = mm(norm1, w_up)
        gate = 0.5 * (1.0 + lax.erf(up * (2.0**-0.5)))
        lifted = (up * gate).astype(bf16)
        h2 = h1 + mm_t(lifted, w_down)
        norm2, unit2, scale2 = norm_forward(h2, small[5], small[6])
        predicted = mm(norm2, w_pred) * D ** (-0.5)
        error = predicted - target
        weighted = pixel_weight * error
        numerator = lax.psum(jnp.sum(weighted * error), ("dp", "fsdp"))

        d_pred = (weighted * (2.0 * D ** (-0.5) / total)).astype(bf16)
        d_norm2 = mm_t(d_pred, w_pred)
        d_h2, d_gain2, d_off2 = norm_backward(d_norm2, unit2, scale2, small[5])
        d_out = d_h2.astype(bf16)
        slope = gate + up * jnp.exp(-0.5 * up * up) * 0.3989422804014327
        d_up = (mm(d_out, w_down) * slope).astype(bf16)
        d_norm1 = mm_t(d_up, w_up)
        d_in, d_gain1, d_off1 = norm_backward(d_norm1, unit1, scale1, small[3])
        d_h1 = d_h2 + d_in
        d_proj_all = ag(d_h1.astype(bf16))
        w_out_own = lax.dynamic_slice_in_dim(w_out, own * wide, wide, axis=0)
        d_mixed = mm_t(d_proj_all, w_out_own).astype(bf16).reshape(row_len, heads_here, HEAD_DIM).transpose(1, 0, 2)
        d_att = jnp.einsum("hqe,hke->hqk", d_mixed, v, preferred_element_type=f32)
        d_v = jnp.einsum("hqk,hqe->khe", att, d_mixed, preferred_element_type=f32)
        lean = jnp.sum(att_soft * d_att, axis=-1, keepdims=True)
        d_score = (att_soft * (d_att - lean) * HEAD_DIM ** (-0.5)).astype(bf16)
        d_q = jnp.einsum("hqk,hke->qhe", d_score, k, preferred_element_type=f32)
        d_k = jnp.einsum("hqk,hqe->khe", d_score, q, preferred_element_type=f32)
        d_part = jnp.stack([d_q, d_k, d_v], axis=1).astype(bf16).reshape(row_len, 3, 1, wide)
        d_qkv_all = lax.all_gather(d_part, "fsdp", axis=2, tiled=True).reshape(row_len, 3 * D)
        d_qkv = lax.dynamic_slice_in_dim(d_qkv_all, own * rows, rows, axis=0)
        d_norm0 = mm_t(d_qkv, w_qkv)
        d_in, d_gain0, d_off0 = norm_backward(d_norm0, unit0, scale0, small[1])
        d_h0 = d_h1 + d_in
        d_agg = d_h0.astype(bf16)
        d_mixed_a = mm_t(agg_out, d_agg).astype(bf16).reshape(HEADS, HEAD_DIM, rows)
        pulled = exact("che,hel->hcl", table_v, d_mixed_a.astype(f32)) * pix_f[None]
        d_share = exact("vc,hcl->hvl", expand.astype(f32), pulled)
        lean_a = jnp.sum(soft * d_share, axis=1, keepdims=True)
        d_score_a = (soft * (d_share - lean_a) * HEAD_DIM ** (-0.5)).astype(bf16)
        spread_score = jnp.einsum("vc,hvl->hcl", expand, d_score_a, preferred_element_type=f32)
        d_folded = jnp.sum(spread_score * pix_f[None], axis=2)
        d_table_v = exact("hcl,hel->che", lifted_share, d_mixed_a.astype(f32)).reshape(MIX, D)
        d_table_k = (d_folded.T[:, :, None] * query[None]).reshape(MIX, D)
        d_query = jnp.sum(d_folded.T[:, :, None] * table_k, axis=0).reshape(D)
        d_bias = jnp.sum(d_h0, axis=0)
        narrow = jnp.stack(
            [d_query, d_gain0, d_off0, d_gain1, d_off1, d_gain2, d_off2, lead * d_bias, d_bias]
            + [jnp.zeros((D,), f32)] * 7
        )
        d_table, narrow = lax.psum((jnp.concatenate([d_table_k, d_table_v], axis=1), narrow), "fsdp")

        def mine(array):
            whole = array.reshape(n_dp, n_f, strip, array.shape[1])
            return lax.dynamic_index_in_dim(whole, own, axis=1, keepdims=False).reshape(n_dp * strip, array.shape[1])

        source = jnp.arange(D)
        pick = (source // strip) % n_f == own
        place = (source // (strip * n_f)) * strip + source % strip
        choose = (pick[:, None] & (place[:, None] == jnp.arange(n_dp * strip)[None, :])).astype(bf16)

        def weight_grad(features, grads):
            return t_mm(mm(features, choose).astype(bf16), grads)

        d_agg_all = ag(d_agg)
        g_attn = jnp.concatenate(
            [weight_grad(ag(norm0), d_qkv_all), weight_grad(mixed_all, d_proj_all)], axis=1
        )
        g_mlp = jnp.concatenate(
            [weight_grad(ag(norm1), ag(d_up)), weight_grad(ag(d_out), ag(lifted))], axis=1
        )
        g_out = weight_grad(ag(mixed_a), d_agg_all)
        g_kv = exact("dc,cx->dx", mine(w240).astype(f32), d_table)
        g_240 = exact("dx,cx->dc", mine(agg_kv).astype(f32), d_table)
        g_pred = weight_grad(ag(norm2), ag(d_pred))
        g_pos = weight_grad(d_agg_all, ag(onehot))
        g_small = mine(narrow.T)[:, :9]
        g_agg = jnp.concatenate([g_kv, g_out], axis=1)
        g_misc = jnp.concatenate(
            [g_240[:, :WIDTH], g_pred, g_240[:, WIDTH:], g_pos, g_small, jnp.zeros((n_dp * strip, 768 - USED - 9), f32)],
            axis=1,
        )
        r_agg, r_attn, r_mlp, r_misc = (
            lax.psum_scatter(g, "dp", scatter_dimension=0, tiled=True) for g in (g_agg, g_attn, g_mlp, g_misc)
        )
        r_io = jnp.concatenate([r_misc[:, :USED], jnp.zeros((strip, w_io.shape[1] - USED), f32)], axis=1)
        reduced = (r_agg, r_attn, r_mlp, r_io, r_misc[:, USED : USED + 9])
        squares = lax.psum(sum(jnp.sum(piece * piece) for piece in reduced), ("dp", "fsdp"))
        grad_norm = jnp.sqrt(squares)
        factor = jnp.minimum(1.0, clip_limit / grad_norm)
        loss = numerator / total
        step_value = step_count[0].astype(f32)
        results = [
            adamw(masters[i], reduced[i] * factor, firsts[i], seconds[i], step_value, learn_rates[i]) for i in range(5)
        ]
        return (loss, grad_norm) + tuple(results[i][j] for j in range(4) for i in range(5))

    return local


def solution(mesh):
    flat = P(("dp", "fsdp"), None)
    tokens = P("dp", "fsdp", None)
    return jax.shard_map(
        make_local(mesh.shape["dp"], mesh.shape["fsdp"]),
        mesh=mesh,
        in_specs=(tokens, tokens, tokens, P("dp", "fsdp"), P("dp", None), P("dp", None), P("dp"), P()) + (flat,) * 15,
        out_specs=(P(), P()) + (flat,) * 20,
        check_vma=False,
    )
```

```python
import functools

import jax
import jax.numpy as jnp
from jax import lax
from jax.experimental import pallas as pl
from jax.experimental.pallas import tpu as pltpu
from jax.sharding import PartitionSpec as P

D = 1024
HEADS = 16
HEAD_DIM = 64
FF = 4096
VARS = 48
PIX = 4
LEAD_STEPS = 8
WIDTH = VARS * PIX
SPAN = 256
MIX = WIDTH + VARS
USED = 2 * WIDTH + VARS + SPAN

norm_eps = 1e-05
clip_limit = 1.0
decay_rate = 0.05
adam_eps = 1e-08
learn_rates = (0.03, 0.03, 0.03, 0.2, 0.3)
f32 = jnp.float32
bf16 = jnp.bfloat16
highest = lax.Precision.HIGHEST
MESH = pl.DeviceIdType.MESH
STRIP = 32
CHUNK = 512
DEPTH = 2
LAG = 2
QUEUE = 2
MISC = 1024


def dot(left, right, dims):
    return lax.dot_general(left, right, (dims, ((), ())), preferred_element_type=f32)


def mm(left, right):
    return dot(left, right, ((1,), (0,)))


def mm_t(left, right):
    return dot(left, right, ((1,), (1,)))


def t_mm(left, right):
    return dot(left, right, ((0,), (0,)))


def exact(eq, left, right):
    return jnp.einsum(eq, left, right, precision=highest, preferred_element_type=f32)


def norm_forward(values, gain, offset):
    average = jnp.mean(values, axis=-1, keepdims=True)
    centred = values - average
    scale = lax.rsqrt(jnp.mean(centred * centred, axis=-1, keepdims=True) + norm_eps)
    unit = centred * scale
    return (unit * gain[None] + offset[None]).astype(bf16), unit, scale


def norm_backward(grad, unit, scale, gain):
    inner = grad * gain[None]
    mean_inner = jnp.mean(inner, axis=-1, keepdims=True)
    mean_product = jnp.mean(inner * unit, axis=-1, keepdims=True)
    back = scale * (inner - mean_inner - unit * mean_product)
    return back, jnp.sum(grad * unit, axis=0), jnp.sum(grad, axis=0)


def adamw(weight, grad, moment, second, step_value, learn_rate):
    moment = 0.5 * moment + 0.5 * grad
    second = 0.5 * second + 0.5 * grad * grad
    correct = 1.0 - jnp.power(f32(0.5), step_value)
    update = moment / correct / (jnp.sqrt(second / correct) + adam_eps) + decay_rate * weight
    fresh = weight - learn_rate * update
    return (fresh, fresh.astype(bf16), moment, second)


PIECES = (
    (0, 0, 1920, "yzx"), (2, 0, 2688, "zxy"), (0, 1920, 1920, "yzx"), (2, 2688, 2816, "zxy"),
    (1, 0, 1920, "yzx"), (2, 5504, 2688, "zxy"), (1, 1920, 2176, "zxy"),
)


def gather_kernel(*refs):
    shards, num_ref, wholes, stat_ref = refs[0:3], refs[3], refs[4:7], refs[7]
    quad_buf, line_buf, own_sem, s_send, s_recv, sends, arrive, pass_on = refs[8:]
    dp, own = lax.axis_index("dp"), lax.axis_index("fsdp")
    z, y, x, core = dp // 2, dp % 2, own // 2, own % 2
    sibling = x * 2 + 1 - core
    barrier = pltpu.get_barrier_semaphore()
    for d in range(1, 8):
        pl.semaphore_signal(barrier, inc=1, device_id=(lax.rem(dp + d, 8), own), device_id_type=MESH)
    for d in range(1, 4):
        pl.semaphore_signal(barrier, inc=1, device_id=(dp, lax.rem(own + d, 4)), device_id_type=MESH)
    pl.semaphore_wait(barrier, 10)

    def view(p, ident, plane):
        a, start, width, order = PIECES[p]
        row = pl.multiple_of(((ident // 2) * 4 + (ident % 2) * 2 + plane) * STRIP, STRIP)
        return wholes[a].at[pl.ds(row, STRIP), pl.ds(start, width)]

    def copy(p, ident, slot, to, mine=False):
        a, start, width, order = PIECES[p]
        src = shards[a].at[:, pl.ds(start, width)] if mine else view(p, ident, core)
        sem = pass_on if slot == 4 else arrive
        return pltpu.make_async_remote_copy(
            src_ref=src, dst_ref=view(p, ident, core), send_sem=sends.at[p, ident, slot], recv_sem=sem.at[p, ident],
            device_id=to, device_id_type=MESH,
        )

    def arrival(p, ident, plane, sem):
        return pltpu.make_async_copy(view(p, ident, plane), view(p, ident, plane), sem.at[p, ident])

    def targets(p, rx, ry, rz):
        order = PIECES[p][3]
        moved = {"x": rx != 0, "y": ry != 0, "z": rz is not None}
        stage = max([k for k in range(3) if moved[order[k]]], default=-1)
        found = []
        if stage >= 0 and order[stage] == "z":
            found.append((0, (rz < 0) & (z < 3), ((dp + 2) % 8, own)))
            found.append((1, (rz > 0) & (z > 0), ((dp + 6) % 8, own)))
        for k in range(stage + 1, 3):
            if order[k] == "z":
                found.append((0, z < 3, ((dp + 2) % 8, own)))
                found.append((1, z > 0, ((dp + 6) % 8, own)))
            elif order[k] == "x":
                found.append((2, None, (dp, (1 - x) * 2 + core)))
            else:
                found.append((3, None, (z * 2 + 1 - y, own)))
        found.append((4, None, (dp, sibling)))
        return found

    def source(rx, ry, rz):
        sz = z if rz is None else z + rz
        sy = 1 - y if ry else y
        sx = 1 - x if rx else x
        return sz, (sz * 2 + sy) * 2 + sx

    def each(rx, ry, rz, act, mine=False):
        sz, ident = source(rx, ry, rz)

        def body():
            for p in range(len(PIECES)):
                if act == "send" and not mine:
                    arrival(p, ident, core, arrive).wait()
                for slot, when, to in targets(p, rx, ry, rz):
                    def go(slot=slot, to=to):
                        c = copy(p, ident, slot, to, mine)
                        c.start() if act == "send" else c.wait_send()

                    if when is None:
                        go()
                    else:
                        pl.when(when)(go)

        if rz is None:
            body()
        else:
            pl.when((sz >= 0) & (sz < 4))(body)

    def over_z(pairs, act):
        def step(t, carry):
            rz = ((t + 1) // 2) * (1 - 2 * (t % 2))
            for rx, ry in pairs:
                each(rx, ry, rz, act)
            return carry

        lax.fori_loop(1, 7, step, 0)

    def sweep(act):
        each(0, 0, None, act, mine=True)
        if act == "send":
            for a in range(3):
                row = pl.multiple_of((dp * 4 + own) * STRIP, STRIP)
                pltpu.make_async_copy(shards[a], wholes[a].at[pl.ds(row, STRIP), :], own_sem.at[a]).start()
            scalars()
        each(1, 0, None, act)
        each(0, 1, None, act)
        over_z([(0, 0)], act)
        each(1, 1, None, act)
        over_z([(1, 0), (0, 1)], act)
        over_z([(1, 1)], act)

    def share(buf, k, where, at):
        return pltpu.make_async_remote_copy(
            src_ref=buf.at[at], dst_ref=buf.at[at], send_sem=s_send.at[k], recv_sem=s_recv.at[k],
            device_id=where, device_id_type=MESH,
        )

    def scalars():
        quad_buf[own] = num_ref[...]
        for d in range(1, 4):
            share(quad_buf, d, (dp, lax.rem(own + d, 4)), own).start()

    sweep("send")
    for d in range(1, 4):
        share(quad_buf, d, (dp, own), lax.rem(own + 4 - d, 4)).wait_recv()
    line_buf[dp] = (quad_buf[0] + quad_buf[1]) + (quad_buf[2] + quad_buf[3])
    for d in range(1, 8):
        share(line_buf, 3 + d, (lax.rem(dp + d, 8), own), dp).start()

    def closing(ident, carry):
        for p in range(len(PIECES)):
            arrival(p, ident, 1 - core, pass_on).wait()
        return carry

    lax.fori_loop(0, 16, closing, 0)
    for a in range(3):
        row = pl.multiple_of((dp * 4 + own) * STRIP, STRIP)
        pltpu.make_async_copy(shards[a], wholes[a].at[pl.ds(row, STRIP), :], own_sem.at[a]).wait()
    sweep("drain")
    for d in range(1, 8):
        share(line_buf, 3 + d, (dp, own), lax.rem(dp + 8 - d, 8)).wait_recv()
    stat = line_buf[0]
    for d in range(1, 8):
        stat = stat + line_buf[d]
    stat_ref[...] = stat
    for d in range(1, 4):
        share(quad_buf, d, (dp, own), own).wait_send()
    for d in range(1, 8):
        share(line_buf, 3 + d, (dp, own), dp).wait_send()


def gather_weights(head, attn, mlp, number):
    any_space = pl.BlockSpec(memory_space=pl.ANY)
    vmem = pl.BlockSpec(memory_space=pltpu.VMEM)
    n = len(PIECES)
    return pl.pallas_call(
        gather_kernel,
        out_shape=[jax.ShapeDtypeStruct((D, a.shape[1]), bf16) for a in (head, attn, mlp)]
        + [jax.ShapeDtypeStruct((8, 128), f32)],
        in_specs=[any_space] * 3 + [vmem],
        out_specs=[any_space] * 3 + [vmem],
        scratch_shapes=[
            pltpu.VMEM((4, 8, 128), f32),
            pltpu.VMEM((8, 8, 128), f32),
            pltpu.SemaphoreType.DMA((3,)),
            pltpu.SemaphoreType.DMA((11,)),
            pltpu.SemaphoreType.DMA((11,)),
            pltpu.SemaphoreType.DMA((n, 16, 5)),
            pltpu.SemaphoreType.DMA((n, 16)),
            pltpu.SemaphoreType.DMA((n, 16)),
        ],
        compiler_params=pltpu.CompilerParams(collective_id=0, has_side_effects=True),
        name="gather_weights",
    )(head, attn, mlp, number)


def reduce_kernel(widths, outs_at, *refs):
    n_in = len(widths)
    keep, give = refs[:n_in], refs[n_in : 2 * n_in]
    num_ref = refs[2 * n_in]
    outs = refs[2 * n_in + 1 : 2 * n_in + 1 + len(outs_at)]
    stat_ref = refs[2 * n_in + 1 + len(outs_at)]
    (own_buf, give_buf, got, rise, fall, done, tally, quad_buf, line_buf,
     own_sem, give_sem, y_send, y_recv, z_send, z_recv, s_send, s_recv) = refs[2 * n_in + 2 + len(outs_at) :]
    dp, own = lax.axis_index("dp"), lax.axis_index("fsdp")
    z, y = dp // 2, dp % 2
    over = z * 2 + 1 - y
    barrier = pltpu.get_barrier_semaphore()
    for d in range(1, 8):
        pl.semaphore_signal(barrier, inc=1, device_id=(lax.rem(dp + d, 8), own), device_id_type=MESH)
    for d in range(1, 4):
        pl.semaphore_signal(barrier, inc=1, device_id=(dp, lax.rem(own + d, 4)), device_id_type=MESH)
    pl.semaphore_wait(barrier, 10)
    places = [(i, j) for i in range(n_in) for j in range(widths[i] // CHUNK)]
    n = len(places)

    def load(c):
        i, j = places[c]
        return pltpu.make_async_copy(keep[i].at[:, pl.ds(j * CHUNK, CHUNK)], own_buf.at[c], own_sem.at[c])

    def stage(c):
        i, j = places[c]
        return pltpu.make_async_copy(give[i].at[:, pl.ds(j * CHUNK, CHUNK)], give_buf.at[c], give_sem.at[c])

    def cross(c):
        return pltpu.make_async_remote_copy(
            src_ref=give_buf.at[c], dst_ref=got.at[c], send_sem=y_send.at[c],
            recv_sem=y_recv.at[c], device_id=(over, own), device_id_type=MESH,
        )

    for c in range(n):
        stage(c).start()
    for c in range(n):
        load(c).start()
    for c in range(DEPTH):
        stage(c).wait()
        cross(c).start()
    for c in range(DEPTH, n):
        stage(c).wait()
    tally[...] = jnp.zeros_like(tally)

    def hop(buf, way, c, b, to):
        return pltpu.make_async_remote_copy(
            src_ref=buf.at[c, b], dst_ref=buf.at[c, b], send_sem=z_send.at[way, c, b], recv_sem=z_recv.at[way, c, b],
            device_id=(to * 2 + y, own), device_id_type=MESH,
        )

    def here(c, b):
        at = pl.ds(b * STRIP, STRIP)
        return own_buf[c, at, :] + got[c, at, :].astype(f32)

    early, late = LAG * jnp.minimum(z, 3 - z), LAG * jnp.maximum(z, 3 - z)

    def step(t, carry):
        first = t - early

        @pl.when((first >= 0) & (first < n))
        def _():
            pltpu.make_async_copy(own_buf.at[first], own_buf.at[first], own_sem.at[first]).wait()
            cross(first).wait()

            @pl.when(first + DEPTH < n)
            def _():
                cross(first + DEPTH).start()

        for way, buf, lag, to, back in ((0, rise, LAG * z, z + 1, z - 1), (1, fall, LAG * (3 - z), z - 1, z + 1)):
            c = t - lag

            @pl.when((c >= 0) & (c < n))
            def _():
                for b in range(4):
                    beyond = (b > z) if way == 0 else (b < z)

                    @pl.when(beyond & (lag == 0))
                    def _():
                        buf[c, b] = here(c, b)

                    @pl.when(beyond & (lag > 0))
                    def _():
                        hop(buf, way, c, b, back).wait_recv()
                        buf[c, b] = buf[c, b] + here(c, b)

                    @pl.when(beyond & (c >= QUEUE))
                    def _():
                        hop(buf, way, c - QUEUE, b, to).wait_send()

                    @pl.when(beyond)
                    def _():
                        hop(buf, way, c, b, to).start()

        last = t - late

        @pl.when((last >= 0) & (last < n))
        def _():
            at = pl.ds(pl.multiple_of(z * STRIP, STRIP), STRIP)
            done[last] = own_buf[last, at, :] + got[last, at, :].astype(f32)

            @pl.when(z > 0)
            def _():
                hop(rise, 0, last, z, z - 1).wait_recv()
                done[last] = done[last] + rise[last, z]

            @pl.when(z < 3)
            def _():
                hop(fall, 1, last, z, z + 1).wait_recv()
                done[last] = done[last] + fall[last, z]

            value = done[last]
            square = value * value
            total = square[0:8, 0:128]
            for r in range(0, STRIP, 8):
                for k in range(0, CHUNK, 128):
                    if r or k:
                        total = total + square[r : r + 8, k : k + 128]
            tally[...] = tally[...] + total

        return carry

    lax.fori_loop(0, n + 3 * LAG, step, 0)
    summed = jnp.sum(tally[...])
    lane = lax.broadcasted_iota(jnp.int32, (8, 128), 1)
    mine = jnp.where(lane == 0, summed, jnp.where(lane == 1, num_ref[...], 0.0))
    quad_buf[own] = mine

    def share(buf, k, where, at):
        return pltpu.make_async_remote_copy(
            src_ref=buf.at[at], dst_ref=buf.at[at], send_sem=s_send.at[k], recv_sem=s_recv.at[k],
            device_id=where, device_id_type=MESH,
        )

    for d in range(1, 4):
        share(quad_buf, d, (dp, lax.rem(own + d, 4)), own).start()
    for (i, j), c in zip(places, range(n)):
        target, base = outs_at_of(outs_at, i)
        outs[target][:, base + j * CHUNK : base + (j + 1) * CHUNK] = done[c]
    for d in range(1, 4):
        share(quad_buf, d, (dp, own), lax.rem(own + 4 - d, 4)).wait_recv()
    line_buf[dp] = (quad_buf[0] + quad_buf[1]) + (quad_buf[2] + quad_buf[3])
    for d in range(1, 8):
        share(line_buf, 3 + d, (lax.rem(dp + d, 8), own), dp).start()
    for d in range(1, 8):
        share(line_buf, 3 + d, (dp, own), lax.rem(dp + 8 - d, 8)).wait_recv()
    stat = line_buf[0]
    for d in range(1, 8):
        stat = stat + line_buf[d]
    stat_ref[...] = stat
    for d in range(1, 4):
        share(quad_buf, d, (dp, own), own).wait_send()
    for d in range(1, 8):
        share(line_buf, 3 + d, (dp, own), dp).wait_send()

    def drain(c, carry):
        for b in range(4):
            @pl.when(b > z)
            def _():
                hop(rise, 0, c, b, z + 1).wait_send()

            @pl.when(b < z)
            def _():
                hop(fall, 1, c, b, z - 1).wait_send()
        return carry

    lax.fori_loop(n - QUEUE, n, drain, 0)


def outs_at_of(outs_at, i):
    for target, members in enumerate(outs_at):
        for index, base in members:
            if index == i:
                return target, base


def reduce_blocks(keep, give, numerator, outs_at, out_widths):
    widths = [a.shape[1] for a in keep]
    n = sum(widths) // CHUNK
    any_space = pl.BlockSpec(memory_space=pl.ANY)
    vmem = pl.BlockSpec(memory_space=pltpu.VMEM)
    half = 4 * STRIP
    return pl.pallas_call(
        functools.partial(reduce_kernel, tuple(widths), outs_at),
        out_shape=[jax.ShapeDtypeStruct((STRIP, w), f32) for w in out_widths] + [jax.ShapeDtypeStruct((8, 128), f32)],
        in_specs=[any_space] * (2 * len(keep)) + [vmem],
        out_specs=[vmem] * (len(out_widths) + 1),
        scratch_shapes=[
            pltpu.VMEM((n, half, CHUNK), f32),
            pltpu.VMEM((n, half, CHUNK), bf16),
            pltpu.VMEM((n, half, CHUNK), bf16),
            pltpu.VMEM((n, 4, STRIP, CHUNK), f32),
            pltpu.VMEM((n, 4, STRIP, CHUNK), f32),
            pltpu.VMEM((n, STRIP, CHUNK), f32),
            pltpu.VMEM((8, 128), f32),
            pltpu.VMEM((4, 8, 128), f32),
            pltpu.VMEM((8, 8, 128), f32),
            pltpu.SemaphoreType.DMA((n,)),
            pltpu.SemaphoreType.DMA((n,)),
            pltpu.SemaphoreType.DMA((n,)),
            pltpu.SemaphoreType.DMA((n,)),
            pltpu.SemaphoreType.DMA((2, n, 4)),
            pltpu.SemaphoreType.DMA((2, n, 4)),
            pltpu.SemaphoreType.DMA((11,)),
            pltpu.SemaphoreType.DMA((11,)),
        ],
        compiler_params=pltpu.CompilerParams(
            collective_id=1, has_side_effects=True, vmem_limit_bytes=52 * 2**20
        ),
        name="reduce_blocks",
    )(*keep, *give, numerator)


def ag(part):
    return lax.all_gather(part, "fsdp", axis=0, tiled=True)


def make_local(n_dp, n_f):
    fast = n_dp == 8 and n_f == 4

    def local(
        pixels, targets, valid_mask, lat_weight, segment_ids, present_vars, lead_index, step_count,
        w_agg, w_attn, w_mlp, w_io, w_small,
        m_agg, m_attn, m_mlp, m_io, m_small,
        v_agg, v_attn, v_mlp, v_io, v_small,
    ):
        masters = (w_agg, w_attn, w_mlp, w_io, w_small)
        firsts = (m_agg, m_attn, m_mlp, m_io, m_small)
        seconds = (v_agg, v_attn, v_mlp, v_io, v_small)
        rows = pixels.shape[1]
        row_len = segment_ids.shape[1]
        strip = w_agg.shape[0]
        own = lax.axis_index("fsdp")
        heads_here = HEADS // n_f
        wide = heads_here * HEAD_DIM

        seg = segment_ids[0]
        seg_own = lax.dynamic_slice_in_dim(seg, own * rows, rows)
        below = jnp.sum((seg[None, :] < seg_own[:, None]).astype(jnp.int32), axis=1)
        pos = own * rows + jnp.arange(rows, dtype=jnp.int32) - below
        onehot = (pos[:, None] == jnp.arange(SPAN, dtype=jnp.int32)[None, :]).astype(bf16)
        lead = (lead_index[0].astype(f32) + 1.0) / LEAD_STEPS
        pixel_rows = pixels[0]
        target = targets[0].astype(f32)
        present = present_vars[0]
        spread = (jnp.arange(MIX) // PIX)[None, :] == jnp.arange(VARS)[:, None]
        embed_col = (jnp.arange(MIX) - WIDTH)[None, :] == jnp.arange(VARS)[:, None]
        in_pixels = (jnp.arange(MIX) < WIDTH)[None, :]
        expand = jnp.where(in_pixels, spread, embed_col).astype(bf16)
        present_cols = jnp.repeat(present.astype(f32), PIX)
        pixel_weight = lat_weight[0][:, None] * valid_mask[0].astype(f32) * present_cols[None, :]
        weight_sum = jnp.sum(pixel_weight)

        pack = jnp.concatenate(
            [
                w_io[:, :USED].astype(bf16),
                w_small.astype(bf16),
                jnp.zeros((strip, 768 - USED - 9), bf16),
                w_agg.astype(bf16),
            ],
            axis=1,
        )
        if fast:
            head, attn, mlp, stat = gather_weights(
                pack, w_attn.astype(bf16), w_mlp.astype(bf16), jnp.full((8, 128), weight_sum, f32)
            )
            total = stat[0, 0]
        else:
            head = lax.all_gather(pack, ("dp", "fsdp"), axis=0, tiled=True)
            attn = lax.all_gather(w_attn.astype(bf16), ("dp", "fsdp"), axis=0, tiled=True)
            mlp = lax.all_gather(w_mlp.astype(bf16), ("dp", "fsdp"), axis=0, tiled=True)
            total = lax.psum(weight_sum, ("dp", "fsdp"))
        w240 = jnp.concatenate([head[:, :WIDTH], head[:, 2 * WIDTH : 2 * WIDTH + VARS]], axis=1)
        w_pred = head[:, WIDTH : 2 * WIDTH]
        w_pos = head[:, 2 * WIDTH + VARS : USED]
        small = head[:, USED : USED + 9].astype(f32).T
        agg_kv = head[:, 768 : 768 + 2 * D]
        agg_out = head[:, 768 + 2 * D :]
        w_qkv = attn[:, : 3 * D]
        w_out = attn[:, 3 * D :]
        w_up = mlp[:, :FF]
        w_down = mlp[:, FF:]

        pix_t = jnp.concatenate([pixel_rows.T, jnp.ones((VARS, rows), bf16)], axis=0)
        table = t_mm(w240, agg_kv)
        table_k = table[:, :D].reshape(MIX, HEADS, HEAD_DIM)
        table_v = table[:, D:].reshape(MIX, HEADS, HEAD_DIM)
        query = small[0].reshape(HEADS, HEAD_DIM)
        folded = jnp.sum(table_k * query[None], axis=2)
        block = folded.T[:, None, :] * expand.astype(f32)[None]
        score = exact("xc,cl->xl", block.reshape(HEADS * VARS, MIX), pix_t.astype(f32))
        score = score.reshape(HEADS, VARS, rows) * HEAD_DIM ** (-0.5)
        score = jnp.where(present[None, :, None] > 0, score, -1000000000.0)
        top = jnp.max(score, axis=1, keepdims=True)
        power = jnp.exp(score - top)
        soft = power / jnp.sum(power, axis=1, keepdims=True)
        share = soft.astype(bf16)
        pix_f = pix_t.astype(f32)
        lifted_share = jnp.einsum("vc,hvl->hcl", expand, share, preferred_element_type=f32) * pix_f[None]
        mixed_a = exact("che,hcl->hel", table_v, lifted_share).reshape(D, rows).T.astype(bf16)
        lead_embed = lead * small[7] + small[8]
        h0 = mm(mixed_a, agg_out) + mm_t(onehot, w_pos) + lead_embed[None]
        norm0, unit0, scale0 = norm_forward(h0, small[1], small[2])
        qkv = mm(norm0, w_qkv).astype(bf16)
        part = qkv.reshape(rows, 3, n_f, wide)
        part = lax.all_to_all(part, "fsdp", split_axis=2, concat_axis=0, tiled=True)
        part = part.reshape(row_len, 3, heads_here, HEAD_DIM)
        q, k, v = (part[:, i].transpose(1, 0, 2) for i in range(3))
        att_score = jnp.einsum("hqe,hke->hqk", q, k, preferred_element_type=f32) * HEAD_DIM ** (-0.5)
        same = seg[:, None] == seg[None, :]
        att_score = jnp.where(same[None], att_score, -1000000000.0)
        att_top = jnp.max(att_score, axis=-1, keepdims=True)
        att_power = jnp.exp(att_score - att_top)
        att_soft = att_power / jnp.sum(att_power, axis=-1, keepdims=True)
        att = att_soft.astype(bf16)
        mixed_h = jnp.einsum("hqk,hke->qhe", att, v, preferred_element_type=f32)
        mixed_h = mixed_h.reshape(row_len, wide).astype(bf16)
        mixed_all = lax.all_gather(mixed_h, "fsdp", axis=1, tiled=True)
        mixed = lax.dynamic_slice_in_dim(mixed_all, own * rows, rows, axis=0)
        h1 = h0 + mm(mixed, w_out)
        norm1, unit1, scale1 = norm_forward(h1, small[3], small[4])
        up = mm(norm1, w_up)
        gate = 0.5 * (1.0 + lax.erf(up * (2.0**-0.5)))
        lifted = (up * gate).astype(bf16)
        h2 = h1 + mm_t(lifted, w_down)
        norm2, unit2, scale2 = norm_forward(h2, small[5], small[6])
        predicted = mm(norm2, w_pred) * D ** (-0.5)
        error = predicted - target
        weighted = pixel_weight * error
        numerator = jnp.sum(weighted * error)

        d_pred = (weighted * (2.0 * D ** (-0.5) / total)).astype(bf16)
        d_norm2 = mm_t(d_pred, w_pred)
        d_h2, d_gain2, d_off2 = norm_backward(d_norm2, unit2, scale2, small[5])
        d_out = d_h2.astype(bf16)
        slope = gate + up * jnp.exp(-0.5 * up * up) * 0.3989422804014327
        d_up = (mm(d_out, w_down) * slope).astype(bf16)
        d_norm1 = mm_t(d_up, w_up)
        d_in, d_gain1, d_off1 = norm_backward(d_norm1, unit1, scale1, small[3])
        d_h1 = d_h2 + d_in
        d_proj_all = ag(d_h1.astype(bf16))
        w_out_own = lax.dynamic_slice_in_dim(w_out, own * wide, wide, axis=0)
        d_mixed = mm_t(d_proj_all, w_out_own).astype(bf16).reshape(row_len, heads_here, HEAD_DIM).transpose(1, 0, 2)
        d_att = jnp.einsum("hqe,hke->hqk", d_mixed, v, preferred_element_type=f32)
        d_v = jnp.einsum("hqk,hqe->khe", att, d_mixed, preferred_element_type=f32)
        lean = jnp.sum(att_soft * d_att, axis=-1, keepdims=True)
        d_score = (att_soft * (d_att - lean) * HEAD_DIM ** (-0.5)).astype(bf16)
        d_q = jnp.einsum("hqk,hke->qhe", d_score, k, preferred_element_type=f32)
        d_k = jnp.einsum("hqk,hqe->khe", d_score, q, preferred_element_type=f32)
        d_part = jnp.stack([d_q, d_k, d_v], axis=1).astype(bf16).reshape(row_len, 3, 1, wide)
        d_qkv_all = lax.all_gather(d_part, "fsdp", axis=2, tiled=True).reshape(row_len, 3 * D)
        d_qkv = lax.dynamic_slice_in_dim(d_qkv_all, own * rows, rows, axis=0)
        d_norm0 = mm_t(d_qkv, w_qkv)
        d_in, d_gain0, d_off0 = norm_backward(d_norm0, unit0, scale0, small[1])
        d_h0 = d_h1 + d_in
        d_agg = d_h0.astype(bf16)
        d_mixed_a = mm_t(agg_out, d_agg).astype(bf16).reshape(HEADS, HEAD_DIM, rows)
        pulled = exact("che,hel->hcl", table_v, d_mixed_a.astype(f32)) * pix_f[None]
        d_share = exact("vc,hcl->hvl", expand.astype(f32), pulled)
        lean_a = jnp.sum(soft * d_share, axis=1, keepdims=True)
        d_score_a = (soft * (d_share - lean_a) * HEAD_DIM ** (-0.5)).astype(bf16)
        spread_score = jnp.einsum("vc,hvl->hcl", expand, d_score_a, preferred_element_type=f32)
        d_folded = jnp.sum(spread_score * pix_f[None], axis=2)
        d_table_v = exact("hcl,hel->che", lifted_share, d_mixed_a.astype(f32)).reshape(MIX, D)
        d_table_k = (d_folded.T[:, :, None] * query[None]).reshape(MIX, D)
        d_query = jnp.sum(d_folded.T[:, :, None] * table_k, axis=0).reshape(D)
        d_bias = jnp.sum(d_h0, axis=0)
        narrow = jnp.stack(
            [d_query, d_gain0, d_off0, d_gain1, d_off1, d_gain2, d_off2, lead * d_bias, d_bias]
            + [jnp.zeros((D,), f32)] * 7
        )
        d_table, narrow = lax.psum((jnp.concatenate([d_table_k, d_table_v], axis=1), narrow), "fsdp")

        source = jnp.arange(D)
        pick = (source // strip) % n_f == own
        if fast:
            line, side = source // 256, (source // 128) % 2
            here = lax.axis_index("dp") % 2
            place = jnp.where(side == here, 0, 4 * strip) + line * strip + source % strip
        else:
            place = (source // (strip * n_f)) * strip + source % strip
        choose = (pick[:, None] & (place[:, None] == jnp.arange(n_dp * strip)[None, :])).astype(bf16)

        def mine(array):
            width = array.shape[1]
            if not fast:
                whole = array.reshape(n_dp, n_f, strip, width)
                return (lax.dynamic_index_in_dim(whole, own, 1, False).reshape(n_dp * strip, width),)
            whole = array.reshape(4, 2 * n_f, strip, width)
            return tuple(
                lax.dynamic_index_in_dim(whole, at * n_f + own, 1, False).reshape(4 * strip, width)
                for at in (here, 1 - here)
            )

        def split(picked):
            if not fast:
                return (picked,)
            return picked[:, : 4 * strip], picked[:, 4 * strip :]

        def weight_grad(features, grads):
            return tuple(t_mm(part, grads) for part in split(mm(features, choose).astype(bf16)))

        d_agg_all = ag(d_agg)
        g_qkv = weight_grad(ag(norm0), d_qkv_all)
        g_proj = weight_grad(mixed_all, d_proj_all)
        g_up = weight_grad(ag(norm1), ag(d_up))
        g_down = weight_grad(ag(d_out), ag(lifted))
        g_out = weight_grad(ag(mixed_a), d_agg_all)
        g_kv = tuple(exact("dc,cx->dx", part.astype(f32), d_table) for part in mine(w240))
        g_240 = tuple(exact("dx,cx->dc", part.astype(f32), d_table) for part in mine(agg_kv))
        g_pred = weight_grad(ag(norm2), ag(d_pred))
        g_pos = weight_grad(d_agg_all, ag(onehot))
        g_small = mine(narrow.T)
        g_misc = tuple(
            jnp.concatenate(
                [a[:, :WIDTH], b, a[:, WIDTH:], c, d[:, :9], jnp.zeros((a.shape[0], MISC - USED - 9), f32)], axis=1
            )
            for a, b, c, d in zip(g_240, g_pred, g_pos, g_small)
        )
        groups = (g_kv, g_out, g_qkv, g_proj, g_up, g_down, g_misc)
        if fast:
            lane = lax.broadcasted_iota(jnp.int32, (8, 128), 1)
            r_agg, r_attn, r_mlp, r_misc, stat = reduce_blocks(
                [g[0] for g in groups],
                [g[1].astype(bf16) for g in groups],
                jnp.where(lane == 1, numerator, 0.0),
                (((0, 0), (1, 2 * D)), ((2, 0), (3, 3 * D)), ((4, 0), (5, FF)), ((6, 0),)),
                (3 * D, 4 * D, 2 * FF, MISC),
            )
            squares, numerator = stat[0, 0], stat[0, 1]
        else:
            r_kv, r_out, r_qkv, r_proj, r_up, r_down, r_misc = (
                lax.psum_scatter(g[0], "dp", scatter_dimension=0, tiled=True) for g in groups
            )
            r_agg = jnp.concatenate([r_kv, r_out], axis=1)
            r_attn = jnp.concatenate([r_qkv, r_proj], axis=1)
            r_mlp = jnp.concatenate([r_up, r_down], axis=1)
            local_squares = sum(jnp.sum(piece * piece) for piece in (r_agg, r_attn, r_mlp, r_misc))
            squares, numerator = lax.psum((local_squares, numerator), ("dp", "fsdp"))
        r_io = jnp.concatenate([r_misc[:, :USED], jnp.zeros((strip, w_io.shape[1] - USED), f32)], axis=1)
        reduced = (r_agg, r_attn, r_mlp, r_io, r_misc[:, USED : USED + 9])
        grad_norm = jnp.sqrt(squares)
        factor = jnp.minimum(1.0, clip_limit / grad_norm)
        loss = numerator / total
        step_value = step_count[0].astype(f32)
        results = [
            adamw(masters[i], reduced[i] * factor, firsts[i], seconds[i], step_value, learn_rates[i]) for i in range(5)
        ]
        return (loss, grad_norm) + tuple(results[i][j] for j in range(4) for i in range(5))

    return local


def solution(mesh):
    flat = P(("dp", "fsdp"), None)
    tokens = P("dp", "fsdp", None)
    return jax.shard_map(
        make_local(mesh.shape["dp"], mesh.shape["fsdp"]),
        mesh=mesh,
        in_specs=(tokens, tokens, tokens, P("dp", "fsdp"), P("dp", None), P("dp", None), P("dp"), P()) + (flat,) * 15,
        out_specs=(P(), P()) + (flat,) * 20,
        check_vma=False,
    )
```

```python
import functools

import jax
import jax.numpy as jnp
from jax import lax
from jax.experimental import pallas as pl
from jax.experimental.pallas import tpu as pltpu
from jax.sharding import PartitionSpec as P

D = 1024
HEADS = 16
HEAD_DIM = 64
FF = 4096
VARS = 48
PIX = 4
LEAD_STEPS = 8
WIDTH = VARS * PIX
SPAN = 256
MIX = 256
HEAD = 896

norm_eps = 1e-05
clip_limit = 1.0
decay_rate = 0.05
adam_eps = 1e-08
learn_rates = (0.03, 0.03, 0.03, 0.2, 0.3)
f32 = jnp.float32
bf16 = jnp.bfloat16
highest = lax.Precision.HIGHEST
MESH = pl.DeviceIdType.MESH
STRIP = 32
CHUNK = 512
LAG = 2
QUEUE = 2


def dot(left, right, dims):
    return lax.dot_general(left, right, (dims, ((), ())), preferred_element_type=f32)


def mm(left, right):
    return dot(left, right, ((1,), (0,)))


def mm_t(left, right):
    return dot(left, right, ((1,), (1,)))


def t_mm(left, right):
    return dot(left, right, ((0,), (0,)))


def exact(eq, left, right):
    return jnp.einsum(eq, left, right, precision=highest, preferred_element_type=f32)


def norm_forward(values, gain, offset):
    average = jnp.mean(values, axis=-1, keepdims=True)
    centred = values - average
    scale = lax.rsqrt(jnp.mean(centred * centred, axis=-1, keepdims=True) + norm_eps)
    unit = centred * scale
    return (unit * gain[None] + offset[None]).astype(bf16), unit, scale


def norm_backward(grad, unit, scale, gain):
    inner = grad * gain[None]
    mean_inner = jnp.mean(inner, axis=-1, keepdims=True)
    mean_product = jnp.mean(inner * unit, axis=-1, keepdims=True)
    back = scale * (inner - mean_inner - unit * mean_product)
    return back, jnp.sum(grad * unit, axis=0), jnp.sum(grad, axis=0)


def adamw(weight, grad, moment, second, step_value, learn_rate):
    moment = 0.5 * moment + 0.5 * grad
    second = 0.5 * second + 0.5 * grad * grad
    correct = 1.0 - jnp.power(f32(0.5), step_value)
    update = moment / correct / (jnp.sqrt(second / correct) + adam_eps) + decay_rate * weight
    fresh = weight - learn_rate * update
    return (fresh, fresh.astype(bf16), moment, second)


PIECES = (
    (0, 0, 1920, "yzx"), (2, 0, 2688, "zxy"), (0, 1920, 2048, "yzx"), (2, 2688, 2816, "zxy"),
    (1, 0, 1920, "yzx"), (2, 5504, 2688, "zxy"), (1, 1920, 2176, "zxy"),
)


def gather_kernel(*refs):
    shards, num_ref, wholes, stat_ref = refs[0:3], refs[3], refs[4:7], refs[7]
    quad_buf, line_buf, own_sem, s_send, s_recv, sends, arrive, pass_on = refs[8:]
    dp, own = lax.axis_index("dp"), lax.axis_index("fsdp")
    z, y, x, core = dp // 2, dp % 2, own // 2, own % 2
    sibling = x * 2 + 1 - core
    barrier = pltpu.get_barrier_semaphore()
    for d in range(1, 8):
        pl.semaphore_signal(barrier, inc=1, device_id=(lax.rem(dp + d, 8), own), device_id_type=MESH)
    for d in range(1, 4):
        pl.semaphore_signal(barrier, inc=1, device_id=(dp, lax.rem(own + d, 4)), device_id_type=MESH)
    pl.semaphore_wait(barrier, 10)

    def view(p, ident, plane):
        a, start, width, order = PIECES[p]
        row = pl.multiple_of(((ident // 2) * 4 + (ident % 2) * 2 + plane) * STRIP, STRIP)
        return wholes[a].at[pl.ds(row, STRIP), pl.ds(start, width)]

    def copy(p, ident, slot, to, mine=False):
        a, start, width, order = PIECES[p]
        src = shards[a].at[:, pl.ds(start, width)] if mine else view(p, ident, core)
        sem = pass_on if slot == 4 else arrive
        return pltpu.make_async_remote_copy(
            src_ref=src, dst_ref=view(p, ident, core), send_sem=sends.at[p, ident, slot], recv_sem=sem.at[p, ident],
            device_id=to, device_id_type=MESH,
        )

    def arrival(p, ident, plane, sem):
        return pltpu.make_async_copy(view(p, ident, plane), view(p, ident, plane), sem.at[p, ident])

    def targets(p, rx, ry, rz):
        order = PIECES[p][3]
        moved = {"x": rx != 0, "y": ry != 0, "z": rz is not None}
        stage = max([k for k in range(3) if moved[order[k]]], default=-1)
        found = []
        if stage >= 0 and order[stage] == "z":
            found.append((0, (rz < 0) & (z < 3), ((dp + 2) % 8, own)))
            found.append((1, (rz > 0) & (z > 0), ((dp + 6) % 8, own)))
        for k in range(stage + 1, 3):
            if order[k] == "z":
                found.append((0, z < 3, ((dp + 2) % 8, own)))
                found.append((1, z > 0, ((dp + 6) % 8, own)))
            elif order[k] == "x":
                found.append((2, None, (dp, (1 - x) * 2 + core)))
            else:
                found.append((3, None, (z * 2 + 1 - y, own)))
        found.append((4, None, (dp, sibling)))
        return found

    def source(rx, ry, rz):
        sz = z if rz is None else z + rz
        sy = 1 - y if ry else y
        sx = 1 - x if rx else x
        return sz, (sz * 2 + sy) * 2 + sx

    def each(rx, ry, rz, act, mine=False):
        sz, ident = source(rx, ry, rz)

        def body():
            for p in range(len(PIECES)):
                if act == "send" and not mine:
                    arrival(p, ident, core, arrive).wait()
                for slot, when, to in targets(p, rx, ry, rz):
                    def go(slot=slot, to=to):
                        c = copy(p, ident, slot, to, mine)
                        c.start() if act == "send" else c.wait_send()

                    if when is None:
                        go()
                    else:
                        pl.when(when)(go)

        if rz is None:
            body()
        else:
            pl.when((sz >= 0) & (sz < 4))(body)

    def over_z(pairs, act):
        def step(t, carry):
            rz = ((t + 1) // 2) * (1 - 2 * (t % 2))
            for rx, ry in pairs:
                each(rx, ry, rz, act)
            return carry

        lax.fori_loop(1, 7, step, 0)

    def sweep(act):
        each(0, 0, None, act, mine=True)
        if act == "send":
            for a in range(3):
                row = pl.multiple_of((dp * 4 + own) * STRIP, STRIP)
                pltpu.make_async_copy(shards[a], wholes[a].at[pl.ds(row, STRIP), :], own_sem.at[a]).start()
            scalars()
        each(1, 0, None, act)
        each(0, 1, None, act)
        over_z([(0, 0)], act)
        each(1, 1, None, act)
        over_z([(1, 0), (0, 1)], act)
        over_z([(1, 1)], act)

    def share(buf, k, where, at):
        return pltpu.make_async_remote_copy(
            src_ref=buf.at[at], dst_ref=buf.at[at], send_sem=s_send.at[k], recv_sem=s_recv.at[k],
            device_id=where, device_id_type=MESH,
        )

    def scalars():
        quad_buf[own] = num_ref[...]
        for d in range(1, 4):
            share(quad_buf, d, (dp, lax.rem(own + d, 4)), own).start()

    sweep("send")
    for d in range(1, 4):
        share(quad_buf, d, (dp, own), lax.rem(own + 4 - d, 4)).wait_recv()
    line_buf[dp] = (quad_buf[0] + quad_buf[1]) + (quad_buf[2] + quad_buf[3])
    for d in range(1, 8):
        share(line_buf, 3 + d, (lax.rem(dp + d, 8), own), dp).start()

    def closing(ident, carry):
        for p in range(len(PIECES)):
            arrival(p, ident, 1 - core, pass_on).wait()
        return carry

    lax.fori_loop(0, 16, closing, 0)
    for a in range(3):
        row = pl.multiple_of((dp * 4 + own) * STRIP, STRIP)
        pltpu.make_async_copy(shards[a], wholes[a].at[pl.ds(row, STRIP), :], own_sem.at[a]).wait()
    sweep("drain")
    for d in range(1, 8):
        share(line_buf, 3 + d, (dp, own), lax.rem(dp + 8 - d, 8)).wait_recv()
    stat = line_buf[0]
    for d in range(1, 8):
        stat = stat + line_buf[d]
    stat_ref[...] = stat
    for d in range(1, 4):
        share(quad_buf, d, (dp, own), own).wait_send()
    for d in range(1, 8):
        share(line_buf, 3 + d, (dp, own), dp).wait_send()


def gather_weights(head, attn, mlp, number):
    any_space = pl.BlockSpec(memory_space=pl.ANY)
    vmem = pl.BlockSpec(memory_space=pltpu.VMEM)
    n = len(PIECES)
    return pl.pallas_call(
        gather_kernel,
        out_shape=[jax.ShapeDtypeStruct((D, a.shape[1]), bf16) for a in (head, attn, mlp)]
        + [jax.ShapeDtypeStruct((8, 128), f32)],
        in_specs=[any_space] * 3 + [vmem],
        out_specs=[any_space] * 3 + [vmem],
        scratch_shapes=[
            pltpu.VMEM((4, 8, 128), f32),
            pltpu.VMEM((8, 8, 128), f32),
            pltpu.SemaphoreType.DMA((3,)),
            pltpu.SemaphoreType.DMA((11,)),
            pltpu.SemaphoreType.DMA((11,)),
            pltpu.SemaphoreType.DMA((n, 16, 5)),
            pltpu.SemaphoreType.DMA((n, 16)),
            pltpu.SemaphoreType.DMA((n, 16)),
        ],
        compiler_params=pltpu.CompilerParams(collective_id=0, has_side_effects=True),
        name="gather_weights",
    )(head, attn, mlp, number)


SEGMENTS = ((0, 2, 0), (2, 8, 1), (8, 16, 2), (16, 24, 3), (24, 26, 4))
N_STD, N_ALL, FIRST_SENT, AHEAD, BASE = 26, 32, 8, 4, 2


def gradient_kernel(*refs):
    (mixed_t, norm0_t, norm1_t, out_t, mixa_t, norm2_t, agg_t,
     d_proj, d_qkv, d_up, lifted, d_agg, d_pred, onehot, d_table, narrow, head, num_ref) = refs[:18]
    r_agg, r_attn, r_mlp, r_misc, stat_ref = refs[18:23]
    (feats, ys, tabs, preds, hots, narrows, w240, wkv, acc240, own_buf, give_buf, got, rise, fall, tally, quad_buf,
     line_buf, load_sem, feat_send, feat_recv, y_xsend, y_xrecv, tab_send, tab_recv, pred_send, pred_recv,
     nar_send, nar_recv, y_send, y_recv, z_send, z_recv, s_send, s_recv) = refs[23:]
    dp, own = lax.axis_index("dp"), lax.axis_index("fsdp")
    z, y, x, core = dp // 2, dp % 2, own // 2, own % 2
    sibling, across, diagonal = x * 2 + 1 - core, (1 - x) * 2 + core, (1 - x) * 2 + 1 - core
    over = z * 2 + 1 - y
    barrier = pltpu.get_barrier_semaphore()
    for d in range(1, 8):
        pl.semaphore_signal(barrier, inc=1, device_id=(lax.rem(dp + d, 8), own), device_id_type=MESH)
    for d in range(1, 4):
        pl.semaphore_signal(barrier, inc=1, device_id=(dp, lax.rem(own + d, 4)), device_id_type=MESH)
    pl.semaphore_wait(barrier, 10)
    n = N_ALL
    row = pl.ds(pl.multiple_of(own * 128, 128), 128)
    sent_feats = (norm0_t, norm1_t, out_t, mixa_t, norm2_t, agg_t)

    def remote(src, dst, send, recv, to):
        return pltpu.make_async_remote_copy(
            src_ref=src, dst_ref=dst, send_sem=send, recv_sem=recv, device_id=(dp, to), device_id_type=MESH
        )

    loads = []

    def load(src, dst):
        copy = pltpu.make_async_copy(src, dst, load_sem.at[len(loads)])
        copy.start()
        loads.append(copy)

    def feat_send_all(k, d):
        to = lax.rem(own + d, 4)
        for half in range(2):
            side = y if half == 0 else 1 - y
            remote(
                sent_feats[k].at[:, side, to], feats.at[k + 1, half, :, :, row], feat_send.at[k, d, half],
                feat_recv.at[k, d, half], to,
            ).start()

    for k in range(6):
        for d in range(1, 4):
            feat_send_all(k, d)
    for half in range(2):
        load(mixed_t.at[:, y if half == 0 else 1 - y, own], feats.at[0, half])
    for c in range(2):
        load(d_proj.at[:, pl.ds(c * CHUNK, CHUNK)], ys.at[c])
    for k in range(6):
        for half in range(2):
            load(sent_feats[k].at[:, y if half == 0 else 1 - y, own], feats.at[k + 1, half, :, :, row])
    for c in range(6):
        load(d_qkv.at[:, pl.ds(c * CHUNK, CHUNK)], ys.at[2 + c])
    staged = len(loads)
    for source, width, at in ((d_up, FF, 8), (lifted, FF, 16), (d_agg, D, 24)):
        for c in range(width // CHUNK):
            load(source.at[:, pl.ds(c * CHUNK, CHUNK)], ys.at[at + c, row, :])
    for v in range(4):
        load(d_table.at[:, pl.ds(v * CHUNK, CHUNK)], tabs.at[v, own])
    load(d_pred, preds.at[row, :])
    load(onehot, hots)
    for half in range(2):
        side = y if half == 0 else 1 - y
        load(narrow.at[:, side, own], narrows.at[own, half])
        load(head.at[:, side, own, :, pl.ds(0, 256)], w240.at[half])
        load(head.at[:, side, own, :, pl.ds(HEAD, 2 * D)], wkv.at[half])

    def unit(u, who, slot, to):
        block = ys.at[FIRST_SENT + u, pl.ds(pl.multiple_of(who * 128, 128), 128), :]
        return remote(block, block, y_xsend.at[u, slot], y_xrecv.at[u, who], to)

    def table(v, who, slot, to):
        return remote(tabs.at[v, who], tabs.at[v, who], tab_send.at[v, slot], tab_recv.at[v, who], to)

    for copy in loads[staged:]:
        copy.wait()

    def begin(u, carry):
        unit(u, own, 0, across).start()
        unit(u, own, 1, sibling).start()
        return carry

    lax.fori_loop(0, N_STD - FIRST_SENT, begin, 0)
    for v in range(4):
        table(v, own, 0, across).start()
        table(v, own, 1, sibling).start()

    def pred_copy(d, who, to):
        block = preds.at[pl.ds(pl.multiple_of(who * 128, 128), 128), :]
        return remote(block, block, pred_send.at[d], pred_recv.at[d], to)

    def narrow_copy(d, half, who, to):
        side = y if half == 0 else 1 - y
        return remote(narrow.at[:, side, to], narrows.at[who, half], nar_send.at[d, half], nar_recv.at[d, half], to)

    for d in range(1, 4):
        pred_copy(d, own, lax.rem(own + d, 4)).start()
        for half in range(2):
            narrow_copy(d, half, own, lax.rem(own + d, 4)).start()
    for copy in loads[:staged]:
        copy.wait()
    tally[...] = jnp.zeros_like(tally)
    acc240[...] = jnp.zeros_like(acc240)

    def feat_wait(k):
        for d in range(1, 4):
            for half in range(2):
                place = feats.at[k + 1, half, :, :, row]
                remote(place, place, feat_send.at[k, d, half], feat_recv.at[k, d, half], own).wait_recv()

    def put(c, value):
        own_buf[c] = value[:128]
        give_buf[c] = value[128:].astype(bf16)

    def feature(k):
        return feats[k].reshape(256, 512)

    def matmul(a, b):
        return lax.dot_general(a, b, (((1,), (0,)), ((), ())), preferred_element_type=f32)

    def two(value):
        high = value.astype(bf16)
        return high, (value - high.astype(f32)).astype(bf16)

    def summed_table(v):
        total = tabs[v, 0].astype(f32) + tabs[v, 1].astype(f32)
        return two(total + tabs[v, 2].astype(f32) + tabs[v, 3].astype(f32))

    def compute(c):
        for low, high, k in SEGMENTS:
            if k > 0:
                pl.when(c == low)(functools.partial(feat_wait, k - 1))

            @pl.when((c >= low) & (c < high))
            def _():
                if low >= FIRST_SENT:
                    u = c - FIRST_SENT
                    unit(u, sibling, 1, own).wait_recv()
                    unit(u, diagonal, 2, own).wait_recv()
                put(c, matmul(feature(k), ys[c]))

        @pl.when((c >= N_STD) & (c < N_STD + 4))
        def _():
            v = c - N_STD
            table(v, sibling, 1, own).wait_recv()
            table(v, diagonal, 2, own).wait_recv()
            high, low = summed_table(v)
            rows = w240[...].reshape(256, 256)
            put(c, matmul(rows, high) + matmul(rows, low))

        for v in range(4):
            @pl.when(c == N_STD + v)
            def _():
                high, low = summed_table(v)
                rows = wkv[:, :, :, v * CHUNK : (v + 1) * CHUNK].reshape(256, CHUNK)
                dims = (((1,), (1,)), ((), ()))
                acc240[...] = (
                    acc240[...]
                    + lax.dot_general(rows, high, dims, preferred_element_type=f32)
                    + lax.dot_general(rows, low, dims, preferred_element_type=f32)
                )

        @pl.when(c == N_STD + 4)
        def _():
            feat_wait(4)
            for d in range(1, 4):
                pred_copy(d, lax.rem(own + 4 - d, 4), own).wait_recv()
            value = matmul(feature(5), preds[...])
            own_buf[c, :, 0:256] = acc240[:128]
            own_buf[c, :, 256:512] = value[:128]
            give_buf[c, :, 0:256] = acc240[128:].astype(bf16)
            give_buf[c, :, 256:512] = value[128:].astype(bf16)

        @pl.when(c == N_STD + 5)
        def _():
            feat_wait(5)
            for d in range(1, 4):
                for half in range(2):
                    place = narrows.at[lax.rem(own + 4 - d, 4), half]
                    remote(place, place, nar_send.at[d, half], nar_recv.at[d, half], own).wait_recv()
            value = matmul(feature(6), hots[...])
            small = ((narrows[0] + narrows[1]) + (narrows[2] + narrows[3])).reshape(256, 128)
            empty = jnp.zeros((128, 128), f32)
            own_buf[c, :, 0:256] = value[:128]
            own_buf[c, :, 256:384] = small[:128]
            own_buf[c, :, 384:512] = empty
            give_buf[c, :, 0:256] = value[128:].astype(bf16)
            give_buf[c, :, 256:384] = small[128:].astype(bf16)
            give_buf[c, :, 384:512] = empty.astype(bf16)

    def cross(c):
        return pltpu.make_async_remote_copy(
            src_ref=give_buf.at[c], dst_ref=got.at[c], send_sem=y_send.at[c],
            recv_sem=y_recv.at[c], device_id=(over, own), device_id_type=MESH,
        )

    def hop(buf, way, c, b, to):
        at = b - 1 if way == 0 else b
        return pltpu.make_async_remote_copy(
            src_ref=buf.at[c, at], dst_ref=buf.at[c, at], send_sem=z_send.at[way, c, at], recv_sem=z_recv.at[way, c, at],
            device_id=(to * 2 + y, own), device_id_type=MESH,
        )

    def here(c, b):
        at = pl.ds(b * STRIP, STRIP)
        return own_buf[c, at, :] + got[c, at, :].astype(f32)

    early, late = LAG * jnp.minimum(z, 3 - z), LAG * jnp.maximum(z, 3 - z)

    def step(t, carry):
        u = t - AHEAD

        @pl.when((u >= 0) & (u < N_STD - FIRST_SENT))
        def _():
            unit(u, across, 0, own).wait_recv()
            unit(u, across, 2, sibling).start()

        v = u - (N_STD - FIRST_SENT)

        @pl.when((v >= 0) & (v < 4))
        def _():
            table(v, across, 0, own).wait_recv()
            table(v, across, 2, sibling).start()

        @pl.when(t < n)
        def _():
            compute(t)
            cross(t).start()

        first = t - BASE - early

        @pl.when((first >= 0) & (first < n))
        def _():
            cross(first).wait()

        for way, buf, lag, to, back in ((0, rise, LAG * z, z + 1, z - 1), (1, fall, LAG * (3 - z), z - 1, z + 1)):
            c = t - BASE - lag

            @pl.when((c >= 0) & (c < n))
            def _():
                for b in ((1, 2, 3) if way == 0 else (0, 1, 2)):
                    beyond = (b > z) if way == 0 else (b < z)
                    at = b - 1 if way == 0 else b

                    @pl.when(beyond & (lag == 0))
                    def _():
                        buf[c, at] = here(c, b)

                    @pl.when(beyond & (lag > 0))
                    def _():
                        hop(buf, way, c, b, back).wait_recv()
                        buf[c, at] = buf[c, at] + here(c, b)

                    @pl.when(beyond & (c >= QUEUE))
                    def _():
                        hop(buf, way, c - QUEUE, b, to).wait_send()

                    @pl.when(beyond)
                    def _():
                        hop(buf, way, c, b, to).start()

        last = t - BASE - late

        @pl.when((last >= 0) & (last < n))
        def _():
            at = pl.ds(pl.multiple_of(z * STRIP, STRIP), STRIP)
            value = own_buf[last, at, :] + got[last, at, :].astype(f32)
            own_buf[last, 0:STRIP, :] = value

            @pl.when(z > 0)
            def _():
                hop(rise, 0, last, z, z - 1).wait_recv()
                own_buf[last, 0:STRIP, :] = own_buf[last, 0:STRIP, :] + rise[last, z - 1]

            @pl.when(z < 3)
            def _():
                hop(fall, 1, last, z, z + 1).wait_recv()
                own_buf[last, 0:STRIP, :] = own_buf[last, 0:STRIP, :] + fall[last, z]

            value = own_buf[last, 0:STRIP, :]
            square = value * value
            total = square[0:8, 0:128]
            for r in range(0, STRIP, 8):
                for k in range(0, CHUNK, 128):
                    if r or k:
                        total = total + square[r : r + 8, k : k + 128]
            tally[...] = tally[...] + total

        return carry

    lax.fori_loop(0, n + BASE + 3 * LAG, step, 0)
    summed = jnp.sum(tally[...])
    lane = lax.broadcasted_iota(jnp.int32, (8, 128), 1)
    quad_buf[own] = jnp.where(lane == 0, summed, jnp.where(lane == 1, num_ref[...], 0.0))

    def share(buf, k, where, at):
        return pltpu.make_async_remote_copy(
            src_ref=buf.at[at], dst_ref=buf.at[at], send_sem=s_send.at[k], recv_sem=s_recv.at[k],
            device_id=where, device_id_type=MESH,
        )

    for d in range(1, 4):
        share(quad_buf, d, (dp, lax.rem(own + d, 4)), own).start()
    for out, base, low, high in (
        (r_attn, 3 * D, 0, 2), (r_attn, 0, 2, 8), (r_mlp, 0, 8, 24), (r_agg, 2 * D, 24, 26), (r_agg, 0, 26, 30),
        (r_misc, 0, 30, 32),
    ):
        for c in range(low, high):
            out[:, base + (c - low) * CHUNK : base + (c - low + 1) * CHUNK] = own_buf[c, 0:STRIP, :]
    for d in range(1, 4):
        share(quad_buf, d, (dp, own), lax.rem(own + 4 - d, 4)).wait_recv()
    line_buf[dp] = (quad_buf[0] + quad_buf[1]) + (quad_buf[2] + quad_buf[3])
    for d in range(1, 8):
        share(line_buf, 3 + d, (lax.rem(dp + d, 8), own), dp).start()
    for d in range(1, 8):
        share(line_buf, 3 + d, (dp, own), lax.rem(dp + 8 - d, 8)).wait_recv()
    stat = line_buf[0]
    for d in range(1, 8):
        stat = stat + line_buf[d]
    stat_ref[...] = stat
    for d in range(1, 4):
        share(quad_buf, d, (dp, own), own).wait_send()
    for d in range(1, 8):
        share(line_buf, 3 + d, (dp, own), dp).wait_send()
    for k in range(6):
        for d in range(1, 4):
            for half in range(2):
                place = feats.at[k + 1, half, :, :, row]
                remote(place, place, feat_send.at[k, d, half], feat_recv.at[k, d, half], own).wait_send()
    for d in range(1, 4):
        pred_copy(d, own, own).wait_send()
        for half in range(2):
            narrow_copy(d, half, own, own).wait_send()
    for v in range(4):
        for slot, who in ((0, own), (1, own), (2, across)):
            table(v, who, slot, own).wait_send()

    def finish(u, carry):
        for slot, who in ((0, own), (1, own), (2, across)):
            unit(u, who, slot, own).wait_send()
        return carry

    lax.fori_loop(0, N_STD - FIRST_SENT, finish, 0)

    def drain(c, carry):
        for b in (1, 2, 3):
            pl.when(b > z)(lambda: hop(rise, 0, c, b, z).wait_send())
        for b in (0, 1, 2):
            pl.when(b < z)(lambda: hop(fall, 1, c, b, z).wait_send())
        return carry

    lax.fori_loop(n - QUEUE, n, drain, 0)


def gradient_blocks(operands, numbers):
    any_space = pl.BlockSpec(memory_space=pl.ANY)
    vmem = pl.BlockSpec(memory_space=pltpu.VMEM)
    n = N_ALL
    units = N_STD - FIRST_SENT
    dma = pltpu.SemaphoreType.DMA
    widths = (3 * D, 4 * D, 2 * FF, 2 * CHUNK)
    return pl.pallas_call(
        gradient_kernel,
        out_shape=[jax.ShapeDtypeStruct((STRIP, w), f32) for w in widths] + [jax.ShapeDtypeStruct((8, 128), f32)],
        in_specs=[any_space] * 17 + [vmem],
        out_specs=[vmem] * 5,
        scratch_shapes=[
            pltpu.VMEM((7, 2, 4, STRIP, 512), bf16),
            pltpu.VMEM((N_STD, 512, CHUNK), bf16),
            pltpu.VMEM((4, 4, 256, CHUNK), bf16),
            pltpu.VMEM((512, 256), bf16),
            pltpu.VMEM((512, 256), bf16),
            pltpu.VMEM((4, 2, 4, STRIP, 128), f32),
            pltpu.VMEM((2, 4, STRIP, 256), bf16),
            pltpu.VMEM((2, 4, STRIP, 2 * D), bf16),
            pltpu.VMEM((256, 256), f32),
            pltpu.VMEM((n, 4 * STRIP, CHUNK), f32),
            pltpu.VMEM((n, 4 * STRIP, CHUNK), bf16),
            pltpu.VMEM((n, 4 * STRIP, CHUNK), bf16),
            pltpu.VMEM((n, 3, STRIP, CHUNK), f32),
            pltpu.VMEM((n, 3, STRIP, CHUNK), f32),
            pltpu.VMEM((8, 128), f32),
            pltpu.VMEM((4, 8, 128), f32),
            pltpu.VMEM((8, 8, 128), f32),
            dma((56,)),
            dma((6, 4, 2)),
            dma((6, 4, 2)),
            dma((units, 3)),
            dma((units, 4)),
            dma((4, 3)),
            dma((4, 4)),
            dma((4,)),
            dma((4,)),
            dma((4, 2)),
            dma((4, 2)),
            dma((n,)),
            dma((n,)),
            dma((2, n, 3)),
            dma((2, n, 3)),
            dma((11,)),
            dma((11,)),
        ],
        compiler_params=pltpu.CompilerParams(
            collective_id=1, has_side_effects=True, vmem_limit_bytes=60 * 2**20
        ),
        name="gradient_blocks",
    )(*operands, numbers)


def ag(part):
    return lax.all_gather(part, "fsdp", axis=0, tiled=True)


def make_local(n_dp, n_f):
    fast = n_dp == 8 and n_f == 4

    def local(
        pixels, targets, valid_mask, lat_weight, segment_ids, present_vars, lead_index, step_count,
        w_agg, w_attn, w_mlp, w_io, w_small,
        m_agg, m_attn, m_mlp, m_io, m_small,
        v_agg, v_attn, v_mlp, v_io, v_small,
    ):
        masters = (w_agg, w_attn, w_mlp, w_io, w_small)
        firsts = (m_agg, m_attn, m_mlp, m_io, m_small)
        seconds = (v_agg, v_attn, v_mlp, v_io, v_small)
        rows = pixels.shape[1]
        row_len = segment_ids.shape[1]
        strip = w_agg.shape[0]
        own = lax.axis_index("fsdp")
        heads_here = HEADS // n_f
        wide = heads_here * HEAD_DIM

        seg = segment_ids[0]
        below = jnp.sum((seg[None, :] < seg[:, None]).astype(jnp.int32), axis=1)
        pos = jnp.arange(row_len, dtype=jnp.int32) - below
        onehot_all = (pos[:, None] == jnp.arange(SPAN, dtype=jnp.int32)[None, :]).astype(bf16)
        onehot = lax.dynamic_slice_in_dim(onehot_all, own * rows, rows)
        lead = (lead_index[0].astype(f32) + 1.0) / LEAD_STEPS
        pixel_rows = pixels[0]
        target = targets[0].astype(f32)
        present = present_vars[0]
        spread = (jnp.arange(MIX) // PIX)[None, :] == jnp.arange(VARS)[:, None]
        embed_col = (jnp.arange(MIX) - WIDTH)[None, :] == jnp.arange(VARS)[:, None]
        in_pixels = (jnp.arange(MIX) < WIDTH)[None, :]
        expand = jnp.where(in_pixels, spread, embed_col).astype(bf16)
        present_cols = jnp.repeat(present.astype(f32), PIX)
        pixel_weight = lat_weight[0][:, None] * valid_mask[0].astype(f32) * present_cols[None, :]
        weight_sum = jnp.sum(pixel_weight)

        def blank(width):
            return jnp.zeros((strip, width), bf16)

        io_low = w_io.astype(bf16)
        emb = 2 * WIDTH + VARS
        pack = jnp.concatenate(
            [
                io_low[:, :WIDTH],
                io_low[:, 2 * WIDTH : emb],
                blank(MIX - WIDTH - VARS),
                io_low[:, WIDTH : 2 * WIDTH],
                blank(256 - WIDTH),
                io_low[:, emb : emb + SPAN],
                w_small.astype(bf16),
                blank(128 - w_small.shape[1]),
                w_agg.astype(bf16),
            ],
            axis=1,
        )
        if fast:
            head, attn, mlp, stat = gather_weights(
                pack, w_attn.astype(bf16), w_mlp.astype(bf16), jnp.full((8, 128), weight_sum, f32)
            )
            total = stat[0, 0]
        else:
            head = lax.all_gather(pack, ("dp", "fsdp"), axis=0, tiled=True)
            attn = lax.all_gather(w_attn.astype(bf16), ("dp", "fsdp"), axis=0, tiled=True)
            mlp = lax.all_gather(w_mlp.astype(bf16), ("dp", "fsdp"), axis=0, tiled=True)
            total = lax.psum(weight_sum, ("dp", "fsdp"))
        w240 = head[:, :MIX]
        w_pred = head[:, 256 : 256 + WIDTH]
        w_pos = head[:, 512 : 512 + SPAN]
        small = head[:, 768:777].astype(f32).T
        agg_kv = head[:, HEAD : HEAD + 2 * D]
        agg_out = head[:, HEAD + 2 * D :]
        w_qkv = attn[:, : 3 * D]
        w_out = attn[:, 3 * D :]
        w_up = mlp[:, :FF]
        w_down = mlp[:, FF:]

        pix_t = jnp.concatenate(
            [pixel_rows.T, jnp.ones((VARS, rows), bf16), jnp.zeros((MIX - WIDTH - VARS, rows), bf16)], axis=0
        )
        table = t_mm(w240, agg_kv)
        table_k = table[:, :D].reshape(MIX, HEADS, HEAD_DIM)
        table_v = table[:, D:].reshape(MIX, HEADS, HEAD_DIM)
        query = small[0].reshape(HEADS, HEAD_DIM)
        folded = jnp.sum(table_k * query[None], axis=2)
        block = folded.T[:, None, :] * expand.astype(f32)[None]
        score = exact("xc,cl->xl", block.reshape(HEADS * VARS, MIX), pix_t.astype(f32))
        score = score.reshape(HEADS, VARS, rows) * HEAD_DIM ** (-0.5)
        score = jnp.where(present[None, :, None] > 0, score, -1000000000.0)
        top = jnp.max(score, axis=1, keepdims=True)
        power = jnp.exp(score - top)
        soft = power / jnp.sum(power, axis=1, keepdims=True)
        share = soft.astype(bf16)
        pix_f = pix_t.astype(f32)
        lifted_share = jnp.einsum("vc,hvl->hcl", expand, share, preferred_element_type=f32) * pix_f[None]
        mixed_a = exact("che,hcl->hel", table_v, lifted_share).reshape(D, rows).T.astype(bf16)
        lead_embed = lead * small[7] + small[8]
        h0 = mm(mixed_a, agg_out) + mm_t(onehot, w_pos) + lead_embed[None]
        norm0, unit0, scale0 = norm_forward(h0, small[1], small[2])
        qkv = mm(norm0, w_qkv).astype(bf16)
        part = qkv.reshape(rows, 3, n_f, wide)
        part = lax.all_to_all(part, "fsdp", split_axis=2, concat_axis=0, tiled=True)
        part = part.reshape(row_len, 3, heads_here, HEAD_DIM)
        q, k, v = (part[:, i].transpose(1, 0, 2) for i in range(3))
        att_score = jnp.einsum("hqe,hke->hqk", q, k, preferred_element_type=f32) * HEAD_DIM ** (-0.5)
        same = seg[:, None] == seg[None, :]
        att_score = jnp.where(same[None], att_score, -1000000000.0)
        att_top = jnp.max(att_score, axis=-1, keepdims=True)
        att_power = jnp.exp(att_score - att_top)
        att_soft = att_power / jnp.sum(att_power, axis=-1, keepdims=True)
        att = att_soft.astype(bf16)
        mixed_h = jnp.einsum("hqk,hke->qhe", att, v, preferred_element_type=f32)
        mixed_h = mixed_h.reshape(row_len, wide).astype(bf16)
        mixed_all = lax.all_gather(mixed_h, "fsdp", axis=1, tiled=True)
        mixed = lax.dynamic_slice_in_dim(mixed_all, own * rows, rows, axis=0)
        h1 = h0 + mm(mixed, w_out)
        norm1, unit1, scale1 = norm_forward(h1, small[3], small[4])
        up = mm(norm1, w_up)
        gate = 0.5 * (1.0 + lax.erf(up * (2.0**-0.5)))
        lifted = (up * gate).astype(bf16)
        h2 = h1 + mm_t(lifted, w_down)
        norm2, unit2, scale2 = norm_forward(h2, small[5], small[6])
        predicted = mm(norm2, w_pred) * D ** (-0.5)
        error = predicted - target
        weighted = pixel_weight * error
        numerator = jnp.sum(weighted * error)

        d_pred = (weighted * (2.0 * D ** (-0.5) / total)).astype(bf16)
        d_norm2 = mm_t(d_pred, w_pred)
        d_h2, d_gain2, d_off2 = norm_backward(d_norm2, unit2, scale2, small[5])
        d_out = d_h2.astype(bf16)
        slope = gate + up * jnp.exp(-0.5 * up * up) * 0.3989422804014327
        d_up = (mm(d_out, w_down) * slope).astype(bf16)
        d_norm1 = mm_t(d_up, w_up)
        d_in, d_gain1, d_off1 = norm_backward(d_norm1, unit1, scale1, small[3])
        d_h1 = d_h2 + d_in
        d_proj_all = ag(d_h1.astype(bf16))
        w_out_own = lax.dynamic_slice_in_dim(w_out, own * wide, wide, axis=0)
        d_mixed = mm_t(d_proj_all, w_out_own).astype(bf16).reshape(row_len, heads_here, HEAD_DIM).transpose(1, 0, 2)
        d_att = jnp.einsum("hqe,hke->hqk", d_mixed, v, preferred_element_type=f32)
        d_v = jnp.einsum("hqk,hqe->khe", att, d_mixed, preferred_element_type=f32)
        lean = jnp.sum(att_soft * d_att, axis=-1, keepdims=True)
        d_score = (att_soft * (d_att - lean) * HEAD_DIM ** (-0.5)).astype(bf16)
        d_q = jnp.einsum("hqk,hke->qhe", d_score, k, preferred_element_type=f32)
        d_k = jnp.einsum("hqk,hqe->khe", d_score, q, preferred_element_type=f32)
        d_part = jnp.stack([d_q, d_k, d_v], axis=1).astype(bf16).reshape(row_len, 3, 1, wide)
        d_qkv_all = lax.all_gather(d_part, "fsdp", axis=2, tiled=True).reshape(row_len, 3 * D)
        d_qkv = lax.dynamic_slice_in_dim(d_qkv_all, own * rows, rows, axis=0)
        d_norm0 = mm_t(d_qkv, w_qkv)
        d_in, d_gain0, d_off0 = norm_backward(d_norm0, unit0, scale0, small[1])
        d_h0 = d_h1 + d_in
        d_agg = d_h0.astype(bf16)
        d_mixed_a = mm_t(agg_out, d_agg).astype(bf16).reshape(HEADS, HEAD_DIM, rows)
        pulled = exact("che,hel->hcl", table_v, d_mixed_a.astype(f32)) * pix_f[None]
        d_share = exact("vc,hcl->hvl", expand.astype(f32), pulled)
        lean_a = jnp.sum(soft * d_share, axis=1, keepdims=True)
        d_score_a = (soft * (d_share - lean_a) * HEAD_DIM ** (-0.5)).astype(bf16)
        spread_score = jnp.einsum("vc,hvl->hcl", expand, d_score_a, preferred_element_type=f32)
        d_folded = jnp.sum(spread_score * pix_f[None], axis=2)
        d_table_v = exact("hcl,hel->che", lifted_share, d_mixed_a.astype(f32)).reshape(MIX, D)
        d_table_k = (d_folded.T[:, :, None] * query[None]).reshape(MIX, D)
        d_query = jnp.sum(d_folded.T[:, :, None] * table_k, axis=0).reshape(D)
        d_bias = jnp.sum(d_h0, axis=0)
        narrow = jnp.stack(
            [d_query, d_gain0, d_off0, d_gain1, d_off1, d_gain2, d_off2, lead * d_bias, d_bias]
            + [jnp.zeros((D,), f32)] * 7
        )
        d_table = jnp.concatenate([d_table_k, d_table_v], axis=1)
        if fast:

            def sorted_rows(array):
                return array.reshape(4, 2, n_f, strip, array.shape[1])

            lane = lax.broadcasted_iota(jnp.int32, (8, 128), 1)
            r_agg, r_attn, r_mlp, r_misc, stat = gradient_blocks(
                [sorted_rows(part.T) for part in (mixed_all, norm0, norm1, d_out, mixed_a, norm2, d_agg)]
                + [d_proj_all, d_qkv_all, d_up, lifted, d_agg, jnp.pad(d_pred, ((0, 0), (0, 256 - WIDTH)))]
                + [onehot_all, d_table.astype(bf16)]
                + [sorted_rows(jnp.pad(narrow.T, ((0, 0), (0, 128 - narrow.shape[0])))), sorted_rows(head)],
                jnp.where(lane == 1, numerator, 0.0),
            )
            squares, numerator = stat[0, 0], stat[0, 1]
        else:
            d_table, narrow = lax.psum((d_table, narrow), "fsdp")
            source = jnp.arange(D)
            pick = (source // strip) % n_f == own
            place = (source // (strip * n_f)) * strip + source % strip
            choose = (pick[:, None] & (place[:, None] == jnp.arange(n_dp * strip)[None, :])).astype(bf16)

            def mine(array):
                whole = array.reshape(n_dp, n_f, strip, array.shape[1])
                return lax.dynamic_index_in_dim(whole, own, 1, False).reshape(n_dp * strip, array.shape[1])

            def weight_grad(features, grads):
                return t_mm(mm(features, choose).astype(bf16), grads)

            def gap(width):
                return jnp.zeros((n_dp * strip, width), f32)

            d_agg_all = ag(d_agg)
            g_kv = exact("dc,cx->dx", mine(w240).astype(f32), d_table)
            g_240 = exact("dx,cx->dc", mine(agg_kv).astype(f32), d_table)
            groups = (
                (g_kv, weight_grad(ag(mixed_a), d_agg_all)),
                (weight_grad(ag(norm0), d_qkv_all), weight_grad(mixed_all, d_proj_all)),
                (weight_grad(ag(norm1), ag(d_up)), weight_grad(ag(d_out), ag(lifted))),
                (
                    g_240, weight_grad(ag(norm2), ag(d_pred)), gap(256 - WIDTH),
                    weight_grad(d_agg_all, onehot_all), mine(narrow.T)[:, :9], gap(256 - 9),
                ),
            )
            r_agg, r_attn, r_mlp, r_misc = (
                lax.psum_scatter(jnp.concatenate(g, axis=1), "dp", scatter_dimension=0, tiled=True) for g in groups
            )
            local_squares = sum(jnp.sum(piece * piece) for piece in (r_agg, r_attn, r_mlp, r_misc))
            squares, numerator = lax.psum((local_squares, numerator), ("dp", "fsdp"))
        r_io = jnp.concatenate(
            [
                r_misc[:, :WIDTH], r_misc[:, 256 : 256 + WIDTH], r_misc[:, WIDTH : WIDTH + VARS],
                r_misc[:, 512 : 512 + SPAN], jnp.zeros((strip, w_io.shape[1] - emb - SPAN), f32),
            ],
            axis=1,
        )
        reduced = (r_agg, r_attn, r_mlp, r_io, r_misc[:, 768:777])
        grad_norm = jnp.sqrt(squares)
        factor = jnp.minimum(1.0, clip_limit / grad_norm)
        loss = numerator / total
        step_value = step_count[0].astype(f32)
        results = [
            adamw(masters[i], reduced[i] * factor, firsts[i], seconds[i], step_value, learn_rates[i]) for i in range(5)
        ]
        return (loss, grad_norm) + tuple(results[i][j] for j in range(4) for i in range(5))

    return local


def solution(mesh):
    flat = P(("dp", "fsdp"), None)
    tokens = P("dp", "fsdp", None)
    return jax.shard_map(
        make_local(mesh.shape["dp"], mesh.shape["fsdp"]),
        mesh=mesh,
        in_specs=(tokens, tokens, tokens, P("dp", "fsdp"), P("dp", None), P("dp", None), P("dp"), P()) + (flat,) * 15,
        out_specs=(P(), P()) + (flat,) * 20,
        check_vma=False,
    )
```

```python
import functools

import jax
import jax.numpy as jnp
from jax import lax
from jax.experimental import pallas as pl
from jax.experimental.pallas import tpu as pltpu
from jax.sharding import PartitionSpec as P

D = 1024
HEADS = 16
HEAD_DIM = 64
FF = 4096
VARS = 48
PIX = 4
LEAD_STEPS = 8
WIDTH = VARS * PIX
SPAN = 256
MIX = 256
HEAD = 896

norm_eps = 1e-05
clip_limit = 1.0
decay_rate = 0.05
adam_eps = 1e-08
learn_rates = (0.03, 0.03, 0.03, 0.2, 0.3)
f32 = jnp.float32
bf16 = jnp.bfloat16
highest = lax.Precision.HIGHEST
MESH = pl.DeviceIdType.MESH
STRIP = 32
CHUNK = 512
LAG = 2
QUEUE = 2


def dot(left, right, dims):
    return lax.dot_general(left, right, (dims, ((), ())), preferred_element_type=f32)


def mm(left, right):
    return dot(left, right, ((1,), (0,)))


def mm_t(left, right):
    return dot(left, right, ((1,), (1,)))


def t_mm(left, right):
    return dot(left, right, ((0,), (0,)))


def exact(eq, left, right):
    return jnp.einsum(eq, left, right, precision=highest, preferred_element_type=f32)


def norm_forward(values, gain, offset):
    average = jnp.mean(values, axis=-1, keepdims=True)
    centred = values - average
    scale = lax.rsqrt(jnp.mean(centred * centred, axis=-1, keepdims=True) + norm_eps)
    unit = centred * scale
    return (unit * gain[None] + offset[None]).astype(bf16), unit, scale


def norm_backward(grad, unit, scale, gain):
    inner = grad * gain[None]
    mean_inner = jnp.mean(inner, axis=-1, keepdims=True)
    mean_product = jnp.mean(inner * unit, axis=-1, keepdims=True)
    back = scale * (inner - mean_inner - unit * mean_product)
    return back, jnp.sum(grad * unit, axis=0), jnp.sum(grad, axis=0)


def adamw(weight, grad, moment, second, step_value, learn_rate):
    moment = 0.5 * moment + 0.5 * grad
    second = 0.5 * second + 0.5 * grad * grad
    correct = 1.0 - jnp.power(f32(0.5), step_value)
    update = moment / correct / (jnp.sqrt(second / correct) + adam_eps) + decay_rate * weight
    fresh = weight - learn_rate * update
    return (fresh, fresh.astype(bf16), moment, second)


PIECES = (
    (0, 0, 1920, "yzx"), (2, 0, 2688, "zxy"), (0, 1920, 2048, "yzx"), (2, 2688, 2816, "zxy"),
    (1, 0, 1920, "yzx"), (2, 5504, 2688, "zxy"), (1, 1920, 2176, "zxy"),
)


def gather_kernel(*refs):
    shards, num_ref, wholes, stat_ref = refs[0:3], refs[3], refs[4:7], refs[7]
    quad_buf, line_buf, own_sem, s_send, s_recv, sends, arrive, pass_on = refs[8:]
    dp, own = lax.axis_index("dp"), lax.axis_index("fsdp")
    z, y, x, core = dp // 2, dp % 2, own // 2, own % 2
    sibling = x * 2 + 1 - core
    barrier = pltpu.get_barrier_semaphore()
    for d in range(1, 8):
        pl.semaphore_signal(barrier, inc=1, device_id=(lax.rem(dp + d, 8), own), device_id_type=MESH)
    for d in range(1, 4):
        pl.semaphore_signal(barrier, inc=1, device_id=(dp, lax.rem(own + d, 4)), device_id_type=MESH)
    pl.semaphore_wait(barrier, 10)

    def view(p, ident, plane):
        a, start, width, order = PIECES[p]
        row = pl.multiple_of(((ident // 2) * 4 + (ident % 2) * 2 + plane) * STRIP, STRIP)
        return wholes[a].at[pl.ds(row, STRIP), pl.ds(start, width)]

    def copy(p, ident, slot, to, mine=False):
        a, start, width, order = PIECES[p]
        src = shards[a].at[:, pl.ds(start, width)] if mine else view(p, ident, core)
        sem = pass_on if slot == 4 else arrive
        return pltpu.make_async_remote_copy(
            src_ref=src, dst_ref=view(p, ident, core), send_sem=sends.at[p, ident, slot], recv_sem=sem.at[p, ident],
            device_id=to, device_id_type=MESH,
        )

    def arrival(p, ident, plane, sem):
        return pltpu.make_async_copy(view(p, ident, plane), view(p, ident, plane), sem.at[p, ident])

    def targets(p, rx, ry, rz):
        order = PIECES[p][3]
        moved = {"x": rx != 0, "y": ry != 0, "z": rz is not None}
        stage = max([k for k in range(3) if moved[order[k]]], default=-1)
        found = []
        if stage >= 0 and order[stage] == "z":
            found.append((0, (rz < 0) & (z < 3), ((dp + 2) % 8, own)))
            found.append((1, (rz > 0) & (z > 0), ((dp + 6) % 8, own)))
        for k in range(stage + 1, 3):
            if order[k] == "z":
                found.append((0, z < 3, ((dp + 2) % 8, own)))
                found.append((1, z > 0, ((dp + 6) % 8, own)))
            elif order[k] == "x":
                found.append((2, None, (dp, (1 - x) * 2 + core)))
            else:
                found.append((3, None, (z * 2 + 1 - y, own)))
        found.append((4, None, (dp, sibling)))
        return found

    def source(rx, ry, rz):
        sz = z if rz is None else z + rz
        sy = 1 - y if ry else y
        sx = 1 - x if rx else x
        return sz, (sz * 2 + sy) * 2 + sx

    def each(rx, ry, rz, act, mine=False):
        sz, ident = source(rx, ry, rz)

        def body():
            for p in range(len(PIECES)):
                if act == "send" and not mine:
                    arrival(p, ident, core, arrive).wait()
                for slot, when, to in targets(p, rx, ry, rz):
                    def go(slot=slot, to=to):
                        c = copy(p, ident, slot, to, mine)
                        c.start() if act == "send" else c.wait_send()

                    if when is None:
                        go()
                    else:
                        pl.when(when)(go)

        if rz is None:
            body()
        else:
            pl.when((sz >= 0) & (sz < 4))(body)

    def over_z(pairs, act):
        def step(t, carry):
            rz = ((t + 1) // 2) * (1 - 2 * (t % 2))
            for rx, ry in pairs:
                each(rx, ry, rz, act)
            return carry

        lax.fori_loop(1, 7, step, 0)

    def sweep(act):
        each(0, 0, None, act, mine=True)
        if act == "send":
            for a in range(3):
                row = pl.multiple_of((dp * 4 + own) * STRIP, STRIP)
                pltpu.make_async_copy(shards[a], wholes[a].at[pl.ds(row, STRIP), :], own_sem.at[a]).start()
            scalars()
        each(1, 0, None, act)
        each(0, 1, None, act)
        over_z([(0, 0)], act)
        each(1, 1, None, act)
        over_z([(1, 0), (0, 1)], act)
        over_z([(1, 1)], act)

    def share(buf, k, where, at):
        return pltpu.make_async_remote_copy(
            src_ref=buf.at[at], dst_ref=buf.at[at], send_sem=s_send.at[k], recv_sem=s_recv.at[k],
            device_id=where, device_id_type=MESH,
        )

    def scalars():
        quad_buf[own] = num_ref[...]
        for d in range(1, 4):
            share(quad_buf, d, (dp, lax.rem(own + d, 4)), own).start()

    sweep("send")
    for d in range(1, 4):
        share(quad_buf, d, (dp, own), lax.rem(own + 4 - d, 4)).wait_recv()
    line_buf[dp] = (quad_buf[0] + quad_buf[1]) + (quad_buf[2] + quad_buf[3])
    for d in range(1, 8):
        share(line_buf, 3 + d, (lax.rem(dp + d, 8), own), dp).start()

    def closing(ident, carry):
        for p in range(len(PIECES)):
            arrival(p, ident, 1 - core, pass_on).wait()
        return carry

    lax.fori_loop(0, 16, closing, 0)
    for a in range(3):
        row = pl.multiple_of((dp * 4 + own) * STRIP, STRIP)
        pltpu.make_async_copy(shards[a], wholes[a].at[pl.ds(row, STRIP), :], own_sem.at[a]).wait()
    sweep("drain")
    for d in range(1, 8):
        share(line_buf, 3 + d, (dp, own), lax.rem(dp + 8 - d, 8)).wait_recv()
    stat = line_buf[0]
    for d in range(1, 8):
        stat = stat + line_buf[d]
    stat_ref[...] = stat
    for d in range(1, 4):
        share(quad_buf, d, (dp, own), own).wait_send()
    for d in range(1, 8):
        share(line_buf, 3 + d, (dp, own), dp).wait_send()


def gather_weights(head, attn, mlp, number):
    any_space = pl.BlockSpec(memory_space=pl.ANY)
    vmem = pl.BlockSpec(memory_space=pltpu.VMEM)
    n = len(PIECES)
    return pl.pallas_call(
        gather_kernel,
        out_shape=[jax.ShapeDtypeStruct((D, a.shape[1]), bf16) for a in (head, attn, mlp)]
        + [jax.ShapeDtypeStruct((8, 128), f32)],
        in_specs=[any_space] * 3 + [vmem],
        out_specs=[any_space] * 3 + [vmem],
        scratch_shapes=[
            pltpu.VMEM((4, 8, 128), f32),
            pltpu.VMEM((8, 8, 128), f32),
            pltpu.SemaphoreType.DMA((3,)),
            pltpu.SemaphoreType.DMA((11,)),
            pltpu.SemaphoreType.DMA((11,)),
            pltpu.SemaphoreType.DMA((n, 16, 5)),
            pltpu.SemaphoreType.DMA((n, 16)),
            pltpu.SemaphoreType.DMA((n, 16)),
        ],
        compiler_params=pltpu.CompilerParams(collective_id=0, has_side_effects=True),
        name="gather_weights",
    )(head, attn, mlp, number)


def greet(dp, own):
    barrier = pltpu.get_barrier_semaphore()
    for d in range(1, 4):
        pl.semaphore_signal(barrier, inc=1, device_id=(dp, lax.rem(own + d, 4)), device_id_type=MESH)
    pl.semaphore_wait(barrier, 3)


def turned_softmax(parts, seg_col, seg_row, h):
    at = slice(h * HEAD_DIM, (h + 1) * HEAD_DIM)
    q, k, v = (parts[i, :, at] for i in range(3))
    score = lax.dot_general(k, q, (((1,), (1,)), ((), ())), preferred_element_type=f32) * HEAD_DIM ** (-0.5)
    score = jnp.where(seg_col[:, 0:1] == seg_row[0:1, :], score, -1000000000.0)
    power = jnp.exp(score - jnp.max(score, axis=0, keepdims=True))
    soft = power / jnp.sum(power, axis=0, keepdims=True)
    return q, k, v, soft, soft.astype(bf16)


def attend_kernel(qkv, seg_col, seg_row, mixed, mixed_t, parts_out, parts, turned, whole, gathered,
                  load_sem, in_send, in_recv, out_send, out_recv):
    dp, own = lax.axis_index("dp"), lax.axis_index("fsdp")
    greet(dp, own)
    row = pl.ds(pl.multiple_of(own * 128, 128), 128)

    def piece(i, to):
        return qkv.at[:, pl.ds(pl.multiple_of(i * D + to * 256, 256), 256)]

    def into(d, i):
        to = lax.rem(own + d, 4)
        return pltpu.make_async_remote_copy(
            src_ref=piece(i, to), dst_ref=parts.at[i, row, :], send_sem=in_send.at[d, i], recv_sem=in_recv.at[d, i],
            device_id=(dp, to), device_id_type=MESH,
        )

    for i in range(3):
        for d in (2, 1, 3):
            into(d, i).start()
    for i in range(3):
        pltpu.make_async_copy(piece(i, own), parts.at[i, row, :], load_sem.at[i]).start()
    for i in range(3):
        pltpu.make_async_copy(piece(i, own), parts.at[i, row, :], load_sem.at[i]).wait()
        for d in range(1, 4):
            into(d, i).wait_recv()
    for h in range(4):
        q, k, v, soft, share = turned_softmax(parts, seg_col, seg_row, h)
        turned[h * HEAD_DIM : (h + 1) * HEAD_DIM, :] = lax.dot_general(
            v, share, (((0,), (0,)), ((), ())), preferred_element_type=f32
        )
    whole[...] = turned[...].T.astype(bf16)
    column = pl.ds(pl.multiple_of(own * 256, 256), 256)

    def back(d):
        to = lax.rem(own + d, 4)
        return pltpu.make_async_remote_copy(
            src_ref=whole.at[pl.ds(pl.multiple_of(to * 128, 128), 128), :], dst_ref=gathered.at[:, column],
            send_sem=out_send.at[d], recv_sem=out_recv.at[d], device_id=(dp, to), device_id_type=MESH,
        )

    for d in (2, 1, 3):
        back(d).start()
    keep = pltpu.make_async_copy(whole.at[row, :], gathered.at[:, column], load_sem.at[3])
    keep.start()
    mixed_t[...] = turned[...].astype(bf16)
    parts_out[...] = parts[...]
    keep.wait()
    for d in range(1, 4):
        back(d).wait_recv()
    mixed[...] = gathered[...]
    for d in range(1, 4):
        back(d).wait_send()
        for i in range(3):
            into(d, i).wait_send()


def attend(qkv, seg_col, seg_row):
    vmem = pl.BlockSpec(memory_space=pltpu.VMEM)
    dma = pltpu.SemaphoreType.DMA
    return pl.pallas_call(
        attend_kernel,
        out_shape=[
            jax.ShapeDtypeStruct((128, D), bf16), jax.ShapeDtypeStruct((256, 512), bf16),
            jax.ShapeDtypeStruct((3, 512, 256), bf16),
        ],
        in_specs=[pl.BlockSpec(memory_space=pl.ANY), vmem, vmem],
        out_specs=[vmem] * 3,
        scratch_shapes=[
            pltpu.VMEM((3, 512, 256), bf16), pltpu.VMEM((256, 512), f32), pltpu.VMEM((512, 256), bf16),
            pltpu.VMEM((128, D), bf16), dma((4,)), dma((4, 3)), dma((4, 3)), dma((4,)), dma((4,)),
        ],
        compiler_params=pltpu.CompilerParams(collective_id=2, has_side_effects=True, vmem_limit_bytes=40 * 2**20),
        name="attend",
    )(qkv, seg_col, seg_row)


def attend_back_kernel(d_proj, attn, parts, seg_col, seg_row, d_own, d_parts_out, d_all_out, every, proj, d_mixed,
                       d_parts, gathered, load_sem, up_send, up_recv, out_send, out_recv):
    dp, own = lax.axis_index("dp"), lax.axis_index("fsdp")
    x, core = own // 2, own % 2
    sibling, across, diagonal = x * 2 + 1 - core, (1 - x) * 2 + core, (1 - x) * 2 + 1 - core
    rows = pl.ds(pl.multiple_of(own * 256, 256), 256)
    fetch = pltpu.make_async_copy(attn.at[rows, pl.ds(3 * D, D)], proj, load_sem.at[0])
    fetch.start()
    row = pl.ds(pl.multiple_of(own * 128, 128), 128)
    mine = pltpu.make_async_copy(d_proj, every.at[row, :], load_sem.at[1])
    mine.start()
    greet(dp, own)
    mine.wait()

    def up(i, who, slot, to):
        block = every.at[pl.ds(pl.multiple_of(who * 128, 128), 128), i * 512 : (i + 1) * 512]
        return pltpu.make_async_remote_copy(
            src_ref=block, dst_ref=block, send_sem=up_send.at[i, slot], recv_sem=up_recv.at[i, who],
            device_id=(dp, to), device_id_type=MESH,
        )

    for i in range(2):
        up(i, own, 0, across).start()
    for i in range(2):
        up(i, own, 1, sibling).start()
    for i in range(2):
        up(i, across, 0, own).wait_recv()
        up(i, across, 2, sibling).start()
    fetch.wait()
    for i in range(2):
        up(i, sibling, 1, own).wait_recv()
        up(i, diagonal, 2, own).wait_recv()
    d_mixed[...] = lax.dot_general(
        every[...], proj[...], (((1,), (1,)), ((), ())), preferred_element_type=f32
    ).astype(bf16)
    for h in range(4):
        at = slice(h * HEAD_DIM, (h + 1) * HEAD_DIM)
        q, k, v, soft, share = turned_softmax(parts, seg_col, seg_row, h)
        d_head = d_mixed[:, at]
        d_soft = lax.dot_general(v, d_head, (((1,), (1,)), ((), ())), preferred_element_type=f32)
        lean = jnp.sum(soft * d_soft, axis=0, keepdims=True)
        d_score = (soft * (d_soft - lean) * HEAD_DIM ** (-0.5)).astype(bf16)
        d_parts[2, :, at] = mm(share, d_head).astype(bf16)
        d_parts[1, :, at] = mm(d_score, q).astype(bf16)
        d_parts[0, :, at] = t_mm(d_score, k).astype(bf16)

    def back(d, i):
        to = lax.rem(own + d, 4)
        return pltpu.make_async_remote_copy(
            src_ref=d_parts.at[i, pl.ds(pl.multiple_of(to * 128, 128), 128), :],
            dst_ref=gathered.at[:, pl.ds(pl.multiple_of(i * D + own * 256, 256), 256)],
            send_sem=out_send.at[d, i], recv_sem=out_recv.at[d, i], device_id=(dp, to), device_id_type=MESH,
        )

    for i in range(3):
        for d in (2, 1, 3):
            back(d, i).start()
    keeps = [
        pltpu.make_async_copy(
            d_parts.at[i, row, :], gathered.at[:, pl.ds(pl.multiple_of(i * D + own * 256, 256), 256)], load_sem.at[2 + i]
        )
        for i in range(3)
    ]
    for keep in keeps:
        keep.start()
    d_parts_out[...] = d_parts[...]
    d_all_out[...] = every[...]
    for keep in keeps:
        keep.wait()
    for i in range(3):
        for d in range(1, 4):
            back(d, i).wait_recv()
    d_own[...] = gathered[...]
    for d in range(1, 4):
        for i in range(3):
            back(d, i).wait_send()
    for i in range(2):
        for slot, who in ((0, own), (1, own), (2, across)):
            up(i, who, slot, own).wait_send()


def attend_back(d_proj, attn, parts, seg_col, seg_row):
    vmem = pl.BlockSpec(memory_space=pltpu.VMEM)
    any_space = pl.BlockSpec(memory_space=pl.ANY)
    dma = pltpu.SemaphoreType.DMA
    return pl.pallas_call(
        attend_back_kernel,
        out_shape=[
            jax.ShapeDtypeStruct((128, 3 * D), bf16), jax.ShapeDtypeStruct((3, 512, 256), bf16),
            jax.ShapeDtypeStruct((512, D), bf16),
        ],
        in_specs=[any_space, any_space, vmem, vmem, vmem],
        out_specs=[vmem] * 3,
        scratch_shapes=[
            pltpu.VMEM((512, D), bf16), pltpu.VMEM((256, D), bf16), pltpu.VMEM((512, 256), bf16),
            pltpu.VMEM((3, 512, 256), bf16), pltpu.VMEM((128, 3 * D), bf16),
            dma((5,)), dma((2, 3)), dma((2, 4)), dma((4, 3)), dma((4, 3)),
        ],
        compiler_params=pltpu.CompilerParams(collective_id=3, has_side_effects=True, vmem_limit_bytes=40 * 2**20),
        name="attend_back",
    )(d_proj, attn, parts, seg_col, seg_row)


SEGMENTS = ((0, 8, 0), (8, 16, 1), (16, 22, 2), (22, 24, 3), (24, 26, 4))
N_STD, N_ALL, SHIFT, BASE = 26, 32, 2, 2


FAR = ({2: 0, 3: 1}, {0: 0, 1: 1})


def preds_at(preds, who):
    return preds.at[pl.ds(pl.multiple_of(who * 128, 128), 128), :]


def gradient_kernel(*refs):
    (norm1_t, out_t, norm0_t, mixed_t, mixa_t, norm2_t, agg_t,
     d_proj, d_parts, d_up, lifted, d_agg, d_pred, onehot, d_table, narrow, head, num_ref) = refs[:18]
    r_agg, r_attn, r_mlp, r_misc, stat_ref = refs[18:23]
    (feats, ys, tabs, pairs, preds, hots, narrows, w240, wkv, acc240, own_buf, give_buf, got, rise, fall, far, tally,
     quad_buf, line_buf, load_sem, feat_send, feat_recv, y_xsend, y_xrecv, part_send, part_recv, tab_send, tab_recv, pred_send, pred_recv,
     nar_send, nar_recv, y_send, y_recv, z_send, z_recv, s_send, s_recv) = refs[23:]
    dp, own = lax.axis_index("dp"), lax.axis_index("fsdp")
    z, y, x, core = dp // 2, dp % 2, own // 2, own % 2
    sibling, across, diagonal = x * 2 + 1 - core, (1 - x) * 2 + core, (1 - x) * 2 + 1 - core
    over = z * 2 + 1 - y
    barrier = pltpu.get_barrier_semaphore()
    for d in range(1, 8):
        pl.semaphore_signal(barrier, inc=1, device_id=(lax.rem(dp + d, 8), own), device_id_type=MESH)
    for d in range(1, 4):
        pl.semaphore_signal(barrier, inc=1, device_id=(dp, lax.rem(own + d, 4)), device_id_type=MESH)
    pl.semaphore_wait(barrier, 10)
    n = N_ALL
    row = pl.ds(pl.multiple_of(own * 128, 128), 128)
    sent_feats = {0: norm1_t, 1: out_t, 2: norm0_t, 4: mixa_t, 5: norm2_t, 6: agg_t}

    def remote(src, dst, send, recv, to):
        return pltpu.make_async_remote_copy(
            src_ref=src, dst_ref=dst, send_sem=send, recv_sem=recv, device_id=(dp, to), device_id_type=MESH
        )

    def feat_copy(k, d, half, to):
        side = y if half == 0 else 1 - y
        if k == 3:
            src, dst = mixed_t.at[side, to], feats.at[3, half, own]
        else:
            src, dst = sent_feats[k].at[:, side, to], feats.at[k, half, :, :, row]
        return remote(src, dst, feat_send.at[k, d, half], feat_recv.at[k, d, half], to)

    def feat_start(k):
        for d in (2, 1, 3):
            for half in range(2):
                feat_copy(k, d, half, lax.rem(own + d, 4)).start()

    def unit_block(c, who):
        return ys.at[c, pl.ds(pl.multiple_of(who * 128, 128), 128), :]

    def unit(c, who, slot, to):
        return remote(unit_block(c, who), unit_block(c, who), y_xsend.at[c, slot], y_xrecv.at[c, who], to)

    def part_block(i, who):
        return ys.at[16 + i * 2 + who // 2, :, pl.ds(pl.multiple_of((who % 2) * 256, 256), 256)]

    def part(i, who, slot, to):
        return remote(part_block(i, who), part_block(i, who), part_send.at[i, slot], part_recv.at[i, who], to)

    def table_raw(v, to):
        return remote(tabs.at[0, v], tabs.at[1, v], tab_send.at[v, 0], tab_recv.at[v, 0], to)

    def table(v, who, slot, to):
        return remote(pairs.at[who, v], pairs.at[who, v], tab_send.at[v, slot], tab_recv.at[v, 1 + who], to)

    def pred_copy(d, who, to):
        return remote(preds_at(preds, who), preds_at(preds, who), pred_send.at[d], pred_recv.at[d], to)

    def narrow_copy(d, who, to):
        return remote(narrows.at[who], narrows.at[who], nar_send.at[d], nar_recv.at[d], to)

    loads = {}

    def load(name, src, dst):
        copy = pltpu.make_async_copy(src, dst, load_sem.at[len(loads)])
        copy.start()
        loads[name] = copy

    for c in range(8):
        load(("u", c), d_up.at[:, pl.ds(c * CHUNK, CHUNK)], unit_block(c, own))
    for c in range(8):
        load(("u", 8 + c), lifted.at[:, pl.ds(c * CHUNK, CHUNK)], unit_block(8 + c, own))
    for i in range(3):
        load(("p", i), d_parts.at[i], part_block(i, own))
    for c in range(2):
        load(("u", 24 + c), d_agg.at[:, pl.ds(c * CHUNK, CHUNK)], unit_block(24 + c, own))
    for v in range(4):
        load(("t", v), d_table.at[:, pl.ds(v * CHUNK, CHUNK)], tabs.at[0, v])
    load("pred", d_pred, preds_at(preds, own))
    load("narrow", narrow, narrows.at[own])
    count = len(loads)
    for k in range(7):
        for half in range(2):
            side = y if half == 0 else 1 - y
            if k == 3:
                load(("f", k, half), mixed_t.at[side, own], feats.at[3, half, own])
            else:
                load(("f", k, half), sent_feats[k].at[:, side, own], feats.at[k, half, :, :, row])
    for c in range(2):
        load(("j", c), d_proj.at[:, pl.ds(c * CHUNK, CHUNK)], ys.at[22 + c])
    load("hot", onehot, hots)
    for half in range(2):
        side = y if half == 0 else 1 - y
        load(("w", half), head.at[:, side, own, :, pl.ds(0, 256)], w240.at[half])
        load(("k", half), head.at[:, side, own, :, pl.ds(HEAD, 2 * D)], wkv.at[half])
    feat_start(0)
    names = list(loads)
    for name in names[:count]:
        loads[name].wait()

    def begin(first):
        def body(c, carry):
            unit(c, own, 0, across).start()
            unit(c, own, 1, sibling).start()
            return carry

        return body

    lax.fori_loop(0, 8, begin(0), 0)
    feat_start(1)
    lax.fori_loop(8, 16, begin(8), 0)
    feat_start(2)
    for i in range(3):
        part(i, own, 0, across).start()
        part(i, own, 1, sibling).start()
    feat_start(3)
    feat_start(4)
    lax.fori_loop(24, 26, begin(24), 0)
    for w in range(2):
        table_raw((1 - core) * 2 + w, sibling).start()
    feat_start(5)
    feat_start(6)
    for d in (2, 1, 3):
        pred_copy(d, own, lax.rem(own + d, 4)).start()
        narrow_copy(d, own, lax.rem(own + d, 4)).start()
    for name in names[count:]:
        loads[name].wait()
    tally[...] = jnp.zeros_like(tally)
    acc240[...] = jnp.zeros_like(acc240)
    for w in range(2):
        v = core * 2 + w
        table_raw(v, own).wait_recv()
        pairs[x, v] = (tabs[0, v].astype(f32) + tabs[1, v].astype(f32)).astype(bf16)
        table(v, x, 1, across).start()
        table(v, x, 2, sibling).start()

    def feat_wait(k):
        for d in range(1, 4):
            for half in range(2):
                feat_copy(k, d, half, own).wait_recv()

    def put(c, value):
        own_buf[c] = value[:128]
        give_buf[c] = value[128:].astype(bf16)

    def feature(k):
        return feats[k].reshape(256, 512)

    def matmul(a, b):
        return lax.dot_general(a, b, (((1,), (0,)), ((), ())), preferred_element_type=f32)

    def two(value):
        high = value.astype(bf16)
        return high, (value - high.astype(f32)).astype(bf16)

    def summed_table(v):
        return two(pairs[0, v].astype(f32) + pairs[1, v].astype(f32))

    def compute(c):
        for i in range(3):
            @pl.when(c == 16 + i * 2)
            def _():
                part(i, sibling, 1, own).wait_recv()
                part(i, diagonal, 2, own).wait_recv()

        for low, high, k in SEGMENTS:
            pl.when(c == low)(functools.partial(feat_wait, k))

            @pl.when((c >= low) & (c < high))
            def _():
                if k in (0, 1, 4):
                    unit(c, sibling, 1, own).wait_recv()
                    unit(c, diagonal, 2, own).wait_recv()
                put(c, matmul(feature(k), ys[c]))

        @pl.when((c >= N_STD) & (c < N_STD + 4))
        def _():
            v = c - N_STD

            @pl.when(v // 2 != core)
            def _():
                table(v, x, 2, own).wait_recv()
                table(v, 1 - x, 3, own).wait_recv()

            high, low = summed_table(v)
            rows = w240[...].reshape(256, 256)
            put(c, matmul(rows, high) + matmul(rows, low))

        for v in range(4):
            @pl.when(c == N_STD + v)
            def _():
                high, low = summed_table(v)
                rows = wkv[:, :, :, v * CHUNK : (v + 1) * CHUNK].reshape(256, CHUNK)
                dims = (((1,), (1,)), ((), ()))
                acc240[...] = (
                    acc240[...]
                    + lax.dot_general(rows, high, dims, preferred_element_type=f32)
                    + lax.dot_general(rows, low, dims, preferred_element_type=f32)
                )

        @pl.when(c == N_STD + 4)
        def _():
            feat_wait(5)
            for d in range(1, 4):
                pred_copy(d, lax.rem(own + 4 - d, 4), own).wait_recv()
            value = matmul(feature(5), preds[...])
            own_buf[c, :, 0:256] = acc240[:128]
            own_buf[c, :, 256:512] = value[:128]
            give_buf[c, :, 0:256] = acc240[128:].astype(bf16)
            give_buf[c, :, 256:512] = value[128:].astype(bf16)

        @pl.when(c == N_STD + 5)
        def _():
            feat_wait(6)
            for d in range(1, 4):
                narrow_copy(d, lax.rem(own + 4 - d, 4), own).wait_recv()
            value = matmul(feature(6), hots[...])
            place = lax.broadcasted_iota(jnp.int32, (256, D), 0)
            source = lax.broadcasted_iota(jnp.int32, (256, D), 1)
            side = jnp.where(place < 128, y, 1 - y)
            wanted = ((place >> 5) & 3) * 256 + side * 128 + own * STRIP + (place & 31)
            choose = jnp.where(source == wanted, 1.0, 0.0).astype(bf16)
            total = (narrows[0] + narrows[1]) + (narrows[2] + narrows[3])
            total = jnp.concatenate([total, jnp.zeros((112, D), f32)], axis=0)
            high = total.astype(bf16)
            rest = total - high.astype(f32)
            middle = rest.astype(bf16)
            low = (rest - middle.astype(f32)).astype(bf16)
            dims = (((1,), (1,)), ((), ()))
            small = (
                lax.dot_general(choose, high, dims, preferred_element_type=f32)
                + lax.dot_general(choose, middle, dims, preferred_element_type=f32)
                + lax.dot_general(choose, low, dims, preferred_element_type=f32)
            )
            empty = jnp.zeros((128, 128), f32)
            own_buf[c, :, 0:256] = value[:128]
            own_buf[c, :, 256:384] = small[:128]
            own_buf[c, :, 384:512] = empty
            give_buf[c, :, 0:256] = value[128:].astype(bf16)
            give_buf[c, :, 256:384] = small[128:].astype(bf16)
            give_buf[c, :, 384:512] = empty.astype(bf16)

    def cross(c):
        return pltpu.make_async_remote_copy(
            src_ref=give_buf.at[c], dst_ref=got.at[c], send_sem=y_send.at[c],
            recv_sem=y_recv.at[c], device_id=(over, own), device_id_type=MESH,
        )

    def hop(buf, way, c, b, to):
        at = b - 1 if way == 0 else b
        return pltpu.make_async_remote_copy(
            src_ref=buf.at[c, at], dst_ref=buf.at[c, at], send_sem=z_send.at[way, c, at], recv_sem=z_recv.at[way, c, at],
            device_id=(to * 2 + y, own), device_id_type=MESH,
        )

    def far_hop(way, c, b, to):
        at = FAR[way][b]
        return pltpu.make_async_remote_copy(
            src_ref=far.at[way, c, at], dst_ref=far.at[way, c, at], send_sem=z_send.at[way, c, 3 + at],
            recv_sem=z_recv.at[way, c, 3 + at], device_id=(to * 2 + y, own), device_id_type=MESH,
        )

    def here(c, b):
        at = pl.ds(b * STRIP, STRIP)
        return own_buf[c, at, :] + got[c, at, :].astype(f32)

    early, late = LAG * jnp.minimum(z, 3 - z), LAG * jnp.maximum(z, 3 - z)

    def step(t, carry):
        @pl.when(t < 16)
        def _():
            unit(t, across, 0, own).wait_recv()
            unit(t, across, 2, sibling).start()

        for i in range(3):
            @pl.when(t == 16 + i)
            def _():
                part(i, across, 0, own).wait_recv()
                part(i, across, 2, sibling).start()

        @pl.when((t == 19) | (t == 20))
        def _():
            unit(t + 5, across, 0, own).wait_recv()
            unit(t + 5, across, 2, sibling).start()

        @pl.when((t == 21) | (t == 22))
        def _():
            v = core * 2 + t - 21
            table(v, 1 - x, 1, own).wait_recv()
            table(v, 1 - x, 3, sibling).start()

        @pl.when((t >= SHIFT) & (t < n + SHIFT))
        def _():
            compute(t - SHIFT)
            cross(t - SHIFT).start()

        first = t - SHIFT - BASE - early

        @pl.when((first >= 0) & (first < n))
        def _():
            cross(first).wait()

        for way, buf, lag, to, back in ((0, rise, LAG * z, z + 1, z - 1), (1, fall, LAG * (3 - z), z - 1, z + 1)):
            c = t - SHIFT - BASE - lag

            @pl.when((c >= 0) & (c < n))
            def _():
                for b in ((1, 2, 3) if way == 0 else (0, 1, 2)):
                    beyond = (b > z) if way == 0 else (b < z)
                    at = b - 1 if way == 0 else b

                    @pl.when(beyond & (lag == 0))
                    def _():
                        if b == (1 if way == 0 else 2):
                            buf[c, at] = here(c, b)
                        else:
                            far[way, c, FAR[way][b]] = here(c, b).astype(bf16)

                    @pl.when(beyond & (lag > 0))
                    def _():
                        if b == (1 if way == 0 else 2):
                            hop(buf, way, c, b, back).wait_recv()
                            buf[c, at] = buf[c, at] + here(c, b)
                        else:
                            @pl.when(lag == LAG)
                            def _():
                                far_hop(way, c, b, back).wait_recv()
                                buf[c, at] = far[way, c, FAR[way][b]].astype(f32) + here(c, b)

                            @pl.when(lag > LAG)
                            def _():
                                hop(buf, way, c, b, back).wait_recv()
                                buf[c, at] = buf[c, at] + here(c, b)

                    def send(c, act):
                        if b == (1 if way == 0 else 2):
                            copy = hop(buf, way, c, b, to)
                            copy.start() if act else copy.wait_send()
                        else:
                            @pl.when(lag == 0)
                            def _():
                                copy = far_hop(way, c, b, to)
                                copy.start() if act else copy.wait_send()

                            @pl.when(lag > 0)
                            def _():
                                copy = hop(buf, way, c, b, to)
                                copy.start() if act else copy.wait_send()

                    @pl.when(beyond & (c >= QUEUE))
                    def _():
                        send(c - QUEUE, False)

                    @pl.when(beyond)
                    def _():
                        send(c, True)

        last = t - SHIFT - BASE - late

        @pl.when((last >= 0) & (last < n))
        def _():
            at = pl.ds(pl.multiple_of(z * STRIP, STRIP), STRIP)
            value = own_buf[last, at, :] + got[last, at, :].astype(f32)
            own_buf[last, 0:STRIP, :] = value

            @pl.when(z > 0)
            def _():
                hop(rise, 0, last, z, z - 1).wait_recv()
                own_buf[last, 0:STRIP, :] = own_buf[last, 0:STRIP, :] + rise[last, z - 1]

            @pl.when(z < 3)
            def _():
                hop(fall, 1, last, z, z + 1).wait_recv()
                own_buf[last, 0:STRIP, :] = own_buf[last, 0:STRIP, :] + fall[last, z]

            value = own_buf[last, 0:STRIP, :]
            square = value * value
            total = square[0:8, 0:128]
            for r in range(0, STRIP, 8):
                for k in range(0, CHUNK, 128):
                    if r or k:
                        total = total + square[r : r + 8, k : k + 128]
            tally[...] = tally[...] + total

        return carry

    lax.fori_loop(0, n + SHIFT + BASE + 3 * LAG, step, 0)
    summed = jnp.sum(tally[...])
    lane = lax.broadcasted_iota(jnp.int32, (8, 128), 1)
    quad_buf[own] = jnp.where(lane == 0, summed, jnp.where(lane == 1, num_ref[...], 0.0))

    def share(buf, k, where, at):
        return pltpu.make_async_remote_copy(
            src_ref=buf.at[at], dst_ref=buf.at[at], send_sem=s_send.at[k], recv_sem=s_recv.at[k],
            device_id=where, device_id_type=MESH,
        )

    for d in range(1, 4):
        share(quad_buf, d, (dp, lax.rem(own + d, 4)), own).start()
    for out, base, low, high in (
        (r_mlp, 0, 0, 16), (r_attn, 0, 16, 22), (r_attn, 3 * D, 22, 24), (r_agg, 2 * D, 24, 26), (r_agg, 0, 26, 30),
        (r_misc, 0, 30, 32),
    ):
        for c in range(low, high):
            out[:, base + (c - low) * CHUNK : base + (c - low + 1) * CHUNK] = own_buf[c, 0:STRIP, :]
    for d in range(1, 4):
        share(quad_buf, d, (dp, own), lax.rem(own + 4 - d, 4)).wait_recv()
    line_buf[dp] = (quad_buf[0] + quad_buf[1]) + (quad_buf[2] + quad_buf[3])
    for d in range(1, 8):
        share(line_buf, 3 + d, (lax.rem(dp + d, 8), own), dp).start()
    for d in range(1, 8):
        share(line_buf, 3 + d, (dp, own), lax.rem(dp + 8 - d, 8)).wait_recv()
    stat = line_buf[0]
    for d in range(1, 8):
        stat = stat + line_buf[d]
    stat_ref[...] = stat
    for d in range(1, 4):
        share(quad_buf, d, (dp, own), own).wait_send()
    for d in range(1, 8):
        share(line_buf, 3 + d, (dp, own), dp).wait_send()
    for d in range(1, 4):
        for k in range(7):
            for half in range(2):
                feat_copy(k, d, half, own).wait_send()
        pred_copy(d, own, own).wait_send()
        narrow_copy(d, own, own).wait_send()
    for w in range(2):
        table_raw((1 - core) * 2 + w, own).wait_send()
        for slot, who in ((1, x), (2, x), (3, 1 - x)):
            table(core * 2 + w, who, slot, own).wait_send()
    relays = ((0, own), (1, own), (2, across))
    for i in range(3):
        for slot, who in relays:
            part(i, who, slot, own).wait_send()

    def finish(c, carry):
        for slot, who in relays:
            unit(c, who, slot, own).wait_send()
        return carry

    lax.fori_loop(0, 16, finish, 0)
    lax.fori_loop(24, 26, finish, 0)

    def drain(c, carry):
        for way, buf, inner, outer in ((0, rise, z > 0, z == 0), (1, fall, z < 3, z == 3)):
            for b in ((1, 2, 3) if way == 0 else (0, 1, 2)):
                beyond = (b > z) if way == 0 else (b < z)
                if b == (1 if way == 0 else 2):
                    pl.when(beyond)(lambda: hop(buf, way, c, b, z).wait_send())
                else:
                    pl.when(beyond & inner)(lambda: hop(buf, way, c, b, z).wait_send())
                    pl.when(beyond & outer)(lambda: far_hop(way, c, b, z).wait_send())
        return carry

    lax.fori_loop(n - QUEUE, n, drain, 0)


def gradient_blocks(operands, numbers):
    any_space = pl.BlockSpec(memory_space=pl.ANY)
    vmem = pl.BlockSpec(memory_space=pltpu.VMEM)
    n = N_ALL
    dma = pltpu.SemaphoreType.DMA
    widths = (3 * D, 4 * D, 2 * FF, 2 * CHUNK)
    return pl.pallas_call(
        gradient_kernel,
        out_shape=[jax.ShapeDtypeStruct((STRIP, w), f32) for w in widths] + [jax.ShapeDtypeStruct((8, 128), f32)],
        in_specs=[any_space] * 17 + [vmem],
        out_specs=[vmem] * 5,
        scratch_shapes=[
            pltpu.VMEM((7, 2, 4, STRIP, 512), bf16),
            pltpu.VMEM((N_STD, 512, CHUNK), bf16),
            pltpu.VMEM((2, 4, 256, CHUNK), bf16),
            pltpu.VMEM((2, 4, 256, CHUNK), bf16),
            pltpu.VMEM((512, 256), bf16),
            pltpu.VMEM((512, 256), bf16),
            pltpu.VMEM((4, 16, D), f32),
            pltpu.VMEM((2, 4, STRIP, 256), bf16),
            pltpu.VMEM((2, 4, STRIP, 2 * D), bf16),
            pltpu.VMEM((256, 256), f32),
            pltpu.VMEM((n, 4 * STRIP, CHUNK), f32),
            pltpu.VMEM((n, 4 * STRIP, CHUNK), bf16),
            pltpu.VMEM((n, 4 * STRIP, CHUNK), bf16),
            pltpu.VMEM((n, 3, STRIP, CHUNK), f32),
            pltpu.VMEM((n, 3, STRIP, CHUNK), f32),
            pltpu.VMEM((2, n, 2, STRIP, CHUNK), bf16),
            pltpu.VMEM((8, 128), f32),
            pltpu.VMEM((4, 8, 128), f32),
            pltpu.VMEM((8, 8, 128), f32),
            dma((56,)),
            dma((7, 4, 2)),
            dma((7, 4, 2)),
            dma((N_STD, 3)),
            dma((N_STD, 4)),
            dma((3, 3)),
            dma((3, 4)),
            dma((4, 4)),
            dma((4, 3)),
            dma((4,)),
            dma((4,)),
            dma((4,)),
            dma((4,)),
            dma((n,)),
            dma((n,)),
            dma((2, n, 5)),
            dma((2, n, 5)),
            dma((11,)),
            dma((11,)),
        ],
        compiler_params=pltpu.CompilerParams(
            collective_id=1, has_side_effects=True, vmem_limit_bytes=62 * 2**20
        ),
        name="gradient_blocks",
    )(*operands, numbers)


def ag(part):
    return lax.all_gather(part, "fsdp", axis=0, tiled=True)


def make_local(n_dp, n_f):
    fast = n_dp == 8 and n_f == 4

    def local(
        pixels, targets, valid_mask, lat_weight, segment_ids, present_vars, lead_index, step_count,
        w_agg, w_attn, w_mlp, w_io, w_small,
        m_agg, m_attn, m_mlp, m_io, m_small,
        v_agg, v_attn, v_mlp, v_io, v_small,
    ):
        masters = (w_agg, w_attn, w_mlp, w_io, w_small)
        firsts = (m_agg, m_attn, m_mlp, m_io, m_small)
        seconds = (v_agg, v_attn, v_mlp, v_io, v_small)
        rows = pixels.shape[1]
        row_len = segment_ids.shape[1]
        strip = w_agg.shape[0]
        own = lax.axis_index("fsdp")
        heads_here = HEADS // n_f
        wide = heads_here * HEAD_DIM

        seg = segment_ids[0]
        below = jnp.sum((seg[None, :] < seg[:, None]).astype(jnp.int32), axis=1)
        pos = jnp.arange(row_len, dtype=jnp.int32) - below
        onehot_all = (pos[:, None] == jnp.arange(SPAN, dtype=jnp.int32)[None, :]).astype(bf16)
        onehot = lax.dynamic_slice_in_dim(onehot_all, own * rows, rows)
        lead = (lead_index[0].astype(f32) + 1.0) / LEAD_STEPS
        pixel_rows = pixels[0]
        target = targets[0].astype(f32)
        present = present_vars[0]
        spread = (jnp.arange(MIX) // PIX)[None, :] == jnp.arange(VARS)[:, None]
        embed_col = (jnp.arange(MIX) - WIDTH)[None, :] == jnp.arange(VARS)[:, None]
        in_pixels = (jnp.arange(MIX) < WIDTH)[None, :]
        expand = jnp.where(in_pixels, spread, embed_col).astype(bf16)
        present_cols = jnp.repeat(present.astype(f32), PIX)
        pixel_weight = lat_weight[0][:, None] * valid_mask[0].astype(f32) * present_cols[None, :]
        weight_sum = jnp.sum(pixel_weight)

        def blank(width):
            return jnp.zeros((strip, width), bf16)

        io_low = w_io.astype(bf16)
        emb = 2 * WIDTH + VARS
        pack = jnp.concatenate(
            [
                io_low[:, :WIDTH],
                io_low[:, 2 * WIDTH : emb],
                blank(MIX - WIDTH - VARS),
                io_low[:, WIDTH : 2 * WIDTH],
                blank(256 - WIDTH),
                io_low[:, emb : emb + SPAN],
                w_small.astype(bf16),
                blank(128 - w_small.shape[1]),
                w_agg.astype(bf16),
            ],
            axis=1,
        )
        if fast:
            head, attn, mlp, stat = gather_weights(
                pack, w_attn.astype(bf16), w_mlp.astype(bf16), jnp.full((8, 128), weight_sum, f32)
            )
            total = stat[0, 0]
        else:
            head = lax.all_gather(pack, ("dp", "fsdp"), axis=0, tiled=True)
            attn = lax.all_gather(w_attn.astype(bf16), ("dp", "fsdp"), axis=0, tiled=True)
            mlp = lax.all_gather(w_mlp.astype(bf16), ("dp", "fsdp"), axis=0, tiled=True)
            total = lax.psum(weight_sum, ("dp", "fsdp"))
        w240 = head[:, :MIX]
        w_pred = head[:, 256 : 256 + WIDTH]
        w_pos = head[:, 512 : 512 + SPAN]
        small = lax.optimization_barrier(head[:, 768:896])[:, :9].astype(f32).T
        agg_kv = head[:, HEAD : HEAD + 2 * D]
        agg_out = head[:, HEAD + 2 * D :]
        w_qkv = attn[:, : 3 * D]
        w_out = attn[:, 3 * D :]
        w_up = mlp[:, :FF]
        w_down = mlp[:, FF:]

        pix_t = jnp.concatenate(
            [pixel_rows.T, jnp.ones((VARS, rows), bf16), jnp.zeros((MIX - WIDTH - VARS, rows), bf16)], axis=0
        )
        table = t_mm(w240, agg_kv)
        table_k = table[:, :D].reshape(MIX, HEADS, HEAD_DIM)
        table_v = table[:, D:].reshape(MIX, HEADS, HEAD_DIM)
        query = small[0].reshape(HEADS, HEAD_DIM)
        folded = jnp.sum(table_k * query[None], axis=2)
        block = folded.T[:, None, :] * expand.astype(f32)[None]
        score = exact("xc,cl->xl", block.reshape(HEADS * VARS, MIX), pix_t.astype(f32))
        score = score.reshape(HEADS, VARS, rows) * HEAD_DIM ** (-0.5)
        score = jnp.where(present[None, :, None] > 0, score, -1000000000.0)
        top = jnp.max(score, axis=1, keepdims=True)
        power = jnp.exp(score - top)
        soft = power / jnp.sum(power, axis=1, keepdims=True)
        share = soft.astype(bf16)
        pix_f = pix_t.astype(f32)
        lifted_share = jnp.einsum("vc,hvl->hcl", expand, share, preferred_element_type=f32) * pix_f[None]
        mixed_a = exact("che,hcl->hel", table_v, lifted_share).reshape(D, rows).T.astype(bf16)
        lead_embed = lead * small[7] + small[8]
        h0 = mm(mixed_a, agg_out) + mm_t(onehot, w_pos) + lead_embed[None]
        norm0, unit0, scale0 = norm_forward(h0, small[1], small[2])
        qkv = mm(norm0, w_qkv).astype(bf16)
        if fast:
            seg_col = jnp.broadcast_to(seg[:, None], (row_len, 128))
            seg_row = jnp.broadcast_to(seg[None, :], (8, row_len))
            mixed, mixed_t, parts = attend(qkv, seg_col, seg_row)
        else:
            part = qkv.reshape(rows, 3, n_f, wide)
            part = lax.all_to_all(part, "fsdp", split_axis=2, concat_axis=0, tiled=True)
            part = part.reshape(row_len, 3, heads_here, HEAD_DIM)
            q, k, v = (part[:, i].transpose(1, 0, 2) for i in range(3))
            att_score = jnp.einsum("hqe,hke->hqk", q, k, preferred_element_type=f32) * HEAD_DIM ** (-0.5)
            same = seg[:, None] == seg[None, :]
            att_score = jnp.where(same[None], att_score, -1000000000.0)
            att_top = jnp.max(att_score, axis=-1, keepdims=True)
            att_power = jnp.exp(att_score - att_top)
            att_soft = att_power / jnp.sum(att_power, axis=-1, keepdims=True)
            att = att_soft.astype(bf16)
            mixed_h = jnp.einsum("hqk,hke->qhe", att, v, preferred_element_type=f32)
            mixed_h = mixed_h.reshape(row_len, wide).astype(bf16)
            mixed_all = lax.all_gather(mixed_h, "fsdp", axis=1, tiled=True)
            mixed = lax.dynamic_slice_in_dim(mixed_all, own * rows, rows, axis=0)
        h1 = h0 + mm(mixed, w_out)
        norm1, unit1, scale1 = norm_forward(h1, small[3], small[4])
        up = mm(norm1, w_up)
        gate = 0.5 * (1.0 + lax.erf(up * (2.0**-0.5)))
        lifted = (up * gate).astype(bf16)
        h2 = h1 + mm_t(lifted, w_down)
        norm2, unit2, scale2 = norm_forward(h2, small[5], small[6])
        predicted = mm(norm2, w_pred) * D ** (-0.5)
        error = predicted - target
        weighted = pixel_weight * error
        numerator = jnp.sum(weighted * error)

        d_pred = (weighted * (2.0 * D ** (-0.5) / total)).astype(bf16)
        d_norm2 = mm_t(d_pred, w_pred)
        d_h2, d_gain2, d_off2 = norm_backward(d_norm2, unit2, scale2, small[5])
        d_out = d_h2.astype(bf16)
        slope = gate + up * jnp.exp(-0.5 * up * up) * 0.3989422804014327
        d_up = (mm(d_out, w_down) * slope).astype(bf16)
        d_norm1 = mm_t(d_up, w_up)
        d_in, d_gain1, d_off1 = norm_backward(d_norm1, unit1, scale1, small[3])
        d_h1 = d_h2 + d_in
        if fast:
            d_qkv, d_parts, d_proj_all = attend_back(d_h1.astype(bf16), attn, parts, seg_col, seg_row)
        else:
            d_proj_all = ag(d_h1.astype(bf16))
            w_out_own = lax.dynamic_slice_in_dim(w_out, own * wide, wide, axis=0)
            d_mixed = mm_t(d_proj_all, w_out_own).astype(bf16).reshape(row_len, heads_here, HEAD_DIM).transpose(1, 0, 2)
            d_att = jnp.einsum("hqe,hke->hqk", d_mixed, v, preferred_element_type=f32)
            d_v = jnp.einsum("hqk,hqe->khe", att, d_mixed, preferred_element_type=f32)
            lean = jnp.sum(att_soft * d_att, axis=-1, keepdims=True)
            d_score = (att_soft * (d_att - lean) * HEAD_DIM ** (-0.5)).astype(bf16)
            d_q = jnp.einsum("hqk,hke->qhe", d_score, k, preferred_element_type=f32)
            d_k = jnp.einsum("hqk,hqe->khe", d_score, q, preferred_element_type=f32)
            d_part = jnp.stack([d_q, d_k, d_v], axis=1).astype(bf16).reshape(row_len, 3, 1, wide)
            d_qkv_all = lax.all_gather(d_part, "fsdp", axis=2, tiled=True).reshape(row_len, 3 * D)
            d_qkv = lax.dynamic_slice_in_dim(d_qkv_all, own * rows, rows, axis=0)
        d_norm0 = mm_t(d_qkv, w_qkv)
        d_in, d_gain0, d_off0 = norm_backward(d_norm0, unit0, scale0, small[1])
        d_h0 = d_h1 + d_in
        d_agg = d_h0.astype(bf16)
        d_mixed_a = mm_t(agg_out, d_agg).astype(bf16).reshape(HEADS, HEAD_DIM, rows)
        pulled = exact("che,hel->hcl", table_v, d_mixed_a.astype(f32)) * pix_f[None]
        d_share = exact("vc,hcl->hvl", expand.astype(f32), pulled)
        lean_a = jnp.sum(soft * d_share, axis=1, keepdims=True)
        d_score_a = (soft * (d_share - lean_a) * HEAD_DIM ** (-0.5)).astype(bf16)
        spread_score = jnp.einsum("vc,hvl->hcl", expand, d_score_a, preferred_element_type=f32)
        d_folded = jnp.sum(spread_score * pix_f[None], axis=2)
        d_table_v = exact("hcl,hel->che", lifted_share, d_mixed_a.astype(f32)).reshape(MIX, D)
        d_table_k = (d_folded.T[:, :, None] * query[None]).reshape(MIX, D)
        d_query = jnp.sum(d_folded.T[:, :, None] * table_k, axis=0).reshape(D)
        d_bias = jnp.sum(d_h0, axis=0)
        narrow = jnp.stack(
            [d_query, d_gain0, d_off0, d_gain1, d_off1, d_gain2, d_off2, lead * d_bias, d_bias]
            + [jnp.zeros((D,), f32)] * 7
        )
        d_table = jnp.concatenate([d_table_k, d_table_v], axis=1)
        if fast:

            def sorted_rows(array):
                return array.reshape(4, 2, n_f, strip, array.shape[1])

            lane = lax.broadcasted_iota(jnp.int32, (8, 128), 1)
            r_agg, r_attn, r_mlp, r_misc, stat = gradient_blocks(
                [sorted_rows(part.T) for part in (norm1, d_out, norm0)]
                + [mixed_t.reshape(2, n_f, strip, row_len)]
                + [sorted_rows(part.T) for part in (mixed_a, norm2, d_agg)]
                + [d_proj_all, d_parts, d_up, lifted, d_agg, jnp.pad(d_pred, ((0, 0), (0, 256 - WIDTH)))]
                + [onehot_all, d_table.astype(bf16), narrow, sorted_rows(head)],
                jnp.where(lane == 1, numerator, 0.0),
            )
            squares, numerator = stat[0, 0], stat[0, 1]
        else:
            d_table, narrow = lax.psum((d_table, narrow), "fsdp")
            source = jnp.arange(D)
            pick = (source // strip) % n_f == own
            place = (source // (strip * n_f)) * strip + source % strip
            choose = (pick[:, None] & (place[:, None] == jnp.arange(n_dp * strip)[None, :])).astype(bf16)

            def mine(array):
                whole = array.reshape(n_dp, n_f, strip, array.shape[1])
                return lax.dynamic_index_in_dim(whole, own, 1, False).reshape(n_dp * strip, array.shape[1])

            def weight_grad(features, grads):
                return t_mm(mm(features, choose).astype(bf16), grads)

            def gap(width):
                return jnp.zeros((n_dp * strip, width), f32)

            d_agg_all = ag(d_agg)
            g_kv = exact("dc,cx->dx", mine(w240).astype(f32), d_table)
            g_240 = exact("dx,cx->dc", mine(agg_kv).astype(f32), d_table)
            groups = (
                (g_kv, weight_grad(ag(mixed_a), d_agg_all)),
                (weight_grad(ag(norm0), d_qkv_all), weight_grad(mixed_all, d_proj_all)),
                (weight_grad(ag(norm1), ag(d_up)), weight_grad(ag(d_out), ag(lifted))),
                (
                    g_240, weight_grad(ag(norm2), ag(d_pred)), gap(256 - WIDTH),
                    weight_grad(d_agg_all, onehot_all), mine(narrow.T)[:, :9], gap(256 - 9),
                ),
            )
            r_agg, r_attn, r_mlp, r_misc = (
                lax.psum_scatter(jnp.concatenate(g, axis=1), "dp", scatter_dimension=0, tiled=True) for g in groups
            )
            local_squares = sum(jnp.sum(piece * piece) for piece in (r_agg, r_attn, r_mlp, r_misc))
            squares, numerator = lax.psum((local_squares, numerator), ("dp", "fsdp"))
        r_io = jnp.concatenate(
            [
                r_misc[:, :WIDTH], r_misc[:, 256 : 256 + WIDTH], r_misc[:, WIDTH : WIDTH + VARS],
                r_misc[:, 512 : 512 + SPAN], jnp.zeros((strip, w_io.shape[1] - emb - SPAN), f32),
            ],
            axis=1,
        )
        reduced = (r_agg, r_attn, r_mlp, r_io, r_misc[:, 768:777])
        grad_norm = jnp.sqrt(squares)
        factor = jnp.minimum(1.0, clip_limit / grad_norm)
        loss = numerator / total
        step_value = step_count[0].astype(f32)
        results = [
            adamw(masters[i], reduced[i] * factor, firsts[i], seconds[i], step_value, learn_rates[i]) for i in range(5)
        ]
        return (loss, grad_norm) + tuple(results[i][j] for j in range(4) for i in range(5))

    return local


def solution(mesh):
    flat = P(("dp", "fsdp"), None)
    tokens = P("dp", "fsdp", None)
    return jax.shard_map(
        make_local(mesh.shape["dp"], mesh.shape["fsdp"]),
        mesh=mesh,
        in_specs=(tokens, tokens, tokens, P("dp", "fsdp"), P("dp", None), P("dp", None), P("dp"), P()) + (flat,) * 15,
        out_specs=(P(), P()) + (flat,) * 20,
        check_vma=False,
    )
```

```python
import functools

import jax
import jax.numpy as jnp
from jax import lax
from jax.experimental import pallas as pl
from jax.experimental.pallas import tpu as pltpu
from jax.sharding import PartitionSpec as P

D = 1024
HEADS = 16
HEAD_DIM = 64
FF = 4096
VARS = 48
PIX = 4
LEAD_STEPS = 8
WIDTH = VARS * PIX
SPAN = 256
MIX = 256
HEAD = 896

norm_eps = 1e-05
clip_limit = 1.0
decay_rate = 0.05
adam_eps = 1e-08
learn_rates = (0.03, 0.03, 0.03, 0.2, 0.3)
f32 = jnp.float32
bf16 = jnp.bfloat16
highest = lax.Precision.HIGHEST
MESH = pl.DeviceIdType.MESH
STRIP = 32
CHUNK = 512
LAG = 2
QUEUE = 2


def dot(left, right, dims):
    return lax.dot_general(left, right, (dims, ((), ())), preferred_element_type=f32)


def mm(left, right):
    return dot(left, right, ((1,), (0,)))


def mm_t(left, right):
    return dot(left, right, ((1,), (1,)))


def t_mm(left, right):
    return dot(left, right, ((0,), (0,)))


def exact(eq, left, right):
    return jnp.einsum(eq, left, right, precision=highest, preferred_element_type=f32)


def norm_forward(values, gain, offset):
    average = jnp.mean(values, axis=-1, keepdims=True)
    centred = values - average
    scale = lax.rsqrt(jnp.mean(centred * centred, axis=-1, keepdims=True) + norm_eps)
    unit = centred * scale
    return (unit * gain[None] + offset[None]).astype(bf16), unit, scale


def norm_backward(grad, unit, scale, gain):
    inner = grad * gain[None]
    mean_inner = jnp.mean(inner, axis=-1, keepdims=True)
    mean_product = jnp.mean(inner * unit, axis=-1, keepdims=True)
    back = scale * (inner - mean_inner - unit * mean_product)
    return back, jnp.sum(grad * unit, axis=0), jnp.sum(grad, axis=0)


def adamw(weight, grad, moment, second, step_value, learn_rate):
    moment = 0.5 * moment + 0.5 * grad
    second = 0.5 * second + 0.5 * grad * grad
    correct = 1.0 - jnp.power(f32(0.5), step_value)
    update = moment / correct / (jnp.sqrt(second / correct) + adam_eps) + decay_rate * weight
    fresh = weight - learn_rate * update
    return (fresh, fresh.astype(bf16), moment, second)


PIECES = (
    (0, 1024, 1536, "yzx"), (1, 0, 2048, "zxy"), (0, 2560, 1408, "yzx"), (1, 2048, 2048, "zxy"), (0, 0, 1024, "zxy"),
)


def gather_kernel(*refs):
    w_io, w_small, w_agg, w_attn, num_ref = refs[:5]
    wholes, small_ref, stat_ref = refs[5:7], refs[7], refs[8]
    quad_buf, line_buf, small_buf, pack, attn_low, own_sem, s_send, s_recv, sends, arrive, pass_on = refs[9:]
    shards = (pack, attn_low)
    dp, own = lax.axis_index("dp"), lax.axis_index("fsdp")
    z, y, x, core = dp // 2, dp % 2, own // 2, own % 2
    sibling = x * 2 + 1 - core
    barrier = pltpu.get_barrier_semaphore()
    for d in range(1, 8):
        pl.semaphore_signal(barrier, inc=1, device_id=(lax.rem(dp + d, 8), own), device_id_type=MESH)
    for d in range(1, 4):
        pl.semaphore_signal(barrier, inc=1, device_id=(dp, lax.rem(own + d, 4)), device_id_type=MESH)
    emb = 2 * WIDTH + VARS

    def gap(width):
        return jnp.zeros((STRIP, width), f32)

    pack[:, :HEAD] = jnp.concatenate(
        [
            w_io[:, :WIDTH], w_io[:, 2 * WIDTH : emb], gap(MIX - WIDTH - VARS), w_io[:, WIDTH : 2 * WIDTH],
            gap(256 - WIDTH), w_io[:, emb : emb + SPAN], w_small[...], gap(128 - w_small.shape[1]),
        ],
        axis=1,
    ).astype(bf16)
    pack[:, HEAD:] = w_agg[...].astype(bf16)
    attn_low[...] = w_attn[...].astype(bf16)
    pl.semaphore_wait(barrier, 10)

    def view(p, ident, plane):
        a, start, width, order = PIECES[p]
        row = pl.multiple_of(((ident // 2) * 4 + (ident % 2) * 2 + plane) * STRIP, STRIP)
        return wholes[a].at[pl.ds(row, STRIP), pl.ds(start, width)]

    def copy(p, ident, slot, to, mine=False):
        a, start, width, order = PIECES[p]
        src = shards[a].at[:, pl.ds(start, width)] if mine else view(p, ident, core)
        sem = pass_on if slot == 4 else arrive
        return pltpu.make_async_remote_copy(
            src_ref=src, dst_ref=view(p, ident, core), send_sem=sends.at[p, ident, slot], recv_sem=sem.at[p, ident],
            device_id=to, device_id_type=MESH,
        )

    def arrival(p, ident, plane, sem):
        return pltpu.make_async_copy(view(p, ident, plane), view(p, ident, plane), sem.at[p, ident])

    def targets(p, rx, ry, rz):
        order = PIECES[p][3]
        moved = {"x": rx != 0, "y": ry != 0, "z": rz is not None}
        stage = max([k for k in range(3) if moved[order[k]]], default=-1)
        found = []
        if stage >= 0 and order[stage] == "z":
            found.append((0, (rz < 0) & (z < 3), ((dp + 2) % 8, own)))
            found.append((1, (rz > 0) & (z > 0), ((dp + 6) % 8, own)))
        for k in range(stage + 1, 3):
            if order[k] == "z":
                found.append((0, z < 3, ((dp + 2) % 8, own)))
                found.append((1, z > 0, ((dp + 6) % 8, own)))
            elif order[k] == "x":
                found.append((2, None, (dp, (1 - x) * 2 + core)))
            else:
                found.append((3, None, (z * 2 + 1 - y, own)))
        found.append((4, None, (dp, sibling)))
        return found

    def source(rx, ry, rz):
        sz = z if rz is None else z + rz
        sy = 1 - y if ry else y
        sx = 1 - x if rx else x
        return sz, (sz * 2 + sy) * 2 + sx

    def each(rx, ry, rz, act, mine=False):
        sz, ident = source(rx, ry, rz)

        def body():
            for p in range(len(PIECES)):
                if act == "send" and not mine:
                    arrival(p, ident, core, arrive).wait()
                for slot, when, to in targets(p, rx, ry, rz):
                    def go(slot=slot, to=to):
                        c = copy(p, ident, slot, to, mine)
                        c.start() if act == "send" else c.wait_send()

                    if when is None:
                        go()
                    else:
                        pl.when(when)(go)

        if rz is None:
            body()
        else:
            pl.when((sz >= 0) & (sz < 4))(body)

    def over_z(pairs, act):
        def step(t, carry):
            rz = ((t + 1) // 2) * (1 - 2 * (t % 2))
            for rx, ry in pairs:
                each(rx, ry, rz, act)
            return carry

        lax.fori_loop(1, 7, step, 0)

    def sweep(act):
        each(0, 0, None, act, mine=True)
        if act == "send":
            for a in range(2):
                row = pl.multiple_of((dp * 4 + own) * STRIP, STRIP)
                pltpu.make_async_copy(shards[a], wholes[a].at[pl.ds(row, STRIP), :], own_sem.at[a]).start()
            scalars()
        each(1, 0, None, act)
        each(0, 1, None, act)
        over_z([(0, 0)], act)
        each(1, 1, None, act)
        over_z([(1, 0), (0, 1)], act)
        over_z([(1, 1)], act)

    def share(buf, k, where, at):
        return pltpu.make_async_remote_copy(
            src_ref=buf.at[at], dst_ref=buf.at[at], send_sem=s_send.at[k], recv_sem=s_recv.at[k],
            device_id=where, device_id_type=MESH,
        )

    def scalars():
        quad_buf[own] = num_ref[...]
        for d in range(1, 4):
            share(quad_buf, d, (dp, lax.rem(own + d, 4)), own).start()

    sweep("send")
    for d in range(1, 4):
        share(quad_buf, d, (dp, own), lax.rem(own + 4 - d, 4)).wait_recv()
    line_buf[dp] = (quad_buf[0] + quad_buf[1]) + (quad_buf[2] + quad_buf[3])
    for d in range(1, 8):
        share(line_buf, 3 + d, (lax.rem(dp + d, 8), own), dp).start()

    def closing(ident, carry):
        for p in range(len(PIECES)):
            arrival(p, ident, 1 - core, pass_on).wait()
        return carry

    lax.fori_loop(0, 16, closing, 0)
    for a in range(2):
        row = pl.multiple_of((dp * 4 + own) * STRIP, STRIP)
        pltpu.make_async_copy(shards[a], wholes[a].at[pl.ds(row, STRIP), :], own_sem.at[a]).wait()
    narrow = pltpu.make_async_copy(wholes[0].at[:, pl.ds(768, 128)], small_buf, own_sem.at[0])
    narrow.start()
    sweep("drain")
    narrow.wait()
    small_ref[...] = small_buf[...].astype(f32).T[:16]
    for d in range(1, 8):
        share(line_buf, 3 + d, (dp, own), lax.rem(dp + 8 - d, 8)).wait_recv()
    stat = line_buf[0]
    for d in range(1, 8):
        stat = stat + line_buf[d]
    stat_ref[...] = stat
    for d in range(1, 4):
        share(quad_buf, d, (dp, own), own).wait_send()
    for d in range(1, 8):
        share(line_buf, 3 + d, (dp, own), dp).wait_send()


def gather_weights(w_io, w_small, w_agg, w_attn, number):
    any_space = pl.BlockSpec(memory_space=pl.ANY)
    vmem = pl.BlockSpec(memory_space=pltpu.VMEM)
    n = len(PIECES)
    return pl.pallas_call(
        gather_kernel,
        out_shape=[jax.ShapeDtypeStruct((D, w), bf16) for w in (HEAD + 3 * D, 4 * D)]
        + [jax.ShapeDtypeStruct((16, D), f32), jax.ShapeDtypeStruct((8, 128), f32)],
        in_specs=[vmem] * 5,
        out_specs=[any_space] * 2 + [vmem] * 2,
        scratch_shapes=[
            pltpu.VMEM((4, 8, 128), f32),
            pltpu.VMEM((8, 8, 128), f32),
            pltpu.VMEM((D, 128), bf16),
            pltpu.VMEM((STRIP, HEAD + 3 * D), bf16),
            pltpu.VMEM((STRIP, 4 * D), bf16),
            pltpu.SemaphoreType.DMA((3,)),
            pltpu.SemaphoreType.DMA((11,)),
            pltpu.SemaphoreType.DMA((11,)),
            pltpu.SemaphoreType.DMA((n, 16, 5)),
            pltpu.SemaphoreType.DMA((n, 16)),
            pltpu.SemaphoreType.DMA((n, 16)),
        ],
        compiler_params=pltpu.CompilerParams(collective_id=0, has_side_effects=True),
        cost_estimate=pl.CostEstimate(flops=0, bytes_accessed=250_000_000, transcendentals=0),
        name="gather_weights",
    )(w_io, w_small, w_agg, w_attn, number)


def greet(dp, own):
    barrier = pltpu.get_barrier_semaphore()
    for d in range(1, 4):
        pl.semaphore_signal(barrier, inc=1, device_id=(dp, lax.rem(own + d, 4)), device_id_type=MESH)
    pl.semaphore_wait(barrier, 3)


def turned_softmax(parts, seg_col, seg_row, h):
    at = slice(h * HEAD_DIM, (h + 1) * HEAD_DIM)
    q, k, v = (parts[i, :, at] for i in range(3))
    score = lax.dot_general(k, q, (((1,), (1,)), ((), ())), preferred_element_type=f32) * HEAD_DIM ** (-0.5)
    score = jnp.where(seg_col[:, 0:1] == seg_row[0:1, :], score, -1000000000.0)
    power = jnp.exp(score - jnp.max(score, axis=0, keepdims=True))
    soft = power / jnp.sum(power, axis=0, keepdims=True)
    return q, k, v, soft, soft.astype(bf16)


def attend_kernel(qkv, seg_col, seg_row, mixed, mixed_t, parts_out, parts, turned, whole, gathered,
                  load_sem, in_send, in_recv, out_send, out_recv):
    dp, own = lax.axis_index("dp"), lax.axis_index("fsdp")
    greet(dp, own)
    row = pl.ds(pl.multiple_of(own * 128, 128), 128)

    def piece(i, to):
        return qkv.at[:, pl.ds(pl.multiple_of(i * D + to * 256, 256), 256)]

    def into(d, i):
        to = lax.rem(own + d, 4)
        return pltpu.make_async_remote_copy(
            src_ref=piece(i, to), dst_ref=parts.at[i, row, :], send_sem=in_send.at[d, i], recv_sem=in_recv.at[d, i],
            device_id=(dp, to), device_id_type=MESH,
        )

    for i in range(3):
        for d in (2, 1, 3):
            into(d, i).start()
    for i in range(3):
        pltpu.make_async_copy(piece(i, own), parts.at[i, row, :], load_sem.at[i]).start()
    for i in range(3):
        pltpu.make_async_copy(piece(i, own), parts.at[i, row, :], load_sem.at[i]).wait()
        for d in range(1, 4):
            into(d, i).wait_recv()
    for h in range(4):
        q, k, v, soft, share = turned_softmax(parts, seg_col, seg_row, h)
        turned[h * HEAD_DIM : (h + 1) * HEAD_DIM, :] = lax.dot_general(
            v, share, (((0,), (0,)), ((), ())), preferred_element_type=f32
        )
    whole[...] = turned[...].T.astype(bf16)
    column = pl.ds(pl.multiple_of(own * 256, 256), 256)

    def back(d):
        to = lax.rem(own + d, 4)
        return pltpu.make_async_remote_copy(
            src_ref=whole.at[pl.ds(pl.multiple_of(to * 128, 128), 128), :], dst_ref=gathered.at[:, column],
            send_sem=out_send.at[d], recv_sem=out_recv.at[d], device_id=(dp, to), device_id_type=MESH,
        )

    for d in (2, 1, 3):
        back(d).start()
    keep = pltpu.make_async_copy(whole.at[row, :], gathered.at[:, column], load_sem.at[3])
    keep.start()
    mixed_t[...] = turned[...].astype(bf16)
    parts_out[...] = parts[...]
    keep.wait()
    for d in range(1, 4):
        back(d).wait_recv()
    mixed[...] = gathered[...]
    for d in range(1, 4):
        back(d).wait_send()
        for i in range(3):
            into(d, i).wait_send()


def attend(qkv, seg_col, seg_row):
    vmem = pl.BlockSpec(memory_space=pltpu.VMEM)
    dma = pltpu.SemaphoreType.DMA
    return pl.pallas_call(
        attend_kernel,
        out_shape=[
            jax.ShapeDtypeStruct((128, D), bf16), jax.ShapeDtypeStruct((256, 512), bf16),
            jax.ShapeDtypeStruct((3, 512, 256), bf16),
        ],
        in_specs=[pl.BlockSpec(memory_space=pl.ANY), vmem, vmem],
        out_specs=[vmem] * 3,
        scratch_shapes=[
            pltpu.VMEM((3, 512, 256), bf16), pltpu.VMEM((256, 512), f32), pltpu.VMEM((512, 256), bf16),
            pltpu.VMEM((128, D), bf16), dma((4,)), dma((4, 3)), dma((4, 3)), dma((4,)), dma((4,)),
        ],
        compiler_params=pltpu.CompilerParams(collective_id=2, has_side_effects=True, vmem_limit_bytes=40 * 2**20),
        name="attend",
    )(qkv, seg_col, seg_row)


def attend_back_kernel(d_proj, attn, parts, seg_col, seg_row, d_own, d_parts_out, d_all_out, every, proj, d_mixed,
                       d_parts, gathered, load_sem, up_send, up_recv, out_send, out_recv):
    dp, own = lax.axis_index("dp"), lax.axis_index("fsdp")
    x, core = own // 2, own % 2
    sibling, across, diagonal = x * 2 + 1 - core, (1 - x) * 2 + core, (1 - x) * 2 + 1 - core
    rows = pl.ds(pl.multiple_of(own * 256, 256), 256)
    fetch = pltpu.make_async_copy(attn.at[rows, pl.ds(3 * D, D)], proj, load_sem.at[0])
    fetch.start()
    row = pl.ds(pl.multiple_of(own * 128, 128), 128)
    mine = pltpu.make_async_copy(d_proj, every.at[row, :], load_sem.at[1])
    mine.start()
    greet(dp, own)
    mine.wait()

    def up(i, who, slot, to):
        block = every.at[pl.ds(pl.multiple_of(who * 128, 128), 128), i * 512 : (i + 1) * 512]
        return pltpu.make_async_remote_copy(
            src_ref=block, dst_ref=block, send_sem=up_send.at[i, slot], recv_sem=up_recv.at[i, who],
            device_id=(dp, to), device_id_type=MESH,
        )

    for i in range(2):
        up(i, own, 0, across).start()
    for i in range(2):
        up(i, own, 1, sibling).start()
    for i in range(2):
        up(i, across, 0, own).wait_recv()
        up(i, across, 2, sibling).start()
    fetch.wait()
    for i in range(2):
        up(i, sibling, 1, own).wait_recv()
        up(i, diagonal, 2, own).wait_recv()
    d_mixed[...] = lax.dot_general(
        every[...], proj[...], (((1,), (1,)), ((), ())), preferred_element_type=f32
    ).astype(bf16)
    for h in range(4):
        at = slice(h * HEAD_DIM, (h + 1) * HEAD_DIM)
        q, k, v, soft, share = turned_softmax(parts, seg_col, seg_row, h)
        d_head = d_mixed[:, at]
        d_soft = lax.dot_general(v, d_head, (((1,), (1,)), ((), ())), preferred_element_type=f32)
        lean = jnp.sum(soft * d_soft, axis=0, keepdims=True)
        d_score = (soft * (d_soft - lean) * HEAD_DIM ** (-0.5)).astype(bf16)
        d_parts[2, :, at] = mm(share, d_head).astype(bf16)
        d_parts[1, :, at] = mm(d_score, q).astype(bf16)
        d_parts[0, :, at] = t_mm(d_score, k).astype(bf16)

    def back(d, i):
        to = lax.rem(own + d, 4)
        return pltpu.make_async_remote_copy(
            src_ref=d_parts.at[i, pl.ds(pl.multiple_of(to * 128, 128), 128), :],
            dst_ref=gathered.at[:, pl.ds(pl.multiple_of(i * D + own * 256, 256), 256)],
            send_sem=out_send.at[d, i], recv_sem=out_recv.at[d, i], device_id=(dp, to), device_id_type=MESH,
        )

    for i in range(3):
        for d in (2, 1, 3):
            back(d, i).start()
    keeps = [
        pltpu.make_async_copy(
            d_parts.at[i, row, :], gathered.at[:, pl.ds(pl.multiple_of(i * D + own * 256, 256), 256)], load_sem.at[2 + i]
        )
        for i in range(3)
    ]
    for keep in keeps:
        keep.start()
    d_parts_out[...] = d_parts[...]
    d_all_out[...] = every[...]
    for keep in keeps:
        keep.wait()
    for i in range(3):
        for d in range(1, 4):
            back(d, i).wait_recv()
    d_own[...] = gathered[...]
    for d in range(1, 4):
        for i in range(3):
            back(d, i).wait_send()
    for i in range(2):
        for slot, who in ((0, own), (1, own), (2, across)):
            up(i, who, slot, own).wait_send()


def attend_back(d_proj, attn, parts, seg_col, seg_row):
    vmem = pl.BlockSpec(memory_space=pltpu.VMEM)
    any_space = pl.BlockSpec(memory_space=pl.ANY)
    dma = pltpu.SemaphoreType.DMA
    return pl.pallas_call(
        attend_back_kernel,
        out_shape=[
            jax.ShapeDtypeStruct((128, 3 * D), bf16), jax.ShapeDtypeStruct((3, 512, 256), bf16),
            jax.ShapeDtypeStruct((512, D), bf16),
        ],
        in_specs=[any_space, any_space, vmem, vmem, vmem],
        out_specs=[vmem] * 3,
        scratch_shapes=[
            pltpu.VMEM((512, D), bf16), pltpu.VMEM((256, D), bf16), pltpu.VMEM((512, 256), bf16),
            pltpu.VMEM((3, 512, 256), bf16), pltpu.VMEM((128, 3 * D), bf16),
            dma((5,)), dma((2, 3)), dma((2, 4)), dma((4, 3)), dma((4, 3)),
        ],
        compiler_params=pltpu.CompilerParams(collective_id=3, has_side_effects=True, vmem_limit_bytes=40 * 2**20),
        name="attend_back",
    )(d_proj, attn, parts, seg_col, seg_row)


SEGMENTS = ((0, 2, 3), (2, 10, 1), (10, 18, 0), (18, 24, 2), (24, 26, 4))
N_STD, N_ALL, SHIFT, BASE = 26, 32, 1, 2


FAR = ({2: 0, 3: 1}, {0: 0, 1: 1})


def preds_at(preds, who):
    return preds.at[pl.ds(pl.multiple_of(who * 128, 128), 128), :]


def gradient_kernel(*refs):
    (norm1_t, out_t, norm0_t, mixed_t, mixa_t, norm2_t, agg_t,
     d_proj, d_parts, d_up, lifted, d_agg, d_pred, onehot, d_table, narrow, head, num_ref) = refs[:18]
    r_agg, r_attn, r_mlp, r_io, r_small, stat_ref = refs[18:24]
    (feats, ys, tabs, pairs, preds, hots, narrows, w240, wkv, acc240, own_buf, give_buf, got, rise, fall, far, tally,
     quad_buf, line_buf, load_sem, feat_send, feat_recv, y_xsend, y_xrecv, part_send, part_recv, tab_send, tab_recv, pred_send, pred_recv,
     nar_send, nar_recv, y_send, y_recv, z_send, z_recv, s_send, s_recv) = refs[24:]
    dp, own = lax.axis_index("dp"), lax.axis_index("fsdp")
    z, y, x, core = dp // 2, dp % 2, own // 2, own % 2
    sibling, across, diagonal = x * 2 + 1 - core, (1 - x) * 2 + core, (1 - x) * 2 + 1 - core
    over = z * 2 + 1 - y
    n = N_ALL
    row = pl.ds(pl.multiple_of(own * 128, 128), 128)
    sent_feats = {0: norm1_t, 1: out_t, 2: norm0_t, 4: mixa_t, 5: norm2_t, 6: agg_t}

    def remote(src, dst, send, recv, to):
        return pltpu.make_async_remote_copy(
            src_ref=src, dst_ref=dst, send_sem=send, recv_sem=recv, device_id=(dp, to), device_id_type=MESH
        )

    def feat_copy(k, d, half, to):
        side = y if half == 0 else 1 - y
        if k == 3:
            src, dst = mixed_t.at[side, to], feats.at[3, half, own]
        else:
            src, dst = sent_feats[k].at[:, side, to], feats.at[k, half, :, :, row]
        return remote(src, dst, feat_send.at[k, d, half], feat_recv.at[k, d, half], to)

    def feat_start(k):
        for d in (2, 1, 3):
            for half in range(2):
                feat_copy(k, d, half, lax.rem(own + d, 4)).start()

    def unit_block(c, who):
        return ys.at[c, pl.ds(pl.multiple_of(who * 128, 128), 128), :]

    def unit(c, who, slot, to):
        return remote(unit_block(c, who), unit_block(c, who), y_xsend.at[c, slot], y_xrecv.at[c, who], to)

    def part_block(i, who):
        return ys.at[18 + i * 2 + who // 2, :, pl.ds(pl.multiple_of((who % 2) * 256, 256), 256)]

    def part(i, who, slot, to):
        return remote(part_block(i, who), part_block(i, who), part_send.at[i, slot], part_recv.at[i, who], to)

    def table_raw(v, to):
        return remote(tabs.at[0, v], tabs.at[1, v], tab_send.at[v, 0], tab_recv.at[v, 0], to)

    def table(v, who, slot, to):
        return remote(pairs.at[who, v], pairs.at[who, v], tab_send.at[v, slot], tab_recv.at[v, 1 + who], to)

    def pred_copy(d, who, to):
        return remote(preds_at(preds, who), preds_at(preds, who), pred_send.at[d], pred_recv.at[d], to)

    def narrow_copy(d, who, to):
        return remote(narrows.at[who], narrows.at[who], nar_send.at[d], nar_recv.at[d], to)

    loads = {}

    def load(name, src, dst):
        copy = pltpu.make_async_copy(src, dst, load_sem.at[len(loads)])
        copy.start()
        loads[name] = copy

    def load_feat(k):
        for half in range(2):
            side = y if half == 0 else 1 - y
            if k == 3:
                load(("f", k, half), mixed_t.at[side, own], feats.at[3, half, own])
            else:
                load(("f", k, half), sent_feats[k].at[:, side, own], feats.at[k, half, :, :, row])

    def loaded(*names):
        for name in names:
            loads[name].wait()

    for c in range(2):
        load(("j", c), d_proj.at[:, pl.ds(c * CHUNK, CHUNK)], ys.at[c])
    load_feat(3)
    load_feat(1)
    for c in range(8):
        load(("u", 10 + c), d_up.at[:, pl.ds(c * CHUNK, CHUNK)], unit_block(10 + c, own))
    for c in range(8):
        load(("l", c), lifted.at[:, pl.ds(c * CHUNK, CHUNK)], ys.at[2 + c])
    load_feat(0)
    for i in range(3):
        load(("p", i), d_parts.at[i], part_block(i, own))
    load_feat(2)
    for c in range(2):
        load(("u", 24 + c), d_agg.at[:, pl.ds(c * CHUNK, CHUNK)], unit_block(24 + c, own))
    load_feat(4)
    for v in range(4):
        load(("t", v), d_table.at[:, pl.ds(v * CHUNK, CHUNK)], tabs.at[0, v])
    load("pred", d_pred, preds_at(preds, own))
    load("narrow", narrow, narrows.at[own])
    for half in range(2):
        side = y if half == 0 else 1 - y
        load(("w", half), head.at[:, side, own, :, pl.ds(0, 256)], w240.at[half])
        load(("k", half), head.at[:, side, own, :, pl.ds(HEAD, 2 * D)], wkv.at[half])
    load_feat(5)
    load_feat(6)
    load("hot", onehot, hots)
    barrier = pltpu.get_barrier_semaphore()
    for d in range(1, 8):
        pl.semaphore_signal(barrier, inc=1, device_id=(lax.rem(dp + d, 8), own), device_id_type=MESH)
    for d in range(1, 4):
        pl.semaphore_signal(barrier, inc=1, device_id=(dp, lax.rem(own + d, 4)), device_id_type=MESH)
    pl.semaphore_wait(barrier, 10)
    feat_start(3)
    feat_start(1)
    feat_start(0)
    loaded(*[("u", 10 + c) for c in range(8)])

    def begin(c, carry):
        unit(c, own, 0, across).start()
        unit(c, own, 1, sibling).start()
        return carry

    lax.fori_loop(10, 18, begin, 0)
    feat_start(2)
    loaded(*[("p", i) for i in range(3)], ("u", 24), ("u", 25))
    for i in range(3):
        part(i, own, 0, across).start()
        part(i, own, 1, sibling).start()
    feat_start(4)
    lax.fori_loop(24, 26, begin, 0)
    loaded(*[("t", v) for v in range(4)], "pred", "narrow")
    for w in range(2):
        table_raw((1 - core) * 2 + w, sibling).start()
    tally[...] = jnp.zeros_like(tally)
    acc240[...] = jnp.zeros_like(acc240)
    for w in range(2):
        v = core * 2 + w
        table_raw(v, own).wait_recv()
        pairs[x, v] = (tabs[0, v].astype(f32) + tabs[1, v].astype(f32)).astype(bf16)
        table(v, x, 1, across).start()
        table(v, x, 2, sibling).start()
    feat_start(5)
    feat_start(6)
    for d in (2, 1, 3):
        pred_copy(d, own, lax.rem(own + d, 4)).start()
        narrow_copy(d, own, lax.rem(own + d, 4)).start()

    def feat_wait(k):
        for d in range(1, 4):
            for half in range(2):
                feat_copy(k, d, half, own).wait_recv()

    def put(c, value):
        own_buf[c] = value[:128]
        give_buf[c] = value[128:].astype(bf16)

    def feature(k):
        return feats[k].reshape(256, 512)

    def matmul(a, b):
        return lax.dot_general(a, b, (((1,), (0,)), ((), ())), preferred_element_type=f32)

    def two(value):
        high = value.astype(bf16)
        return high, (value - high.astype(f32)).astype(bf16)

    def summed_table(v):
        return two(pairs[0, v].astype(f32) + pairs[1, v].astype(f32))

    def compute(c):
        for i in range(3):
            @pl.when(c == 18 + i * 2)
            def _():
                part(i, sibling, 1, own).wait_recv()
                part(i, diagonal, 2, own).wait_recv()

        for low, high, k in SEGMENTS:
            @pl.when(c == low)
            def _():
                feat_wait(k)
                loaded(("f", k, 0), ("f", k, 1))
                if k == 3:
                    loaded(("j", 0), ("j", 1))
                if k == 1:
                    loaded(*[("l", i) for i in range(8)])

            @pl.when((c >= low) & (c < high))
            def _():
                if k in (0, 4):
                    unit(c, sibling, 1, own).wait_recv()
                    unit(c, diagonal, 2, own).wait_recv()
                put(c, matmul(feature(k), ys[c]))

        @pl.when(c == N_STD)
        def _():
            loaded(("w", 0), ("w", 1), ("k", 0), ("k", 1))

        @pl.when((c >= N_STD) & (c < N_STD + 4))
        def _():
            v = c - N_STD

            @pl.when(v // 2 != core)
            def _():
                table(v, x, 2, own).wait_recv()
                table(v, 1 - x, 3, own).wait_recv()

            high, low = summed_table(v)
            rows = w240[...].reshape(256, 256)
            put(c, matmul(rows, high) + matmul(rows, low))

        for v in range(4):
            @pl.when(c == N_STD + v)
            def _():
                high, low = summed_table(v)
                rows = wkv[:, :, :, v * CHUNK : (v + 1) * CHUNK].reshape(256, CHUNK)
                dims = (((1,), (1,)), ((), ()))
                acc240[...] = (
                    acc240[...]
                    + lax.dot_general(rows, high, dims, preferred_element_type=f32)
                    + lax.dot_general(rows, low, dims, preferred_element_type=f32)
                )

        @pl.when(c == N_STD + 4)
        def _():
            feat_wait(5)
            loaded(("f", 5, 0), ("f", 5, 1))
            for d in range(1, 4):
                pred_copy(d, lax.rem(own + 4 - d, 4), own).wait_recv()
            value = matmul(feature(5), preds[...])
            own_buf[c, :, 0:256] = acc240[:128]
            own_buf[c, :, 256:512] = value[:128]
            give_buf[c, :, 0:256] = acc240[128:].astype(bf16)
            give_buf[c, :, 256:512] = value[128:].astype(bf16)

        @pl.when(c == N_STD + 5)
        def _():
            feat_wait(6)
            loaded(("f", 6, 0), ("f", 6, 1), "hot")
            for d in range(1, 4):
                narrow_copy(d, lax.rem(own + 4 - d, 4), own).wait_recv()
            value = matmul(feature(6), hots[...])
            place = lax.broadcasted_iota(jnp.int32, (256, D), 0)
            source = lax.broadcasted_iota(jnp.int32, (256, D), 1)
            side = jnp.where(place < 128, y, 1 - y)
            wanted = ((place >> 5) & 3) * 256 + side * 128 + own * STRIP + (place & 31)
            choose = jnp.where(source == wanted, 1.0, 0.0).astype(bf16)
            total = (narrows[0] + narrows[1]) + (narrows[2] + narrows[3])
            total = jnp.concatenate([total, jnp.zeros((112, D), f32)], axis=0)
            high = total.astype(bf16)
            rest = total - high.astype(f32)
            middle = rest.astype(bf16)
            low = (rest - middle.astype(f32)).astype(bf16)
            dims = (((1,), (1,)), ((), ()))
            small = (
                lax.dot_general(choose, high, dims, preferred_element_type=f32)
                + lax.dot_general(choose, middle, dims, preferred_element_type=f32)
                + lax.dot_general(choose, low, dims, preferred_element_type=f32)
            )
            empty = jnp.zeros((128, 128), f32)
            own_buf[c, :, 0:256] = value[:128]
            own_buf[c, :, 256:384] = small[:128]
            own_buf[c, :, 384:512] = empty
            give_buf[c, :, 0:256] = value[128:].astype(bf16)
            give_buf[c, :, 256:384] = small[128:].astype(bf16)
            give_buf[c, :, 384:512] = empty.astype(bf16)

    def cross(c):
        return pltpu.make_async_remote_copy(
            src_ref=give_buf.at[c], dst_ref=got.at[c], send_sem=y_send.at[c],
            recv_sem=y_recv.at[c], device_id=(over, own), device_id_type=MESH,
        )

    def hop(buf, way, c, b, to):
        at = b - 1 if way == 0 else b
        return pltpu.make_async_remote_copy(
            src_ref=buf.at[c, at], dst_ref=buf.at[c, at], send_sem=z_send.at[way, c, at], recv_sem=z_recv.at[way, c, at],
            device_id=(to * 2 + y, own), device_id_type=MESH,
        )

    def far_hop(way, c, b, to):
        at = FAR[way][b]
        return pltpu.make_async_remote_copy(
            src_ref=far.at[way, c, at], dst_ref=far.at[way, c, at], send_sem=z_send.at[way, c, 3 + at],
            recv_sem=z_recv.at[way, c, 3 + at], device_id=(to * 2 + y, own), device_id_type=MESH,
        )

    def here(c, b):
        at = pl.ds(b * STRIP, STRIP)
        return own_buf[c, at, :] + got[c, at, :].astype(f32)

    early, late = LAG * jnp.minimum(z, 3 - z), LAG * jnp.maximum(z, 3 - z)

    def step(t, carry):
        @pl.when((t >= 4) & (t < 12))
        def _():
            unit(t + 6, across, 0, own).wait_recv()
            unit(t + 6, across, 2, sibling).start()

        for i in range(3):
            @pl.when(t == 14 + 2 * i)
            def _():
                part(i, across, 0, own).wait_recv()
                part(i, across, 2, sibling).start()

        @pl.when((t == 20) | (t == 21))
        def _():
            unit(t + 4, across, 0, own).wait_recv()
            unit(t + 4, across, 2, sibling).start()

        @pl.when((t == 24) | (t == 25))
        def _():
            v = core * 2 + t - 24
            table(v, 1 - x, 1, own).wait_recv()
            table(v, 1 - x, 3, sibling).start()

        @pl.when((t >= SHIFT) & (t < n + SHIFT))
        def _():
            compute(t - SHIFT)
            cross(t - SHIFT).start()

        first = t - SHIFT - BASE - early

        @pl.when((first >= 0) & (first < n))
        def _():
            cross(first).wait()

        for way, buf, lag, to, back in ((0, rise, LAG * z, z + 1, z - 1), (1, fall, LAG * (3 - z), z - 1, z + 1)):
            c = t - SHIFT - BASE - lag

            @pl.when((c >= 0) & (c < n))
            def _():
                for b in ((1, 2, 3) if way == 0 else (0, 1, 2)):
                    beyond = (b > z) if way == 0 else (b < z)
                    at = b - 1 if way == 0 else b

                    @pl.when(beyond & (lag == 0))
                    def _():
                        if b == (1 if way == 0 else 2):
                            buf[c, at] = here(c, b)
                        else:
                            far[way, c, FAR[way][b]] = here(c, b).astype(bf16)

                    @pl.when(beyond & (lag > 0))
                    def _():
                        if b == (1 if way == 0 else 2):
                            hop(buf, way, c, b, back).wait_recv()
                            buf[c, at] = buf[c, at] + here(c, b)
                        else:
                            @pl.when(lag == LAG)
                            def _():
                                far_hop(way, c, b, back).wait_recv()
                                buf[c, at] = far[way, c, FAR[way][b]].astype(f32) + here(c, b)

                            @pl.when(lag > LAG)
                            def _():
                                hop(buf, way, c, b, back).wait_recv()
                                buf[c, at] = buf[c, at] + here(c, b)

                    def send(c, act):
                        if b == (1 if way == 0 else 2):
                            copy = hop(buf, way, c, b, to)
                            copy.start() if act else copy.wait_send()
                        else:
                            @pl.when(lag == 0)
                            def _():
                                copy = far_hop(way, c, b, to)
                                copy.start() if act else copy.wait_send()

                            @pl.when(lag > 0)
                            def _():
                                copy = hop(buf, way, c, b, to)
                                copy.start() if act else copy.wait_send()

                    @pl.when(beyond & (c >= QUEUE))
                    def _():
                        send(c - QUEUE, False)

                    @pl.when(beyond)
                    def _():
                        send(c, True)

        last = t - SHIFT - BASE - late

        @pl.when((last >= 0) & (last < n))
        def _():
            at = pl.ds(pl.multiple_of(z * STRIP, STRIP), STRIP)
            value = own_buf[last, at, :] + got[last, at, :].astype(f32)
            own_buf[last, 0:STRIP, :] = value

            @pl.when(z > 0)
            def _():
                hop(rise, 0, last, z, z - 1).wait_recv()
                own_buf[last, 0:STRIP, :] = own_buf[last, 0:STRIP, :] + rise[last, z - 1]

            @pl.when(z < 3)
            def _():
                hop(fall, 1, last, z, z + 1).wait_recv()
                own_buf[last, 0:STRIP, :] = own_buf[last, 0:STRIP, :] + fall[last, z]

            value = own_buf[last, 0:STRIP, :]
            square = value * value
            total = square[0:8, 0:128]
            for r in range(0, STRIP, 8):
                for k in range(0, CHUNK, 128):
                    if r or k:
                        total = total + square[r : r + 8, k : k + 128]
            tally[...] = tally[...] + total

        return carry

    lax.fori_loop(0, n + SHIFT + BASE + 3 * LAG, step, 0)
    summed = jnp.sum(tally[...])
    lane = lax.broadcasted_iota(jnp.int32, (8, 128), 1)
    quad_buf[own] = jnp.where(lane == 0, summed, jnp.where(lane == 1, num_ref[...], 0.0))

    def share(buf, k, where, at):
        return pltpu.make_async_remote_copy(
            src_ref=buf.at[at], dst_ref=buf.at[at], send_sem=s_send.at[k], recv_sem=s_recv.at[k],
            device_id=where, device_id_type=MESH,
        )

    for d in range(1, 4):
        share(quad_buf, d, (dp, lax.rem(own + d, 4)), own).start()
    for out, base, low, high in (
        (r_attn, 3 * D, 0, 2), (r_mlp, FF, 2, 10), (r_mlp, 0, 10, 18), (r_attn, 0, 18, 24), (r_agg, 2 * D, 24, 26), (r_agg, 0, 26, 30),
    ):
        for c in range(low, high):
            out[:, base + (c - low) * CHUNK : base + (c - low + 1) * CHUNK] = own_buf[c, 0:STRIP, :]
    left, right = own_buf[30, 0:STRIP, :], own_buf[31, 0:STRIP, :]
    r_io[:, 0:WIDTH] = left[:, 0:WIDTH]
    r_io[:, WIDTH : 2 * WIDTH] = left[:, 256 : 256 + WIDTH]
    r_io[:, 2 * WIDTH : 2 * WIDTH + VARS] = left[:, WIDTH : WIDTH + VARS]
    r_io[:, 2 * WIDTH + VARS : 2 * WIDTH + VARS + SPAN] = right[:, 0:SPAN]
    r_io[:, 2 * WIDTH + VARS + SPAN :] = jnp.zeros((STRIP, r_io.shape[1] - 2 * WIDTH - VARS - SPAN), f32)
    r_small[...] = right[:, 256:384].T[:16]
    for d in range(1, 4):
        share(quad_buf, d, (dp, own), lax.rem(own + 4 - d, 4)).wait_recv()
    line_buf[dp] = (quad_buf[0] + quad_buf[1]) + (quad_buf[2] + quad_buf[3])
    for d in range(1, 8):
        share(line_buf, 3 + d, (lax.rem(dp + d, 8), own), dp).start()
    for d in range(1, 8):
        share(line_buf, 3 + d, (dp, own), lax.rem(dp + 8 - d, 8)).wait_recv()
    stat = line_buf[0]
    for d in range(1, 8):
        stat = stat + line_buf[d]
    stat_ref[...] = stat
    for d in range(1, 4):
        share(quad_buf, d, (dp, own), own).wait_send()
    for d in range(1, 8):
        share(line_buf, 3 + d, (dp, own), dp).wait_send()
    for d in range(1, 4):
        for k in range(7):
            for half in range(2):
                feat_copy(k, d, half, own).wait_send()
        pred_copy(d, own, own).wait_send()
        narrow_copy(d, own, own).wait_send()
    for w in range(2):
        table_raw((1 - core) * 2 + w, own).wait_send()
        for slot, who in ((1, x), (2, x), (3, 1 - x)):
            table(core * 2 + w, who, slot, own).wait_send()
    relays = ((0, own), (1, own), (2, across))
    for i in range(3):
        for slot, who in relays:
            part(i, who, slot, own).wait_send()

    def finish(c, carry):
        for slot, who in relays:
            unit(c, who, slot, own).wait_send()
        return carry

    lax.fori_loop(10, 18, finish, 0)
    lax.fori_loop(24, 26, finish, 0)

    def drain(c, carry):
        for way, buf, inner, outer in ((0, rise, z > 0, z == 0), (1, fall, z < 3, z == 3)):
            for b in ((1, 2, 3) if way == 0 else (0, 1, 2)):
                beyond = (b > z) if way == 0 else (b < z)
                if b == (1 if way == 0 else 2):
                    pl.when(beyond)(lambda: hop(buf, way, c, b, z).wait_send())
                else:
                    pl.when(beyond & inner)(lambda: hop(buf, way, c, b, z).wait_send())
                    pl.when(beyond & outer)(lambda: far_hop(way, c, b, z).wait_send())
        return carry

    lax.fori_loop(n - QUEUE, n, drain, 0)


def gradient_blocks(operands, numbers):
    any_space = pl.BlockSpec(memory_space=pl.ANY)
    vmem = pl.BlockSpec(memory_space=pltpu.VMEM)
    n = N_ALL
    dma = pltpu.SemaphoreType.DMA
    widths = (3 * D, 4 * D, 2 * FF, 944)
    return pl.pallas_call(
        gradient_kernel,
        out_shape=[jax.ShapeDtypeStruct((STRIP, w), f32) for w in widths]
        + [jax.ShapeDtypeStruct((16, STRIP), f32), jax.ShapeDtypeStruct((8, 128), f32)],
        in_specs=[any_space] * 17 + [vmem],
        out_specs=[vmem] * 6,
        scratch_shapes=[
            pltpu.VMEM((7, 2, 4, STRIP, 512), bf16),
            pltpu.VMEM((N_STD, 512, CHUNK), bf16),
            pltpu.VMEM((2, 4, 256, CHUNK), bf16),
            pltpu.VMEM((2, 4, 256, CHUNK), bf16),
            pltpu.VMEM((512, 256), bf16),
            pltpu.VMEM((512, 256), bf16),
            pltpu.VMEM((4, 16, D), f32),
            pltpu.VMEM((2, 4, STRIP, 256), bf16),
            pltpu.VMEM((2, 4, STRIP, 2 * D), bf16),
            pltpu.VMEM((256, 256), f32),
            pltpu.VMEM((n, 4 * STRIP, CHUNK), f32),
            pltpu.VMEM((n, 4 * STRIP, CHUNK), bf16),
            pltpu.VMEM((n, 4 * STRIP, CHUNK), bf16),
            pltpu.VMEM((n, 3, STRIP, CHUNK), f32),
            pltpu.VMEM((n, 3, STRIP, CHUNK), f32),
            pltpu.VMEM((2, n, 2, STRIP, CHUNK), bf16),
            pltpu.VMEM((8, 128), f32),
            pltpu.VMEM((4, 8, 128), f32),
            pltpu.VMEM((8, 8, 128), f32),
            dma((56,)),
            dma((7, 4, 2)),
            dma((7, 4, 2)),
            dma((N_STD, 3)),
            dma((N_STD, 4)),
            dma((3, 3)),
            dma((3, 4)),
            dma((4, 4)),
            dma((4, 3)),
            dma((4,)),
            dma((4,)),
            dma((4,)),
            dma((4,)),
            dma((n,)),
            dma((n,)),
            dma((2, n, 5)),
            dma((2, n, 5)),
            dma((11,)),
            dma((11,)),
        ],
        compiler_params=pltpu.CompilerParams(
            collective_id=1, has_side_effects=True, vmem_limit_bytes=62 * 2**20
        ),
        name="gradient_blocks",
    )(*operands, numbers)


def ag(part):
    return lax.all_gather(part, "fsdp", axis=0, tiled=True)


def make_local(n_dp, n_f):
    fast = n_dp == 8 and n_f == 4

    def local(
        pixels, targets, valid_mask, lat_weight, segment_ids, present_vars, lead_index, step_count,
        w_agg, w_attn, w_mlp, w_io, w_small,
        m_agg, m_attn, m_mlp, m_io, m_small,
        v_agg, v_attn, v_mlp, v_io, v_small,
    ):
        masters = (w_agg, w_attn, w_mlp, w_io, w_small)
        firsts = (m_agg, m_attn, m_mlp, m_io, m_small)
        seconds = (v_agg, v_attn, v_mlp, v_io, v_small)
        rows = pixels.shape[1]
        row_len = segment_ids.shape[1]
        strip = w_agg.shape[0]
        own = lax.axis_index("fsdp")
        heads_here = HEADS // n_f
        wide = heads_here * HEAD_DIM

        seg = segment_ids[0]
        below = jnp.sum((seg[None, :] < seg[:, None]).astype(jnp.int32), axis=1)
        pos = jnp.arange(row_len, dtype=jnp.int32) - below
        onehot_all = (pos[:, None] == jnp.arange(SPAN, dtype=jnp.int32)[None, :]).astype(bf16)
        onehot = lax.dynamic_slice_in_dim(onehot_all, own * rows, rows)
        lead = (lead_index[0].astype(f32) + 1.0) / LEAD_STEPS
        pixel_rows = pixels[0]
        target = targets[0].astype(f32)
        present = present_vars[0]
        spread = (jnp.arange(MIX) // PIX)[None, :] == jnp.arange(VARS)[:, None]
        embed_col = (jnp.arange(MIX) - WIDTH)[None, :] == jnp.arange(VARS)[:, None]
        in_pixels = (jnp.arange(MIX) < WIDTH)[None, :]
        expand = jnp.where(in_pixels, spread, embed_col).astype(bf16)
        present_cols = jnp.repeat(present.astype(f32), PIX)
        pixel_weight = lat_weight[0][:, None] * valid_mask[0].astype(f32) * present_cols[None, :]
        weight_sum = jnp.sum(pixel_weight)

        emb = 2 * WIDTH + VARS
        if fast:
            mlp = lax.all_gather(w_mlp.astype(bf16), ("dp", "fsdp"), axis=0, tiled=True)
            head, attn, small, stat = gather_weights(
                w_io, w_small, w_agg, w_attn, jnp.full((8, 128), weight_sum, f32)
            )
            total = stat[0, 0]
        else:

            def blank(width):
                return jnp.zeros((strip, width), bf16)

            io_low = w_io.astype(bf16)
            pack = jnp.concatenate(
                [
                    io_low[:, :WIDTH],
                    io_low[:, 2 * WIDTH : emb],
                    blank(MIX - WIDTH - VARS),
                    io_low[:, WIDTH : 2 * WIDTH],
                    blank(256 - WIDTH),
                    io_low[:, emb : emb + SPAN],
                    w_small.astype(bf16),
                    blank(128 - w_small.shape[1]),
                    w_agg.astype(bf16),
                ],
                axis=1,
            )
            head = lax.all_gather(pack, ("dp", "fsdp"), axis=0, tiled=True)
            attn = lax.all_gather(w_attn.astype(bf16), ("dp", "fsdp"), axis=0, tiled=True)
            mlp = lax.all_gather(w_mlp.astype(bf16), ("dp", "fsdp"), axis=0, tiled=True)
            total = lax.psum(weight_sum, ("dp", "fsdp"))
        w240 = head[:, :MIX]
        w_pred = head[:, 256 : 256 + WIDTH]
        w_pos = head[:, 512 : 512 + SPAN]
        if not fast:
            small = head[:, 768:777].astype(f32).T
        agg_kv = head[:, HEAD : HEAD + 2 * D]
        agg_out = head[:, HEAD + 2 * D :]
        w_qkv = attn[:, : 3 * D]
        w_out = attn[:, 3 * D :]
        w_up = mlp[:, :FF]
        w_down = mlp[:, FF:]

        pix_t = jnp.concatenate(
            [pixel_rows.T, jnp.ones((VARS, rows), bf16), jnp.zeros((MIX - WIDTH - VARS, rows), bf16)], axis=0
        )
        table = t_mm(w240, agg_kv)
        table_k = table[:, :D].reshape(MIX, HEADS, HEAD_DIM)
        table_v = table[:, D:].reshape(MIX, HEADS, HEAD_DIM)
        query = small[0].reshape(HEADS, HEAD_DIM)
        folded = jnp.sum(table_k * query[None], axis=2)
        block = folded.T[:, None, :] * expand.astype(f32)[None]
        score = exact("xc,cl->xl", block.reshape(HEADS * VARS, MIX), pix_t.astype(f32))
        score = score.reshape(HEADS, VARS, rows) * HEAD_DIM ** (-0.5)
        score = jnp.where(present[None, :, None] > 0, score, -1000000000.0)
        top = jnp.max(score, axis=1, keepdims=True)
        power = jnp.exp(score - top)
        soft = power / jnp.sum(power, axis=1, keepdims=True)
        share = soft.astype(bf16)
        pix_f = pix_t.astype(f32)
        lifted_share = jnp.einsum("vc,hvl->hcl", expand, share, preferred_element_type=f32) * pix_f[None]
        mixed_a = exact("che,hcl->hel", table_v, lifted_share).reshape(D, rows).T.astype(bf16)
        lead_embed = lead * small[7] + small[8]
        h0 = mm(mixed_a, agg_out) + mm_t(onehot, w_pos) + lead_embed[None]
        norm0, unit0, scale0 = norm_forward(h0, small[1], small[2])
        qkv = mm(norm0, w_qkv).astype(bf16)
        if fast:
            seg_col = jnp.broadcast_to(seg[:, None], (row_len, 128))
            seg_row = jnp.broadcast_to(seg[None, :], (8, row_len))
            mixed, mixed_t, parts = attend(qkv, seg_col, seg_row)
        else:
            part = qkv.reshape(rows, 3, n_f, wide)
            part = lax.all_to_all(part, "fsdp", split_axis=2, concat_axis=0, tiled=True)
            part = part.reshape(row_len, 3, heads_here, HEAD_DIM)
            q, k, v = (part[:, i].transpose(1, 0, 2) for i in range(3))
            att_score = jnp.einsum("hqe,hke->hqk", q, k, preferred_element_type=f32) * HEAD_DIM ** (-0.5)
            same = seg[:, None] == seg[None, :]
            att_score = jnp.where(same[None], att_score, -1000000000.0)
            att_top = jnp.max(att_score, axis=-1, keepdims=True)
            att_power = jnp.exp(att_score - att_top)
            att_soft = att_power / jnp.sum(att_power, axis=-1, keepdims=True)
            att = att_soft.astype(bf16)
            mixed_h = jnp.einsum("hqk,hke->qhe", att, v, preferred_element_type=f32)
            mixed_h = mixed_h.reshape(row_len, wide).astype(bf16)
            mixed_all = lax.all_gather(mixed_h, "fsdp", axis=1, tiled=True)
            mixed = lax.dynamic_slice_in_dim(mixed_all, own * rows, rows, axis=0)
        h1 = h0 + mm(mixed, w_out)
        norm1, unit1, scale1 = norm_forward(h1, small[3], small[4])
        up = mm(norm1, w_up)
        gate = 0.5 * (1.0 + lax.erf(up * (2.0**-0.5)))
        lifted = (up * gate).astype(bf16)
        lifted_all = ag(lifted)
        h2 = h1 + mm_t(lifted, w_down)
        norm2, unit2, scale2 = norm_forward(h2, small[5], small[6])
        predicted = mm(norm2, w_pred) * D ** (-0.5)
        error = predicted - target
        weighted = pixel_weight * error
        numerator = jnp.sum(weighted * error)

        d_pred = (weighted * (2.0 * D ** (-0.5) / total)).astype(bf16)
        d_norm2 = mm_t(d_pred, w_pred)
        d_h2, d_gain2, d_off2 = norm_backward(d_norm2, unit2, scale2, small[5])
        d_out = d_h2.astype(bf16)
        slope = gate + up * jnp.exp(-0.5 * up * up) * 0.3989422804014327
        d_up = (mm(d_out, w_down) * slope).astype(bf16)
        d_norm1 = mm_t(d_up, w_up)
        d_in, d_gain1, d_off1 = norm_backward(d_norm1, unit1, scale1, small[3])
        d_h1 = d_h2 + d_in
        if fast:
            d_qkv, d_parts, d_proj_all = attend_back(d_h1.astype(bf16), attn, parts, seg_col, seg_row)
        else:
            d_proj_all = ag(d_h1.astype(bf16))
            w_out_own = lax.dynamic_slice_in_dim(w_out, own * wide, wide, axis=0)
            d_mixed = mm_t(d_proj_all, w_out_own).astype(bf16).reshape(row_len, heads_here, HEAD_DIM).transpose(1, 0, 2)
            d_att = jnp.einsum("hqe,hke->hqk", d_mixed, v, preferred_element_type=f32)
            d_v = jnp.einsum("hqk,hqe->khe", att, d_mixed, preferred_element_type=f32)
            lean = jnp.sum(att_soft * d_att, axis=-1, keepdims=True)
            d_score = (att_soft * (d_att - lean) * HEAD_DIM ** (-0.5)).astype(bf16)
            d_q = jnp.einsum("hqk,hke->qhe", d_score, k, preferred_element_type=f32)
            d_k = jnp.einsum("hqk,hqe->khe", d_score, q, preferred_element_type=f32)
            d_part = jnp.stack([d_q, d_k, d_v], axis=1).astype(bf16).reshape(row_len, 3, 1, wide)
            d_qkv_all = lax.all_gather(d_part, "fsdp", axis=2, tiled=True).reshape(row_len, 3 * D)
            d_qkv = lax.dynamic_slice_in_dim(d_qkv_all, own * rows, rows, axis=0)
        d_norm0 = mm_t(d_qkv, w_qkv)
        d_in, d_gain0, d_off0 = norm_backward(d_norm0, unit0, scale0, small[1])
        d_h0 = d_h1 + d_in
        d_agg = d_h0.astype(bf16)
        d_mixed_a = mm_t(agg_out, d_agg).astype(bf16).reshape(HEADS, HEAD_DIM, rows)
        pulled = exact("che,hel->hcl", table_v, d_mixed_a.astype(f32)) * pix_f[None]
        d_share = exact("vc,hcl->hvl", expand.astype(f32), pulled)
        lean_a = jnp.sum(soft * d_share, axis=1, keepdims=True)
        d_score_a = (soft * (d_share - lean_a) * HEAD_DIM ** (-0.5)).astype(bf16)
        spread_score = jnp.einsum("vc,hvl->hcl", expand, d_score_a, preferred_element_type=f32)
        d_folded = jnp.sum(spread_score * pix_f[None], axis=2)
        d_table_v = exact("hcl,hel->che", lifted_share, d_mixed_a.astype(f32)).reshape(MIX, D)
        d_table_k = (d_folded.T[:, :, None] * query[None]).reshape(MIX, D)
        d_query = jnp.sum(d_folded.T[:, :, None] * table_k, axis=0).reshape(D)
        d_bias = jnp.sum(d_h0, axis=0)
        narrow = jnp.stack(
            [d_query, d_gain0, d_off0, d_gain1, d_off1, d_gain2, d_off2, lead * d_bias, d_bias]
            + [jnp.zeros((D,), f32)] * 7
        )
        d_table = jnp.concatenate([d_table_k, d_table_v], axis=1)
        if fast:

            def sorted_rows(array):
                return array.reshape(4, 2, n_f, strip, array.shape[1])

            lane = lax.broadcasted_iota(jnp.int32, (8, 128), 1)
            r_agg, r_attn, r_mlp, r_io, r_small, stat = gradient_blocks(
                [sorted_rows(part.T) for part in (norm1, d_out, norm0)]
                + [mixed_t.reshape(2, n_f, strip, row_len)]
                + [sorted_rows(part.T) for part in (mixed_a, norm2, d_agg)]
                + [d_proj_all, d_parts, d_up, lifted_all, d_agg, jnp.pad(d_pred, ((0, 0), (0, 256 - WIDTH)))]
                + [onehot_all, d_table.astype(bf16), narrow, sorted_rows(head)],
                jnp.where(lane == 1, numerator, 0.0),
            )
            r_small = r_small[:9].T
            squares, numerator = stat[0, 0], stat[0, 1]
        else:
            d_table, narrow = lax.psum((d_table, narrow), "fsdp")
            source = jnp.arange(D)
            pick = (source // strip) % n_f == own
            place = (source // (strip * n_f)) * strip + source % strip
            choose = (pick[:, None] & (place[:, None] == jnp.arange(n_dp * strip)[None, :])).astype(bf16)

            def mine(array):
                whole = array.reshape(n_dp, n_f, strip, array.shape[1])
                return lax.dynamic_index_in_dim(whole, own, 1, False).reshape(n_dp * strip, array.shape[1])

            def weight_grad(features, grads):
                return t_mm(mm(features, choose).astype(bf16), grads)

            def gap(width):
                return jnp.zeros((n_dp * strip, width), f32)

            d_agg_all = ag(d_agg)
            g_kv = exact("dc,cx->dx", mine(w240).astype(f32), d_table)
            g_240 = exact("dx,cx->dc", mine(agg_kv).astype(f32), d_table)
            groups = (
                (g_kv, weight_grad(ag(mixed_a), d_agg_all)),
                (weight_grad(ag(norm0), d_qkv_all), weight_grad(mixed_all, d_proj_all)),
                (weight_grad(ag(norm1), ag(d_up)), weight_grad(ag(d_out), lifted_all)),
                (
                    g_240, weight_grad(ag(norm2), ag(d_pred)), gap(256 - WIDTH),
                    weight_grad(d_agg_all, onehot_all), mine(narrow.T)[:, :9], gap(256 - 9),
                ),
            )
            r_agg, r_attn, r_mlp, r_misc = (
                lax.psum_scatter(jnp.concatenate(g, axis=1), "dp", scatter_dimension=0, tiled=True) for g in groups
            )
            local_squares = sum(jnp.sum(piece * piece) for piece in (r_agg, r_attn, r_mlp, r_misc))
            squares, numerator = lax.psum((local_squares, numerator), ("dp", "fsdp"))
            r_io = jnp.concatenate(
                [
                    r_misc[:, :WIDTH], r_misc[:, 256 : 256 + WIDTH], r_misc[:, WIDTH : WIDTH + VARS],
                    r_misc[:, 512 : 512 + SPAN], jnp.zeros((strip, w_io.shape[1] - emb - SPAN), f32),
                ],
                axis=1,
            )
            r_small = r_misc[:, 768:777]
        reduced = (r_agg, r_attn, r_mlp, r_io, r_small)
        grad_norm = jnp.sqrt(squares)
        factor = jnp.minimum(1.0, clip_limit / grad_norm)
        loss = numerator / total
        step_value = step_count[0].astype(f32)
        results = [
            adamw(masters[i], reduced[i] * factor, firsts[i], seconds[i], step_value, learn_rates[i]) for i in range(5)
        ]
        return (loss, grad_norm) + tuple(results[i][j] for j in range(4) for i in range(5))

    return local


def solution(mesh):
    flat = P(("dp", "fsdp"), None)
    tokens = P("dp", "fsdp", None)
    return jax.shard_map(
        make_local(mesh.shape["dp"], mesh.shape["fsdp"]),
        mesh=mesh,
        in_specs=(tokens, tokens, tokens, P("dp", "fsdp"), P("dp", None), P("dp", None), P("dp"), P()) + (flat,) * 15,
        out_specs=(P(), P()) + (flat,) * 20,
        check_vma=False,
    )
```

```python
import functools

import jax
import jax.numpy as jnp
from jax import lax
from jax.experimental import pallas as pl
from jax.experimental.pallas import tpu as pltpu
from jax.sharding import PartitionSpec as P

D = 1024
HEADS = 16
HEAD_DIM = 64
FF = 4096
VARS = 48
PIX = 4
LEAD_STEPS = 8
WIDTH = VARS * PIX
SPAN = 256
MIX = 256
HEAD = 896

norm_eps = 1e-05
clip_limit = 1.0
decay_rate = 0.05
adam_eps = 1e-08
learn_rates = (0.03, 0.03, 0.03, 0.2, 0.3)
f32 = jnp.float32
bf16 = jnp.bfloat16
highest = lax.Precision.HIGHEST
MESH = pl.DeviceIdType.MESH
STRIP = 32
CHUNK = 512
LAG = 2
QUEUE = 2


def dot(left, right, dims):
    return lax.dot_general(left, right, (dims, ((), ())), preferred_element_type=f32)


def mm(left, right):
    return dot(left, right, ((1,), (0,)))


def mm_t(left, right):
    return dot(left, right, ((1,), (1,)))


def t_mm(left, right):
    return dot(left, right, ((0,), (0,)))


def exact(eq, left, right):
    return jnp.einsum(eq, left, right, precision=highest, preferred_element_type=f32)


def norm_forward(values, gain, offset):
    average = jnp.mean(values, axis=-1, keepdims=True)
    centred = values - average
    scale = lax.rsqrt(jnp.mean(centred * centred, axis=-1, keepdims=True) + norm_eps)
    unit = centred * scale
    return (unit * gain[None] + offset[None]).astype(bf16), unit, scale


def norm_backward(grad, unit, scale, gain):
    inner = grad * gain[None]
    mean_inner = jnp.mean(inner, axis=-1, keepdims=True)
    mean_product = jnp.mean(inner * unit, axis=-1, keepdims=True)
    back = scale * (inner - mean_inner - unit * mean_product)
    return back, jnp.sum(grad * unit, axis=0), jnp.sum(grad, axis=0)


def adamw(weight, grad, moment, second, step_value, learn_rate):
    moment = 0.5 * moment + 0.5 * grad
    second = 0.5 * second + 0.5 * grad * grad
    correct = 1.0 - jnp.power(f32(0.5), step_value)
    update = moment / correct / (jnp.sqrt(second / correct) + adam_eps) + decay_rate * weight
    fresh = weight - learn_rate * update
    return (fresh, fresh.astype(bf16), moment, second)


PIECES = (
    (0, 1408, 1280, "yzx"), (1, 0, 1536, "zxy"), (0, 2688, 1280, "yzx"), (1, 1536, 1536, "zxy"), (0, 0, 1408, "zxy"),
)


def gather_kernel(*refs):
    w_io, w_small, w_agg, w_attn, num_ref = refs[:5]
    wholes, small_ref, stat_ref = refs[5:7], refs[7], refs[8]
    quad_buf, line_buf, small_buf, pack, attn_low, own_sem, s_send, s_recv, sends, arrive, pass_on = refs[9:]
    shards = (pack, attn_low)
    dp, own = lax.axis_index("dp"), lax.axis_index("fsdp")
    z, y, x, core = dp // 2, dp % 2, own // 2, own % 2
    sibling = x * 2 + 1 - core
    barrier = pltpu.get_barrier_semaphore()
    for d in range(1, 8):
        pl.semaphore_signal(barrier, inc=1, device_id=(lax.rem(dp + d, 8), own), device_id_type=MESH)
    for d in range(1, 4):
        pl.semaphore_signal(barrier, inc=1, device_id=(dp, lax.rem(own + d, 4)), device_id_type=MESH)
    emb = 2 * WIDTH + VARS

    def gap(width):
        return jnp.zeros((STRIP, width), f32)

    pack[:, :HEAD] = jnp.concatenate(
        [
            w_io[:, :WIDTH], w_io[:, 2 * WIDTH : emb], gap(MIX - WIDTH - VARS), w_io[:, WIDTH : 2 * WIDTH],
            gap(256 - WIDTH), w_io[:, emb : emb + SPAN], w_small[...], gap(128 - w_small.shape[1]),
        ],
        axis=1,
    ).astype(bf16)
    pack[:, HEAD:] = w_agg[...].astype(bf16)
    attn_low[...] = w_attn[:, : 3 * D].astype(bf16)
    pl.semaphore_wait(barrier, 10)

    def view(p, ident, plane):
        a, start, width, order = PIECES[p]
        row = pl.multiple_of(((ident // 2) * 4 + (ident % 2) * 2 + plane) * STRIP, STRIP)
        return wholes[a].at[pl.ds(row, STRIP), pl.ds(start, width)]

    def copy(p, ident, slot, to, mine=False):
        a, start, width, order = PIECES[p]
        src = shards[a].at[:, pl.ds(start, width)] if mine else view(p, ident, core)
        sem = pass_on if slot == 4 else arrive
        return pltpu.make_async_remote_copy(
            src_ref=src, dst_ref=view(p, ident, core), send_sem=sends.at[p, ident, slot], recv_sem=sem.at[p, ident],
            device_id=to, device_id_type=MESH,
        )

    def arrival(p, ident, plane, sem):
        return pltpu.make_async_copy(view(p, ident, plane), view(p, ident, plane), sem.at[p, ident])

    def targets(p, rx, ry, rz):
        order = PIECES[p][3]
        moved = {"x": rx != 0, "y": ry != 0, "z": rz is not None}
        stage = max([k for k in range(3) if moved[order[k]]], default=-1)
        found = []
        if stage >= 0 and order[stage] == "z":
            found.append((0, (rz < 0) & (z < 3), ((dp + 2) % 8, own)))
            found.append((1, (rz > 0) & (z > 0), ((dp + 6) % 8, own)))
        for k in range(stage + 1, 3):
            if order[k] == "z":
                found.append((0, z < 3, ((dp + 2) % 8, own)))
                found.append((1, z > 0, ((dp + 6) % 8, own)))
            elif order[k] == "x":
                found.append((2, None, (dp, (1 - x) * 2 + core)))
            else:
                found.append((3, None, (z * 2 + 1 - y, own)))
        found.append((4, None, (dp, sibling)))
        return found

    def source(rx, ry, rz):
        sz = z if rz is None else z + rz
        sy = 1 - y if ry else y
        sx = 1 - x if rx else x
        return sz, (sz * 2 + sy) * 2 + sx

    def each(rx, ry, rz, act, mine=False):
        sz, ident = source(rx, ry, rz)

        def body():
            for p in range(len(PIECES)):
                if act == "send" and not mine:
                    arrival(p, ident, core, arrive).wait()
                for slot, when, to in targets(p, rx, ry, rz):
                    def go(slot=slot, to=to):
                        c = copy(p, ident, slot, to, mine)
                        c.start() if act == "send" else c.wait_send()

                    if when is None:
                        go()
                    else:
                        pl.when(when)(go)

        if rz is None:
            body()
        else:
            pl.when((sz >= 0) & (sz < 4))(body)

    def over_z(pairs, act):
        def step(t, carry):
            rz = ((t + 1) // 2) * (1 - 2 * (t % 2))
            for rx, ry in pairs:
                each(rx, ry, rz, act)
            return carry

        lax.fori_loop(1, 7, step, 0)

    def sweep(act):
        each(0, 0, None, act, mine=True)
        if act == "send":
            for a in range(2):
                row = pl.multiple_of((dp * 4 + own) * STRIP, STRIP)
                pltpu.make_async_copy(shards[a], wholes[a].at[pl.ds(row, STRIP), :], own_sem.at[a]).start()
            scalars()
        each(1, 0, None, act)
        each(0, 1, None, act)
        over_z([(0, 0)], act)
        each(1, 1, None, act)
        over_z([(1, 0), (0, 1)], act)
        over_z([(1, 1)], act)

    def share(buf, k, where, at):
        return pltpu.make_async_remote_copy(
            src_ref=buf.at[at], dst_ref=buf.at[at], send_sem=s_send.at[k], recv_sem=s_recv.at[k],
            device_id=where, device_id_type=MESH,
        )

    def scalars():
        quad_buf[own] = num_ref[...]
        for d in range(1, 4):
            share(quad_buf, d, (dp, lax.rem(own + d, 4)), own).start()

    sweep("send")
    for d in range(1, 4):
        share(quad_buf, d, (dp, own), lax.rem(own + 4 - d, 4)).wait_recv()
    line_buf[dp] = (quad_buf[0] + quad_buf[1]) + (quad_buf[2] + quad_buf[3])
    for d in range(1, 8):
        share(line_buf, 3 + d, (lax.rem(dp + d, 8), own), dp).start()

    def closing(ident, carry):
        for p in range(len(PIECES)):
            arrival(p, ident, 1 - core, pass_on).wait()
        return carry

    lax.fori_loop(0, 16, closing, 0)
    for a in range(2):
        row = pl.multiple_of((dp * 4 + own) * STRIP, STRIP)
        pltpu.make_async_copy(shards[a], wholes[a].at[pl.ds(row, STRIP), :], own_sem.at[a]).wait()
    narrow = pltpu.make_async_copy(wholes[0].at[:, pl.ds(768, 128)], small_buf, own_sem.at[0])
    narrow.start()
    sweep("drain")
    narrow.wait()
    small_ref[...] = small_buf[...].astype(f32).T[:16]
    for d in range(1, 8):
        share(line_buf, 3 + d, (dp, own), lax.rem(dp + 8 - d, 8)).wait_recv()
    stat = line_buf[0]
    for d in range(1, 8):
        stat = stat + line_buf[d]
    stat_ref[...] = stat
    for d in range(1, 4):
        share(quad_buf, d, (dp, own), own).wait_send()
    for d in range(1, 8):
        share(line_buf, 3 + d, (dp, own), dp).wait_send()


def gather_weights(w_io, w_small, w_agg, w_attn, number):
    any_space = pl.BlockSpec(memory_space=pl.ANY)
    vmem = pl.BlockSpec(memory_space=pltpu.VMEM)
    n = len(PIECES)
    return pl.pallas_call(
        gather_kernel,
        out_shape=[jax.ShapeDtypeStruct((D, w), bf16) for w in (HEAD + 3 * D, 3 * D)]
        + [jax.ShapeDtypeStruct((16, D), f32), jax.ShapeDtypeStruct((8, 128), f32)],
        in_specs=[vmem] * 5,
        out_specs=[any_space] * 2 + [vmem] * 2,
        scratch_shapes=[
            pltpu.VMEM((4, 8, 128), f32),
            pltpu.VMEM((8, 8, 128), f32),
            pltpu.VMEM((D, 128), bf16),
            pltpu.VMEM((STRIP, HEAD + 3 * D), bf16),
            pltpu.VMEM((STRIP, 3 * D), bf16),
            pltpu.SemaphoreType.DMA((3,)),
            pltpu.SemaphoreType.DMA((11,)),
            pltpu.SemaphoreType.DMA((11,)),
            pltpu.SemaphoreType.DMA((n, 16, 5)),
            pltpu.SemaphoreType.DMA((n, 16)),
            pltpu.SemaphoreType.DMA((n, 16)),
        ],
        compiler_params=pltpu.CompilerParams(collective_id=0, has_side_effects=True),
        cost_estimate=pl.CostEstimate(flops=0, bytes_accessed=250_000_000, transcendentals=0),
        name="gather_weights",
    )(w_io, w_small, w_agg, w_attn, number)


def greet(dp, own):
    barrier = pltpu.get_barrier_semaphore()
    for d in range(1, 4):
        pl.semaphore_signal(barrier, inc=1, device_id=(dp, lax.rem(own + d, 4)), device_id_type=MESH)
    pl.semaphore_wait(barrier, 3)


def turned_softmax(parts, seg_col, seg_row, h):
    at = slice(h * HEAD_DIM, (h + 1) * HEAD_DIM)
    q, k, v = (parts[i, :, at] for i in range(3))
    score = lax.dot_general(k, q, (((1,), (1,)), ((), ())), preferred_element_type=f32) * HEAD_DIM ** (-0.5)
    score = jnp.where(seg_col[:, 0:1] == seg_row[0:1, :], score, -1000000000.0)
    power = jnp.exp(score - jnp.max(score, axis=0, keepdims=True))
    soft = power / jnp.sum(power, axis=0, keepdims=True)
    return q, k, v, soft, soft.astype(bf16)


def attend_kernel(qkv, seg_col, seg_row, norm0, mixed, mixed_t, parts_out, norm0_t, parts, turned, whole, gathered,
                  load_sem, in_send, in_recv, out_send, out_recv):
    dp, own = lax.axis_index("dp"), lax.axis_index("fsdp")
    greet(dp, own)
    row = pl.ds(pl.multiple_of(own * 128, 128), 128)

    def piece(i, to):
        return qkv.at[:, pl.ds(pl.multiple_of(i * D + to * 256, 256), 256)]

    def into(d, i):
        to = lax.rem(own + d, 4)
        return pltpu.make_async_remote_copy(
            src_ref=piece(i, to), dst_ref=parts.at[i, row, :], send_sem=in_send.at[d, i], recv_sem=in_recv.at[d, i],
            device_id=(dp, to), device_id_type=MESH,
        )

    for i in range(3):
        for d in (2, 1, 3):
            into(d, i).start()
    for i in range(3):
        pltpu.make_async_copy(piece(i, own), parts.at[i, row, :], load_sem.at[i]).start()
    norm0_t[...] = norm0[...].astype(f32).T.astype(bf16)
    for i in range(3):
        pltpu.make_async_copy(piece(i, own), parts.at[i, row, :], load_sem.at[i]).wait()
        for d in range(1, 4):
            into(d, i).wait_recv()
    for h in range(4):
        q, k, v, soft, share = turned_softmax(parts, seg_col, seg_row, h)
        turned[h * HEAD_DIM : (h + 1) * HEAD_DIM, :] = lax.dot_general(
            v, share, (((0,), (0,)), ((), ())), preferred_element_type=f32
        )
    whole[...] = turned[...].T.astype(bf16)
    column = pl.ds(pl.multiple_of(own * 256, 256), 256)

    def back(d):
        to = lax.rem(own + d, 4)
        return pltpu.make_async_remote_copy(
            src_ref=whole.at[pl.ds(pl.multiple_of(to * 128, 128), 128), :], dst_ref=gathered.at[:, column],
            send_sem=out_send.at[d], recv_sem=out_recv.at[d], device_id=(dp, to), device_id_type=MESH,
        )

    for d in (2, 1, 3):
        back(d).start()
    keep = pltpu.make_async_copy(whole.at[row, :], gathered.at[:, column], load_sem.at[3])
    keep.start()
    mixed_t[...] = turned[...].astype(bf16)
    parts_out[...] = parts[...]
    keep.wait()
    for d in range(1, 4):
        back(d).wait_recv()
    mixed[...] = gathered[...]
    for d in range(1, 4):
        back(d).wait_send()
        for i in range(3):
            into(d, i).wait_send()


def attend(qkv, seg_col, seg_row, norm0):
    vmem = pl.BlockSpec(memory_space=pltpu.VMEM)
    dma = pltpu.SemaphoreType.DMA
    return pl.pallas_call(
        attend_kernel,
        out_shape=[
            jax.ShapeDtypeStruct((128, D), bf16), jax.ShapeDtypeStruct((256, 512), bf16),
            jax.ShapeDtypeStruct((3, 512, 256), bf16), jax.ShapeDtypeStruct((D, 128), bf16),
        ],
        in_specs=[pl.BlockSpec(memory_space=pl.ANY), vmem, vmem, vmem],
        out_specs=[vmem] * 4,
        scratch_shapes=[
            pltpu.VMEM((3, 512, 256), bf16), pltpu.VMEM((256, 512), f32), pltpu.VMEM((512, 256), bf16),
            pltpu.VMEM((128, D), bf16), dma((4,)), dma((4, 3)), dma((4, 3)), dma((4,)), dma((4,)),
        ],
        compiler_params=pltpu.CompilerParams(collective_id=2, has_side_effects=True, vmem_limit_bytes=40 * 2**20),
        name="attend",
    )(qkv, seg_col, seg_row, norm0)


def attend_back_kernel(d_proj, rear, parts, seg_col, seg_row, norm1, d_out, norm2, d_own, d_parts_out, d_all_out,
                       norm1_t, out_t, norm2_t, every, proj, d_mixed,
                       d_parts, gathered, load_sem, up_send, up_recv, out_send, out_recv):
    dp, own = lax.axis_index("dp"), lax.axis_index("fsdp")
    x, core = own // 2, own % 2
    sibling, across, diagonal = x * 2 + 1 - core, (1 - x) * 2 + core, (1 - x) * 2 + 1 - core
    rows = pl.ds(pl.multiple_of(own * 256, 256), 256)
    fetch = pltpu.make_async_copy(rear.at[rows, pl.ds(0, D)], proj, load_sem.at[0])
    fetch.start()
    row = pl.ds(pl.multiple_of(own * 128, 128), 128)
    mine = pltpu.make_async_copy(d_proj, every.at[row, :], load_sem.at[1])
    mine.start()
    greet(dp, own)
    mine.wait()

    def up(i, who, slot, to):
        block = every.at[pl.ds(pl.multiple_of(who * 128, 128), 128), i * 512 : (i + 1) * 512]
        return pltpu.make_async_remote_copy(
            src_ref=block, dst_ref=block, send_sem=up_send.at[i, slot], recv_sem=up_recv.at[i, who],
            device_id=(dp, to), device_id_type=MESH,
        )

    for i in range(2):
        up(i, own, 0, across).start()
    for i in range(2):
        up(i, own, 1, sibling).start()
    for source, turned in ((norm1, norm1_t), (d_out, out_t), (norm2, norm2_t)):
        turned[...] = source[...].astype(f32).T.astype(bf16)
    for i in range(2):
        up(i, across, 0, own).wait_recv()
        up(i, across, 2, sibling).start()
    fetch.wait()
    for i in range(2):
        up(i, sibling, 1, own).wait_recv()
        up(i, diagonal, 2, own).wait_recv()
    d_mixed[...] = lax.dot_general(
        every[...], proj[...], (((1,), (1,)), ((), ())), preferred_element_type=f32
    ).astype(bf16)
    for h in range(4):
        at = slice(h * HEAD_DIM, (h + 1) * HEAD_DIM)
        q, k, v, soft, share = turned_softmax(parts, seg_col, seg_row, h)
        d_head = d_mixed[:, at]
        d_soft = lax.dot_general(v, d_head, (((1,), (1,)), ((), ())), preferred_element_type=f32)
        lean = jnp.sum(soft * d_soft, axis=0, keepdims=True)
        d_score = (soft * (d_soft - lean) * HEAD_DIM ** (-0.5)).astype(bf16)
        d_parts[2, :, at] = mm(share, d_head).astype(bf16)
        d_parts[1, :, at] = mm(d_score, q).astype(bf16)
        d_parts[0, :, at] = t_mm(d_score, k).astype(bf16)

    def back(d, i):
        to = lax.rem(own + d, 4)
        return pltpu.make_async_remote_copy(
            src_ref=d_parts.at[i, pl.ds(pl.multiple_of(to * 128, 128), 128), :],
            dst_ref=gathered.at[:, pl.ds(pl.multiple_of(i * D + own * 256, 256), 256)],
            send_sem=out_send.at[d, i], recv_sem=out_recv.at[d, i], device_id=(dp, to), device_id_type=MESH,
        )

    for i in range(3):
        for d in (2, 1, 3):
            back(d, i).start()
    keeps = [
        pltpu.make_async_copy(
            d_parts.at[i, row, :], gathered.at[:, pl.ds(pl.multiple_of(i * D + own * 256, 256), 256)], load_sem.at[2 + i]
        )
        for i in range(3)
    ]
    for keep in keeps:
        keep.start()
    d_parts_out[...] = d_parts[...]
    d_all_out[...] = every[...]
    for keep in keeps:
        keep.wait()
    for i in range(3):
        for d in range(1, 4):
            back(d, i).wait_recv()
    d_own[...] = gathered[...]
    for d in range(1, 4):
        for i in range(3):
            back(d, i).wait_send()
    for i in range(2):
        for slot, who in ((0, own), (1, own), (2, across)):
            up(i, who, slot, own).wait_send()


def attend_back(d_proj, rear, parts, seg_col, seg_row, *features):
    vmem = pl.BlockSpec(memory_space=pltpu.VMEM)
    any_space = pl.BlockSpec(memory_space=pl.ANY)
    dma = pltpu.SemaphoreType.DMA
    return pl.pallas_call(
        attend_back_kernel,
        out_shape=[
            jax.ShapeDtypeStruct((128, 3 * D), bf16), jax.ShapeDtypeStruct((3, 512, 256), bf16),
            jax.ShapeDtypeStruct((512, D), bf16),
        ]
        + [jax.ShapeDtypeStruct((D, 128), bf16)] * 3,
        in_specs=[any_space, any_space] + [vmem] * 6,
        out_specs=[vmem] * 6,
        scratch_shapes=[
            pltpu.VMEM((512, D), bf16), pltpu.VMEM((256, D), bf16), pltpu.VMEM((512, 256), bf16),
            pltpu.VMEM((3, 512, 256), bf16), pltpu.VMEM((128, 3 * D), bf16),
            dma((5,)), dma((2, 3)), dma((2, 4)), dma((4, 3)), dma((4, 3)),
        ],
        compiler_params=pltpu.CompilerParams(collective_id=3, has_side_effects=True, vmem_limit_bytes=40 * 2**20),
        name="attend_back",
    )(d_proj, rear, parts, seg_col, seg_row, *features)


SEGMENTS = ((0, 2, 3), (2, 10, 1), (10, 18, 0), (18, 24, 2), (24, 26, 4))
N_STD, N_ALL, SHIFT, BASE = 26, 32, 1, 2


FAR = ({2: 0, 3: 1}, {0: 0, 1: 1})


def preds_at(preds, who):
    return preds.at[pl.ds(pl.multiple_of(who * 128, 128), 128), :]


def gradient_kernel(*refs):
    (norm1_t, out_t, norm0_t, mixed_t, mixa_t, norm2_t, agg_t,
     d_proj, d_parts, d_up, lifted, d_agg, d_pred, onehot, d_table, narrow, head, num_ref) = refs[:18]
    r_agg, r_attn, r_mlp, r_io, r_small, stat_ref = refs[18:24]
    (feats, ys, tabs, pairs, preds, hots, narrows, w240, wkv, acc240, own_buf, give_buf, got, rise, fall, far, tally,
     quad_buf, line_buf, load_sem, feat_send, feat_recv, y_xsend, y_xrecv, part_send, part_recv, tab_send, tab_recv, pred_send, pred_recv,
     nar_send, nar_recv, y_send, y_recv, z_send, z_recv, s_send, s_recv) = refs[24:]
    dp, own = lax.axis_index("dp"), lax.axis_index("fsdp")
    z, y, x, core = dp // 2, dp % 2, own // 2, own % 2
    sibling, across, diagonal = x * 2 + 1 - core, (1 - x) * 2 + core, (1 - x) * 2 + 1 - core
    over = z * 2 + 1 - y
    n = N_ALL
    row = pl.ds(pl.multiple_of(own * 128, 128), 128)
    sent_feats = {0: norm1_t, 1: out_t, 2: norm0_t, 4: mixa_t, 5: norm2_t, 6: agg_t}

    def remote(src, dst, send, recv, to):
        return pltpu.make_async_remote_copy(
            src_ref=src, dst_ref=dst, send_sem=send, recv_sem=recv, device_id=(dp, to), device_id_type=MESH
        )

    def feat_copy(k, d, half, to):
        side = y if half == 0 else 1 - y
        if k == 3:
            src, dst = mixed_t.at[side, to], feats.at[3, half, own]
        else:
            src, dst = sent_feats[k].at[:, side, to], feats.at[k, half, :, :, row]
        return remote(src, dst, feat_send.at[k, d, half], feat_recv.at[k, d, half], to)

    def feat_start(k):
        for d in (2, 1, 3):
            for half in range(2):
                feat_copy(k, d, half, lax.rem(own + d, 4)).start()

    def unit_block(c, who):
        return ys.at[c, pl.ds(pl.multiple_of(who * 128, 128), 128), :]

    def unit(c, who, slot, to):
        return remote(unit_block(c, who), unit_block(c, who), y_xsend.at[c, slot], y_xrecv.at[c, who], to)

    def part_block(i, who):
        return ys.at[18 + i * 2 + who // 2, :, pl.ds(pl.multiple_of((who % 2) * 256, 256), 256)]

    def part(i, who, slot, to):
        return remote(part_block(i, who), part_block(i, who), part_send.at[i, slot], part_recv.at[i, who], to)

    def table_raw(v, to):
        return remote(tabs.at[0, v], tabs.at[1, v], tab_send.at[v, 0], tab_recv.at[v, 0], to)

    def table(v, who, slot, to):
        return remote(pairs.at[who, v], pairs.at[who, v], tab_send.at[v, slot], tab_recv.at[v, 1 + who], to)

    def pred_copy(d, who, to):
        return remote(preds_at(preds, who), preds_at(preds, who), pred_send.at[d], pred_recv.at[d], to)

    def narrow_copy(d, who, to):
        return remote(narrows.at[who], narrows.at[who], nar_send.at[d], nar_recv.at[d], to)

    loads = {}

    def load(name, src, dst):
        copy = pltpu.make_async_copy(src, dst, load_sem.at[len(loads)])
        copy.start()
        loads[name] = copy

    def load_feat(k):
        for half in range(2):
            side = y if half == 0 else 1 - y
            if k == 3:
                load(("f", k, half), mixed_t.at[side, own], feats.at[3, half, own])
            else:
                load(("f", k, half), sent_feats[k].at[:, side, own], feats.at[k, half, :, :, row])

    def loaded(*names):
        for name in names:
            loads[name].wait()

    for c in range(2):
        load(("j", c), d_proj.at[:, pl.ds(c * CHUNK, CHUNK)], ys.at[c])
    load_feat(3)
    load_feat(1)
    for c in range(8):
        load(("u", 10 + c), d_up.at[:, pl.ds(c * CHUNK, CHUNK)], unit_block(10 + c, own))
    for c in range(8):
        load(("l", c), lifted.at[:, pl.ds(c * CHUNK, CHUNK)], ys.at[2 + c])
    load_feat(0)
    for i in range(3):
        load(("p", i), d_parts.at[i], part_block(i, own))
    load_feat(2)
    for c in range(2):
        load(("u", 24 + c), d_agg.at[:, pl.ds(c * CHUNK, CHUNK)], unit_block(24 + c, own))
    load_feat(4)
    for v in range(4):
        load(("t", v), d_table.at[pl.ds(v * CHUNK, CHUNK), :], tabs.at[0, v])
    load("pred", d_pred, preds_at(preds, own))
    load("narrow", narrow, narrows.at[own])
    for half in range(2):
        side = y if half == 0 else 1 - y
        load(("w", half), head.at[:, side, own, :, pl.ds(0, 256)], w240.at[half])
        load(("k", half), head.at[:, side, own, :, pl.ds(HEAD, 2 * D)], wkv.at[half])
    load_feat(5)
    load_feat(6)
    load("hot", onehot, hots)
    barrier = pltpu.get_barrier_semaphore()
    for d in range(1, 8):
        pl.semaphore_signal(barrier, inc=1, device_id=(lax.rem(dp + d, 8), own), device_id_type=MESH)
    for d in range(1, 4):
        pl.semaphore_signal(barrier, inc=1, device_id=(dp, lax.rem(own + d, 4)), device_id_type=MESH)
    pl.semaphore_wait(barrier, 10)
    feat_start(3)
    feat_start(1)
    feat_start(0)
    loaded(*[("u", 10 + c) for c in range(8)])

    def begin(c, carry):
        unit(c, own, 0, across).start()
        unit(c, own, 1, sibling).start()
        return carry

    lax.fori_loop(10, 18, begin, 0)
    feat_start(2)
    loaded(*[("p", i) for i in range(3)], ("u", 24), ("u", 25))
    for i in range(3):
        part(i, own, 0, across).start()
        part(i, own, 1, sibling).start()
    feat_start(4)
    lax.fori_loop(24, 26, begin, 0)
    loaded(*[("t", v) for v in range(4)], "pred", "narrow")
    for w in range(2):
        table_raw((1 - core) * 2 + w, sibling).start()
    tally[...] = jnp.zeros_like(tally)
    acc240[...] = jnp.zeros_like(acc240)
    for w in range(2):
        v = core * 2 + w
        table_raw(v, own).wait_recv()
        pairs[x, v] = (tabs[0, v].astype(f32) + tabs[1, v].astype(f32)).astype(bf16)
        table(v, x, 1, across).start()
        table(v, x, 2, sibling).start()
    feat_start(5)
    feat_start(6)
    for d in (2, 1, 3):
        pred_copy(d, own, lax.rem(own + d, 4)).start()
        narrow_copy(d, own, lax.rem(own + d, 4)).start()

    def feat_wait(k):
        for d in range(1, 4):
            for half in range(2):
                feat_copy(k, d, half, own).wait_recv()

    def put(c, value):
        own_buf[c] = value[:128]
        give_buf[c] = value[128:].astype(bf16)

    def feature(k):
        return feats[k].reshape(256, 512)

    def matmul(a, b):
        return lax.dot_general(a, b, (((1,), (0,)), ((), ())), preferred_element_type=f32)

    def two(value):
        high = value.astype(bf16)
        return high, (value - high.astype(f32)).astype(bf16)

    def summed_table(v):
        return two(pairs[0, v].astype(f32) + pairs[1, v].astype(f32))

    def compute(c):
        for i in range(3):
            @pl.when(c == 18 + i * 2)
            def _():
                part(i, sibling, 1, own).wait_recv()
                part(i, diagonal, 2, own).wait_recv()

        for low, high, k in SEGMENTS:
            @pl.when(c == low)
            def _():
                feat_wait(k)
                loaded(("f", k, 0), ("f", k, 1))
                if k == 3:
                    loaded(("j", 0), ("j", 1))
                if k == 1:
                    loaded(*[("l", i) for i in range(8)])

            @pl.when((c >= low) & (c < high))
            def _():
                if k in (0, 4):
                    unit(c, sibling, 1, own).wait_recv()
                    unit(c, diagonal, 2, own).wait_recv()
                put(c, matmul(feature(k), ys[c]))

        @pl.when(c == N_STD)
        def _():
            loaded(("w", 0), ("w", 1), ("k", 0), ("k", 1))

        @pl.when((c >= N_STD) & (c < N_STD + 4))
        def _():
            v = c - N_STD

            @pl.when(v // 2 != core)
            def _():
                table(v, x, 2, own).wait_recv()
                table(v, 1 - x, 3, own).wait_recv()

            high, low = summed_table(v)
            rows = w240[...].reshape(256, 256)
            dims = (((1,), (1,)), ((), ()))
            put(
                c,
                lax.dot_general(rows, high, dims, preferred_element_type=f32)
                + lax.dot_general(rows, low, dims, preferred_element_type=f32),
            )

        for v in range(4):
            @pl.when(c == N_STD + v)
            def _():
                high, low = summed_table(v)
                rows = wkv[:, :, :, v * CHUNK : (v + 1) * CHUNK].reshape(256, CHUNK)
                acc240[...] = acc240[...] + matmul(rows, high) + matmul(rows, low)

        @pl.when(c == N_STD + 4)
        def _():
            feat_wait(5)
            loaded(("f", 5, 0), ("f", 5, 1))
            for d in range(1, 4):
                pred_copy(d, lax.rem(own + 4 - d, 4), own).wait_recv()
            value = matmul(feature(5), preds[...])
            own_buf[c, :, 0:256] = acc240[:128]
            own_buf[c, :, 256:512] = value[:128]
            give_buf[c, :, 0:256] = acc240[128:].astype(bf16)
            give_buf[c, :, 256:512] = value[128:].astype(bf16)

        @pl.when(c == N_STD + 5)
        def _():
            feat_wait(6)
            loaded(("f", 6, 0), ("f", 6, 1), "hot")
            for d in range(1, 4):
                narrow_copy(d, lax.rem(own + 4 - d, 4), own).wait_recv()
            value = matmul(feature(6), hots[...])
            place = lax.broadcasted_iota(jnp.int32, (256, D), 0)
            source = lax.broadcasted_iota(jnp.int32, (256, D), 1)
            side = jnp.where(place < 128, y, 1 - y)
            wanted = ((place >> 5) & 3) * 256 + side * 128 + own * STRIP + (place & 31)
            choose = jnp.where(source == wanted, 1.0, 0.0).astype(bf16)
            total = (narrows[0] + narrows[1]) + (narrows[2] + narrows[3])
            total = jnp.concatenate([total, jnp.zeros((112, D), f32)], axis=0)
            high = total.astype(bf16)
            rest = total - high.astype(f32)
            middle = rest.astype(bf16)
            low = (rest - middle.astype(f32)).astype(bf16)
            dims = (((1,), (1,)), ((), ()))
            small = (
                lax.dot_general(choose, high, dims, preferred_element_type=f32)
                + lax.dot_general(choose, middle, dims, preferred_element_type=f32)
                + lax.dot_general(choose, low, dims, preferred_element_type=f32)
            )
            empty = jnp.zeros((128, 128), f32)
            own_buf[c, :, 0:256] = value[:128]
            own_buf[c, :, 256:384] = small[:128]
            own_buf[c, :, 384:512] = empty
            give_buf[c, :, 0:256] = value[128:].astype(bf16)
            give_buf[c, :, 256:384] = small[128:].astype(bf16)
            give_buf[c, :, 384:512] = empty.astype(bf16)

    def cross(c):
        return pltpu.make_async_remote_copy(
            src_ref=give_buf.at[c], dst_ref=got.at[c], send_sem=y_send.at[c],
            recv_sem=y_recv.at[c], device_id=(over, own), device_id_type=MESH,
        )

    def hop(buf, way, c, b, to):
        at = b - 1 if way == 0 else b
        return pltpu.make_async_remote_copy(
            src_ref=buf.at[c, at], dst_ref=buf.at[c, at], send_sem=z_send.at[way, c, at], recv_sem=z_recv.at[way, c, at],
            device_id=(to * 2 + y, own), device_id_type=MESH,
        )

    def far_hop(way, c, b, to):
        at = FAR[way][b]
        return pltpu.make_async_remote_copy(
            src_ref=far.at[way, c, at], dst_ref=far.at[way, c, at], send_sem=z_send.at[way, c, 3 + at],
            recv_sem=z_recv.at[way, c, 3 + at], device_id=(to * 2 + y, own), device_id_type=MESH,
        )

    def here(c, b):
        at = pl.ds(b * STRIP, STRIP)
        return own_buf[c, at, :] + got[c, at, :].astype(f32)

    early, late = LAG * jnp.minimum(z, 3 - z), LAG * jnp.maximum(z, 3 - z)

    def step(t, carry):
        @pl.when((t >= 4) & (t < 12))
        def _():
            unit(t + 6, across, 0, own).wait_recv()
            unit(t + 6, across, 2, sibling).start()

        for i in range(3):
            @pl.when(t == 14 + 2 * i)
            def _():
                part(i, across, 0, own).wait_recv()
                part(i, across, 2, sibling).start()

        @pl.when((t == 20) | (t == 21))
        def _():
            unit(t + 4, across, 0, own).wait_recv()
            unit(t + 4, across, 2, sibling).start()

        @pl.when((t == 24) | (t == 25))
        def _():
            v = core * 2 + t - 24
            table(v, 1 - x, 1, own).wait_recv()
            table(v, 1 - x, 3, sibling).start()

        @pl.when((t >= SHIFT) & (t < n + SHIFT))
        def _():
            compute(t - SHIFT)
            cross(t - SHIFT).start()

        first = t - SHIFT - BASE - early

        @pl.when((first >= 0) & (first < n))
        def _():
            cross(first).wait()

        for way, buf, lag, to, back in ((0, rise, LAG * z, z + 1, z - 1), (1, fall, LAG * (3 - z), z - 1, z + 1)):
            c = t - SHIFT - BASE - lag

            @pl.when((c >= 0) & (c < n))
            def _():
                for b in ((1, 2, 3) if way == 0 else (0, 1, 2)):
                    beyond = (b > z) if way == 0 else (b < z)
                    at = b - 1 if way == 0 else b

                    @pl.when(beyond & (lag == 0))
                    def _():
                        if b == (1 if way == 0 else 2):
                            buf[c, at] = here(c, b)
                        else:
                            far[way, c, FAR[way][b]] = here(c, b).astype(bf16)

                    @pl.when(beyond & (lag > 0))
                    def _():
                        if b == (1 if way == 0 else 2):
                            hop(buf, way, c, b, back).wait_recv()
                            buf[c, at] = buf[c, at] + here(c, b)
                        else:
                            @pl.when(lag == LAG)
                            def _():
                                far_hop(way, c, b, back).wait_recv()
                                buf[c, at] = far[way, c, FAR[way][b]].astype(f32) + here(c, b)

                            @pl.when(lag > LAG)
                            def _():
                                hop(buf, way, c, b, back).wait_recv()
                                buf[c, at] = buf[c, at] + here(c, b)

                    def send(c, act):
                        if b == (1 if way == 0 else 2):
                            copy = hop(buf, way, c, b, to)
                            copy.start() if act else copy.wait_send()
                        else:
                            @pl.when(lag == 0)
                            def _():
                                copy = far_hop(way, c, b, to)
                                copy.start() if act else copy.wait_send()

                            @pl.when(lag > 0)
                            def _():
                                copy = hop(buf, way, c, b, to)
                                copy.start() if act else copy.wait_send()

                    @pl.when(beyond & (c >= QUEUE))
                    def _():
                        send(c - QUEUE, False)

                    @pl.when(beyond)
                    def _():
                        send(c, True)

        last = t - SHIFT - BASE - late

        @pl.when((last >= 0) & (last < n))
        def _():
            at = pl.ds(pl.multiple_of(z * STRIP, STRIP), STRIP)
            value = own_buf[last, at, :] + got[last, at, :].astype(f32)
            own_buf[last, 0:STRIP, :] = value

            @pl.when(z > 0)
            def _():
                hop(rise, 0, last, z, z - 1).wait_recv()
                own_buf[last, 0:STRIP, :] = own_buf[last, 0:STRIP, :] + rise[last, z - 1]

            @pl.when(z < 3)
            def _():
                hop(fall, 1, last, z, z + 1).wait_recv()
                own_buf[last, 0:STRIP, :] = own_buf[last, 0:STRIP, :] + fall[last, z]

            value = own_buf[last, 0:STRIP, :]
            square = value * value
            total = square[0:8, 0:128]
            for r in range(0, STRIP, 8):
                for k in range(0, CHUNK, 128):
                    if r or k:
                        total = total + square[r : r + 8, k : k + 128]
            tally[...] = tally[...] + total

        return carry

    lax.fori_loop(0, n + SHIFT + BASE + 3 * LAG, step, 0)
    summed = jnp.sum(tally[...])
    lane = lax.broadcasted_iota(jnp.int32, (8, 128), 1)
    quad_buf[own] = jnp.where(lane == 0, summed, jnp.where(lane == 1, num_ref[...], 0.0))

    def share(buf, k, where, at):
        return pltpu.make_async_remote_copy(
            src_ref=buf.at[at], dst_ref=buf.at[at], send_sem=s_send.at[k], recv_sem=s_recv.at[k],
            device_id=where, device_id_type=MESH,
        )

    for d in range(1, 4):
        share(quad_buf, d, (dp, lax.rem(own + d, 4)), own).start()
    for out, base, low, high in (
        (r_attn, 3 * D, 0, 2), (r_mlp, FF, 2, 10), (r_mlp, 0, 10, 18), (r_attn, 0, 18, 24), (r_agg, 2 * D, 24, 26), (r_agg, 0, 26, 30),
    ):
        for c in range(low, high):
            out[:, base + (c - low) * CHUNK : base + (c - low + 1) * CHUNK] = own_buf[c, 0:STRIP, :]
    left, right = own_buf[30, 0:STRIP, :], own_buf[31, 0:STRIP, :]
    r_io[:, 0:WIDTH] = left[:, 0:WIDTH]
    r_io[:, WIDTH : 2 * WIDTH] = left[:, 256 : 256 + WIDTH]
    r_io[:, 2 * WIDTH : 2 * WIDTH + VARS] = left[:, WIDTH : WIDTH + VARS]
    r_io[:, 2 * WIDTH + VARS : 2 * WIDTH + VARS + SPAN] = right[:, 0:SPAN]
    r_io[:, 2 * WIDTH + VARS + SPAN :] = jnp.zeros((STRIP, r_io.shape[1] - 2 * WIDTH - VARS - SPAN), f32)
    r_small[...] = right[:, 256:384].T[:16]
    for d in range(1, 4):
        share(quad_buf, d, (dp, own), lax.rem(own + 4 - d, 4)).wait_recv()
    line_buf[dp] = (quad_buf[0] + quad_buf[1]) + (quad_buf[2] + quad_buf[3])
    for d in range(1, 8):
        share(line_buf, 3 + d, (lax.rem(dp + d, 8), own), dp).start()
    for d in range(1, 8):
        share(line_buf, 3 + d, (dp, own), lax.rem(dp + 8 - d, 8)).wait_recv()
    stat = line_buf[0]
    for d in range(1, 8):
        stat = stat + line_buf[d]
    stat_ref[...] = stat
    for d in range(1, 4):
        share(quad_buf, d, (dp, own), own).wait_send()
    for d in range(1, 8):
        share(line_buf, 3 + d, (dp, own), dp).wait_send()
    for d in range(1, 4):
        for k in range(7):
            for half in range(2):
                feat_copy(k, d, half, own).wait_send()
        pred_copy(d, own, own).wait_send()
        narrow_copy(d, own, own).wait_send()
    for w in range(2):
        table_raw((1 - core) * 2 + w, own).wait_send()
        for slot, who in ((1, x), (2, x), (3, 1 - x)):
            table(core * 2 + w, who, slot, own).wait_send()
    relays = ((0, own), (1, own), (2, across))
    for i in range(3):
        for slot, who in relays:
            part(i, who, slot, own).wait_send()

    def finish(c, carry):
        for slot, who in relays:
            unit(c, who, slot, own).wait_send()
        return carry

    lax.fori_loop(10, 18, finish, 0)
    lax.fori_loop(24, 26, finish, 0)

    def drain(c, carry):
        for way, buf, inner, outer in ((0, rise, z > 0, z == 0), (1, fall, z < 3, z == 3)):
            for b in ((1, 2, 3) if way == 0 else (0, 1, 2)):
                beyond = (b > z) if way == 0 else (b < z)
                if b == (1 if way == 0 else 2):
                    pl.when(beyond)(lambda: hop(buf, way, c, b, z).wait_send())
                else:
                    pl.when(beyond & inner)(lambda: hop(buf, way, c, b, z).wait_send())
                    pl.when(beyond & outer)(lambda: far_hop(way, c, b, z).wait_send())
        return carry

    lax.fori_loop(n - QUEUE, n, drain, 0)


def gradient_blocks(operands, numbers):
    any_space = pl.BlockSpec(memory_space=pl.ANY)
    vmem = pl.BlockSpec(memory_space=pltpu.VMEM)
    n = N_ALL
    dma = pltpu.SemaphoreType.DMA
    widths = (3 * D, 4 * D, 2 * FF, 944)
    return pl.pallas_call(
        gradient_kernel,
        out_shape=[jax.ShapeDtypeStruct((STRIP, w), f32) for w in widths]
        + [jax.ShapeDtypeStruct((16, STRIP), f32), jax.ShapeDtypeStruct((8, 128), f32)],
        in_specs=[any_space] * 17 + [vmem],
        out_specs=[vmem] * 6,
        scratch_shapes=[
            pltpu.VMEM((7, 2, 4, STRIP, 512), bf16),
            pltpu.VMEM((N_STD, 512, CHUNK), bf16),
            pltpu.VMEM((2, 4, CHUNK, 256), bf16),
            pltpu.VMEM((2, 4, CHUNK, 256), bf16),
            pltpu.VMEM((512, 256), bf16),
            pltpu.VMEM((512, 256), bf16),
            pltpu.VMEM((4, 16, D), f32),
            pltpu.VMEM((2, 4, STRIP, 256), bf16),
            pltpu.VMEM((2, 4, STRIP, 2 * D), bf16),
            pltpu.VMEM((256, 256), f32),
            pltpu.VMEM((n, 4 * STRIP, CHUNK), f32),
            pltpu.VMEM((n, 4 * STRIP, CHUNK), bf16),
            pltpu.VMEM((n, 4 * STRIP, CHUNK), bf16),
            pltpu.VMEM((n, 3, STRIP, CHUNK), f32),
            pltpu.VMEM((n, 3, STRIP, CHUNK), f32),
            pltpu.VMEM((2, n, 2, STRIP, CHUNK), bf16),
            pltpu.VMEM((8, 128), f32),
            pltpu.VMEM((4, 8, 128), f32),
            pltpu.VMEM((8, 8, 128), f32),
            dma((56,)),
            dma((7, 4, 2)),
            dma((7, 4, 2)),
            dma((N_STD, 3)),
            dma((N_STD, 4)),
            dma((3, 3)),
            dma((3, 4)),
            dma((4, 4)),
            dma((4, 3)),
            dma((4,)),
            dma((4,)),
            dma((4,)),
            dma((4,)),
            dma((n,)),
            dma((n,)),
            dma((2, n, 5)),
            dma((2, n, 5)),
            dma((11,)),
            dma((11,)),
        ],
        compiler_params=pltpu.CompilerParams(
            collective_id=1, has_side_effects=True, vmem_limit_bytes=62 * 2**20
        ),
        name="gradient_blocks",
    )(*operands, numbers)


def ag(part):
    return lax.all_gather(part, "fsdp", axis=0, tiled=True)


def make_local(n_dp, n_f):
    fast = n_dp == 8 and n_f == 4

    def local(
        pixels, targets, valid_mask, lat_weight, segment_ids, present_vars, lead_index, step_count,
        w_agg, w_attn, w_mlp, w_io, w_small,
        m_agg, m_attn, m_mlp, m_io, m_small,
        v_agg, v_attn, v_mlp, v_io, v_small,
    ):
        masters = (w_agg, w_attn, w_mlp, w_io, w_small)
        firsts = (m_agg, m_attn, m_mlp, m_io, m_small)
        seconds = (v_agg, v_attn, v_mlp, v_io, v_small)
        rows = pixels.shape[1]
        row_len = segment_ids.shape[1]
        strip = w_agg.shape[0]
        own = lax.axis_index("fsdp")
        heads_here = HEADS // n_f
        wide = heads_here * HEAD_DIM

        seg = segment_ids[0]
        below = jnp.sum((seg[None, :] < seg[:, None]).astype(jnp.int32), axis=1)
        pos = jnp.arange(row_len, dtype=jnp.int32) - below
        onehot_all = (pos[:, None] == jnp.arange(SPAN, dtype=jnp.int32)[None, :]).astype(bf16)
        onehot = lax.dynamic_slice_in_dim(onehot_all, own * rows, rows)
        lead = (lead_index[0].astype(f32) + 1.0) / LEAD_STEPS
        pixel_rows = pixels[0]
        target = targets[0].astype(f32)
        present = present_vars[0]
        spread = (jnp.arange(MIX) // PIX)[None, :] == jnp.arange(VARS)[:, None]
        embed_col = (jnp.arange(MIX) - WIDTH)[None, :] == jnp.arange(VARS)[:, None]
        in_pixels = (jnp.arange(MIX) < WIDTH)[None, :]
        expand = jnp.where(in_pixels, spread, embed_col).astype(bf16)
        present_cols = jnp.repeat(present.astype(f32), PIX)
        pixel_weight = lat_weight[0][:, None] * valid_mask[0].astype(f32) * present_cols[None, :]
        weight_sum = jnp.sum(pixel_weight)

        emb = 2 * WIDTH + VARS
        if fast:
            rear = jnp.concatenate([w_attn[:, 3 * D :], w_mlp], axis=1).astype(bf16)
            rear = lax.all_gather(rear, ("dp", "fsdp"), axis=0, tiled=True)
            head, w_qkv, small, stat = gather_weights(
                w_io, w_small, w_agg, w_attn, jnp.full((8, 128), weight_sum, f32)
            )
            total = stat[0, 0]
        else:

            def blank(width):
                return jnp.zeros((strip, width), bf16)

            io_low = w_io.astype(bf16)
            pack = jnp.concatenate(
                [
                    io_low[:, :WIDTH],
                    io_low[:, 2 * WIDTH : emb],
                    blank(MIX - WIDTH - VARS),
                    io_low[:, WIDTH : 2 * WIDTH],
                    blank(256 - WIDTH),
                    io_low[:, emb : emb + SPAN],
                    w_small.astype(bf16),
                    blank(128 - w_small.shape[1]),
                    w_agg.astype(bf16),
                ],
                axis=1,
            )
            head = lax.all_gather(pack, ("dp", "fsdp"), axis=0, tiled=True)
            attn = lax.all_gather(w_attn.astype(bf16), ("dp", "fsdp"), axis=0, tiled=True)
            mlp = lax.all_gather(w_mlp.astype(bf16), ("dp", "fsdp"), axis=0, tiled=True)
            w_qkv = attn[:, : 3 * D]
            rear = jnp.concatenate([attn[:, 3 * D :], mlp], axis=1)
            total = lax.psum(weight_sum, ("dp", "fsdp"))
        w240 = head[:, :MIX]
        w_pred = head[:, 256 : 256 + WIDTH]
        w_pos = head[:, 512 : 512 + SPAN]
        if not fast:
            small = head[:, 768:777].astype(f32).T
        agg_kv = head[:, HEAD : HEAD + 2 * D]
        agg_out = head[:, HEAD + 2 * D :]
        w_out = rear[:, :D]
        w_up = rear[:, D : D + FF]
        w_down = rear[:, D + FF :]

        pix_t = jnp.concatenate(
            [pixel_rows.T, jnp.ones((VARS, rows), bf16), jnp.zeros((MIX - WIDTH - VARS, rows), bf16)], axis=0
        )
        table = t_mm(agg_kv, w240)
        table_k = table[:D].reshape(HEADS, HEAD_DIM, MIX)
        table_v = table[D:].reshape(HEADS, HEAD_DIM, MIX)
        query = small[0].reshape(HEADS, HEAD_DIM)
        folded = jnp.sum(table_k * query[:, :, None], axis=1)
        block = folded[:, None, :] * expand.astype(f32)[None]
        score = exact("xc,cl->xl", block.reshape(HEADS * VARS, MIX), pix_t.astype(f32))
        score = score.reshape(HEADS, VARS, rows) * HEAD_DIM ** (-0.5)
        score = jnp.where(present[None, :, None] > 0, score, -1000000000.0)
        top = jnp.max(score, axis=1, keepdims=True)
        power = jnp.exp(score - top)
        soft = power / jnp.sum(power, axis=1, keepdims=True)
        share = soft.astype(bf16)
        pix_f = pix_t.astype(f32)
        lifted_share = jnp.einsum("vc,hvl->hcl", expand, share, preferred_element_type=f32) * pix_f[None]
        mixed_a = exact("hec,hcl->hel", table_v, lifted_share).reshape(D, rows).astype(bf16)
        lead_embed = lead * small[7] + small[8]
        h0 = t_mm(mixed_a, agg_out) + mm_t(onehot, w_pos) + lead_embed[None]
        norm0, unit0, scale0 = norm_forward(h0, small[1], small[2])
        qkv = mm(norm0, w_qkv).astype(bf16)
        if fast:
            seg_col = jnp.broadcast_to(seg[:, None], (row_len, 128))
            seg_row = jnp.broadcast_to(seg[None, :], (8, row_len))
            mixed, mixed_t, parts, norm0_t = attend(qkv, seg_col, seg_row, norm0)
        else:
            part = qkv.reshape(rows, 3, n_f, wide)
            part = lax.all_to_all(part, "fsdp", split_axis=2, concat_axis=0, tiled=True)
            part = part.reshape(row_len, 3, heads_here, HEAD_DIM)
            q, k, v = (part[:, i].transpose(1, 0, 2) for i in range(3))
            att_score = jnp.einsum("hqe,hke->hqk", q, k, preferred_element_type=f32) * HEAD_DIM ** (-0.5)
            same = seg[:, None] == seg[None, :]
            att_score = jnp.where(same[None], att_score, -1000000000.0)
            att_top = jnp.max(att_score, axis=-1, keepdims=True)
            att_power = jnp.exp(att_score - att_top)
            att_soft = att_power / jnp.sum(att_power, axis=-1, keepdims=True)
            att = att_soft.astype(bf16)
            mixed_h = jnp.einsum("hqk,hke->qhe", att, v, preferred_element_type=f32)
            mixed_h = mixed_h.reshape(row_len, wide).astype(bf16)
            mixed_all = lax.all_gather(mixed_h, "fsdp", axis=1, tiled=True)
            mixed = lax.dynamic_slice_in_dim(mixed_all, own * rows, rows, axis=0)
        h1 = h0 + mm(mixed, w_out)
        norm1, unit1, scale1 = norm_forward(h1, small[3], small[4])
        up = mm(norm1, w_up)
        gate = 0.5 * (1.0 + lax.erf(up * (2.0**-0.5)))
        lifted = (up * gate).astype(bf16)
        lifted_all = ag(lifted)
        h2 = h1 + mm_t(lifted, w_down)
        norm2, unit2, scale2 = norm_forward(h2, small[5], small[6])
        predicted = mm(norm2, w_pred) * D ** (-0.5)
        error = predicted - target
        weighted = pixel_weight * error
        numerator = jnp.sum(weighted * error)

        d_pred = (weighted * (2.0 * D ** (-0.5) / total)).astype(bf16)
        d_norm2 = mm_t(d_pred, w_pred)
        d_h2, d_gain2, d_off2 = norm_backward(d_norm2, unit2, scale2, small[5])
        d_out = d_h2.astype(bf16)
        slope = gate + up * jnp.exp(-0.5 * up * up) * 0.3989422804014327
        d_up = (mm(d_out, w_down) * slope).astype(bf16)
        d_norm1 = mm_t(d_up, w_up)
        d_in, d_gain1, d_off1 = norm_backward(d_norm1, unit1, scale1, small[3])
        d_h1 = d_h2 + d_in
        if fast:
            d_qkv, d_parts, d_proj_all, norm1_t, out_t, norm2_t = attend_back(
                d_h1.astype(bf16), rear, parts, seg_col, seg_row, norm1, d_out, norm2
            )
        else:
            d_proj_all = ag(d_h1.astype(bf16))
            w_out_own = lax.dynamic_slice_in_dim(w_out, own * wide, wide, axis=0)
            d_mixed = mm_t(d_proj_all, w_out_own).astype(bf16).reshape(row_len, heads_here, HEAD_DIM).transpose(1, 0, 2)
            d_att = jnp.einsum("hqe,hke->hqk", d_mixed, v, preferred_element_type=f32)
            d_v = jnp.einsum("hqk,hqe->khe", att, d_mixed, preferred_element_type=f32)
            lean = jnp.sum(att_soft * d_att, axis=-1, keepdims=True)
            d_score = (att_soft * (d_att - lean) * HEAD_DIM ** (-0.5)).astype(bf16)
            d_q = jnp.einsum("hqk,hke->qhe", d_score, k, preferred_element_type=f32)
            d_k = jnp.einsum("hqk,hqe->khe", d_score, q, preferred_element_type=f32)
            d_part = jnp.stack([d_q, d_k, d_v], axis=1).astype(bf16).reshape(row_len, 3, 1, wide)
            d_qkv_all = lax.all_gather(d_part, "fsdp", axis=2, tiled=True).reshape(row_len, 3 * D)
            d_qkv = lax.dynamic_slice_in_dim(d_qkv_all, own * rows, rows, axis=0)
        d_norm0 = mm_t(d_qkv, w_qkv)
        d_in, d_gain0, d_off0 = norm_backward(d_norm0, unit0, scale0, small[1])
        d_h0 = d_h1 + d_in
        d_agg = d_h0.astype(bf16)
        d_mixed_a = mm_t(agg_out, d_agg).astype(bf16).reshape(HEADS, HEAD_DIM, rows)
        pulled = exact("hec,hel->hcl", table_v, d_mixed_a.astype(f32)) * pix_f[None]
        d_share = exact("vc,hcl->hvl", expand.astype(f32), pulled)
        lean_a = jnp.sum(soft * d_share, axis=1, keepdims=True)
        d_score_a = (soft * (d_share - lean_a) * HEAD_DIM ** (-0.5)).astype(bf16)
        spread_score = jnp.einsum("vc,hvl->hcl", expand, d_score_a, preferred_element_type=f32)
        d_folded = jnp.sum(spread_score * pix_f[None], axis=2)
        d_table_v = exact("hel,hcl->hec", d_mixed_a.astype(f32), lifted_share).reshape(D, MIX)
        d_table_k = (query[:, :, None] * d_folded[:, None, :]).reshape(D, MIX)
        d_query = jnp.sum(d_folded[:, None, :] * table_k, axis=2).reshape(D)
        d_bias = jnp.sum(d_h0, axis=0)
        narrow = jnp.stack(
            [d_query, d_gain0, d_off0, d_gain1, d_off1, d_gain2, d_off2, lead * d_bias, d_bias]
            + [jnp.zeros((D,), f32)] * 7
        )
        d_table = jnp.concatenate([d_table_k, d_table_v], axis=0)
        if fast:

            def sorted_rows(array):
                return array.reshape(4, 2, n_f, strip, array.shape[1])

            lane = lax.broadcasted_iota(jnp.int32, (8, 128), 1)
            r_agg, r_attn, r_mlp, r_io, r_small, stat = gradient_blocks(
                [sorted_rows(part) for part in (norm1_t, out_t, norm0_t)]
                + [mixed_t.reshape(2, n_f, strip, row_len)]
                + [sorted_rows(part) for part in (mixed_a, norm2_t, d_agg.T)]
                + [d_proj_all, d_parts, d_up, lifted_all, d_agg, jnp.pad(d_pred, ((0, 0), (0, 256 - WIDTH)))]
                + [onehot_all, d_table.astype(bf16), narrow, sorted_rows(head)],
                jnp.where(lane == 1, numerator, 0.0),
            )
            r_small = r_small[:9].T
            squares, numerator = stat[0, 0], stat[0, 1]
        else:
            d_table, narrow = lax.psum((d_table, narrow), "fsdp")
            source = jnp.arange(D)
            pick = (source // strip) % n_f == own
            place = (source // (strip * n_f)) * strip + source % strip
            choose = (pick[:, None] & (place[:, None] == jnp.arange(n_dp * strip)[None, :])).astype(bf16)

            def mine(array):
                whole = array.reshape(n_dp, n_f, strip, array.shape[1])
                return lax.dynamic_index_in_dim(whole, own, 1, False).reshape(n_dp * strip, array.shape[1])

            def weight_grad(features, grads):
                return t_mm(mm(features, choose).astype(bf16), grads)

            def gap(width):
                return jnp.zeros((n_dp * strip, width), f32)

            d_agg_all = ag(d_agg)
            g_kv = exact("dc,xc->dx", mine(w240).astype(f32), d_table)
            g_240 = exact("dx,xc->dc", mine(agg_kv).astype(f32), d_table)
            groups = (
                (g_kv, weight_grad(ag(mixed_a.T), d_agg_all)),
                (weight_grad(ag(norm0), d_qkv_all), weight_grad(mixed_all, d_proj_all)),
                (weight_grad(ag(norm1), ag(d_up)), weight_grad(ag(d_out), lifted_all)),
                (
                    g_240, weight_grad(ag(norm2), ag(d_pred)), gap(256 - WIDTH),
                    weight_grad(d_agg_all, onehot_all), mine(narrow.T)[:, :9], gap(256 - 9),
                ),
            )
            r_agg, r_attn, r_mlp, r_misc = (
                lax.psum_scatter(jnp.concatenate(g, axis=1), "dp", scatter_dimension=0, tiled=True) for g in groups
            )
            local_squares = sum(jnp.sum(piece * piece) for piece in (r_agg, r_attn, r_mlp, r_misc))
            squares, numerator = lax.psum((local_squares, numerator), ("dp", "fsdp"))
            r_io = jnp.concatenate(
                [
                    r_misc[:, :WIDTH], r_misc[:, 256 : 256 + WIDTH], r_misc[:, WIDTH : WIDTH + VARS],
                    r_misc[:, 512 : 512 + SPAN], jnp.zeros((strip, w_io.shape[1] - emb - SPAN), f32),
                ],
                axis=1,
            )
            r_small = r_misc[:, 768:777]
        reduced = (r_agg, r_attn, r_mlp, r_io, r_small)
        grad_norm = jnp.sqrt(squares)
        factor = jnp.minimum(1.0, clip_limit / grad_norm)
        loss = numerator / total
        step_value = step_count[0].astype(f32)
        results = [
            adamw(masters[i], reduced[i] * factor, firsts[i], seconds[i], step_value, learn_rates[i]) for i in range(5)
        ]
        return (loss, grad_norm) + tuple(results[i][j] for j in range(4) for i in range(5))

    return local


def solution(mesh):
    flat = P(("dp", "fsdp"), None)
    tokens = P("dp", "fsdp", None)
    return jax.shard_map(
        make_local(mesh.shape["dp"], mesh.shape["fsdp"]),
        mesh=mesh,
        in_specs=(tokens, tokens, tokens, P("dp", "fsdp"), P("dp", None), P("dp", None), P("dp"), P()) + (flat,) * 15,
        out_specs=(P(), P()) + (flat,) * 20,
        check_vma=False,
    )
```

```python
import functools

import jax
import jax.numpy as jnp
from jax import lax
from jax.experimental import pallas as pl
from jax.experimental.pallas import tpu as pltpu
from jax.sharding import PartitionSpec as P

D = 1024
HEADS = 16
HEAD_DIM = 64
FF = 4096
VARS = 48
PIX = 4
LEAD_STEPS = 8
WIDTH = VARS * PIX
SPAN = 256
MIX = 256
HEAD = 896

norm_eps = 1e-05
clip_limit = 1.0
decay_rate = 0.05
adam_eps = 1e-08
learn_rates = (0.03, 0.03, 0.03, 0.2, 0.3)
f32 = jnp.float32
bf16 = jnp.bfloat16
highest = lax.Precision.HIGHEST
MESH = pl.DeviceIdType.MESH
STRIP = 32
CHUNK = 512
LAG = 2
QUEUE = 2


def dot(left, right, dims):
    return lax.dot_general(left, right, (dims, ((), ())), preferred_element_type=f32)


def mm(left, right):
    return dot(left, right, ((1,), (0,)))


def mm_t(left, right):
    return dot(left, right, ((1,), (1,)))


def t_mm(left, right):
    return dot(left, right, ((0,), (0,)))


def exact(eq, left, right):
    return jnp.einsum(eq, left, right, precision=highest, preferred_element_type=f32)


def norm_forward(values, gain, offset):
    average = jnp.mean(values, axis=-1, keepdims=True)
    centred = values - average
    scale = lax.rsqrt(jnp.mean(centred * centred, axis=-1, keepdims=True) + norm_eps)
    unit = centred * scale
    return (unit * gain[None] + offset[None]).astype(bf16), unit, scale


def norm_backward(grad, unit, scale, gain):
    inner = grad * gain[None]
    mean_inner = jnp.mean(inner, axis=-1, keepdims=True)
    mean_product = jnp.mean(inner * unit, axis=-1, keepdims=True)
    back = scale * (inner - mean_inner - unit * mean_product)
    return back, jnp.sum(grad * unit, axis=0), jnp.sum(grad, axis=0)


def adamw(weight, grad, moment, second, step_value, learn_rate):
    moment = 0.5 * moment + 0.5 * grad
    second = 0.5 * second + 0.5 * grad * grad
    correct = 1.0 - jnp.power(f32(0.5), step_value)
    update = moment / correct / (jnp.sqrt(second / correct) + adam_eps) + decay_rate * weight
    fresh = weight - learn_rate * update
    return (fresh, fresh.astype(bf16), moment, second)


PIECES = (
    (0, 1408, 1280, "yzx"), (1, 0, 1536, "zxy"), (0, 2688, 1280, "yzx"), (1, 1536, 1536, "zxy"), (0, 0, 1408, "zxy"),
)


def gather_kernel(*refs):
    w_io, w_small, w_agg, w_attn, num_ref = refs[:5]
    wholes, small_ref, stat_ref = refs[5:7], refs[7], refs[8]
    quad_buf, line_buf, small_buf, pack, attn_low, own_sem, s_send, s_recv, sends, arrive, pass_on = refs[9:]
    shards = (pack, attn_low)
    dp, own = lax.axis_index("dp"), lax.axis_index("fsdp")
    z, y, x, core = dp // 2, dp % 2, own // 2, own % 2
    sibling = x * 2 + 1 - core
    barrier = pltpu.get_barrier_semaphore()
    for d in range(1, 8):
        pl.semaphore_signal(barrier, inc=1, device_id=(lax.rem(dp + d, 8), own), device_id_type=MESH)
    for d in range(1, 4):
        pl.semaphore_signal(barrier, inc=1, device_id=(dp, lax.rem(own + d, 4)), device_id_type=MESH)
    emb = 2 * WIDTH + VARS

    def gap(width):
        return jnp.zeros((STRIP, width), f32)

    pack[:, :HEAD] = jnp.concatenate(
        [
            w_io[:, :WIDTH], w_io[:, 2 * WIDTH : emb], gap(MIX - WIDTH - VARS), w_io[:, WIDTH : 2 * WIDTH],
            gap(256 - WIDTH), w_io[:, emb : emb + SPAN], w_small[...], gap(128 - w_small.shape[1]),
        ],
        axis=1,
    ).astype(bf16)
    pack[:, HEAD:] = w_agg[...].astype(bf16)
    attn_low[...] = w_attn[:, : 3 * D].astype(bf16)
    pl.semaphore_wait(barrier, 10)

    def view(p, ident, plane):
        a, start, width, order = PIECES[p]
        row = pl.multiple_of(((ident // 2) * 4 + (ident % 2) * 2 + plane) * STRIP, STRIP)
        return wholes[a].at[pl.ds(row, STRIP), pl.ds(start, width)]

    def copy(p, ident, slot, to, mine=False):
        a, start, width, order = PIECES[p]
        src = shards[a].at[:, pl.ds(start, width)] if mine else view(p, ident, core)
        sem = pass_on if slot == 4 else arrive
        return pltpu.make_async_remote_copy(
            src_ref=src, dst_ref=view(p, ident, core), send_sem=sends.at[p, ident, slot], recv_sem=sem.at[p, ident],
            device_id=to, device_id_type=MESH,
        )

    def arrival(p, ident, plane, sem):
        return pltpu.make_async_copy(view(p, ident, plane), view(p, ident, plane), sem.at[p, ident])

    def targets(p, rx, ry, rz):
        order = PIECES[p][3]
        moved = {"x": rx != 0, "y": ry != 0, "z": rz is not None}
        stage = max([k for k in range(3) if moved[order[k]]], default=-1)
        found = []
        if stage >= 0 and order[stage] == "z":
            found.append((0, (rz < 0) & (z < 3), ((dp + 2) % 8, own)))
            found.append((1, (rz > 0) & (z > 0), ((dp + 6) % 8, own)))
        for k in range(stage + 1, 3):
            if order[k] == "z":
                found.append((0, z < 3, ((dp + 2) % 8, own)))
                found.append((1, z > 0, ((dp + 6) % 8, own)))
            elif order[k] == "x":
                found.append((2, None, (dp, (1 - x) * 2 + core)))
            else:
                found.append((3, None, (z * 2 + 1 - y, own)))
        found.append((4, None, (dp, sibling)))
        return found

    def source(rx, ry, rz):
        sz = z if rz is None else z + rz
        sy = 1 - y if ry else y
        sx = 1 - x if rx else x
        return sz, (sz * 2 + sy) * 2 + sx

    def each(rx, ry, rz, act, mine=False):
        sz, ident = source(rx, ry, rz)

        def body():
            for p in range(len(PIECES)):
                if act == "send" and not mine:
                    arrival(p, ident, core, arrive).wait()
                for slot, when, to in targets(p, rx, ry, rz):
                    def go(slot=slot, to=to):
                        c = copy(p, ident, slot, to, mine)
                        c.start() if act == "send" else c.wait_send()

                    if when is None:
                        go()
                    else:
                        pl.when(when)(go)

        if rz is None:
            body()
        else:
            pl.when((sz >= 0) & (sz < 4))(body)

    def over_z(pairs, act):
        def step(t, carry):
            rz = ((t + 1) // 2) * (1 - 2 * (t % 2))
            for rx, ry in pairs:
                each(rx, ry, rz, act)
            return carry

        lax.fori_loop(1, 7, step, 0)

    def sweep(act):
        each(0, 0, None, act, mine=True)
        if act == "send":
            for a in range(2):
                row = pl.multiple_of((dp * 4 + own) * STRIP, STRIP)
                pltpu.make_async_copy(shards[a], wholes[a].at[pl.ds(row, STRIP), :], own_sem.at[a]).start()
            scalars()
        each(1, 0, None, act)
        each(0, 1, None, act)
        over_z([(0, 0)], act)
        each(1, 1, None, act)
        over_z([(1, 0), (0, 1)], act)
        over_z([(1, 1)], act)

    def share(buf, k, where, at):
        return pltpu.make_async_remote_copy(
            src_ref=buf.at[at], dst_ref=buf.at[at], send_sem=s_send.at[k], recv_sem=s_recv.at[k],
            device_id=where, device_id_type=MESH,
        )

    def scalars():
        quad_buf[own] = num_ref[...]
        for d in range(1, 4):
            share(quad_buf, d, (dp, lax.rem(own + d, 4)), own).start()

    sweep("send")
    for d in range(1, 4):
        share(quad_buf, d, (dp, own), lax.rem(own + 4 - d, 4)).wait_recv()
    line_buf[dp] = (quad_buf[0] + quad_buf[1]) + (quad_buf[2] + quad_buf[3])
    for d in range(1, 8):
        share(line_buf, 3 + d, (lax.rem(dp + d, 8), own), dp).start()

    def closing(ident, carry):
        for p in range(len(PIECES)):
            arrival(p, ident, 1 - core, pass_on).wait()
        return carry

    lax.fori_loop(0, 16, closing, 0)
    for a in range(2):
        row = pl.multiple_of((dp * 4 + own) * STRIP, STRIP)
        pltpu.make_async_copy(shards[a], wholes[a].at[pl.ds(row, STRIP), :], own_sem.at[a]).wait()
    narrow = pltpu.make_async_copy(wholes[0].at[:, pl.ds(768, 128)], small_buf, own_sem.at[0])
    narrow.start()
    sweep("drain")
    narrow.wait()
    small_ref[...] = small_buf[...].astype(f32).T[:16]
    for d in range(1, 8):
        share(line_buf, 3 + d, (dp, own), lax.rem(dp + 8 - d, 8)).wait_recv()
    stat = line_buf[0]
    for d in range(1, 8):
        stat = stat + line_buf[d]
    stat_ref[...] = stat
    for d in range(1, 4):
        share(quad_buf, d, (dp, own), own).wait_send()
    for d in range(1, 8):
        share(line_buf, 3 + d, (dp, own), dp).wait_send()


def gather_weights(w_io, w_small, w_agg, w_attn, number):
    any_space = pl.BlockSpec(memory_space=pl.ANY)
    vmem = pl.BlockSpec(memory_space=pltpu.VMEM)
    n = len(PIECES)
    return pl.pallas_call(
        gather_kernel,
        out_shape=[jax.ShapeDtypeStruct((D, w), bf16) for w in (HEAD + 3 * D, 3 * D)]
        + [jax.ShapeDtypeStruct((16, D), f32), jax.ShapeDtypeStruct((8, 128), f32)],
        in_specs=[vmem] * 5,
        out_specs=[any_space] * 2 + [vmem] * 2,
        scratch_shapes=[
            pltpu.VMEM((4, 8, 128), f32),
            pltpu.VMEM((8, 8, 128), f32),
            pltpu.VMEM((D, 128), bf16),
            pltpu.VMEM((STRIP, HEAD + 3 * D), bf16),
            pltpu.VMEM((STRIP, 3 * D), bf16),
            pltpu.SemaphoreType.DMA((3,)),
            pltpu.SemaphoreType.DMA((11,)),
            pltpu.SemaphoreType.DMA((11,)),
            pltpu.SemaphoreType.DMA((n, 16, 5)),
            pltpu.SemaphoreType.DMA((n, 16)),
            pltpu.SemaphoreType.DMA((n, 16)),
        ],
        compiler_params=pltpu.CompilerParams(collective_id=0, has_side_effects=True),
        cost_estimate=pl.CostEstimate(flops=0, bytes_accessed=250_000_000, transcendentals=0),
        name="gather_weights",
    )(w_io, w_small, w_agg, w_attn, number)


def plain_norm(values, gain, offset):
    centred = values - jnp.mean(values, axis=1, keepdims=True)
    scale = lax.rsqrt(jnp.mean(centred * centred, axis=1, keepdims=True) + norm_eps)
    unit = centred * scale
    return (unit * gain + offset).astype(bf16), unit, scale


def plain_norm_back(grad, unit, scale, gain):
    inner = grad * gain
    mean_inner = jnp.mean(inner, axis=1, keepdims=True)
    mean_product = jnp.mean(inner * unit, axis=1, keepdims=True)
    back = scale * (inner - mean_inner - unit * mean_product)
    return back, jnp.sum(grad * unit, axis=0, keepdims=True), jnp.sum(grad, axis=0, keepdims=True)


def mlp_kernel(mixed, h0, small, target, weight, stat, rear, head, lifted, d_up, norm1, norm2, d_out, d_pred, d_h1,
               d_proj, sums, number, w_out, w_up, w_down, w_pred, slopes, total, unit1, sems):
    blocks = FF // CHUNK

    def fetch(k, start, width, dst):
        return pltpu.make_async_copy(rear.at[:, pl.ds(start, width)], dst, sems.at[k])

    def fetch_up(j):
        return fetch(1 + j, pl.multiple_of(D + j * CHUNK, CHUNK), CHUNK, w_up.at[j])

    def fetch_down(j):
        return fetch(1 + blocks + j, pl.multiple_of(D + FF + j * CHUNK, CHUNK), CHUNK, w_down.at[j])

    first = fetch(0, 0, D, w_out)
    first.start()
    for j in range(blocks):
        fetch_up(j).start()
        fetch_down(j).start()
    last = pltpu.make_async_copy(head.at[:, pl.ds(256, 256)], w_pred, sems.at[1 + 2 * blocks])
    last.start()
    first.wait()
    h1 = h0[...] + mm(mixed[...], w_out[...])
    low1, one, scale1 = plain_norm(h1, small[3:4, :], small[4:5, :])
    norm1[...] = low1
    unit1[...] = one
    total[...] = h1

    def forward(j, carry):
        fetch_up(j).wait()
        fetch_down(j).wait()
        up = mm(norm1[...], w_up[j])
        gate = 0.5 * (1.0 + lax.erf(up * (2.0**-0.5)))
        low = (up * gate).astype(bf16)
        slopes[j] = gate + up * jnp.exp(-0.5 * up * up) * 0.3989422804014327
        lifted[:, pl.ds(pl.multiple_of(j * CHUNK, CHUNK), CHUNK)] = low
        total[...] = total[...] + mm_t(low, w_down[j])
        return carry

    lax.fori_loop(0, blocks, forward, 0)
    low2, two, scale2 = plain_norm(total[...], small[5:6, :], small[6:7, :])
    norm2[...] = low2
    last.wait()
    error = mm(low2, w_pred[...]) * D ** (-0.5) - target[...]
    weighted = weight[...] * error
    number[...] = jnp.broadcast_to(jnp.sum(weighted * error, keepdims=True), (8, 128))
    low_pred = (weighted * ((2.0 * D ** (-0.5)) / stat[0:1, 0:1])).astype(bf16)
    d_pred[...] = low_pred
    d_h2, d_gain2, d_off2 = plain_norm_back(mm_t(low_pred, w_pred[...]), two, scale2, small[5:6, :])
    d_h1[...] = d_h2
    d_out[...] = d_h2.astype(bf16)
    total[...] = jnp.zeros_like(total)

    def backward(j, carry):
        low = (mm(d_out[...], w_down[j]) * slopes[j]).astype(bf16)
        d_up[:, pl.ds(pl.multiple_of(j * CHUNK, CHUNK), CHUNK)] = low
        total[...] = total[...] + mm_t(low, w_up[j])
        return carry

    lax.fori_loop(0, blocks, backward, 0)
    back, d_gain1, d_off1 = plain_norm_back(total[...], unit1[...], scale1, small[3:4, :])
    full = d_h1[...] + back
    d_h1[...] = full
    d_proj[...] = full.astype(bf16)
    sums[...] = jnp.concatenate([d_gain1, d_off1, d_gain2, d_off2, jnp.zeros((4, D), f32)], axis=0)


def mlp_block(mixed, h0, small, target, weight, stat, rear, head):
    vmem = pl.BlockSpec(memory_space=pltpu.VMEM)
    any_space = pl.BlockSpec(memory_space=pl.ANY)
    shape = jax.ShapeDtypeStruct
    blocks = FF // CHUNK
    return pl.pallas_call(
        mlp_kernel,
        out_shape=[
            shape((128, FF), bf16), shape((128, FF), bf16), shape((128, D), bf16), shape((128, D), bf16),
            shape((128, D), bf16), shape((128, 256), bf16), shape((128, D), f32), shape((128, D), bf16),
            shape((8, D), f32), shape((8, 128), f32),
        ],
        in_specs=[vmem] * 6 + [any_space] * 2,
        out_specs=[vmem] * 10,
        scratch_shapes=[
            pltpu.VMEM((D, D), bf16), pltpu.VMEM((blocks, D, CHUNK), bf16), pltpu.VMEM((blocks, D, CHUNK), bf16),
            pltpu.VMEM((D, 256), bf16), pltpu.VMEM((blocks, 128, CHUNK), f32), pltpu.VMEM((128, D), f32),
            pltpu.VMEM((128, D), f32), pltpu.SemaphoreType.DMA((2 * blocks + 2,)),
        ],
        compiler_params=pltpu.CompilerParams(vmem_limit_bytes=48 * 2**20),
        name="mlp_block",
    )(mixed, h0, small, target, weight, stat, rear, head)


def greet(dp, own):
    barrier = pltpu.get_barrier_semaphore()
    for d in range(1, 4):
        pl.semaphore_signal(barrier, inc=1, device_id=(dp, lax.rem(own + d, 4)), device_id_type=MESH)
    pl.semaphore_wait(barrier, 3)


def turned_softmax(parts, seg_col, seg_row, h):
    at = slice(h * HEAD_DIM, (h + 1) * HEAD_DIM)
    q, k, v = (parts[i, :, at] for i in range(3))
    score = lax.dot_general(k, q, (((1,), (1,)), ((), ())), preferred_element_type=f32) * HEAD_DIM ** (-0.5)
    score = jnp.where(seg_col[:, 0:1] == seg_row[0:1, :], score, -1000000000.0)
    power = jnp.exp(score - jnp.max(score, axis=0, keepdims=True))
    soft = power / jnp.sum(power, axis=0, keepdims=True)
    return q, k, v, soft, soft.astype(bf16)


def attend_kernel(qkv, seg_col, seg_row, norm0, mixed, mixed_t, parts_out, norm0_t, parts, turned, whole, gathered,
                  load_sem, in_send, in_recv, out_send, out_recv):
    dp, own = lax.axis_index("dp"), lax.axis_index("fsdp")
    greet(dp, own)
    row = pl.ds(pl.multiple_of(own * 128, 128), 128)

    def piece(i, to, g):
        return qkv.at[:, pl.ds(pl.multiple_of(i * D + to * 256 + g * 128, 128), 128)]

    def into(d, i, g):
        to = lax.rem(own + d, 4)
        return pltpu.make_async_remote_copy(
            src_ref=piece(i, to, g), dst_ref=parts.at[i, row, g * 128 : (g + 1) * 128], send_sem=in_send.at[d, i, g],
            recv_sem=in_recv.at[d, i, g], device_id=(dp, to), device_id_type=MESH,
        )

    def local_part(i, g):
        return pltpu.make_async_copy(piece(i, own, g), parts.at[i, row, g * 128 : (g + 1) * 128], load_sem.at[i, g])

    def back(d, g):
        to = lax.rem(own + d, 4)
        return pltpu.make_async_remote_copy(
            src_ref=whole.at[pl.ds(pl.multiple_of(to * 128, 128), 128), g * 128 : (g + 1) * 128],
            dst_ref=gathered.at[:, pl.ds(pl.multiple_of(own * 256 + g * 128, 128), 128)],
            send_sem=out_send.at[d, g], recv_sem=out_recv.at[d, g], device_id=(dp, to), device_id_type=MESH,
        )

    def keep(g):
        return pltpu.make_async_copy(
            whole.at[row, g * 128 : (g + 1) * 128],
            gathered.at[:, pl.ds(pl.multiple_of(own * 256 + g * 128, 128), 128)], load_sem.at[3, g],
        )

    for g in range(2):
        for i in range(3):
            for d in (2, 1, 3):
                into(d, i, g).start()
    for g in range(2):
        for i in range(3):
            local_part(i, g).start()
    norm0_t[...] = norm0[...].astype(f32).T.astype(bf16)
    for g in range(2):
        for i in range(3):
            local_part(i, g).wait()
            for d in range(1, 4):
                into(d, i, g).wait_recv()
        for h in (2 * g, 2 * g + 1):
            q, k, v, soft, share = turned_softmax(parts, seg_col, seg_row, h)
            turned[h * HEAD_DIM : (h + 1) * HEAD_DIM, :] = lax.dot_general(
                v, share, (((0,), (0,)), ((), ())), preferred_element_type=f32
            )
        whole[:, g * 128 : (g + 1) * 128] = turned[g * 128 : (g + 1) * 128, :].T.astype(bf16)
        for d in (2, 1, 3):
            back(d, g).start()
        keep(g).start()
    mixed_t[...] = turned[...].astype(bf16)
    parts_out[...] = parts[...]
    for g in range(2):
        keep(g).wait()
        for d in range(1, 4):
            back(d, g).wait_recv()
    mixed[...] = gathered[...]
    for g in range(2):
        for d in range(1, 4):
            back(d, g).wait_send()
            for i in range(3):
                into(d, i, g).wait_send()


def attend(qkv, seg_col, seg_row, norm0):
    vmem = pl.BlockSpec(memory_space=pltpu.VMEM)
    dma = pltpu.SemaphoreType.DMA
    return pl.pallas_call(
        attend_kernel,
        out_shape=[
            jax.ShapeDtypeStruct((128, D), bf16), jax.ShapeDtypeStruct((256, 512), bf16),
            jax.ShapeDtypeStruct((3, 512, 256), bf16), jax.ShapeDtypeStruct((D, 128), bf16),
        ],
        in_specs=[pl.BlockSpec(memory_space=pl.ANY), vmem, vmem, vmem],
        out_specs=[vmem] * 4,
        scratch_shapes=[
            pltpu.VMEM((3, 512, 256), bf16), pltpu.VMEM((256, 512), f32), pltpu.VMEM((512, 256), bf16),
            pltpu.VMEM((128, D), bf16), dma((4, 2)), dma((4, 3, 2)), dma((4, 3, 2)), dma((4, 2)), dma((4, 2)),
        ],
        compiler_params=pltpu.CompilerParams(collective_id=2, has_side_effects=True, vmem_limit_bytes=40 * 2**20),
        name="attend",
    )(qkv, seg_col, seg_row, norm0)


def attend_back_kernel(d_proj, rear, parts, seg_col, seg_row, norm1, d_out, norm2, d_own, d_parts_out, d_all_out,
                       norm1_t, out_t, norm2_t, every, proj, d_mixed,
                       d_parts, gathered, load_sem, up_send, up_recv, out_send, out_recv):
    dp, own = lax.axis_index("dp"), lax.axis_index("fsdp")
    x, core = own // 2, own % 2
    sibling, across, diagonal = x * 2 + 1 - core, (1 - x) * 2 + core, (1 - x) * 2 + 1 - core
    rows = pl.ds(pl.multiple_of(own * 256, 256), 256)
    fetch = pltpu.make_async_copy(rear.at[rows, pl.ds(0, D)], proj, load_sem.at[0, 0])
    fetch.start()
    row = pl.ds(pl.multiple_of(own * 128, 128), 128)
    mine = pltpu.make_async_copy(d_proj, every.at[row, :], load_sem.at[1, 0])
    mine.start()
    greet(dp, own)
    mine.wait()

    def up(i, who, slot, to):
        block = every.at[pl.ds(pl.multiple_of(who * 128, 128), 128), i * 512 : (i + 1) * 512]
        return pltpu.make_async_remote_copy(
            src_ref=block, dst_ref=block, send_sem=up_send.at[i, slot], recv_sem=up_recv.at[i, who],
            device_id=(dp, to), device_id_type=MESH,
        )

    for i in range(2):
        up(i, own, 0, across).start()
    for i in range(2):
        up(i, own, 1, sibling).start()
    for source, turned in ((norm1, norm1_t), (d_out, out_t), (norm2, norm2_t)):
        turned[...] = source[...].astype(f32).T.astype(bf16)
    for i in range(2):
        up(i, across, 0, own).wait_recv()
        up(i, across, 2, sibling).start()
    fetch.wait()
    for i in range(2):
        up(i, sibling, 1, own).wait_recv()
        up(i, diagonal, 2, own).wait_recv()
    d_mixed[...] = lax.dot_general(
        every[...], proj[...], (((1,), (1,)), ((), ())), preferred_element_type=f32
    ).astype(bf16)
    def column(i, g):
        return pl.ds(pl.multiple_of(i * D + own * 256 + g * 128, 128), 128)

    def back(d, i, g):
        to = lax.rem(own + d, 4)
        return pltpu.make_async_remote_copy(
            src_ref=d_parts.at[i, pl.ds(pl.multiple_of(to * 128, 128), 128), g * 128 : (g + 1) * 128],
            dst_ref=gathered.at[:, column(i, g)], send_sem=out_send.at[d, i, g], recv_sem=out_recv.at[d, i, g],
            device_id=(dp, to), device_id_type=MESH,
        )

    def keep(i, g):
        return pltpu.make_async_copy(
            d_parts.at[i, row, g * 128 : (g + 1) * 128], gathered.at[:, column(i, g)], load_sem.at[2 + i, g]
        )

    for g in range(2):
        for h in (2 * g, 2 * g + 1):
            at = slice(h * HEAD_DIM, (h + 1) * HEAD_DIM)
            q, k, v, soft, share = turned_softmax(parts, seg_col, seg_row, h)
            d_head = d_mixed[:, at]
            d_soft = lax.dot_general(v, d_head, (((1,), (1,)), ((), ())), preferred_element_type=f32)
            lean = jnp.sum(soft * d_soft, axis=0, keepdims=True)
            d_score = (soft * (d_soft - lean) * HEAD_DIM ** (-0.5)).astype(bf16)
            d_parts[2, :, at] = mm(share, d_head).astype(bf16)
            d_parts[1, :, at] = mm(d_score, q).astype(bf16)
            d_parts[0, :, at] = t_mm(d_score, k).astype(bf16)
        for i in range(3):
            for d in (2, 1, 3):
                back(d, i, g).start()
            keep(i, g).start()
    d_parts_out[...] = d_parts[...]
    d_all_out[...] = every[...]
    for g in range(2):
        for i in range(3):
            keep(i, g).wait()
            for d in range(1, 4):
                back(d, i, g).wait_recv()
    d_own[...] = gathered[...]
    for g in range(2):
        for d in range(1, 4):
            for i in range(3):
                back(d, i, g).wait_send()
    for i in range(2):
        for slot, who in ((0, own), (1, own), (2, across)):
            up(i, who, slot, own).wait_send()


def attend_back(d_proj, rear, parts, seg_col, seg_row, *features):
    vmem = pl.BlockSpec(memory_space=pltpu.VMEM)
    any_space = pl.BlockSpec(memory_space=pl.ANY)
    dma = pltpu.SemaphoreType.DMA
    return pl.pallas_call(
        attend_back_kernel,
        out_shape=[
            jax.ShapeDtypeStruct((128, 3 * D), bf16), jax.ShapeDtypeStruct((3, 512, 256), bf16),
            jax.ShapeDtypeStruct((512, D), bf16),
        ]
        + [jax.ShapeDtypeStruct((D, 128), bf16)] * 3,
        in_specs=[any_space, any_space] + [vmem] * 6,
        out_specs=[vmem] * 6,
        scratch_shapes=[
            pltpu.VMEM((512, D), bf16), pltpu.VMEM((256, D), bf16), pltpu.VMEM((512, 256), bf16),
            pltpu.VMEM((3, 512, 256), bf16), pltpu.VMEM((128, 3 * D), bf16),
            dma((5, 2)), dma((2, 3)), dma((2, 4)), dma((4, 3, 2)), dma((4, 3, 2)),
        ],
        compiler_params=pltpu.CompilerParams(collective_id=3, has_side_effects=True, vmem_limit_bytes=40 * 2**20),
        name="attend_back",
    )(d_proj, rear, parts, seg_col, seg_row, *features)


SEGMENTS = ((0, 2, 3), (2, 10, 1), (10, 18, 0), (18, 24, 2), (24, 26, 4))
N_STD, N_ALL, SHIFT, BASE = 26, 32, 1, 2


FAR = ({2: 0, 3: 1}, {0: 0, 1: 1})


def preds_at(preds, who):
    return preds.at[pl.ds(pl.multiple_of(who * 128, 128), 128), :]


def gradient_kernel(*refs):
    (norm1_t, out_t, norm0_t, mixed_t, mixa_t, norm2_t, agg_t,
     d_proj, d_parts, d_up, lifted, d_agg, d_pred, onehot, d_table, narrow, head, num_ref) = refs[:18]
    r_agg, r_attn, r_mlp, r_io, r_small, stat_ref = refs[18:24]
    (feats, ys, tabs, pairs, preds, hots, narrows, w240, wkv, acc240, own_buf, give_buf, got, rise, fall, far, tally,
     quad_buf, line_buf, load_sem, feat_send, feat_recv, y_xsend, y_xrecv, part_send, part_recv, tab_send, tab_recv, pred_send, pred_recv,
     nar_send, nar_recv, y_send, y_recv, z_send, z_recv, s_send, s_recv) = refs[24:]
    dp, own = lax.axis_index("dp"), lax.axis_index("fsdp")
    z, y, x, core = dp // 2, dp % 2, own // 2, own % 2
    sibling, across, diagonal = x * 2 + 1 - core, (1 - x) * 2 + core, (1 - x) * 2 + 1 - core
    over = z * 2 + 1 - y
    n = N_ALL
    row = pl.ds(pl.multiple_of(own * 128, 128), 128)
    sent_feats = {0: norm1_t, 1: out_t, 2: norm0_t, 4: mixa_t, 5: norm2_t, 6: agg_t}

    def remote(src, dst, send, recv, to):
        return pltpu.make_async_remote_copy(
            src_ref=src, dst_ref=dst, send_sem=send, recv_sem=recv, device_id=(dp, to), device_id_type=MESH
        )

    def feat_copy(k, d, half, to):
        side = y if half == 0 else 1 - y
        if k == 3:
            src, dst = mixed_t.at[side, to], feats.at[3, half, own]
        else:
            src, dst = sent_feats[k].at[:, side, to], feats.at[k, half, :, :, row]
        return remote(src, dst, feat_send.at[k, d, half], feat_recv.at[k, d, half], to)

    def feat_start(k):
        for d in (2, 1, 3):
            for half in range(2):
                feat_copy(k, d, half, lax.rem(own + d, 4)).start()

    def unit_block(c, who):
        return ys.at[c, pl.ds(pl.multiple_of(who * 128, 128), 128), :]

    def unit(c, who, slot, to):
        return remote(unit_block(c, who), unit_block(c, who), y_xsend.at[c, slot], y_xrecv.at[c, who], to)

    def part_block(i, who):
        return ys.at[18 + i * 2 + who // 2, :, pl.ds(pl.multiple_of((who % 2) * 256, 256), 256)]

    def part(i, who, slot, to):
        return remote(part_block(i, who), part_block(i, who), part_send.at[i, slot], part_recv.at[i, who], to)

    def table_raw(v, to):
        return remote(tabs.at[0, v], tabs.at[1, v], tab_send.at[v, 0], tab_recv.at[v, 0], to)

    def table(v, who, slot, to):
        return remote(pairs.at[who, v], pairs.at[who, v], tab_send.at[v, slot], tab_recv.at[v, 1 + who], to)

    def pred_copy(d, who, to):
        return remote(preds_at(preds, who), preds_at(preds, who), pred_send.at[d], pred_recv.at[d], to)

    def narrow_copy(d, who, to):
        return remote(narrows.at[who], narrows.at[who], nar_send.at[d], nar_recv.at[d], to)

    loads = {}

    def load(name, src, dst):
        copy = pltpu.make_async_copy(src, dst, load_sem.at[len(loads)])
        copy.start()
        loads[name] = copy

    def load_feat(k):
        for half in range(2):
            side = y if half == 0 else 1 - y
            if k == 3:
                load(("f", k, half), mixed_t.at[side, own], feats.at[3, half, own])
            else:
                load(("f", k, half), sent_feats[k].at[:, side, own], feats.at[k, half, :, :, row])

    def loaded(*names):
        for name in names:
            loads[name].wait()

    for c in range(2):
        load(("j", c), d_proj.at[:, pl.ds(c * CHUNK, CHUNK)], ys.at[c])
    load_feat(3)
    load_feat(1)
    for c in range(8):
        load(("u", 10 + c), d_up.at[:, pl.ds(c * CHUNK, CHUNK)], unit_block(10 + c, own))
    for c in range(8):
        load(("l", c), lifted.at[:, pl.ds(c * CHUNK, CHUNK)], ys.at[2 + c])
    load_feat(0)
    for i in range(3):
        load(("p", i), d_parts.at[i], part_block(i, own))
    load_feat(2)
    for c in range(2):
        load(("u", 24 + c), d_agg.at[:, pl.ds(c * CHUNK, CHUNK)], unit_block(24 + c, own))
    load_feat(4)
    for v in range(4):
        load(("t", v), d_table.at[pl.ds(v * CHUNK, CHUNK), :], tabs.at[0, v])
    load("pred", d_pred, preds_at(preds, own))
    load("narrow", narrow, narrows.at[own])
    for half in range(2):
        side = y if half == 0 else 1 - y
        load(("w", half), head.at[:, side, own, :, pl.ds(0, 256)], w240.at[half])
        load(("k", half), head.at[:, side, own, :, pl.ds(HEAD, 2 * D)], wkv.at[half])
    load_feat(5)
    load_feat(6)
    load("hot", onehot, hots)
    barrier = pltpu.get_barrier_semaphore()
    for d in range(1, 8):
        pl.semaphore_signal(barrier, inc=1, device_id=(lax.rem(dp + d, 8), own), device_id_type=MESH)
    for d in range(1, 4):
        pl.semaphore_signal(barrier, inc=1, device_id=(dp, lax.rem(own + d, 4)), device_id_type=MESH)
    pl.semaphore_wait(barrier, 10)
    feat_start(3)
    feat_start(1)
    feat_start(0)
    loaded(*[("u", 10 + c) for c in range(8)])

    def begin(c, carry):
        unit(c, own, 0, across).start()
        unit(c, own, 1, sibling).start()
        return carry

    lax.fori_loop(10, 18, begin, 0)
    feat_start(2)
    loaded(*[("p", i) for i in range(3)], ("u", 24), ("u", 25))
    for i in range(3):
        part(i, own, 0, across).start()
        part(i, own, 1, sibling).start()
    feat_start(4)
    lax.fori_loop(24, 26, begin, 0)
    loaded(*[("t", v) for v in range(4)], "pred", "narrow")
    for w in range(2):
        table_raw((1 - core) * 2 + w, sibling).start()
    tally[...] = jnp.zeros_like(tally)
    acc240[...] = jnp.zeros_like(acc240)
    for w in range(2):
        v = core * 2 + w
        table_raw(v, own).wait_recv()
        pairs[x, v] = (tabs[0, v].astype(f32) + tabs[1, v].astype(f32)).astype(bf16)
        table(v, x, 1, across).start()
        table(v, x, 2, sibling).start()
    feat_start(5)
    feat_start(6)
    for d in (2, 1, 3):
        pred_copy(d, own, lax.rem(own + d, 4)).start()
        narrow_copy(d, own, lax.rem(own + d, 4)).start()

    def feat_wait(k):
        for d in range(1, 4):
            for half in range(2):
                feat_copy(k, d, half, own).wait_recv()

    def put(c, value):
        own_buf[c] = value[:128]
        give_buf[c] = value[128:].astype(bf16)

    def feature(k):
        return feats[k].reshape(256, 512)

    def matmul(a, b):
        return lax.dot_general(a, b, (((1,), (0,)), ((), ())), preferred_element_type=f32)

    def two(value):
        high = value.astype(bf16)
        return high, (value - high.astype(f32)).astype(bf16)

    def summed_table(v):
        return two(pairs[0, v].astype(f32) + pairs[1, v].astype(f32))

    def compute(c):
        for i in range(3):
            @pl.when(c == 18 + i * 2)
            def _():
                part(i, sibling, 1, own).wait_recv()
                part(i, diagonal, 2, own).wait_recv()

        for low, high, k in SEGMENTS:
            @pl.when(c == low)
            def _():
                feat_wait(k)
                loaded(("f", k, 0), ("f", k, 1))
                if k == 3:
                    loaded(("j", 0), ("j", 1))
                if k == 1:
                    loaded(*[("l", i) for i in range(8)])

            @pl.when((c >= low) & (c < high))
            def _():
                if k in (0, 4):
                    unit(c, sibling, 1, own).wait_recv()
                    unit(c, diagonal, 2, own).wait_recv()
                put(c, matmul(feature(k), ys[c]))

        @pl.when(c == N_STD)
        def _():
            loaded(("w", 0), ("w", 1), ("k", 0), ("k", 1))

        @pl.when((c >= N_STD) & (c < N_STD + 4))
        def _():
            v = c - N_STD

            @pl.when(v // 2 != core)
            def _():
                table(v, x, 2, own).wait_recv()
                table(v, 1 - x, 3, own).wait_recv()

            high, low = summed_table(v)
            rows = w240[...].reshape(256, 256)
            dims = (((1,), (1,)), ((), ()))
            put(
                c,
                lax.dot_general(rows, high, dims, preferred_element_type=f32)
                + lax.dot_general(rows, low, dims, preferred_element_type=f32),
            )

        for v in range(4):
            @pl.when(c == N_STD + v)
            def _():
                high, low = summed_table(v)
                rows = wkv[:, :, :, v * CHUNK : (v + 1) * CHUNK].reshape(256, CHUNK)
                acc240[...] = acc240[...] + matmul(rows, high) + matmul(rows, low)

        @pl.when(c == N_STD + 4)
        def _():
            feat_wait(5)
            loaded(("f", 5, 0), ("f", 5, 1))
            for d in range(1, 4):
                pred_copy(d, lax.rem(own + 4 - d, 4), own).wait_recv()
            value = matmul(feature(5), preds[...])
            own_buf[c, :, 0:256] = acc240[:128]
            own_buf[c, :, 256:512] = value[:128]
            give_buf[c, :, 0:256] = acc240[128:].astype(bf16)
            give_buf[c, :, 256:512] = value[128:].astype(bf16)

        @pl.when(c == N_STD + 5)
        def _():
            feat_wait(6)
            loaded(("f", 6, 0), ("f", 6, 1), "hot")
            for d in range(1, 4):
                narrow_copy(d, lax.rem(own + 4 - d, 4), own).wait_recv()
            value = matmul(feature(6), hots[...])
            place = lax.broadcasted_iota(jnp.int32, (256, D), 0)
            source = lax.broadcasted_iota(jnp.int32, (256, D), 1)
            side = jnp.where(place < 128, y, 1 - y)
            wanted = ((place >> 5) & 3) * 256 + side * 128 + own * STRIP + (place & 31)
            choose = jnp.where(source == wanted, 1.0, 0.0).astype(bf16)
            total = (narrows[0] + narrows[1]) + (narrows[2] + narrows[3])
            total = jnp.concatenate([total, jnp.zeros((112, D), f32)], axis=0)
            high = total.astype(bf16)
            rest = total - high.astype(f32)
            middle = rest.astype(bf16)
            low = (rest - middle.astype(f32)).astype(bf16)
            dims = (((1,), (1,)), ((), ()))
            small = (
                lax.dot_general(choose, high, dims, preferred_element_type=f32)
                + lax.dot_general(choose, middle, dims, preferred_element_type=f32)
                + lax.dot_general(choose, low, dims, preferred_element_type=f32)
            )
            empty = jnp.zeros((128, 128), f32)
            own_buf[c, :, 0:256] = value[:128]
            own_buf[c, :, 256:384] = small[:128]
            own_buf[c, :, 384:512] = empty
            give_buf[c, :, 0:256] = value[128:].astype(bf16)
            give_buf[c, :, 256:384] = small[128:].astype(bf16)
            give_buf[c, :, 384:512] = empty.astype(bf16)

    def cross(c):
        return pltpu.make_async_remote_copy(
            src_ref=give_buf.at[c], dst_ref=got.at[c], send_sem=y_send.at[c],
            recv_sem=y_recv.at[c], device_id=(over, own), device_id_type=MESH,
        )

    def hop(buf, way, c, b, to):
        at = b - 1 if way == 0 else b
        return pltpu.make_async_remote_copy(
            src_ref=buf.at[c, at], dst_ref=buf.at[c, at], send_sem=z_send.at[way, c, at], recv_sem=z_recv.at[way, c, at],
            device_id=(to * 2 + y, own), device_id_type=MESH,
        )

    def far_hop(way, c, b, to):
        at = FAR[way][b]
        return pltpu.make_async_remote_copy(
            src_ref=far.at[way, c, at], dst_ref=far.at[way, c, at], send_sem=z_send.at[way, c, 3 + at],
            recv_sem=z_recv.at[way, c, 3 + at], device_id=(to * 2 + y, own), device_id_type=MESH,
        )

    def here(c, b):
        at = pl.ds(b * STRIP, STRIP)
        return own_buf[c, at, :] + got[c, at, :].astype(f32)

    early, late = LAG * jnp.minimum(z, 3 - z), LAG * jnp.maximum(z, 3 - z)

    def step(t, carry):
        @pl.when((t >= 4) & (t < 12))
        def _():
            unit(t + 6, across, 0, own).wait_recv()
            unit(t + 6, across, 2, sibling).start()

        for i in range(3):
            @pl.when(t == 14 + 2 * i)
            def _():
                part(i, across, 0, own).wait_recv()
                part(i, across, 2, sibling).start()

        @pl.when((t == 20) | (t == 21))
        def _():
            unit(t + 4, across, 0, own).wait_recv()
            unit(t + 4, across, 2, sibling).start()

        @pl.when((t == 24) | (t == 25))
        def _():
            v = core * 2 + t - 24
            table(v, 1 - x, 1, own).wait_recv()
            table(v, 1 - x, 3, sibling).start()

        @pl.when((t >= SHIFT) & (t < n + SHIFT))
        def _():
            compute(t - SHIFT)
            cross(t - SHIFT).start()

        first = t - SHIFT - BASE - early

        @pl.when((first >= 0) & (first < n))
        def _():
            cross(first).wait()

        for way, buf, lag, to, back in ((0, rise, LAG * z, z + 1, z - 1), (1, fall, LAG * (3 - z), z - 1, z + 1)):
            c = t - SHIFT - BASE - lag

            @pl.when((c >= 0) & (c < n))
            def _():
                for b in ((1, 2, 3) if way == 0 else (0, 1, 2)):
                    beyond = (b > z) if way == 0 else (b < z)
                    at = b - 1 if way == 0 else b

                    @pl.when(beyond & (lag == 0))
                    def _():
                        if b == (1 if way == 0 else 2):
                            buf[c, at] = here(c, b)
                        else:
                            far[way, c, FAR[way][b]] = here(c, b).astype(bf16)

                    @pl.when(beyond & (lag > 0))
                    def _():
                        if b == (1 if way == 0 else 2):
                            hop(buf, way, c, b, back).wait_recv()
                            buf[c, at] = buf[c, at] + here(c, b)
                        else:
                            @pl.when(lag == LAG)
                            def _():
                                far_hop(way, c, b, back).wait_recv()
                                buf[c, at] = far[way, c, FAR[way][b]].astype(f32) + here(c, b)

                            @pl.when(lag > LAG)
                            def _():
                                hop(buf, way, c, b, back).wait_recv()
                                buf[c, at] = buf[c, at] + here(c, b)

                    def send(c, act):
                        if b == (1 if way == 0 else 2):
                            copy = hop(buf, way, c, b, to)
                            copy.start() if act else copy.wait_send()
                        else:
                            @pl.when(lag == 0)
                            def _():
                                copy = far_hop(way, c, b, to)
                                copy.start() if act else copy.wait_send()

                            @pl.when(lag > 0)
                            def _():
                                copy = hop(buf, way, c, b, to)
                                copy.start() if act else copy.wait_send()

                    @pl.when(beyond & (c >= QUEUE))
                    def _():
                        send(c - QUEUE, False)

                    @pl.when(beyond)
                    def _():
                        send(c, True)

        last = t - SHIFT - BASE - late

        @pl.when((last >= 0) & (last < n))
        def _():
            at = pl.ds(pl.multiple_of(z * STRIP, STRIP), STRIP)
            value = own_buf[last, at, :] + got[last, at, :].astype(f32)
            own_buf[last, 0:STRIP, :] = value

            @pl.when(z > 0)
            def _():
                hop(rise, 0, last, z, z - 1).wait_recv()
                own_buf[last, 0:STRIP, :] = own_buf[last, 0:STRIP, :] + rise[last, z - 1]

            @pl.when(z < 3)
            def _():
                hop(fall, 1, last, z, z + 1).wait_recv()
                own_buf[last, 0:STRIP, :] = own_buf[last, 0:STRIP, :] + fall[last, z]

            value = own_buf[last, 0:STRIP, :]
            square = value * value
            total = square[0:8, 0:128]
            for r in range(0, STRIP, 8):
                for k in range(0, CHUNK, 128):
                    if r or k:
                        total = total + square[r : r + 8, k : k + 128]
            tally[...] = tally[...] + total

        return carry

    lax.fori_loop(0, n + SHIFT + BASE + 3 * LAG, step, 0)
    summed = jnp.sum(tally[...])
    lane = lax.broadcasted_iota(jnp.int32, (8, 128), 1)
    quad_buf[own] = jnp.where(lane == 0, summed, jnp.where(lane == 1, num_ref[...], 0.0))

    def share(buf, k, where, at):
        return pltpu.make_async_remote_copy(
            src_ref=buf.at[at], dst_ref=buf.at[at], send_sem=s_send.at[k], recv_sem=s_recv.at[k],
            device_id=where, device_id_type=MESH,
        )

    for d in range(1, 4):
        share(quad_buf, d, (dp, lax.rem(own + d, 4)), own).start()
    for out, base, low, high in (
        (r_attn, 3 * D, 0, 2), (r_mlp, FF, 2, 10), (r_mlp, 0, 10, 18), (r_attn, 0, 18, 24), (r_agg, 2 * D, 24, 26), (r_agg, 0, 26, 30),
    ):
        for c in range(low, high):
            out[:, base + (c - low) * CHUNK : base + (c - low + 1) * CHUNK] = own_buf[c, 0:STRIP, :]
    left, right = own_buf[30, 0:STRIP, :], own_buf[31, 0:STRIP, :]
    r_io[:, 0:WIDTH] = left[:, 0:WIDTH]
    r_io[:, WIDTH : 2 * WIDTH] = left[:, 256 : 256 + WIDTH]
    r_io[:, 2 * WIDTH : 2 * WIDTH + VARS] = left[:, WIDTH : WIDTH + VARS]
    r_io[:, 2 * WIDTH + VARS : 2 * WIDTH + VARS + SPAN] = right[:, 0:SPAN]
    r_io[:, 2 * WIDTH + VARS + SPAN :] = jnp.zeros((STRIP, r_io.shape[1] - 2 * WIDTH - VARS - SPAN), f32)
    r_small[...] = right[:, 256:384].T[:16]
    for d in range(1, 4):
        share(quad_buf, d, (dp, own), lax.rem(own + 4 - d, 4)).wait_recv()
    line_buf[dp] = (quad_buf[0] + quad_buf[1]) + (quad_buf[2] + quad_buf[3])
    for d in range(1, 8):
        share(line_buf, 3 + d, (lax.rem(dp + d, 8), own), dp).start()
    for d in range(1, 8):
        share(line_buf, 3 + d, (dp, own), lax.rem(dp + 8 - d, 8)).wait_recv()
    stat = line_buf[0]
    for d in range(1, 8):
        stat = stat + line_buf[d]
    stat_ref[...] = stat
    for d in range(1, 4):
        share(quad_buf, d, (dp, own), own).wait_send()
    for d in range(1, 8):
        share(line_buf, 3 + d, (dp, own), dp).wait_send()
    for d in range(1, 4):
        for k in range(7):
            for half in range(2):
                feat_copy(k, d, half, own).wait_send()
        pred_copy(d, own, own).wait_send()
        narrow_copy(d, own, own).wait_send()
    for w in range(2):
        table_raw((1 - core) * 2 + w, own).wait_send()
        for slot, who in ((1, x), (2, x), (3, 1 - x)):
            table(core * 2 + w, who, slot, own).wait_send()
    relays = ((0, own), (1, own), (2, across))
    for i in range(3):
        for slot, who in relays:
            part(i, who, slot, own).wait_send()

    def finish(c, carry):
        for slot, who in relays:
            unit(c, who, slot, own).wait_send()
        return carry

    lax.fori_loop(10, 18, finish, 0)
    lax.fori_loop(24, 26, finish, 0)

    def drain(c, carry):
        for way, buf, inner, outer in ((0, rise, z > 0, z == 0), (1, fall, z < 3, z == 3)):
            for b in ((1, 2, 3) if way == 0 else (0, 1, 2)):
                beyond = (b > z) if way == 0 else (b < z)
                if b == (1 if way == 0 else 2):
                    pl.when(beyond)(lambda: hop(buf, way, c, b, z).wait_send())
                else:
                    pl.when(beyond & inner)(lambda: hop(buf, way, c, b, z).wait_send())
                    pl.when(beyond & outer)(lambda: far_hop(way, c, b, z).wait_send())
        return carry

    lax.fori_loop(n - QUEUE, n, drain, 0)


def gradient_blocks(operands, numbers):
    any_space = pl.BlockSpec(memory_space=pl.ANY)
    vmem = pl.BlockSpec(memory_space=pltpu.VMEM)
    n = N_ALL
    dma = pltpu.SemaphoreType.DMA
    widths = (3 * D, 4 * D, 2 * FF, 944)
    return pl.pallas_call(
        gradient_kernel,
        out_shape=[jax.ShapeDtypeStruct((STRIP, w), f32) for w in widths]
        + [jax.ShapeDtypeStruct((16, STRIP), f32), jax.ShapeDtypeStruct((8, 128), f32)],
        in_specs=[any_space] * 17 + [vmem],
        out_specs=[vmem] * 6,
        scratch_shapes=[
            pltpu.VMEM((7, 2, 4, STRIP, 512), bf16),
            pltpu.VMEM((N_STD, 512, CHUNK), bf16),
            pltpu.VMEM((2, 4, CHUNK, 256), bf16),
            pltpu.VMEM((2, 4, CHUNK, 256), bf16),
            pltpu.VMEM((512, 256), bf16),
            pltpu.VMEM((512, 256), bf16),
            pltpu.VMEM((4, 16, D), f32),
            pltpu.VMEM((2, 4, STRIP, 256), bf16),
            pltpu.VMEM((2, 4, STRIP, 2 * D), bf16),
            pltpu.VMEM((256, 256), f32),
            pltpu.VMEM((n, 4 * STRIP, CHUNK), f32),
            pltpu.VMEM((n, 4 * STRIP, CHUNK), bf16),
            pltpu.VMEM((n, 4 * STRIP, CHUNK), bf16),
            pltpu.VMEM((n, 3, STRIP, CHUNK), f32),
            pltpu.VMEM((n, 3, STRIP, CHUNK), f32),
            pltpu.VMEM((2, n, 2, STRIP, CHUNK), bf16),
            pltpu.VMEM((8, 128), f32),
            pltpu.VMEM((4, 8, 128), f32),
            pltpu.VMEM((8, 8, 128), f32),
            dma((56,)),
            dma((7, 4, 2)),
            dma((7, 4, 2)),
            dma((N_STD, 3)),
            dma((N_STD, 4)),
            dma((3, 3)),
            dma((3, 4)),
            dma((4, 4)),
            dma((4, 3)),
            dma((4,)),
            dma((4,)),
            dma((4,)),
            dma((4,)),
            dma((n,)),
            dma((n,)),
            dma((2, n, 5)),
            dma((2, n, 5)),
            dma((11,)),
            dma((11,)),
        ],
        compiler_params=pltpu.CompilerParams(
            collective_id=1, has_side_effects=True, vmem_limit_bytes=62 * 2**20
        ),
        name="gradient_blocks",
    )(*operands, numbers)


def ag(part):
    return lax.all_gather(part, "fsdp", axis=0, tiled=True)


def make_local(n_dp, n_f):
    fast = n_dp == 8 and n_f == 4

    def local(
        pixels, targets, valid_mask, lat_weight, segment_ids, present_vars, lead_index, step_count,
        w_agg, w_attn, w_mlp, w_io, w_small,
        m_agg, m_attn, m_mlp, m_io, m_small,
        v_agg, v_attn, v_mlp, v_io, v_small,
    ):
        masters = (w_agg, w_attn, w_mlp, w_io, w_small)
        firsts = (m_agg, m_attn, m_mlp, m_io, m_small)
        seconds = (v_agg, v_attn, v_mlp, v_io, v_small)
        rows = pixels.shape[1]
        row_len = segment_ids.shape[1]
        strip = w_agg.shape[0]
        own = lax.axis_index("fsdp")
        heads_here = HEADS // n_f
        wide = heads_here * HEAD_DIM

        seg = segment_ids[0]
        below = jnp.sum((seg[None, :] < seg[:, None]).astype(jnp.int32), axis=1)
        pos = jnp.arange(row_len, dtype=jnp.int32) - below
        onehot_all = (pos[:, None] == jnp.arange(SPAN, dtype=jnp.int32)[None, :]).astype(bf16)
        onehot = lax.dynamic_slice_in_dim(onehot_all, own * rows, rows)
        lead = (lead_index[0].astype(f32) + 1.0) / LEAD_STEPS
        pixel_rows = pixels[0]
        target = targets[0].astype(f32)
        present = present_vars[0]
        spread = (jnp.arange(MIX) // PIX)[None, :] == jnp.arange(VARS)[:, None]
        embed_col = (jnp.arange(MIX) - WIDTH)[None, :] == jnp.arange(VARS)[:, None]
        in_pixels = (jnp.arange(MIX) < WIDTH)[None, :]
        expand = jnp.where(in_pixels, spread, embed_col).astype(bf16)
        present_cols = jnp.repeat(present.astype(f32), PIX)
        pixel_weight = lat_weight[0][:, None] * valid_mask[0].astype(f32) * present_cols[None, :]
        weight_sum = jnp.sum(pixel_weight)

        emb = 2 * WIDTH + VARS
        if fast:
            rear = jnp.concatenate([w_attn[:, 3 * D :], w_mlp], axis=1).astype(bf16)
            rear = lax.all_gather(rear, ("dp", "fsdp"), axis=0, tiled=True)
            head, w_qkv, small, stat = gather_weights(
                w_io, w_small, w_agg, w_attn, jnp.full((8, 128), weight_sum, f32)
            )
            total = stat[0, 0]
        else:

            def blank(width):
                return jnp.zeros((strip, width), bf16)

            io_low = w_io.astype(bf16)
            pack = jnp.concatenate(
                [
                    io_low[:, :WIDTH],
                    io_low[:, 2 * WIDTH : emb],
                    blank(MIX - WIDTH - VARS),
                    io_low[:, WIDTH : 2 * WIDTH],
                    blank(256 - WIDTH),
                    io_low[:, emb : emb + SPAN],
                    w_small.astype(bf16),
                    blank(128 - w_small.shape[1]),
                    w_agg.astype(bf16),
                ],
                axis=1,
            )
            head = lax.all_gather(pack, ("dp", "fsdp"), axis=0, tiled=True)
            attn = lax.all_gather(w_attn.astype(bf16), ("dp", "fsdp"), axis=0, tiled=True)
            mlp = lax.all_gather(w_mlp.astype(bf16), ("dp", "fsdp"), axis=0, tiled=True)
            w_qkv = attn[:, : 3 * D]
            rear = jnp.concatenate([attn[:, 3 * D :], mlp], axis=1)
            total = lax.psum(weight_sum, ("dp", "fsdp"))
        w240 = head[:, :MIX]
        w_pred = head[:, 256 : 256 + WIDTH]
        w_pos = head[:, 512 : 512 + SPAN]
        if not fast:
            small = head[:, 768:777].astype(f32).T
        agg_kv = head[:, HEAD : HEAD + 2 * D]
        agg_out = head[:, HEAD + 2 * D :]
        w_out = rear[:, :D]
        w_up = rear[:, D : D + FF]
        w_down = rear[:, D + FF :]

        pix_t = jnp.concatenate(
            [pixel_rows.T, jnp.ones((VARS, rows), bf16), jnp.zeros((MIX - WIDTH - VARS, rows), bf16)], axis=0
        )
        table = t_mm(agg_kv, w240)
        table_k = table[:D].reshape(HEADS, HEAD_DIM, MIX)
        table_v = table[D:].reshape(HEADS, HEAD_DIM, MIX)
        query = small[0].reshape(HEADS, HEAD_DIM)
        folded = jnp.sum(table_k * query[:, :, None], axis=1)
        block = folded[:, None, :] * expand.astype(f32)[None]
        score = exact("xc,cl->xl", block.reshape(HEADS * VARS, MIX), pix_t.astype(f32))
        score = score.reshape(HEADS, VARS, rows) * HEAD_DIM ** (-0.5)
        score = jnp.where(present[None, :, None] > 0, score, -1000000000.0)
        top = jnp.max(score, axis=1, keepdims=True)
        power = jnp.exp(score - top)
        soft = power / jnp.sum(power, axis=1, keepdims=True)
        share = soft.astype(bf16)
        pix_f = pix_t.astype(f32)
        lifted_share = jnp.einsum("vc,hvl->hcl", expand, share, preferred_element_type=f32) * pix_f[None]
        mixed_a = exact("hec,hcl->hel", table_v, lifted_share).reshape(D, rows).astype(bf16)
        lead_embed = lead * small[7] + small[8]
        h0 = t_mm(mixed_a, agg_out) + mm_t(onehot, w_pos) + lead_embed[None]
        norm0, unit0, scale0 = norm_forward(h0, small[1], small[2])
        qkv = mm(norm0, w_qkv).astype(bf16)
        if fast:
            seg_col = jnp.broadcast_to(seg[:, None], (row_len, 128))
            seg_row = jnp.broadcast_to(seg[None, :], (8, row_len))
            mixed, mixed_t, parts, norm0_t = attend(qkv, seg_col, seg_row, norm0)
        else:
            part = qkv.reshape(rows, 3, n_f, wide)
            part = lax.all_to_all(part, "fsdp", split_axis=2, concat_axis=0, tiled=True)
            part = part.reshape(row_len, 3, heads_here, HEAD_DIM)
            q, k, v = (part[:, i].transpose(1, 0, 2) for i in range(3))
            att_score = jnp.einsum("hqe,hke->hqk", q, k, preferred_element_type=f32) * HEAD_DIM ** (-0.5)
            same = seg[:, None] == seg[None, :]
            att_score = jnp.where(same[None], att_score, -1000000000.0)
            att_top = jnp.max(att_score, axis=-1, keepdims=True)
            att_power = jnp.exp(att_score - att_top)
            att_soft = att_power / jnp.sum(att_power, axis=-1, keepdims=True)
            att = att_soft.astype(bf16)
            mixed_h = jnp.einsum("hqk,hke->qhe", att, v, preferred_element_type=f32)
            mixed_h = mixed_h.reshape(row_len, wide).astype(bf16)
            mixed_all = lax.all_gather(mixed_h, "fsdp", axis=1, tiled=True)
            mixed = lax.dynamic_slice_in_dim(mixed_all, own * rows, rows, axis=0)
        if fast:
            lane_gap = ((0, 0), (0, 256 - WIDTH))
            lifted, d_up, norm1, norm2, d_out, d_pred, d_h1, d_proj, sums, number = mlp_block(
                mixed, h0, small, jnp.pad(target, lane_gap), jnp.pad(pixel_weight, lane_gap), stat, rear, head
            )
            lifted_all = ag(lifted)
            d_gain1, d_off1, d_gain2, d_off2 = (sums[i] for i in range(4))
            numerator = number[0, 0]
        else:
            h1 = h0 + mm(mixed, w_out)
            norm1, unit1, scale1 = norm_forward(h1, small[3], small[4])
            up = mm(norm1, w_up)
            gate = 0.5 * (1.0 + lax.erf(up * (2.0**-0.5)))
            lifted = (up * gate).astype(bf16)
            lifted_all = ag(lifted)
            h2 = h1 + mm_t(lifted, w_down)
            norm2, unit2, scale2 = norm_forward(h2, small[5], small[6])
            predicted = mm(norm2, w_pred) * D ** (-0.5)
            error = predicted - target
            weighted = pixel_weight * error
            numerator = jnp.sum(weighted * error)

            d_pred = (weighted * (2.0 * D ** (-0.5) / total)).astype(bf16)
            d_norm2 = mm_t(d_pred, w_pred)
            d_h2, d_gain2, d_off2 = norm_backward(d_norm2, unit2, scale2, small[5])
            d_out = d_h2.astype(bf16)
            slope = gate + up * jnp.exp(-0.5 * up * up) * 0.3989422804014327
            d_up = (mm(d_out, w_down) * slope).astype(bf16)
            d_norm1 = mm_t(d_up, w_up)
            d_in, d_gain1, d_off1 = norm_backward(d_norm1, unit1, scale1, small[3])
            d_h1 = d_h2 + d_in
        if fast:
            d_qkv, d_parts, d_proj_all, norm1_t, out_t, norm2_t = attend_back(
                d_proj, rear, parts, seg_col, seg_row, norm1, d_out, norm2
            )
        else:
            d_proj_all = ag(d_h1.astype(bf16))
            w_out_own = lax.dynamic_slice_in_dim(w_out, own * wide, wide, axis=0)
            d_mixed = mm_t(d_proj_all, w_out_own).astype(bf16).reshape(row_len, heads_here, HEAD_DIM).transpose(1, 0, 2)
            d_att = jnp.einsum("hqe,hke->hqk", d_mixed, v, preferred_element_type=f32)
            d_v = jnp.einsum("hqk,hqe->khe", att, d_mixed, preferred_element_type=f32)
            lean = jnp.sum(att_soft * d_att, axis=-1, keepdims=True)
            d_score = (att_soft * (d_att - lean) * HEAD_DIM ** (-0.5)).astype(bf16)
            d_q = jnp.einsum("hqk,hke->qhe", d_score, k, preferred_element_type=f32)
            d_k = jnp.einsum("hqk,hqe->khe", d_score, q, preferred_element_type=f32)
            d_part = jnp.stack([d_q, d_k, d_v], axis=1).astype(bf16).reshape(row_len, 3, 1, wide)
            d_qkv_all = lax.all_gather(d_part, "fsdp", axis=2, tiled=True).reshape(row_len, 3 * D)
            d_qkv = lax.dynamic_slice_in_dim(d_qkv_all, own * rows, rows, axis=0)
        d_norm0 = mm_t(d_qkv, w_qkv)
        d_in, d_gain0, d_off0 = norm_backward(d_norm0, unit0, scale0, small[1])
        d_h0 = d_h1 + d_in
        d_agg = d_h0.astype(bf16)
        d_mixed_a = mm_t(agg_out, d_agg).astype(bf16).reshape(HEADS, HEAD_DIM, rows)
        pulled = exact("hec,hel->hcl", table_v, d_mixed_a.astype(f32)) * pix_f[None]
        d_share = exact("vc,hcl->hvl", expand.astype(f32), pulled)
        lean_a = jnp.sum(soft * d_share, axis=1, keepdims=True)
        d_score_a = (soft * (d_share - lean_a) * HEAD_DIM ** (-0.5)).astype(bf16)
        spread_score = jnp.einsum("vc,hvl->hcl", expand, d_score_a, preferred_element_type=f32)
        d_folded = jnp.sum(spread_score * pix_f[None], axis=2)
        d_table_v = exact("hel,hcl->hec", d_mixed_a.astype(f32), lifted_share).reshape(D, MIX)
        d_table_k = (query[:, :, None] * d_folded[:, None, :]).reshape(D, MIX)
        d_query = jnp.sum(d_folded[:, None, :] * table_k, axis=2).reshape(D)
        d_bias = jnp.sum(d_h0, axis=0)
        narrow = jnp.stack(
            [d_query, d_gain0, d_off0, d_gain1, d_off1, d_gain2, d_off2, lead * d_bias, d_bias]
            + [jnp.zeros((D,), f32)] * 7
        )
        d_table = jnp.concatenate([d_table_k, d_table_v], axis=0)
        if fast:

            def sorted_rows(array):
                return array.reshape(4, 2, n_f, strip, array.shape[1])

            lane = lax.broadcasted_iota(jnp.int32, (8, 128), 1)
            r_agg, r_attn, r_mlp, r_io, r_small, stat = gradient_blocks(
                [sorted_rows(part) for part in (norm1_t, out_t, norm0_t)]
                + [mixed_t.reshape(2, n_f, strip, row_len)]
                + [sorted_rows(part) for part in (mixed_a, norm2_t, d_agg.T)]
                + [d_proj_all, d_parts, d_up, lifted_all, d_agg, d_pred]
                + [onehot_all, d_table.astype(bf16), narrow, sorted_rows(head)],
                jnp.where(lane == 1, numerator, 0.0),
            )
            r_small = r_small[:9].T
            squares, numerator = stat[0, 0], stat[0, 1]
        else:
            d_table, narrow = lax.psum((d_table, narrow), "fsdp")
            source = jnp.arange(D)
            pick = (source // strip) % n_f == own
            place = (source // (strip * n_f)) * strip + source % strip
            choose = (pick[:, None] & (place[:, None] == jnp.arange(n_dp * strip)[None, :])).astype(bf16)

            def mine(array):
                whole = array.reshape(n_dp, n_f, strip, array.shape[1])
                return lax.dynamic_index_in_dim(whole, own, 1, False).reshape(n_dp * strip, array.shape[1])

            def weight_grad(features, grads):
                return t_mm(mm(features, choose).astype(bf16), grads)

            def gap(width):
                return jnp.zeros((n_dp * strip, width), f32)

            d_agg_all = ag(d_agg)
            g_kv = exact("dc,xc->dx", mine(w240).astype(f32), d_table)
            g_240 = exact("dx,xc->dc", mine(agg_kv).astype(f32), d_table)
            groups = (
                (g_kv, weight_grad(ag(mixed_a.T), d_agg_all)),
                (weight_grad(ag(norm0), d_qkv_all), weight_grad(mixed_all, d_proj_all)),
                (weight_grad(ag(norm1), ag(d_up)), weight_grad(ag(d_out), lifted_all)),
                (
                    g_240, weight_grad(ag(norm2), ag(d_pred)), gap(256 - WIDTH),
                    weight_grad(d_agg_all, onehot_all), mine(narrow.T)[:, :9], gap(256 - 9),
                ),
            )
            r_agg, r_attn, r_mlp, r_misc = (
                lax.psum_scatter(jnp.concatenate(g, axis=1), "dp", scatter_dimension=0, tiled=True) for g in groups
            )
            local_squares = sum(jnp.sum(piece * piece) for piece in (r_agg, r_attn, r_mlp, r_misc))
            squares, numerator = lax.psum((local_squares, numerator), ("dp", "fsdp"))
            r_io = jnp.concatenate(
                [
                    r_misc[:, :WIDTH], r_misc[:, 256 : 256 + WIDTH], r_misc[:, WIDTH : WIDTH + VARS],
                    r_misc[:, 512 : 512 + SPAN], jnp.zeros((strip, w_io.shape[1] - emb - SPAN), f32),
                ],
                axis=1,
            )
            r_small = r_misc[:, 768:777]
        reduced = (r_agg, r_attn, r_mlp, r_io, r_small)
        grad_norm = jnp.sqrt(squares)
        factor = jnp.minimum(1.0, clip_limit / grad_norm)
        loss = numerator / total
        step_value = step_count[0].astype(f32)
        results = [
            adamw(masters[i], reduced[i] * factor, firsts[i], seconds[i], step_value, learn_rates[i]) for i in range(5)
        ]
        return (loss, grad_norm) + tuple(results[i][j] for j in range(4) for i in range(5))

    return local


def solution(mesh):
    flat = P(("dp", "fsdp"), None)
    tokens = P("dp", "fsdp", None)
    return jax.shard_map(
        make_local(mesh.shape["dp"], mesh.shape["fsdp"]),
        mesh=mesh,
        in_specs=(tokens, tokens, tokens, P("dp", "fsdp"), P("dp", None), P("dp", None), P("dp"), P()) + (flat,) * 15,
        out_specs=(P(), P()) + (flat,) * 20,
        check_vma=False,
    )
```

```python
import functools

import jax
import jax.numpy as jnp
from jax import lax
from jax.experimental import pallas as pl
from jax.experimental.pallas import tpu as pltpu
from jax.sharding import PartitionSpec as P

D = 1024
HEADS = 16
HEAD_DIM = 64
FF = 4096
VARS = 48
PIX = 4
LEAD_STEPS = 8
WIDTH = VARS * PIX
SPAN = 256
MIX = 256
HEAD = 896

norm_eps = 1e-05
clip_limit = 1.0
decay_rate = 0.05
adam_eps = 1e-08
learn_rates = (0.03, 0.03, 0.03, 0.2, 0.3)
f32 = jnp.float32
bf16 = jnp.bfloat16
highest = lax.Precision.HIGHEST
MESH = pl.DeviceIdType.MESH
STRIP = 32
CHUNK = 512
LAG = 2
QUEUE = 2


def dot(left, right, dims):
    return lax.dot_general(left, right, (dims, ((), ())), preferred_element_type=f32)


def mm(left, right):
    return dot(left, right, ((1,), (0,)))


def mm_t(left, right):
    return dot(left, right, ((1,), (1,)))


def t_mm(left, right):
    return dot(left, right, ((0,), (0,)))


def exact(eq, left, right):
    return jnp.einsum(eq, left, right, precision=highest, preferred_element_type=f32)


def norm_forward(values, gain, offset):
    average = jnp.mean(values, axis=-1, keepdims=True)
    centred = values - average
    scale = lax.rsqrt(jnp.mean(centred * centred, axis=-1, keepdims=True) + norm_eps)
    unit = centred * scale
    return (unit * gain[None] + offset[None]).astype(bf16), unit, scale


def norm_backward(grad, unit, scale, gain):
    inner = grad * gain[None]
    mean_inner = jnp.mean(inner, axis=-1, keepdims=True)
    mean_product = jnp.mean(inner * unit, axis=-1, keepdims=True)
    back = scale * (inner - mean_inner - unit * mean_product)
    return back, jnp.sum(grad * unit, axis=0), jnp.sum(grad, axis=0)


def adamw(weight, grad, moment, second, step_value, learn_rate):
    moment = 0.5 * moment + 0.5 * grad
    second = 0.5 * second + 0.5 * grad * grad
    correct = 1.0 - jnp.power(f32(0.5), step_value)
    update = moment / correct / (jnp.sqrt(second / correct) + adam_eps) + decay_rate * weight
    fresh = weight - learn_rate * update
    return (fresh, fresh.astype(bf16), moment, second)


PIECES = (
    (0, 1408, 1280, "yzx"), (1, 0, 1536, "zxy"), (0, 2688, 1280, "yzx"), (1, 1536, 1536, "zxy"), (0, 0, 1408, "zxy"),
)


def gather_kernel(*refs):
    w_io, w_small, w_agg, w_attn, num_ref = refs[:5]
    wholes, small_ref, stat_ref = refs[5:7], refs[7], refs[8]
    quad_buf, line_buf, small_buf, pack, attn_low, own_sem, s_send, s_recv, sends, arrive, pass_on = refs[9:]
    shards = (pack, attn_low)
    dp, own = lax.axis_index("dp"), lax.axis_index("fsdp")
    z, y, x, core = dp // 2, dp % 2, own // 2, own % 2
    sibling = x * 2 + 1 - core
    barrier = pltpu.get_barrier_semaphore()
    for d in range(1, 8):
        pl.semaphore_signal(barrier, inc=1, device_id=(lax.rem(dp + d, 8), own), device_id_type=MESH)
    for d in range(1, 4):
        pl.semaphore_signal(barrier, inc=1, device_id=(dp, lax.rem(own + d, 4)), device_id_type=MESH)
    emb = 2 * WIDTH + VARS

    def gap(width):
        return jnp.zeros((STRIP, width), f32)

    pack[:, :HEAD] = jnp.concatenate(
        [
            w_io[:, :WIDTH], w_io[:, 2 * WIDTH : emb], gap(MIX - WIDTH - VARS), w_io[:, WIDTH : 2 * WIDTH],
            gap(256 - WIDTH), w_io[:, emb : emb + SPAN], w_small[...], gap(128 - w_small.shape[1]),
        ],
        axis=1,
    ).astype(bf16)
    pack[:, HEAD:] = w_agg[...].astype(bf16)
    attn_low[...] = w_attn[:, : 3 * D].astype(bf16)
    pl.semaphore_wait(barrier, 10)

    def view(p, ident, plane):
        a, start, width, order = PIECES[p]
        row = pl.multiple_of(((ident // 2) * 4 + (ident % 2) * 2 + plane) * STRIP, STRIP)
        return wholes[a].at[pl.ds(row, STRIP), pl.ds(start, width)]

    def copy(p, ident, slot, to, mine=False):
        a, start, width, order = PIECES[p]
        src = shards[a].at[:, pl.ds(start, width)] if mine else view(p, ident, core)
        sem = pass_on if slot == 4 else arrive
        return pltpu.make_async_remote_copy(
            src_ref=src, dst_ref=view(p, ident, core), send_sem=sends.at[p, ident, slot], recv_sem=sem.at[p, ident],
            device_id=to, device_id_type=MESH,
        )

    def arrival(p, ident, plane, sem):
        return pltpu.make_async_copy(view(p, ident, plane), view(p, ident, plane), sem.at[p, ident])

    def targets(p, rx, ry, rz):
        order = PIECES[p][3]
        moved = {"x": rx != 0, "y": ry != 0, "z": rz is not None}
        stage = max([k for k in range(3) if moved[order[k]]], default=-1)
        found = []
        if stage >= 0 and order[stage] == "z":
            found.append((0, (rz < 0) & (z < 3), ((dp + 2) % 8, own)))
            found.append((1, (rz > 0) & (z > 0), ((dp + 6) % 8, own)))
        for k in range(stage + 1, 3):
            if order[k] == "z":
                found.append((0, z < 3, ((dp + 2) % 8, own)))
                found.append((1, z > 0, ((dp + 6) % 8, own)))
            elif order[k] == "x":
                found.append((2, None, (dp, (1 - x) * 2 + core)))
            else:
                found.append((3, None, (z * 2 + 1 - y, own)))
        found.append((4, None, (dp, sibling)))
        return found

    def source(rx, ry, rz):
        sz = z if rz is None else z + rz
        sy = 1 - y if ry else y
        sx = 1 - x if rx else x
        return sz, (sz * 2 + sy) * 2 + sx

    def each(rx, ry, rz, act, mine=False):
        sz, ident = source(rx, ry, rz)

        def body():
            for p in range(len(PIECES)):
                if act == "send" and not mine:
                    arrival(p, ident, core, arrive).wait()
                for slot, when, to in targets(p, rx, ry, rz):
                    def go(slot=slot, to=to):
                        c = copy(p, ident, slot, to, mine)
                        c.start() if act == "send" else c.wait_send()

                    if when is None:
                        go()
                    else:
                        pl.when(when)(go)

        if rz is None:
            body()
        else:
            pl.when((sz >= 0) & (sz < 4))(body)

    def over_z(pairs, act):
        def step(t, carry):
            rz = ((t + 1) // 2) * (1 - 2 * (t % 2))
            for rx, ry in pairs:
                each(rx, ry, rz, act)
            return carry

        lax.fori_loop(1, 7, step, 0)

    def sweep(act):
        each(0, 0, None, act, mine=True)
        if act == "send":
            for a in range(2):
                row = pl.multiple_of((dp * 4 + own) * STRIP, STRIP)
                pltpu.make_async_copy(shards[a], wholes[a].at[pl.ds(row, STRIP), :], own_sem.at[a]).start()
            scalars()
        each(1, 0, None, act)
        each(0, 1, None, act)
        over_z([(0, 0)], act)
        each(1, 1, None, act)
        over_z([(1, 0), (0, 1)], act)
        over_z([(1, 1)], act)

    def share(buf, k, where, at):
        return pltpu.make_async_remote_copy(
            src_ref=buf.at[at], dst_ref=buf.at[at], send_sem=s_send.at[k], recv_sem=s_recv.at[k],
            device_id=where, device_id_type=MESH,
        )

    def scalars():
        quad_buf[own] = num_ref[...]
        for d in range(1, 4):
            share(quad_buf, d, (dp, lax.rem(own + d, 4)), own).start()

    sweep("send")
    for d in range(1, 4):
        share(quad_buf, d, (dp, own), lax.rem(own + 4 - d, 4)).wait_recv()
    line_buf[dp] = (quad_buf[0] + quad_buf[1]) + (quad_buf[2] + quad_buf[3])
    for d in range(1, 8):
        share(line_buf, 3 + d, (lax.rem(dp + d, 8), own), dp).start()

    def closing(ident, carry):
        for p in range(len(PIECES)):
            arrival(p, ident, 1 - core, pass_on).wait()
        return carry

    lax.fori_loop(0, 16, closing, 0)
    for a in range(2):
        row = pl.multiple_of((dp * 4 + own) * STRIP, STRIP)
        pltpu.make_async_copy(shards[a], wholes[a].at[pl.ds(row, STRIP), :], own_sem.at[a]).wait()
    narrow = pltpu.make_async_copy(wholes[0].at[:, pl.ds(768, 128)], small_buf, own_sem.at[0])
    narrow.start()
    sweep("drain")
    narrow.wait()
    small_ref[...] = small_buf[...].astype(f32).T[:16]
    for d in range(1, 8):
        share(line_buf, 3 + d, (dp, own), lax.rem(dp + 8 - d, 8)).wait_recv()
    stat = line_buf[0]
    for d in range(1, 8):
        stat = stat + line_buf[d]
    stat_ref[...] = stat
    for d in range(1, 4):
        share(quad_buf, d, (dp, own), own).wait_send()
    for d in range(1, 8):
        share(line_buf, 3 + d, (dp, own), dp).wait_send()


def gather_weights(w_io, w_small, w_agg, w_attn, number):
    any_space = pl.BlockSpec(memory_space=pl.ANY)
    vmem = pl.BlockSpec(memory_space=pltpu.VMEM)
    n = len(PIECES)
    return pl.pallas_call(
        gather_kernel,
        out_shape=[jax.ShapeDtypeStruct((D, w), bf16) for w in (HEAD + 3 * D, 3 * D)]
        + [jax.ShapeDtypeStruct((16, D), f32), jax.ShapeDtypeStruct((8, 128), f32)],
        in_specs=[vmem] * 5,
        out_specs=[any_space] * 2 + [vmem] * 2,
        scratch_shapes=[
            pltpu.VMEM((4, 8, 128), f32),
            pltpu.VMEM((8, 8, 128), f32),
            pltpu.VMEM((D, 128), bf16),
            pltpu.VMEM((STRIP, HEAD + 3 * D), bf16),
            pltpu.VMEM((STRIP, 3 * D), bf16),
            pltpu.SemaphoreType.DMA((3,)),
            pltpu.SemaphoreType.DMA((11,)),
            pltpu.SemaphoreType.DMA((11,)),
            pltpu.SemaphoreType.DMA((n, 16, 5)),
            pltpu.SemaphoreType.DMA((n, 16)),
            pltpu.SemaphoreType.DMA((n, 16)),
        ],
        compiler_params=pltpu.CompilerParams(collective_id=0, has_side_effects=True),
        cost_estimate=pl.CostEstimate(flops=0, bytes_accessed=250_000_000, transcendentals=0),
        name="gather_weights",
    )(w_io, w_small, w_agg, w_attn, number)


def greet(dp, own):
    barrier = pltpu.get_barrier_semaphore()
    for d in range(1, 4):
        pl.semaphore_signal(barrier, inc=1, device_id=(dp, lax.rem(own + d, 4)), device_id_type=MESH)
    pl.semaphore_wait(barrier, 3)


def turned_softmax(parts, seg_col, seg_row, h):
    at = slice(h * HEAD_DIM, (h + 1) * HEAD_DIM)
    q, k, v = (parts[i, :, at] for i in range(3))
    score = lax.dot_general(k, q, (((1,), (1,)), ((), ())), preferred_element_type=f32) * HEAD_DIM ** (-0.5)
    score = jnp.where(seg_col[:, 0:1] == seg_row[0:1, :], score, -1000000000.0)
    power = jnp.exp(score - jnp.max(score, axis=0, keepdims=True))
    soft = power / jnp.sum(power, axis=0, keepdims=True)
    return q, k, v, soft, soft.astype(bf16)


def attend_kernel(qkv, seg_col, seg_row, norm0, mixed, mixed_t, parts_out, norm0_t, parts, turned, whole, gathered,
                  load_sem, in_send, in_recv, out_send, out_recv):
    dp, own = lax.axis_index("dp"), lax.axis_index("fsdp")
    greet(dp, own)
    row = pl.ds(pl.multiple_of(own * 128, 128), 128)

    def piece(i, to, g):
        return qkv.at[:, pl.ds(pl.multiple_of(i * D + to * 256 + g * 128, 128), 128)]

    def into(d, i, g):
        to = lax.rem(own + d, 4)
        return pltpu.make_async_remote_copy(
            src_ref=piece(i, to, g), dst_ref=parts.at[i, row, g * 128 : (g + 1) * 128], send_sem=in_send.at[d, i, g],
            recv_sem=in_recv.at[d, i, g], device_id=(dp, to), device_id_type=MESH,
        )

    def local_part(i, g):
        return pltpu.make_async_copy(piece(i, own, g), parts.at[i, row, g * 128 : (g + 1) * 128], load_sem.at[i, g])

    def back(d, g):
        to = lax.rem(own + d, 4)
        return pltpu.make_async_remote_copy(
            src_ref=whole.at[pl.ds(pl.multiple_of(to * 128, 128), 128), g * 128 : (g + 1) * 128],
            dst_ref=gathered.at[:, pl.ds(pl.multiple_of(own * 256 + g * 128, 128), 128)],
            send_sem=out_send.at[d, g], recv_sem=out_recv.at[d, g], device_id=(dp, to), device_id_type=MESH,
        )

    def keep(g):
        return pltpu.make_async_copy(
            whole.at[row, g * 128 : (g + 1) * 128],
            gathered.at[:, pl.ds(pl.multiple_of(own * 256 + g * 128, 128), 128)], load_sem.at[3, g],
        )

    for g in range(2):
        for i in range(3):
            for d in (2, 1, 3):
                into(d, i, g).start()
    for g in range(2):
        for i in range(3):
            local_part(i, g).start()
    norm0_t[...] = norm0[...].astype(f32).T.astype(bf16)
    for g in range(2):
        for i in range(3):
            local_part(i, g).wait()
            for d in range(1, 4):
                into(d, i, g).wait_recv()
        for h in (2 * g, 2 * g + 1):
            q, k, v, soft, share = turned_softmax(parts, seg_col, seg_row, h)
            turned[h * HEAD_DIM : (h + 1) * HEAD_DIM, :] = lax.dot_general(
                v, share, (((0,), (0,)), ((), ())), preferred_element_type=f32
            )
        whole[:, g * 128 : (g + 1) * 128] = turned[g * 128 : (g + 1) * 128, :].T.astype(bf16)
        for d in (2, 1, 3):
            back(d, g).start()
        keep(g).start()
    mixed_t[...] = turned[...].astype(bf16)
    parts_out[...] = parts[...]
    for g in range(2):
        keep(g).wait()
        for d in range(1, 4):
            back(d, g).wait_recv()
    mixed[...] = gathered[...]
    for g in range(2):
        for d in range(1, 4):
            back(d, g).wait_send()
            for i in range(3):
                into(d, i, g).wait_send()


def attend(qkv, seg_col, seg_row, norm0):
    vmem = pl.BlockSpec(memory_space=pltpu.VMEM)
    dma = pltpu.SemaphoreType.DMA
    return pl.pallas_call(
        attend_kernel,
        out_shape=[
            jax.ShapeDtypeStruct((128, D), bf16), jax.ShapeDtypeStruct((256, 512), bf16),
            jax.ShapeDtypeStruct((3, 512, 256), bf16), jax.ShapeDtypeStruct((D, 128), bf16),
        ],
        in_specs=[pl.BlockSpec(memory_space=pl.ANY), vmem, vmem, vmem],
        out_specs=[vmem] * 4,
        scratch_shapes=[
            pltpu.VMEM((3, 512, 256), bf16), pltpu.VMEM((256, 512), f32), pltpu.VMEM((512, 256), bf16),
            pltpu.VMEM((128, D), bf16), dma((4, 2)), dma((4, 3, 2)), dma((4, 3, 2)), dma((4, 2)), dma((4, 2)),
        ],
        compiler_params=pltpu.CompilerParams(collective_id=2, has_side_effects=True, vmem_limit_bytes=40 * 2**20),
        name="attend",
    )(qkv, seg_col, seg_row, norm0)


def attend_back_kernel(d_proj, rear, parts, seg_col, seg_row, norm1, d_out, norm2, d_own, d_parts_out, d_all_out,
                       norm1_t, out_t, norm2_t, every, proj, d_mixed,
                       d_parts, gathered, load_sem, up_send, up_recv, out_send, out_recv):
    dp, own = lax.axis_index("dp"), lax.axis_index("fsdp")
    x, core = own // 2, own % 2
    sibling, across, diagonal = x * 2 + 1 - core, (1 - x) * 2 + core, (1 - x) * 2 + 1 - core
    rows = pl.ds(pl.multiple_of(own * 256, 256), 256)
    fetch = pltpu.make_async_copy(rear.at[rows, pl.ds(0, D)], proj, load_sem.at[0, 0])
    fetch.start()
    row = pl.ds(pl.multiple_of(own * 128, 128), 128)
    mine = pltpu.make_async_copy(d_proj, every.at[row, :], load_sem.at[1, 0])
    mine.start()
    greet(dp, own)
    mine.wait()

    def up(i, who, slot, to):
        block = every.at[pl.ds(pl.multiple_of(who * 128, 128), 128), i * 512 : (i + 1) * 512]
        return pltpu.make_async_remote_copy(
            src_ref=block, dst_ref=block, send_sem=up_send.at[i, slot], recv_sem=up_recv.at[i, who],
            device_id=(dp, to), device_id_type=MESH,
        )

    for i in range(2):
        up(i, own, 0, across).start()
    for i in range(2):
        up(i, own, 1, sibling).start()
    for source, turned in ((norm1, norm1_t), (d_out, out_t), (norm2, norm2_t)):
        turned[...] = source[...].astype(f32).T.astype(bf16)
    for i in range(2):
        up(i, across, 0, own).wait_recv()
        up(i, across, 2, sibling).start()
    fetch.wait()
    for i in range(2):
        up(i, sibling, 1, own).wait_recv()
        up(i, diagonal, 2, own).wait_recv()
    d_mixed[...] = lax.dot_general(
        every[...], proj[...], (((1,), (1,)), ((), ())), preferred_element_type=f32
    ).astype(bf16)
    def column(i, g):
        return pl.ds(pl.multiple_of(i * D + own * 256 + g * 128, 128), 128)

    def back(d, i, g):
        to = lax.rem(own + d, 4)
        return pltpu.make_async_remote_copy(
            src_ref=d_parts.at[i, pl.ds(pl.multiple_of(to * 128, 128), 128), g * 128 : (g + 1) * 128],
            dst_ref=gathered.at[:, column(i, g)], send_sem=out_send.at[d, i, g], recv_sem=out_recv.at[d, i, g],
            device_id=(dp, to), device_id_type=MESH,
        )

    def keep(i, g):
        return pltpu.make_async_copy(
            d_parts.at[i, row, g * 128 : (g + 1) * 128], gathered.at[:, column(i, g)], load_sem.at[2 + i, g]
        )

    for g in range(2):
        for h in (2 * g, 2 * g + 1):
            at = slice(h * HEAD_DIM, (h + 1) * HEAD_DIM)
            q, k, v, soft, share = turned_softmax(parts, seg_col, seg_row, h)
            d_head = d_mixed[:, at]
            d_soft = lax.dot_general(v, d_head, (((1,), (1,)), ((), ())), preferred_element_type=f32)
            lean = jnp.sum(soft * d_soft, axis=0, keepdims=True)
            d_score = (soft * (d_soft - lean) * HEAD_DIM ** (-0.5)).astype(bf16)
            d_parts[2, :, at] = mm(share, d_head).astype(bf16)
            d_parts[1, :, at] = mm(d_score, q).astype(bf16)
            d_parts[0, :, at] = t_mm(d_score, k).astype(bf16)
        for i in range(3):
            for d in (2, 1, 3):
                back(d, i, g).start()
            keep(i, g).start()
    d_parts_out[...] = d_parts[...]
    d_all_out[...] = every[...]
    for g in range(2):
        for i in range(3):
            keep(i, g).wait()
            for d in range(1, 4):
                back(d, i, g).wait_recv()
    d_own[...] = gathered[...]
    for g in range(2):
        for d in range(1, 4):
            for i in range(3):
                back(d, i, g).wait_send()
    for i in range(2):
        for slot, who in ((0, own), (1, own), (2, across)):
            up(i, who, slot, own).wait_send()


def attend_back(d_proj, rear, parts, seg_col, seg_row, *features):
    vmem = pl.BlockSpec(memory_space=pltpu.VMEM)
    any_space = pl.BlockSpec(memory_space=pl.ANY)
    dma = pltpu.SemaphoreType.DMA
    return pl.pallas_call(
        attend_back_kernel,
        out_shape=[
            jax.ShapeDtypeStruct((128, 3 * D), bf16), jax.ShapeDtypeStruct((3, 512, 256), bf16),
            jax.ShapeDtypeStruct((512, D), bf16),
        ]
        + [jax.ShapeDtypeStruct((D, 128), bf16)] * 3,
        in_specs=[any_space, any_space] + [vmem] * 6,
        out_specs=[vmem] * 6,
        scratch_shapes=[
            pltpu.VMEM((512, D), bf16), pltpu.VMEM((256, D), bf16), pltpu.VMEM((512, 256), bf16),
            pltpu.VMEM((3, 512, 256), bf16), pltpu.VMEM((128, 3 * D), bf16),
            dma((5, 2)), dma((2, 3)), dma((2, 4)), dma((4, 3, 2)), dma((4, 3, 2)),
        ],
        compiler_params=pltpu.CompilerParams(collective_id=3, has_side_effects=True, vmem_limit_bytes=40 * 2**20),
        name="attend_back",
    )(d_proj, rear, parts, seg_col, seg_row, *features)


SEGMENTS = ((0, 2, 3), (2, 10, 1), (10, 18, 0), (18, 24, 2), (24, 26, 4))
N_STD, N_ALL, SHIFT, BASE = 26, 32, 1, 2


FAR = ({2: 0, 3: 1}, {0: 0, 1: 1})


def preds_at(preds, who):
    return preds.at[pl.ds(pl.multiple_of(who * 128, 128), 128), :]


def gradient_kernel(*refs):
    (norm1_t, out_t, norm0_t, mixed_t, mixa_t, norm2_t, agg_t,
     d_proj, d_parts, d_up, lifted, d_agg, d_pred, onehot, d_table, narrow, head, num_ref) = refs[:18]
    r_agg, r_attn, r_mlp, r_io, r_small, stat_ref = refs[18:24]
    (feats, ys, tabs, pairs, preds, hots, narrows, w240, wkv, acc240, own_buf, give_buf, got, rise, fall, far, tally,
     quad_buf, line_buf, load_sem, feat_send, feat_recv, y_xsend, y_xrecv, part_send, part_recv, tab_send, tab_recv, pred_send, pred_recv,
     nar_send, nar_recv, y_send, y_recv, z_send, z_recv, s_send, s_recv) = refs[24:]
    dp, own = lax.axis_index("dp"), lax.axis_index("fsdp")
    z, y, x, core = dp // 2, dp % 2, own // 2, own % 2
    sibling, across, diagonal = x * 2 + 1 - core, (1 - x) * 2 + core, (1 - x) * 2 + 1 - core
    over = z * 2 + 1 - y
    n = N_ALL
    row = pl.ds(pl.multiple_of(own * 128, 128), 128)
    sent_feats = {0: norm1_t, 1: out_t, 2: norm0_t, 4: mixa_t, 5: norm2_t, 6: agg_t}

    def remote(src, dst, send, recv, to):
        return pltpu.make_async_remote_copy(
            src_ref=src, dst_ref=dst, send_sem=send, recv_sem=recv, device_id=(dp, to), device_id_type=MESH
        )

    def feat_copy(k, d, half, to):
        side = y if half == 0 else 1 - y
        if k == 3:
            src, dst = mixed_t.at[side, to], feats.at[3, half, own]
        else:
            src, dst = sent_feats[k].at[:, side, to], feats.at[k, half, :, :, row]
        return remote(src, dst, feat_send.at[k, d, half], feat_recv.at[k, d, half], to)

    def feat_start(k):
        for d in (2, 1, 3):
            for half in range(2):
                feat_copy(k, d, half, lax.rem(own + d, 4)).start()

    def unit_block(c, who):
        return ys.at[c, pl.ds(pl.multiple_of(who * 128, 128), 128), :]

    def unit(c, who, slot, to):
        return remote(unit_block(c, who), unit_block(c, who), y_xsend.at[c, slot], y_xrecv.at[c, who], to)

    def part_block(i, who):
        return ys.at[18 + i * 2 + who // 2, :, pl.ds(pl.multiple_of((who % 2) * 256, 256), 256)]

    def part(i, who, slot, to):
        return remote(part_block(i, who), part_block(i, who), part_send.at[i, slot], part_recv.at[i, who], to)

    def table_raw(v, to):
        return remote(tabs.at[0, v], tabs.at[1, v], tab_send.at[v, 0], tab_recv.at[v, 0], to)

    def table(v, who, slot, to):
        return remote(pairs.at[who, v], pairs.at[who, v], tab_send.at[v, slot], tab_recv.at[v, 1 + who], to)

    def pred_copy(d, who, to):
        return remote(preds_at(preds, who), preds_at(preds, who), pred_send.at[d], pred_recv.at[d], to)

    def narrow_copy(d, who, to):
        return remote(narrows.at[who], narrows.at[who], nar_send.at[d], nar_recv.at[d], to)

    loads = {}

    def load(name, src, dst):
        copy = pltpu.make_async_copy(src, dst, load_sem.at[len(loads)])
        copy.start()
        loads[name] = copy

    def load_feat(k):
        for half in range(2):
            side = y if half == 0 else 1 - y
            if k == 3:
                load(("f", k, half), mixed_t.at[side, own], feats.at[3, half, own])
            else:
                load(("f", k, half), sent_feats[k].at[:, side, own], feats.at[k, half, :, :, row])

    def loaded(*names):
        for name in names:
            loads[name].wait()

    for c in range(2):
        load(("j", c), d_proj.at[:, pl.ds(c * CHUNK, CHUNK)], ys.at[c])
    load_feat(3)
    load_feat(1)
    for c in range(8):
        load(("u", 10 + c), d_up.at[:, pl.ds(c * CHUNK, CHUNK)], unit_block(10 + c, own))
    for c in range(8):
        load(("l", c), lifted.at[:, pl.ds(c * CHUNK, CHUNK)], ys.at[2 + c])
    load_feat(0)
    for i in range(3):
        load(("p", i), d_parts.at[i], part_block(i, own))
    load_feat(2)
    for c in range(2):
        load(("u", 24 + c), d_agg.at[:, pl.ds(c * CHUNK, CHUNK)], unit_block(24 + c, own))
    load_feat(4)
    for v in range(4):
        load(("t", v), d_table.at[pl.ds(v * CHUNK, CHUNK), :], tabs.at[0, v])
    load("pred", d_pred, preds_at(preds, own))
    load("narrow", narrow, narrows.at[own])
    for half in range(2):
        side = y if half == 0 else 1 - y
        load(("w", half), head.at[:, side, own, :, pl.ds(0, 256)], w240.at[half])
        load(("k", half), head.at[:, side, own, :, pl.ds(HEAD, 2 * D)], wkv.at[half])
    load_feat(5)
    load_feat(6)
    load("hot", onehot, hots)
    barrier = pltpu.get_barrier_semaphore()
    for d in range(1, 8):
        pl.semaphore_signal(barrier, inc=1, device_id=(lax.rem(dp + d, 8), own), device_id_type=MESH)
    for d in range(1, 4):
        pl.semaphore_signal(barrier, inc=1, device_id=(dp, lax.rem(own + d, 4)), device_id_type=MESH)
    pl.semaphore_wait(barrier, 10)
    feat_start(3)
    feat_start(1)
    feat_start(0)
    loaded(*[("u", 10 + c) for c in range(8)])

    def begin(c, carry):
        unit(c, own, 0, across).start()
        unit(c, own, 1, sibling).start()
        return carry

    lax.fori_loop(10, 18, begin, 0)
    feat_start(2)
    loaded(*[("p", i) for i in range(3)], ("u", 24), ("u", 25))
    for i in range(3):
        part(i, own, 0, across).start()
        part(i, own, 1, sibling).start()
    feat_start(4)
    lax.fori_loop(24, 26, begin, 0)
    loaded(*[("t", v) for v in range(4)], "pred", "narrow")
    for w in range(2):
        table_raw((1 - core) * 2 + w, sibling).start()
    tally[...] = jnp.zeros_like(tally)
    acc240[...] = jnp.zeros_like(acc240)
    for w in range(2):
        v = core * 2 + w
        table_raw(v, own).wait_recv()
        pairs[x, v] = (tabs[0, v].astype(f32) + tabs[1, v].astype(f32)).astype(bf16)
        table(v, x, 1, across).start()
        table(v, x, 2, sibling).start()
    feat_start(5)
    feat_start(6)
    for d in (2, 1, 3):
        pred_copy(d, own, lax.rem(own + d, 4)).start()
        narrow_copy(d, own, lax.rem(own + d, 4)).start()

    def feat_wait(k):
        for d in range(1, 4):
            for half in range(2):
                feat_copy(k, d, half, own).wait_recv()

    def put(c, value):
        own_buf[c] = value[:128]
        give_buf[c] = value[128:].astype(bf16)

    def feature(k):
        return feats[k].reshape(256, 512)

    def matmul(a, b):
        return lax.dot_general(a, b, (((1,), (0,)), ((), ())), preferred_element_type=f32)

    def two(value):
        high = value.astype(bf16)
        return high, (value - high.astype(f32)).astype(bf16)

    def summed_table(v):
        return two(pairs[0, v].astype(f32) + pairs[1, v].astype(f32))

    def compute(c):
        for i in range(3):
            @pl.when(c == 18 + i * 2)
            def _():
                part(i, sibling, 1, own).wait_recv()
                part(i, diagonal, 2, own).wait_recv()

        for low, high, k in SEGMENTS:
            @pl.when(c == low)
            def _():
                feat_wait(k)
                loaded(("f", k, 0), ("f", k, 1))
                if k == 3:
                    loaded(("j", 0), ("j", 1))
                if k == 1:
                    loaded(*[("l", i) for i in range(8)])

            @pl.when((c >= low) & (c < high))
            def _():
                if k in (0, 4):
                    unit(c, sibling, 1, own).wait_recv()
                    unit(c, diagonal, 2, own).wait_recv()
                put(c, matmul(feature(k), ys[c]))

        @pl.when(c == N_STD)
        def _():
            loaded(("w", 0), ("w", 1), ("k", 0), ("k", 1))

        @pl.when((c >= N_STD) & (c < N_STD + 4))
        def _():
            v = c - N_STD

            @pl.when(v // 2 != core)
            def _():
                table(v, x, 2, own).wait_recv()
                table(v, 1 - x, 3, own).wait_recv()

            high, low = summed_table(v)
            rows = w240[...].reshape(256, 256)
            dims = (((1,), (1,)), ((), ()))
            put(
                c,
                lax.dot_general(rows, high, dims, preferred_element_type=f32)
                + lax.dot_general(rows, low, dims, preferred_element_type=f32),
            )

        for v in range(4):
            @pl.when(c == N_STD + v)
            def _():
                high, low = summed_table(v)
                rows = wkv[:, :, :, v * CHUNK : (v + 1) * CHUNK].reshape(256, CHUNK)
                acc240[...] = acc240[...] + matmul(rows, high) + matmul(rows, low)

        @pl.when(c == N_STD + 4)
        def _():
            feat_wait(5)
            loaded(("f", 5, 0), ("f", 5, 1))
            for d in range(1, 4):
                pred_copy(d, lax.rem(own + 4 - d, 4), own).wait_recv()
            value = matmul(feature(5), preds[...])
            own_buf[c, :, 0:256] = acc240[:128]
            own_buf[c, :, 256:512] = value[:128]
            give_buf[c, :, 0:256] = acc240[128:].astype(bf16)
            give_buf[c, :, 256:512] = value[128:].astype(bf16)

        @pl.when(c == N_STD + 5)
        def _():
            feat_wait(6)
            loaded(("f", 6, 0), ("f", 6, 1), "hot")
            for d in range(1, 4):
                narrow_copy(d, lax.rem(own + 4 - d, 4), own).wait_recv()
            value = matmul(feature(6), hots[...])
            place = lax.broadcasted_iota(jnp.int32, (256, D), 0)
            source = lax.broadcasted_iota(jnp.int32, (256, D), 1)
            side = jnp.where(place < 128, y, 1 - y)
            wanted = ((place >> 5) & 3) * 256 + side * 128 + own * STRIP + (place & 31)
            choose = jnp.where(source == wanted, 1.0, 0.0).astype(bf16)
            total = (narrows[0] + narrows[1]) + (narrows[2] + narrows[3])
            total = jnp.concatenate([total, jnp.zeros((112, D), f32)], axis=0)
            high = total.astype(bf16)
            rest = total - high.astype(f32)
            middle = rest.astype(bf16)
            low = (rest - middle.astype(f32)).astype(bf16)
            dims = (((1,), (1,)), ((), ()))
            small = (
                lax.dot_general(choose, high, dims, preferred_element_type=f32)
                + lax.dot_general(choose, middle, dims, preferred_element_type=f32)
                + lax.dot_general(choose, low, dims, preferred_element_type=f32)
            )
            empty = jnp.zeros((128, 128), f32)
            own_buf[c, :, 0:256] = value[:128]
            own_buf[c, :, 256:384] = small[:128]
            own_buf[c, :, 384:512] = empty
            give_buf[c, :, 0:256] = value[128:].astype(bf16)
            give_buf[c, :, 256:384] = small[128:].astype(bf16)
            give_buf[c, :, 384:512] = empty.astype(bf16)

    def cross(c):
        return pltpu.make_async_remote_copy(
            src_ref=give_buf.at[c], dst_ref=got.at[c], send_sem=y_send.at[c],
            recv_sem=y_recv.at[c], device_id=(over, own), device_id_type=MESH,
        )

    def hop(buf, way, c, b, to):
        at = b - 1 if way == 0 else b
        return pltpu.make_async_remote_copy(
            src_ref=buf.at[c, at], dst_ref=buf.at[c, at], send_sem=z_send.at[way, c, at], recv_sem=z_recv.at[way, c, at],
            device_id=(to * 2 + y, own), device_id_type=MESH,
        )

    def far_hop(way, c, b, to):
        at = FAR[way][b]
        return pltpu.make_async_remote_copy(
            src_ref=far.at[way, c, at], dst_ref=far.at[way, c, at], send_sem=z_send.at[way, c, 3 + at],
            recv_sem=z_recv.at[way, c, 3 + at], device_id=(to * 2 + y, own), device_id_type=MESH,
        )

    def here(c, b):
        at = pl.ds(b * STRIP, STRIP)
        return own_buf[c, at, :] + got[c, at, :].astype(f32)

    early, late = LAG * jnp.minimum(z, 3 - z), LAG * jnp.maximum(z, 3 - z)

    def step(t, carry):
        @pl.when((t >= 4) & (t < 12))
        def _():
            unit(t + 6, across, 0, own).wait_recv()
            unit(t + 6, across, 2, sibling).start()

        for i in range(3):
            @pl.when(t == 14 + 2 * i)
            def _():
                part(i, across, 0, own).wait_recv()
                part(i, across, 2, sibling).start()

        @pl.when((t == 20) | (t == 21))
        def _():
            unit(t + 4, across, 0, own).wait_recv()
            unit(t + 4, across, 2, sibling).start()

        @pl.when((t == 24) | (t == 25))
        def _():
            v = core * 2 + t - 24
            table(v, 1 - x, 1, own).wait_recv()
            table(v, 1 - x, 3, sibling).start()

        @pl.when((t >= SHIFT) & (t < n + SHIFT))
        def _():
            compute(t - SHIFT)
            cross(t - SHIFT).start()

        first = t - SHIFT - BASE - early

        @pl.when((first >= 0) & (first < n))
        def _():
            cross(first).wait()

        for way, buf, lag, to, back in ((0, rise, LAG * z, z + 1, z - 1), (1, fall, LAG * (3 - z), z - 1, z + 1)):
            c = t - SHIFT - BASE - lag

            @pl.when((c >= 0) & (c < n))
            def _():
                for b in ((1, 2, 3) if way == 0 else (0, 1, 2)):
                    beyond = (b > z) if way == 0 else (b < z)
                    at = b - 1 if way == 0 else b

                    @pl.when(beyond & (lag == 0))
                    def _():
                        if b == (1 if way == 0 else 2):
                            buf[c, at] = here(c, b)
                        else:
                            far[way, c, FAR[way][b]] = here(c, b).astype(bf16)

                    @pl.when(beyond & (lag > 0))
                    def _():
                        if b == (1 if way == 0 else 2):
                            hop(buf, way, c, b, back).wait_recv()
                            buf[c, at] = buf[c, at] + here(c, b)
                        else:
                            @pl.when(lag == LAG)
                            def _():
                                far_hop(way, c, b, back).wait_recv()
                                buf[c, at] = far[way, c, FAR[way][b]].astype(f32) + here(c, b)

                            @pl.when(lag > LAG)
                            def _():
                                hop(buf, way, c, b, back).wait_recv()
                                buf[c, at] = buf[c, at] + here(c, b)

                    def send(c, act):
                        if b == (1 if way == 0 else 2):
                            copy = hop(buf, way, c, b, to)
                            copy.start() if act else copy.wait_send()
                        else:
                            @pl.when(lag == 0)
                            def _():
                                copy = far_hop(way, c, b, to)
                                copy.start() if act else copy.wait_send()

                            @pl.when(lag > 0)
                            def _():
                                copy = hop(buf, way, c, b, to)
                                copy.start() if act else copy.wait_send()

                    @pl.when(beyond & (c >= QUEUE))
                    def _():
                        send(c - QUEUE, False)

                    @pl.when(beyond)
                    def _():
                        send(c, True)

        last = t - SHIFT - BASE - late

        @pl.when((last >= 0) & (last < n))
        def _():
            at = pl.ds(pl.multiple_of(z * STRIP, STRIP), STRIP)
            value = own_buf[last, at, :] + got[last, at, :].astype(f32)
            own_buf[last, 0:STRIP, :] = value

            @pl.when(z > 0)
            def _():
                hop(rise, 0, last, z, z - 1).wait_recv()
                own_buf[last, 0:STRIP, :] = own_buf[last, 0:STRIP, :] + rise[last, z - 1]

            @pl.when(z < 3)
            def _():
                hop(fall, 1, last, z, z + 1).wait_recv()
                own_buf[last, 0:STRIP, :] = own_buf[last, 0:STRIP, :] + fall[last, z]

            value = own_buf[last, 0:STRIP, :]
            square = value * value
            total = square[0:8, 0:128]
            for r in range(0, STRIP, 8):
                for k in range(0, CHUNK, 128):
                    if r or k:
                        total = total + square[r : r + 8, k : k + 128]
            tally[...] = tally[...] + total

        return carry

    lax.fori_loop(0, n + SHIFT + BASE + 3 * LAG, step, 0)
    summed = jnp.sum(tally[...])
    lane = lax.broadcasted_iota(jnp.int32, (8, 128), 1)
    quad_buf[own] = jnp.where(lane == 0, summed, jnp.where(lane == 1, num_ref[...], 0.0))

    def share(buf, k, where, at):
        return pltpu.make_async_remote_copy(
            src_ref=buf.at[at], dst_ref=buf.at[at], send_sem=s_send.at[k], recv_sem=s_recv.at[k],
            device_id=where, device_id_type=MESH,
        )

    for d in range(1, 4):
        share(quad_buf, d, (dp, lax.rem(own + d, 4)), own).start()
    for out, base, low, high in (
        (r_attn, 3 * D, 0, 2), (r_mlp, FF, 2, 10), (r_mlp, 0, 10, 18), (r_attn, 0, 18, 24), (r_agg, 2 * D, 24, 26), (r_agg, 0, 26, 30),
    ):
        for c in range(low, high):
            out[:, base + (c - low) * CHUNK : base + (c - low + 1) * CHUNK] = own_buf[c, 0:STRIP, :]
    left, right = own_buf[30, 0:STRIP, :], own_buf[31, 0:STRIP, :]
    r_io[:, 0:WIDTH] = left[:, 0:WIDTH]
    r_io[:, WIDTH : 2 * WIDTH] = left[:, 256 : 256 + WIDTH]
    r_io[:, 2 * WIDTH : 2 * WIDTH + VARS] = left[:, WIDTH : WIDTH + VARS]
    r_io[:, 2 * WIDTH + VARS : 2 * WIDTH + VARS + SPAN] = right[:, 0:SPAN]
    r_io[:, 2 * WIDTH + VARS + SPAN :] = jnp.zeros((STRIP, r_io.shape[1] - 2 * WIDTH - VARS - SPAN), f32)
    r_small[...] = right[:, 256:384].T[:16]
    for d in range(1, 4):
        share(quad_buf, d, (dp, own), lax.rem(own + 4 - d, 4)).wait_recv()
    line_buf[dp] = (quad_buf[0] + quad_buf[1]) + (quad_buf[2] + quad_buf[3])
    for d in range(1, 8):
        share(line_buf, 3 + d, (lax.rem(dp + d, 8), own), dp).start()
    for d in range(1, 8):
        share(line_buf, 3 + d, (dp, own), lax.rem(dp + 8 - d, 8)).wait_recv()
    stat = line_buf[0]
    for d in range(1, 8):
        stat = stat + line_buf[d]
    stat_ref[...] = stat
    for d in range(1, 4):
        share(quad_buf, d, (dp, own), own).wait_send()
    for d in range(1, 8):
        share(line_buf, 3 + d, (dp, own), dp).wait_send()
    for d in range(1, 4):
        for k in range(7):
            for half in range(2):
                feat_copy(k, d, half, own).wait_send()
        pred_copy(d, own, own).wait_send()
        narrow_copy(d, own, own).wait_send()
    for w in range(2):
        table_raw((1 - core) * 2 + w, own).wait_send()
        for slot, who in ((1, x), (2, x), (3, 1 - x)):
            table(core * 2 + w, who, slot, own).wait_send()
    relays = ((0, own), (1, own), (2, across))
    for i in range(3):
        for slot, who in relays:
            part(i, who, slot, own).wait_send()

    def finish(c, carry):
        for slot, who in relays:
            unit(c, who, slot, own).wait_send()
        return carry

    lax.fori_loop(10, 18, finish, 0)
    lax.fori_loop(24, 26, finish, 0)

    def drain(c, carry):
        for way, buf, inner, outer in ((0, rise, z > 0, z == 0), (1, fall, z < 3, z == 3)):
            for b in ((1, 2, 3) if way == 0 else (0, 1, 2)):
                beyond = (b > z) if way == 0 else (b < z)
                if b == (1 if way == 0 else 2):
                    pl.when(beyond)(lambda: hop(buf, way, c, b, z).wait_send())
                else:
                    pl.when(beyond & inner)(lambda: hop(buf, way, c, b, z).wait_send())
                    pl.when(beyond & outer)(lambda: far_hop(way, c, b, z).wait_send())
        return carry

    lax.fori_loop(n - QUEUE, n, drain, 0)


def gradient_blocks(operands, numbers):
    any_space = pl.BlockSpec(memory_space=pl.ANY)
    vmem = pl.BlockSpec(memory_space=pltpu.VMEM)
    n = N_ALL
    dma = pltpu.SemaphoreType.DMA
    widths = (3 * D, 4 * D, 2 * FF, 944)
    return pl.pallas_call(
        gradient_kernel,
        out_shape=[jax.ShapeDtypeStruct((STRIP, w), f32) for w in widths]
        + [jax.ShapeDtypeStruct((16, STRIP), f32), jax.ShapeDtypeStruct((8, 128), f32)],
        in_specs=[any_space] * 17 + [vmem],
        out_specs=[vmem] * 6,
        scratch_shapes=[
            pltpu.VMEM((7, 2, 4, STRIP, 512), bf16),
            pltpu.VMEM((N_STD, 512, CHUNK), bf16),
            pltpu.VMEM((2, 4, CHUNK, 256), bf16),
            pltpu.VMEM((2, 4, CHUNK, 256), bf16),
            pltpu.VMEM((512, 256), bf16),
            pltpu.VMEM((512, 256), bf16),
            pltpu.VMEM((4, 16, D), f32),
            pltpu.VMEM((2, 4, STRIP, 256), bf16),
            pltpu.VMEM((2, 4, STRIP, 2 * D), bf16),
            pltpu.VMEM((256, 256), f32),
            pltpu.VMEM((n, 4 * STRIP, CHUNK), f32),
            pltpu.VMEM((n, 4 * STRIP, CHUNK), bf16),
            pltpu.VMEM((n, 4 * STRIP, CHUNK), bf16),
            pltpu.VMEM((n, 3, STRIP, CHUNK), f32),
            pltpu.VMEM((n, 3, STRIP, CHUNK), f32),
            pltpu.VMEM((2, n, 2, STRIP, CHUNK), bf16),
            pltpu.VMEM((8, 128), f32),
            pltpu.VMEM((4, 8, 128), f32),
            pltpu.VMEM((8, 8, 128), f32),
            dma((56,)),
            dma((7, 4, 2)),
            dma((7, 4, 2)),
            dma((N_STD, 3)),
            dma((N_STD, 4)),
            dma((3, 3)),
            dma((3, 4)),
            dma((4, 4)),
            dma((4, 3)),
            dma((4,)),
            dma((4,)),
            dma((4,)),
            dma((4,)),
            dma((n,)),
            dma((n,)),
            dma((2, n, 5)),
            dma((2, n, 5)),
            dma((11,)),
            dma((11,)),
        ],
        compiler_params=pltpu.CompilerParams(
            collective_id=1, has_side_effects=True, vmem_limit_bytes=62 * 2**20
        ),
        name="gradient_blocks",
    )(*operands, numbers)


def ag(part):
    return lax.all_gather(part, "fsdp", axis=0, tiled=True)


def make_local(n_dp, n_f):
    fast = n_dp == 8 and n_f == 4

    def local(
        pixels, targets, valid_mask, lat_weight, segment_ids, present_vars, lead_index, step_count,
        w_agg, w_attn, w_mlp, w_io, w_small,
        m_agg, m_attn, m_mlp, m_io, m_small,
        v_agg, v_attn, v_mlp, v_io, v_small,
    ):
        masters = (w_agg, w_attn, w_mlp, w_io, w_small)
        firsts = (m_agg, m_attn, m_mlp, m_io, m_small)
        seconds = (v_agg, v_attn, v_mlp, v_io, v_small)
        rows = pixels.shape[1]
        row_len = segment_ids.shape[1]
        strip = w_agg.shape[0]
        own = lax.axis_index("fsdp")
        heads_here = HEADS // n_f
        wide = heads_here * HEAD_DIM

        seg = segment_ids[0]
        below = jnp.sum((seg[None, :] < seg[:, None]).astype(jnp.int32), axis=1)
        pos = jnp.arange(row_len, dtype=jnp.int32) - below
        onehot_all = (pos[:, None] == jnp.arange(SPAN, dtype=jnp.int32)[None, :]).astype(bf16)
        onehot = lax.dynamic_slice_in_dim(onehot_all, own * rows, rows)
        lead = (lead_index[0].astype(f32) + 1.0) / LEAD_STEPS
        pixel_rows = pixels[0]
        target = targets[0].astype(f32)
        present = present_vars[0]
        spread = (jnp.arange(MIX) // PIX)[None, :] == jnp.arange(VARS)[:, None]
        embed_col = (jnp.arange(MIX) - WIDTH)[None, :] == jnp.arange(VARS)[:, None]
        in_pixels = (jnp.arange(MIX) < WIDTH)[None, :]
        expand = jnp.where(in_pixels, spread, embed_col).astype(bf16)
        present_cols = jnp.repeat(present.astype(f32), PIX)
        pixel_weight = lat_weight[0][:, None] * valid_mask[0].astype(f32) * present_cols[None, :]
        weight_sum = jnp.sum(pixel_weight)

        emb = 2 * WIDTH + VARS
        if fast:
            rear = jnp.concatenate([w_attn[:, 3 * D :], w_mlp], axis=1).astype(bf16)
            rear = lax.all_gather(rear, ("dp", "fsdp"), axis=0, tiled=True)
            head, w_qkv, small, stat = gather_weights(
                w_io, w_small, w_agg, w_attn, jnp.full((8, 128), weight_sum, f32)
            )
            total = stat[0, 0]
        else:

            def blank(width):
                return jnp.zeros((strip, width), bf16)

            io_low = w_io.astype(bf16)
            pack = jnp.concatenate(
                [
                    io_low[:, :WIDTH],
                    io_low[:, 2 * WIDTH : emb],
                    blank(MIX - WIDTH - VARS),
                    io_low[:, WIDTH : 2 * WIDTH],
                    blank(256 - WIDTH),
                    io_low[:, emb : emb + SPAN],
                    w_small.astype(bf16),
                    blank(128 - w_small.shape[1]),
                    w_agg.astype(bf16),
                ],
                axis=1,
            )
            head = lax.all_gather(pack, ("dp", "fsdp"), axis=0, tiled=True)
            attn = lax.all_gather(w_attn.astype(bf16), ("dp", "fsdp"), axis=0, tiled=True)
            mlp = lax.all_gather(w_mlp.astype(bf16), ("dp", "fsdp"), axis=0, tiled=True)
            w_qkv = attn[:, : 3 * D]
            rear = jnp.concatenate([attn[:, 3 * D :], mlp], axis=1)
            total = lax.psum(weight_sum, ("dp", "fsdp"))
        w240 = head[:, :MIX]
        w_pred = head[:, 256 : 256 + WIDTH]
        w_pos = head[:, 512 : 512 + SPAN]
        if not fast:
            small = head[:, 768:777].astype(f32).T
        agg_kv = head[:, HEAD : HEAD + 2 * D]
        agg_out = head[:, HEAD + 2 * D :]
        w_out = rear[:, :D]
        w_up = rear[:, D : D + FF]
        w_down = rear[:, D + FF :]

        pix_t = jnp.concatenate(
            [pixel_rows.T, jnp.ones((VARS, rows), bf16), jnp.zeros((MIX - WIDTH - VARS, rows), bf16)], axis=0
        )
        table = t_mm(agg_kv, w240)
        table_k = table[:D].reshape(HEADS, HEAD_DIM, MIX)
        table_v = table[D:].reshape(HEADS, HEAD_DIM, MIX)
        query = small[0].reshape(HEADS, HEAD_DIM)
        folded = jnp.sum(table_k * query[:, :, None], axis=1)
        block = folded[:, None, :] * expand.astype(f32)[None]
        score = exact("xc,cl->xl", block.reshape(HEADS * VARS, MIX), pix_t.astype(f32))
        score = score.reshape(HEADS, VARS, rows) * HEAD_DIM ** (-0.5)
        score = jnp.where(present[None, :, None] > 0, score, -1000000000.0)
        top = jnp.max(score, axis=1, keepdims=True)
        power = jnp.exp(score - top)
        soft = power / jnp.sum(power, axis=1, keepdims=True)
        share = soft.astype(bf16)
        pix_f = pix_t.astype(f32)
        lifted_share = jnp.einsum("vc,hvl->hcl", expand, share, preferred_element_type=f32) * pix_f[None]
        mixed_a = exact("hec,hcl->hel", table_v, lifted_share).reshape(D, rows).astype(bf16)
        lead_embed = lead * small[7] + small[8]
        h0 = t_mm(mixed_a, agg_out) + mm_t(onehot, w_pos) + lead_embed[None]
        norm0, unit0, scale0 = norm_forward(h0, small[1], small[2])
        qkv = mm(norm0, w_qkv).astype(bf16)
        if fast:
            seg_col = jnp.broadcast_to(seg[:, None], (row_len, 128))
            seg_row = jnp.broadcast_to(seg[None, :], (8, row_len))
            mixed, mixed_t, parts, norm0_t = attend(qkv, seg_col, seg_row, norm0)
        else:
            part = qkv.reshape(rows, 3, n_f, wide)
            part = lax.all_to_all(part, "fsdp", split_axis=2, concat_axis=0, tiled=True)
            part = part.reshape(row_len, 3, heads_here, HEAD_DIM)
            q, k, v = (part[:, i].transpose(1, 0, 2) for i in range(3))
            att_score = jnp.einsum("hqe,hke->hqk", q, k, preferred_element_type=f32) * HEAD_DIM ** (-0.5)
            same = seg[:, None] == seg[None, :]
            att_score = jnp.where(same[None], att_score, -1000000000.0)
            att_top = jnp.max(att_score, axis=-1, keepdims=True)
            att_power = jnp.exp(att_score - att_top)
            att_soft = att_power / jnp.sum(att_power, axis=-1, keepdims=True)
            att = att_soft.astype(bf16)
            mixed_h = jnp.einsum("hqk,hke->qhe", att, v, preferred_element_type=f32)
            mixed_h = mixed_h.reshape(row_len, wide).astype(bf16)
            mixed_all = lax.all_gather(mixed_h, "fsdp", axis=1, tiled=True)
            mixed = lax.dynamic_slice_in_dim(mixed_all, own * rows, rows, axis=0)
        h1 = h0 + mm(mixed, w_out)
        norm1, unit1, scale1 = norm_forward(h1, small[3], small[4])
        up = mm(norm1, w_up)
        gate = 0.5 * (1.0 + lax.erf(up * (2.0**-0.5)))
        lifted = (up * gate).astype(bf16)
        lifted_all = ag(lifted)
        h2 = h1 + mm_t(lifted, w_down)
        norm2, unit2, scale2 = norm_forward(h2, small[5], small[6])
        predicted = mm(norm2, w_pred) * D ** (-0.5)
        error = predicted - target
        weighted = pixel_weight * error
        numerator = jnp.sum(weighted * error)

        d_pred = (weighted * (2.0 * D ** (-0.5) / total)).astype(bf16)
        d_norm2 = mm_t(d_pred, w_pred)
        d_h2, d_gain2, d_off2 = norm_backward(d_norm2, unit2, scale2, small[5])
        d_out = d_h2.astype(bf16)
        slope = gate + up * jnp.exp(-0.5 * up * up) * 0.3989422804014327
        d_up = (mm(d_out, w_down) * slope).astype(bf16)
        d_norm1 = mm_t(d_up, w_up)
        d_in, d_gain1, d_off1 = norm_backward(d_norm1, unit1, scale1, small[3])
        d_h1 = d_h2 + d_in
        if fast:
            d_qkv, d_parts, d_proj_all, norm1_t, out_t, norm2_t = attend_back(
                d_h1.astype(bf16), rear, parts, seg_col, seg_row, norm1, d_out, norm2
            )
        else:
            d_proj_all = ag(d_h1.astype(bf16))
            w_out_own = lax.dynamic_slice_in_dim(w_out, own * wide, wide, axis=0)
            d_mixed = mm_t(d_proj_all, w_out_own).astype(bf16).reshape(row_len, heads_here, HEAD_DIM).transpose(1, 0, 2)
            d_att = jnp.einsum("hqe,hke->hqk", d_mixed, v, preferred_element_type=f32)
            d_v = jnp.einsum("hqk,hqe->khe", att, d_mixed, preferred_element_type=f32)
            lean = jnp.sum(att_soft * d_att, axis=-1, keepdims=True)
            d_score = (att_soft * (d_att - lean) * HEAD_DIM ** (-0.5)).astype(bf16)
            d_q = jnp.einsum("hqk,hke->qhe", d_score, k, preferred_element_type=f32)
            d_k = jnp.einsum("hqk,hqe->khe", d_score, q, preferred_element_type=f32)
            d_part = jnp.stack([d_q, d_k, d_v], axis=1).astype(bf16).reshape(row_len, 3, 1, wide)
            d_qkv_all = lax.all_gather(d_part, "fsdp", axis=2, tiled=True).reshape(row_len, 3 * D)
            d_qkv = lax.dynamic_slice_in_dim(d_qkv_all, own * rows, rows, axis=0)
        d_norm0 = mm_t(d_qkv, w_qkv)
        d_in, d_gain0, d_off0 = norm_backward(d_norm0, unit0, scale0, small[1])
        d_h0 = d_h1 + d_in
        d_agg = d_h0.astype(bf16)
        d_mixed_a = mm_t(agg_out, d_agg).astype(bf16).reshape(HEADS, HEAD_DIM, rows)
        pulled = exact("hec,hel->hcl", table_v, d_mixed_a.astype(f32)) * pix_f[None]
        d_share = exact("vc,hcl->hvl", expand.astype(f32), pulled)
        lean_a = jnp.sum(soft * d_share, axis=1, keepdims=True)
        d_score_a = (soft * (d_share - lean_a) * HEAD_DIM ** (-0.5)).astype(bf16)
        spread_score = jnp.einsum("vc,hvl->hcl", expand, d_score_a, preferred_element_type=f32)
        d_folded = jnp.sum(spread_score * pix_f[None], axis=2)
        d_table_v = exact("hel,hcl->hec", d_mixed_a.astype(f32), lifted_share).reshape(D, MIX)
        d_table_k = (query[:, :, None] * d_folded[:, None, :]).reshape(D, MIX)
        d_query = jnp.sum(d_folded[:, None, :] * table_k, axis=2).reshape(D)
        d_bias = jnp.sum(d_h0, axis=0)
        narrow = jnp.stack(
            [d_query, d_gain0, d_off0, d_gain1, d_off1, d_gain2, d_off2, lead * d_bias, d_bias]
            + [jnp.zeros((D,), f32)] * 7
        )
        d_table = jnp.concatenate([d_table_k, d_table_v], axis=0)
        if fast:

            def sorted_rows(array):
                return array.reshape(4, 2, n_f, strip, array.shape[1])

            lane = lax.broadcasted_iota(jnp.int32, (8, 128), 1)
            r_agg, r_attn, r_mlp, r_io, r_small, stat = gradient_blocks(
                [sorted_rows(part) for part in (norm1_t, out_t, norm0_t)]
                + [mixed_t.reshape(2, n_f, strip, row_len)]
                + [sorted_rows(part) for part in (mixed_a, norm2_t, d_agg.T)]
                + [d_proj_all, d_parts, d_up, lifted_all, d_agg, jnp.pad(d_pred, ((0, 0), (0, 256 - WIDTH)))]
                + [onehot_all, d_table.astype(bf16), narrow, sorted_rows(head)],
                jnp.where(lane == 1, numerator, 0.0),
            )
            r_small = r_small[:9].T
            squares, numerator = stat[0, 0], stat[0, 1]
        else:
            d_table, narrow = lax.psum((d_table, narrow), "fsdp")
            source = jnp.arange(D)
            pick = (source // strip) % n_f == own
            place = (source // (strip * n_f)) * strip + source % strip
            choose = (pick[:, None] & (place[:, None] == jnp.arange(n_dp * strip)[None, :])).astype(bf16)

            def mine(array):
                whole = array.reshape(n_dp, n_f, strip, array.shape[1])
                return lax.dynamic_index_in_dim(whole, own, 1, False).reshape(n_dp * strip, array.shape[1])

            def weight_grad(features, grads):
                return t_mm(mm(features, choose).astype(bf16), grads)

            def gap(width):
                return jnp.zeros((n_dp * strip, width), f32)

            d_agg_all = ag(d_agg)
            g_kv = exact("dc,xc->dx", mine(w240).astype(f32), d_table)
            g_240 = exact("dx,xc->dc", mine(agg_kv).astype(f32), d_table)
            groups = (
                (g_kv, weight_grad(ag(mixed_a.T), d_agg_all)),
                (weight_grad(ag(norm0), d_qkv_all), weight_grad(mixed_all, d_proj_all)),
                (weight_grad(ag(norm1), ag(d_up)), weight_grad(ag(d_out), lifted_all)),
                (
                    g_240, weight_grad(ag(norm2), ag(d_pred)), gap(256 - WIDTH),
                    weight_grad(d_agg_all, onehot_all), mine(narrow.T)[:, :9], gap(256 - 9),
                ),
            )
            r_agg, r_attn, r_mlp, r_misc = (
                lax.psum_scatter(jnp.concatenate(g, axis=1), "dp", scatter_dimension=0, tiled=True) for g in groups
            )
            local_squares = sum(jnp.sum(piece * piece) for piece in (r_agg, r_attn, r_mlp, r_misc))
            squares, numerator = lax.psum((local_squares, numerator), ("dp", "fsdp"))
            r_io = jnp.concatenate(
                [
                    r_misc[:, :WIDTH], r_misc[:, 256 : 256 + WIDTH], r_misc[:, WIDTH : WIDTH + VARS],
                    r_misc[:, 512 : 512 + SPAN], jnp.zeros((strip, w_io.shape[1] - emb - SPAN), f32),
                ],
                axis=1,
            )
            r_small = r_misc[:, 768:777]
        reduced = (r_agg, r_attn, r_mlp, r_io, r_small)
        grad_norm = jnp.sqrt(squares)
        factor = jnp.minimum(1.0, clip_limit / grad_norm)
        loss = numerator / total
        step_value = step_count[0].astype(f32)
        results = [
            adamw(masters[i], reduced[i] * factor, firsts[i], seconds[i], step_value, learn_rates[i]) for i in range(5)
        ]
        return (loss, grad_norm) + tuple(results[i][j] for j in range(4) for i in range(5))

    return local


def solution(mesh):
    flat = P(("dp", "fsdp"), None)
    tokens = P("dp", "fsdp", None)
    return jax.shard_map(
        make_local(mesh.shape["dp"], mesh.shape["fsdp"]),
        mesh=mesh,
        in_specs=(tokens, tokens, tokens, P("dp", "fsdp"), P("dp", None), P("dp", None), P("dp"), P()) + (flat,) * 15,
        out_specs=(P(), P()) + (flat,) * 20,
        check_vma=False,
    )
```
